32 devices in a mesh: fsdp: 8 (over z, x), seq: 4 (over y, core).
Axes of the slice: x: 2, y: 2, z: 4, core: 2. Of those that a mesh axis runs over, the one named last changes fastest.
Arguments:
- tokens: bfloat16 [16384, 768], P(('fsdp', 'seq')), may hold values from -6 to 6
- read_memory: bfloat16 [8, 10, 768], P('fsdp'), may hold values from -6 to 6
- write_memory: bfloat16 [8, 10, 768], P('fsdp'), may hold values from -6 to 6
- lengths: int32 [8], P('fsdp'), may hold values from 1024 to 2048, as said below
- qkv_weight: bfloat16 [768, 2304], P('fsdp'), may hold values from -0.21875 to 0.21875
- qv_bias: bfloat16 [1536], P('fsdp'), may hold values from -1.5 to 1.5
- out_weight: bfloat16 [768, 768], P('fsdp'), may hold values from -6 to 6
- out_bias: bfloat16 [768], P('fsdp'), may hold values from -1.5 to 1.5
- norm1_gain: bfloat16 [768], P('fsdp'), may hold values from 0.5 to 1.5
- norm1_bias: bfloat16 [768], P('fsdp'), may hold values from -1.5 to 1.5
- up_weight: bfloat16 [768, 3072], P('fsdp'), may hold values from -0.21875 to 0.21875
- up_bias: bfloat16 [3072], P('fsdp'), may hold values from -1.5 to 1.5
- down_weight: bfloat16 [3072, 768], P('fsdp'), may hold values from -0.109375 to 0.109375
- down_bias: bfloat16 [768], P('fsdp'), may hold values from -1.5 to 1.5
- norm2_gain: bfloat16 [768], P('fsdp'), may hold values from 0.5 to 1.5
- norm2_bias: bfloat16 [768], P('fsdp'), may hold values from -1.5 to 1.5
- cotangent: bfloat16 [16384, 768], P(('fsdp', 'seq')), may hold values from -6 to 6
Outputs:
- output: bfloat16 [16384, 768], P(('fsdp', 'seq'))
- input_grad: float32 [16384, 768], P(('fsdp', 'seq'))
- read_grad: float32 [8, 10, 768], P('fsdp')
- write_grad: float32 [8, 10, 768], P('fsdp')
- qkv_weight_grad: float32 [768, 2304], P('fsdp')
- qv_bias_grad: float32 [1536], P('fsdp')
- out_weight_grad: float32 [768, 768], P('fsdp')
- out_bias_grad: float32 [768], P('fsdp')
- norm1_gain_grad: float32 [768], P('fsdp')
- norm1_bias_grad: float32 [768], P('fsdp')
- up_weight_grad: float32 [768, 3072], P('fsdp')
- up_bias_grad: float32 [3072], P('fsdp')
- down_weight_grad: float32 [3072, 768], P('fsdp')
- down_bias_grad: float32 [768], P('fsdp')
- norm2_gain_grad: float32 [768], P('fsdp')
- norm2_bias_grad: float32 [768], P('fsdp')
The draws below stay inside these ranges and needn't reach their ends.
Inputs may be any that keep to these rules, and one draw needn't show every extreme that they name: `lengths`: valid length of each slot in positions, counting its 10 read and 10 write memory tokens; in every draw some slot has length 2048 and some slot 1024.
All inputs are finite; a program needn't handle non-finite values.
Results may differ from the reference program's by a relative error of at most 0.017.
Values may be sent and summed in bfloat16 or wider, within the bound.
A program may use at most 128 MiB of HBM per device.

```python
import jax
import jax.numpy as jnp
from jax import lax

D = 768
HEADS = 12
HEAD = 64
FF = 3072
MEM = 10
SLOT = 2048
SHORTEST = 1024
SLOTS = 8
TOKENS = 16384


def draw_lengths(key, part):
    first_key, second_key, third_key = jax.random.split(key, 3)
    drawn = jax.random.randint(first_key, (SLOTS,), SHORTEST, SLOT + 1)
    longest = jax.random.randint(second_key, (), 0, SLOTS)
    shortest = (longest + 1 + jax.random.randint(third_key, (), 0, SLOTS - 1)) % SLOTS
    position = jnp.arange(SLOTS)
    drawn = jnp.where(position == longest, SLOT, drawn)
    return jnp.where(position == shortest, SHORTEST, drawn).astype(jnp.int32)


def with_spikes(values, rng, source, target, shards_of, factor):
    def block_of(dim):
        return (jnp.arange(values.shape[dim]) // (values.shape[dim] // shards_of)).reshape((-1,) + (1,) * (values.ndim - 1 - dim))

    near = jax.random.permutation(rng, shards_of)[block_of(target)]
    far = (block_of(target) + shards_of // 2) % shards_of
    return jnp.where((block_of(source) == near) | (block_of(source) == far), factor * values, values)


def shard_levels(own_key, shape, pieces, smallest, high):
    loudness = 1.0
    for dim, blocks in pieces:
        draws = jax.random.uniform(jax.random.fold_in(jax.random.fold_in(own_key, 6), dim), (blocks,), jnp.float32, smallest / len(pieces), high / len(pieces))
        loudness = loudness * jnp.repeat(jnp.exp(draws), shape[dim] // blocks).reshape((-1,) + (1,) * (len(shape) - 1 - dim))
    return loudness


def normal_values(key, dims, spread, bound, shards=(), held_as=jnp.bfloat16):
    entries = spread * jax.random.normal(key, dims, jnp.float32)
    if shards:
        entries = entries * shard_levels(key, dims, shards, -0.22, 0.18)
    return jnp.clip(entries, -bound, bound).astype(held_as)


def bell_draw_with(rng, shape, width, limit, pieces, heavy, kind=jnp.bfloat16):
    array = width * jax.random.normal(rng, shape, jnp.float32)
    if pieces:
        array = array * shard_levels(rng, shape, pieces, -0.22, 0.18)
    return jnp.clip(with_spikes(array, jax.random.fold_in(rng, 3), *heavy), -limit, limit).astype(kind)


def setup_inputs(seed: int = 0) -> dict:
    arg_keys = jax.random.split(jax.random.key(seed), 18)
    tokens = normal_values(arg_keys[0], (TOKENS, D), 1.0, 6.0, ((0, 32),))
    read_memory = normal_values(arg_keys[1], (SLOTS, MEM, D), 1.0, 6.0, ((0, 8),))
    write_memory = normal_values(arg_keys[2], (SLOTS, MEM, D), 1.0, 6.0, ((0, 8),))
    lengths = draw_lengths(jax.random.fold_in(arg_keys[17], 71), 0)
    qkv_weight = normal_values(arg_keys[4], (D, 3 * D), D ** -0.5, 0.21875, ((0, 8),))
    qv_bias = normal_values(arg_keys[5], (2 * D,), 0.3, 1.5, ((0, 8),))
    out_weight = normal_values(arg_keys[6], (D, D), (max(1, D // SLOT)) ** -0.5, 6.0, ((0, 8),))
    out_bias = normal_values(arg_keys[7], (D,), 0.3, 1.5, ((0, 8),))
    norm1_gain = jnp.clip(1.0 + 0.1 * jax.random.normal(arg_keys[8], (D,), jnp.float32), 0.5, 1.5).astype(jnp.bfloat16)
    norm1_bias = normal_values(arg_keys[9], (D,), 0.3, 1.5, ((0, 8),))
    up_weight = normal_values(arg_keys[10], (D, FF), D ** -0.5, 0.21875, ((0, 8),))
    up_bias = normal_values(arg_keys[11], (FF,), 0.3, 1.5, ((0, 8),))
    down_weight = normal_values(arg_keys[12], (FF, D), FF ** -0.5, 0.109375, ((0, 8),))
    down_bias = normal_values(arg_keys[13], (D,), 0.3, 1.5, ((0, 8),))
    norm2_gain = jnp.clip(1.0 + 0.1 * jax.random.normal(arg_keys[14], (D,), jnp.float32), 0.5, 1.5).astype(jnp.bfloat16)
    norm2_bias = normal_values(arg_keys[15], (D,), 0.3, 1.5, ((0, 8),))
    cotangent = bell_draw_with(arg_keys[16], (TOKENS, D), 1.0, 6.0, ((0, 32),), (0, 1, 32, 2.75))
    return dict(tokens=tokens, read_memory=read_memory, write_memory=write_memory, lengths=lengths, qkv_weight=qkv_weight, qv_bias=qv_bias, out_weight=out_weight, out_bias=out_bias, norm1_gain=norm1_gain, norm1_bias=norm1_bias, up_weight=up_weight, up_bias=up_bias, down_weight=down_weight, down_bias=down_bias, norm2_gain=norm2_gain, norm2_bias=norm2_bias, cotangent=cotangent)


@jax.custom_vjp
def low(v):
    return lax.optimization_barrier(v.astype(jnp.bfloat16)).astype(jnp.float32)

@jax.custom_vjp
def low_back(v):
    return v

def low_keep(v):
    return (low(v), None)

def low_pass(kept, grad):
    return (grad,)

def back_keep(v):
    return (v, None)

def back_low(kept, grad):
    return (low(grad),)
low.defvjp(low_keep, low_pass)
low_back.defvjp(back_keep, back_low)
norm_epsilon = 1e-06
masked_score = -1e+30
highest = lax.Precision.HIGHEST

def both_round(value):
    return low(low_back(value))

def normalize(values, gain_vec, shift_vec):
    centre = values - lax.optimization_barrier(jnp.mean(values, axis=-1, keepdims=True))
    factor = lax.rsqrt(lax.optimization_barrier(jnp.mean(centre * centre, axis=-1, keepdims=True)) + norm_epsilon)
    return centre * factor * gain_vec + shift_vec

def slot_layer(slot_rows, read_rows, write_rows, length, params):
    qkv_w, qv_b, out_w, out_b, gain_one, shift_one, up_w, up_b, down_w, down_b, gain_two, shift_two = params
    places = jnp.arange(SLOT, dtype=jnp.int32)
    in_slot = places < length
    write_start = length - MEM
    is_read = places < MEM
    is_write = (places >= write_start) & in_slot
    read_pick = jnp.take(read_rows, jnp.clip(places, 0, MEM - 1), axis=0)
    write_pick = jnp.take(write_rows, jnp.clip(places - write_start, 0, MEM - 1), axis=0)
    layer_in = jnp.where(is_read[:, None], read_pick, jnp.where(is_write[:, None], write_pick, slot_rows))
    projected = jnp.dot(layer_in, qkv_w, precision=highest)
    query = both_round(projected[:, :D] + qv_b[:D]).reshape(SLOT, HEADS, HEAD)
    keys = both_round(projected[:, D:2 * D]).reshape(SLOT, HEADS, HEAD)
    values = both_round(projected[:, 2 * D:] + qv_b[D:]).reshape(SLOT, HEADS, HEAD)
    block_rows = min(512, SLOT)

    def attend(block_index):
        query_block = lax.dynamic_slice_in_dim(query, block_index * block_rows, block_rows, 0)
        scores = jnp.einsum('qhd,khd->hqk', query_block, keys, precision=highest) * HEAD ** (-0.5)
        scores = low_back(scores)
        scores = jnp.where(in_slot[None, None, :], scores, masked_score)
        attn_probs = low(jax.nn.softmax(scores, axis=-1))
        return jnp.einsum('hqk,khd->qhd', attn_probs, values, precision=highest)
    mixed_blocks = lax.map(jax.checkpoint(attend), jnp.arange(SLOT // block_rows, dtype=jnp.int32))
    attended = both_round(mixed_blocks.reshape(SLOT, D))
    branch = low_back(jnp.dot(attended, out_w, precision=highest) + out_b)
    middle = normalize(layer_in + branch, gain_one, shift_one)
    up_pre = low_back(jnp.dot(low(middle), up_w, precision=highest) + up_b)
    hidden = low(jax.nn.gelu(up_pre, approximate=False))
    down_pre = low_back(jnp.dot(hidden, down_w, precision=highest) + down_b)
    final = normalize(middle + down_pre, gain_two, shift_two)
    return jnp.where(in_slot[:, None], final, 0.0)

def reference(tokens, read_memory, write_memory, lengths, qkv_weight, qv_bias, out_weight, out_bias, norm1_gain, norm1_bias, up_weight, up_bias, down_weight, down_bias, norm2_gain, norm2_bias, cotangent):
    params = (qkv_weight.astype(jnp.float32), qv_bias.astype(jnp.float32), out_weight.astype(jnp.float32), out_bias.astype(jnp.float32), norm1_gain.astype(jnp.float32), norm1_bias.astype(jnp.float32), up_weight.astype(jnp.float32), up_bias.astype(jnp.float32), down_weight.astype(jnp.float32), down_bias.astype(jnp.float32), norm2_gain.astype(jnp.float32), norm2_bias.astype(jnp.float32))
    all_rows = tokens.astype(jnp.float32).reshape(SLOTS, SLOT, D)
    all_cot = cotangent.astype(jnp.float32).reshape(SLOTS, SLOT, D)
    starting = jax.tree.map(jnp.zeros_like, params)

    def slot_step(running, slot_item):
        slot_rows, read_rows, write_rows, length, cot_rows = slot_item

        def slot_apply(rows_in, read_in, write_in, params_in):
            return slot_layer(rows_in, read_in, write_in, length, params_in)
        result, pullback = jax.vjp(slot_apply, slot_rows, read_rows, write_rows, params)
        grad_rows, grad_read, grad_write, grad_params = pullback(cot_rows)
        running = jax.tree.map(jnp.add, running, grad_params)
        return (running, (result.astype(jnp.bfloat16), grad_rows, grad_read, grad_write))
    totals, (outputs, grad_rows, grad_read, grad_write) = lax.scan(slot_step, starting, (all_rows, read_memory.astype(jnp.float32), write_memory.astype(jnp.float32), lengths, all_cot))
    return (outputs.reshape(TOKENS, D), grad_rows.reshape(TOKENS, D), grad_read, grad_write, totals[0], totals[1], totals[2], totals[3], totals[4], totals[5], totals[6], totals[7], totals[8], totals[9], totals[10], totals[11])
```

```python
from functools import partial

import jax
import jax.numpy as jnp
from jax import lax
from jax.experimental import pallas as pl
from jax.experimental.pallas import tpu as pltpu
from jax.sharding import PartitionSpec as P

HEAD = 64
MEM = 10
WIDE = 128
VMEM_BYTES = 64000 * 1024

norm_epsilon = 1e-06
masked_score = -1e30
low = jnp.bfloat16
full = jnp.float32

NN = (((1,), (0,)), ((), ()))
NT = (((1,), (1,)), ((), ()))
TN = (((0,), (0,)), ((), ()))
TT = (((0,), (1,)), ((), ()))


def mul(left, right, dims=NN):
    return lax.dot_general(left, right, dims, preferred_element_type=full)


def three_parts(value):
    high = value.astype(low)
    rest = value - high.astype(full)
    middle = rest.astype(low)
    return high, middle, (rest - middle.astype(full)).astype(low)


def stack_rows(rows, columns):
    place = lax.broadcasted_iota(jnp.int32, (HEAD, columns), 0)
    block = jnp.zeros((HEAD, columns), full)
    for index, row in enumerate(rows):
        block = jnp.where(place == index, row, block)
    return block.astype(low)


def project_heads(length, rows_ref, weight_ref, bias_ref, q_x, k_t, v_x, k_wide, v_wide):
    slot_rows = rows_ref.shape[0]
    head_cols = k_t.shape[0]
    heads = head_cols // HEAD
    bias = jnp.transpose(bias_ref[...])[:, 0:1]
    step = 512
    for start in range(0, slot_rows, step):
        lanes = slice(start, start + step)
        made = mul(weight_ref[...], rows_ref[lanes, :], TT) + bias[: 3 * head_cols]
        query = made[:head_cols].astype(low) * jnp.asarray(HEAD**-0.5, low)
        k_t[:, lanes] = made[head_cols : 2 * head_cols].astype(low)
        value = made[2 * head_cols :].astype(low)
        place = start + lax.broadcasted_iota(jnp.int32, (1, step), 1)
        key_bias = jnp.where(place < length, 0.0, masked_score)
        one = jnp.ones((1, step), full)
        query_extra = stack_rows([one], step)
        key_extra = stack_rows([key_bias, one, one, one], step)
        value_extra = stack_rows([one, one, one], step)
        for h in range(heads):
            own = slice(h * HEAD, (h + 1) * HEAD)
            q_x[h, :HEAD, lanes] = query[own]
            q_x[h, HEAD:, lanes] = query_extra
            v_x[h, :HEAD, lanes] = value[own]
            v_x[h, HEAD:, lanes] = value_extra
            k_wide[h, lanes, :] = jnp.transpose(
                jnp.concatenate([k_t[own, lanes], key_extra], axis=0)
            )
            v_wide[h, lanes, :] = jnp.transpose(v_x[h, :, lanes])


def attend_block(h, lanes, q_x, k_wide, v_x, mixed, mixed_low, row_stats):
    scores = mul(k_wide[h], q_x[h, :, lanes])
    row_max = jnp.max(scores, axis=0, keepdims=True)
    probs = jnp.exp(scores - row_max).astype(low)
    total = mul(v_x[h, : HEAD + 16], probs)
    row_sum = total[HEAD : HEAD + 1]
    own = pl.ds(h * HEAD, HEAD)
    result = total[:HEAD] / row_sum
    mixed[own, lanes] = result
    mixed_low[own, lanes] = result.astype(low)
    row_stats[h, :, lanes] = jnp.broadcast_to(row_max + jnp.log(row_sum), (8, result.shape[1]))


def forward_kernel(
    length_ref, rows_ref, weight_ref, bias_ref, q_x, k_t, k_wide, v_wide, mixed, mixed_low, row_stats, v_x
):
    project_heads(length_ref[0], rows_ref, weight_ref, bias_ref, q_x, k_t, v_x, k_wide, v_wide)
    heads = q_x.shape[0]
    block = 512
    blocks = q_x.shape[2] // block

    def step(index, carry):
        h = index // blocks
        start = pl.multiple_of(lax.rem(index, blocks) * block, block)
        attend_block(h, pl.ds(start, block), q_x, k_wide, v_x, mixed, mixed_low, row_stats)
        return carry

    lax.fori_loop(0, heads * blocks, step, 0)


def attention_forward(length, rows, weight, bias):
    slot_rows = rows.shape[0]
    head_cols = weight.shape[1] // 3
    heads = head_cols // HEAD
    vmem = pl.BlockSpec(memory_space=pltpu.VMEM)
    return pl.pallas_call(
        forward_kernel,
        in_specs=[pl.BlockSpec(memory_space=pltpu.SMEM), vmem, vmem, vmem],
        out_specs=[vmem] * 7,
        out_shape=[
            jax.ShapeDtypeStruct((heads, WIDE, slot_rows), low),
            jax.ShapeDtypeStruct((head_cols, slot_rows), low),
            jax.ShapeDtypeStruct((heads, slot_rows, WIDE), low),
            jax.ShapeDtypeStruct((heads, slot_rows, WIDE), low),
            jax.ShapeDtypeStruct((head_cols, slot_rows), full),
            jax.ShapeDtypeStruct((head_cols, slot_rows), low),
            jax.ShapeDtypeStruct((heads, 8, slot_rows), full),
        ],
        scratch_shapes=[pltpu.VMEM((heads, WIDE, slot_rows), low)],
        compiler_params=pltpu.CompilerParams(vmem_limit_bytes=VMEM_BYTES),
        name="attention_forward",
    )(length, rows, weight, bias)


def prepare_backward(h, q_x, do_x, grad_t, mixed, row_stats):
    slot_rows = grad_t.shape[1]
    own = slice(h * HEAD, (h + 1) * HEAD)
    grad = grad_t[own, :]
    delta = jnp.sum(grad.astype(full) * mixed[own, :], axis=0, keepdims=True)
    parts = [part.astype(full) for part in three_parts(-delta)]
    do_x[h, :HEAD, :] = grad
    do_x[h, HEAD:, :] = stack_rows(parts, slot_rows)
    parts = [part.astype(full) for part in three_parts(-row_stats[h, 0:1, :])]
    q_x[h, HEAD:, :] = stack_rows([jnp.ones((1, slot_rows), full)] + parts, slot_rows)


def attend_back_block(h, lanes, first, q_x, do_x, k_t, k_wide, v_wide, grad_q, grad_k, grad_v):
    own = pl.ds(h * HEAD, HEAD)
    probs = jnp.exp(mul(k_wide[h], q_x[h, :, lanes]))
    grad_scores = (probs * mul(v_wide[h], do_x[h, :, lanes])).astype(low)
    value_part = mul(do_x[h, :HEAD, lanes], probs.astype(low), NT)
    key_part = mul(q_x[h, :HEAD, lanes], grad_scores, NT)

    @pl.when(first)
    def _():
        grad_v[...] = value_part
        grad_k[...] = key_part

    @pl.when(jnp.logical_not(first))
    def _():
        grad_v[...] += value_part
        grad_k[...] += key_part

    grad_q[own, lanes] = (mul(k_t[own, :], grad_scores) * HEAD**-0.5).astype(low)


def backward_kernel(
    q_in, k_t, k_wide, v_wide, mixed, row_stats, grad_t, rows_ref, weight_ref,
    partial_out, weight_out, sums_out, q_x, do_x, grads, grad_k, grad_v,
):
    heads, _, slot_rows = q_in.shape
    head_cols = heads * HEAD
    q_x[:, :HEAD, :] = q_in[:, :HEAD, :]
    for h in range(heads):
        prepare_backward(h, q_x, do_x, grad_t, mixed, row_stats)
    block = 512
    blocks = slot_rows // block

    def step(index, carry):
        h = index // blocks
        turn = lax.rem(index, blocks)
        start = pl.multiple_of(turn * block, block)
        attend_back_block(
            h, pl.ds(start, block), turn == 0, q_x, do_x, k_t, k_wide, v_wide,
            grads, grad_k, grad_v,
        )

        @pl.when(turn == blocks - 1)
        def _():
            grads[pl.ds(head_cols + h * HEAD, HEAD), :] = grad_k[...].astype(low)
            grads[pl.ds(2 * head_cols + h * HEAD, HEAD), :] = grad_v[...].astype(low)

        return carry

    lax.fori_loop(0, heads * blocks, step, 0)
    for start in range(0, slot_rows, block):
        partial_out[start : start + block, :] = mul(
            grads[:, start : start + block], weight_ref[...], TT
        ).astype(partial_out.dtype)
    weight_out[...] = jnp.transpose(mul(grads[...], rows_ref[...])).astype(weight_out.dtype)
    sums_out[...] = jnp.broadcast_to(
        jnp.sum(grads[...].astype(full), axis=1, keepdims=True), sums_out.shape
    )


def attention_backward(q_x, k_t, k_wide, v_wide, mixed, row_stats, grad_t, rows, weight):
    heads, _, slot_rows = q_x.shape
    width, all_cols = weight.shape
    vmem = pl.BlockSpec(memory_space=pltpu.VMEM)
    return pl.pallas_call(
        backward_kernel,
        in_specs=[vmem] * 9,
        out_specs=[vmem] * 3,
        out_shape=[
            jax.ShapeDtypeStruct((slot_rows, width), low),
            jax.ShapeDtypeStruct((width, all_cols), low),
            jax.ShapeDtypeStruct((all_cols, WIDE), full),
        ],
        scratch_shapes=[
            pltpu.VMEM((heads, WIDE, slot_rows), low),
            pltpu.VMEM((heads, WIDE, slot_rows), low),
            pltpu.VMEM((all_cols, slot_rows), low),
            pltpu.VMEM((HEAD, slot_rows), full),
            pltpu.VMEM((HEAD, slot_rows), full),
        ],
        compiler_params=pltpu.CompilerParams(vmem_limit_bytes=VMEM_BYTES),
        name="attention_backward",
    )(q_x, k_t, k_wide, v_wide, mixed, row_stats, grad_t, rows, weight)


def normalize(values, gain_vec, shift_vec):
    centre = values - jnp.mean(values, axis=-1, keepdims=True)
    factor = lax.rsqrt(jnp.mean(centre * centre, axis=-1, keepdims=True) + norm_epsilon)
    return centre * factor * gain_vec + shift_vec


def column_sums(values):
    return jnp.sum(values, axis=0, dtype=full)


def per_device(
    tokens, read_memory, write_memory, lengths, qkv_weight, qv_bias, out_weight, out_bias, norm1_gain,
    norm1_bias, up_weight, up_bias, down_weight, down_bias, norm2_gain, norm2_bias, cotangent,
):
    seq_count = lax.axis_size("seq")
    fsdp_count = lax.axis_size("fsdp")
    seq_place = lax.axis_index("seq")
    local_rows, width = tokens.shape
    head_cols = width // seq_count
    shard = width // fsdp_count
    length = lengths[0]
    places = seq_place * local_rows + jnp.arange(local_rows, dtype=jnp.int32)
    in_slot = (places < length)[:, None]
    memory_slots = jnp.arange(MEM, dtype=jnp.int32)
    pick_read = places[:, None] == memory_slots[None, :]
    pick_write = places[:, None] == length - MEM + memory_slots[None, :]
    is_memory = jnp.any(pick_read | pick_write, axis=1)[:, None]
    picks = jnp.concatenate([pick_read, pick_write], axis=1).astype(full)
    memory = jnp.concatenate([read_memory[0], write_memory[0]], axis=0)
    layer_in = jnp.where(is_memory, mul(picks.astype(low), memory).astype(low), tokens)

    rows = lax.all_gather(layer_in, "seq", axis=0, tiled=True)
    own_shard = lax.dynamic_slice_in_dim(
        qkv_weight.reshape(shard, 3, seq_count, head_cols), seq_place, 1, 2
    ).reshape(shard, 3 * head_cols)
    weight = lax.all_gather(own_shard, "fsdp", axis=0, tiled=True)
    vectors = (qv_bias, out_bias, norm1_gain, norm1_bias, up_bias, down_bias, norm2_gain, norm2_bias)
    packed = lax.all_gather(jnp.concatenate(vectors).reshape(1, -1), "fsdp", axis=0, tiled=True).astype(full)
    whole, start = [], 0
    for vector in vectors:
        whole.append(packed[:, start : start + vector.shape[0]].reshape(-1))
        start += vector.shape[0]
    qv_vec, out_vec, gain_one, shift_one, up_vec, down_vec, gain_two, shift_two = whole
    own_qv = lax.dynamic_slice_in_dim(qv_vec.reshape(2, seq_count, head_cols), seq_place, 1, 1)
    bias = jnp.concatenate(
        [own_qv[0, 0], jnp.zeros((head_cols,), full), own_qv[1, 0], jnp.zeros((-3 * head_cols % WIDE,), full)]
    )
    bias = jnp.broadcast_to(bias, (8, bias.shape[0]))
    out_full = lax.all_gather(out_weight, "fsdp", axis=0, tiled=True)
    up_full = lax.all_gather(up_weight, "fsdp", axis=0, tiled=True)
    down_full = lax.all_gather(down_weight, "fsdp", axis=0, tiled=True)

    q_x, k_t, k_wide, v_wide, mixed, mixed_low, row_stats = attention_forward(lengths, rows, weight, bias)
    attended = lax.all_to_all(mixed_low, "seq", split_axis=1, concat_axis=0, tiled=True)
    resid_one = layer_in.astype(full) + mul(attended, out_full, TN) + out_vec
    middle, norm_one_back = jax.vjp(normalize, resid_one, gain_one, shift_one)
    middle_low = middle.astype(low)
    up_pre = mul(middle_low, up_full) + up_vec
    gelu_out, gelu_back = jax.vjp(partial(jax.nn.gelu, approximate=False), up_pre)
    hidden = gelu_out.astype(low)
    down_pre = mul(hidden, down_full) + down_vec
    final, norm_two_back = jax.vjp(normalize, middle + down_pre, gain_two, shift_two)
    output = jnp.where(in_slot, final, 0.0).astype(low)
    grad_final = jnp.where(in_slot, cotangent.astype(full), 0.0)
    grad_resid_two, grad_gain_two, grad_shift_two = norm_two_back(grad_final)
    grad_down = grad_resid_two.astype(low)
    grad_down_weight = mul(hidden, grad_down, TN)
    (grad_up_pre,) = gelu_back(mul(grad_down, down_full, NT))
    grad_up = grad_up_pre.astype(low)
    grad_up_weight = mul(middle_low, grad_up, TN)
    grad_middle = grad_resid_two + mul(grad_up, up_full, NT)
    grad_resid_one, grad_gain_one, grad_shift_one = norm_one_back(grad_middle)
    grad_branch = grad_resid_one.astype(low)
    grad_out_weight = mul(attended, grad_branch)
    grad_attended = mul(out_full, grad_branch, NT).astype(low)
    grad_t = lax.all_to_all(grad_attended, "seq", split_axis=0, concat_axis=1, tiled=True)
    partial_in, weight_part, sums = attention_backward(
        q_x, k_t, k_wide, v_wide, mixed, row_stats, grad_t, rows, weight
    )
    from_heads = lax.psum_scatter(partial_in, "seq", scatter_dimension=0, tiled=True).astype(full)
    grad_layer_in = grad_resid_one + from_heads
    input_grad = jnp.where(is_memory, 0.0, grad_layer_in)
    grad_memory = lax.dot_general(
        picks, grad_layer_in, TN, precision=lax.Precision.HIGHEST, preferred_element_type=full
    )
    grad_memory = lax.psum(grad_memory.astype(low), "seq").astype(full)

    sums = sums[:, 0]
    own_sums = jnp.stack([sums[:head_cols], sums[2 * head_cols :]])[:, None]
    zero_qv = jnp.zeros((2, seq_count, head_cols), full)
    qv_grad = lax.dynamic_update_slice_in_dim(zero_qv, own_sums, seq_place, 1).reshape(-1)
    vector_grads = [
        qv_grad, column_sums(grad_branch), grad_gain_one, grad_shift_one, column_sums(grad_up),
        column_sums(grad_down), grad_gain_two, grad_shift_two,
    ]
    packed_grad = jnp.concatenate([v.reshape(fsdp_count, -1) for v in vector_grads], axis=1)
    packed_sum = lax.psum(packed_grad, ("fsdp", "seq"))
    own_vectors = lax.dynamic_index_in_dim(packed_sum, lax.axis_index("fsdp"), 0, False)
    vector_outs, start = [], 0
    for vector in vectors:
        vector_outs.append(own_vectors[start : start + vector.shape[0]])
        start += vector.shape[0]
    qv_out, out_b_out, gain_one_out, shift_one_out, up_b_out, down_b_out, gain_two_out, shift_two_out = vector_outs

    def both_axes(part):
        piece = lax.psum_scatter(part.astype(low), "fsdp", scatter_dimension=0, tiled=True)
        return lax.psum(piece, "seq").astype(full)

    qkv_piece = lax.psum_scatter(weight_part, "fsdp", scatter_dimension=0, tiled=True)
    qkv_parts = lax.all_gather(qkv_piece, "seq", axis=0).reshape(seq_count, shard, 3, head_cols)
    qkv_out = jnp.transpose(qkv_parts, (1, 2, 0, 3)).reshape(shard, 3 * width).astype(full)
    return (
        output, input_grad, grad_memory[None, :MEM], grad_memory[None, MEM:], qkv_out, qv_out,
        both_axes(grad_out_weight), out_b_out, gain_one_out, shift_one_out,
        both_axes(grad_up_weight), up_b_out, both_axes(grad_down_weight), down_b_out,
        gain_two_out, shift_two_out,
    )


def solution(mesh):
    rows, piece = P(("fsdp", "seq"), None), P("fsdp")
    matrix, memory = P("fsdp", None), P("fsdp", None, None)
    in_specs = (
        rows, memory, memory, piece, matrix, piece, matrix, piece, piece, piece, matrix, piece, matrix,
        piece, piece, piece, rows,
    )
    out_specs = (
        rows, rows, memory, memory, matrix, piece, matrix, piece, piece, piece, matrix, piece, matrix,
        piece, piece, piece,
    )
    return jax.shard_map(per_device, mesh=mesh, in_specs=in_specs, out_specs=out_specs, check_vma=False)
```

```python
from functools import partial

import jax
import jax.numpy as jnp
from jax import lax
from jax.experimental import pallas as pl
from jax.experimental.pallas import tpu as pltpu
from jax.sharding import PartitionSpec as P

HEAD = 64
MEM = 10
WIDE = 128
VMEM_BYTES = 64000 * 1024

norm_epsilon = 1e-06
masked_score = -1e30
low = jnp.bfloat16
full = jnp.float32

NN = (((1,), (0,)), ((), ()))
NT = (((1,), (1,)), ((), ()))
TN = (((0,), (0,)), ((), ()))
TT = (((0,), (1,)), ((), ()))


def mul(left, right, dims=NN):
    return lax.dot_general(left, right, dims, preferred_element_type=full)


def three_parts(value):
    high = value.astype(low)
    rest = value - high.astype(full)
    middle = rest.astype(low)
    return high, middle, (rest - middle.astype(full)).astype(low)


def stack_rows(rows, columns):
    place = lax.broadcasted_iota(jnp.int32, (HEAD, columns), 0)
    block = jnp.zeros((HEAD, columns), full)
    for index, row in enumerate(rows):
        block = jnp.where(place == index, row, block)
    return block.astype(low)


def project_block(start, length, rows_ref, weight_ref, bias_q, bias_v, q_x, k_t, v_x, k_wide, v_wide, step):
    head_cols = k_t.shape[0]
    lanes = pl.ds(start, step)
    made = mul(weight_ref[...], rows_ref[lanes, :], TT)
    query = (made[:head_cols] + bias_q).astype(low) * jnp.asarray(HEAD**-0.5, low)
    k_t[:, lanes] = made[head_cols : 2 * head_cols].astype(low)
    value = (made[2 * head_cols :] + bias_v).astype(low)
    place = start + lax.broadcasted_iota(jnp.int32, (1, step), 1)
    key_bias = jnp.where(place < length, 0.0, masked_score)
    one = jnp.ones((1, step), full)
    query_extra = stack_rows([one], step)
    key_extra = stack_rows([key_bias, one, one, one], step)
    value_extra = stack_rows([one, one, one], step)
    for h in range(head_cols // HEAD):
        own = slice(h * HEAD, (h + 1) * HEAD)
        q_x[h, :HEAD, lanes] = query[own]
        q_x[h, HEAD:, lanes] = query_extra
        v_x[h, :HEAD, lanes] = value[own]
        v_x[h, HEAD:, lanes] = value_extra
        k_wide[h, lanes, :] = jnp.transpose(jnp.concatenate([k_t[own, lanes], key_extra], axis=0))
        v_wide[h, lanes, :] = jnp.transpose(v_x[h, :, lanes])


def project_heads(length, rows_ref, weight_ref, bias_ref, q_x, k_t, v_x, k_wide, v_wide):
    head_cols = k_t.shape[0]
    bias = jnp.transpose(bias_ref[...])[:, 0:1]
    for start in range(0, rows_ref.shape[0], 512):
        project_block(
            start, length, rows_ref, weight_ref, bias[:head_cols], bias[2 * head_cols : 3 * head_cols],
            q_x, k_t, v_x, k_wide, v_wide, 512,
        )


def attend_block(h, lanes, q_x, k_wide, v_x, mixed, mixed_low, row_stats):
    scores = mul(k_wide[h], q_x[h, :, lanes])
    row_max = jnp.max(scores, axis=0, keepdims=True)
    probs = jnp.exp(scores - row_max).astype(low)
    total = mul(v_x[h, : HEAD + 16], probs)
    row_sum = total[HEAD : HEAD + 1]
    own = pl.ds(h * HEAD, HEAD)
    result = total[:HEAD] / row_sum
    mixed[own, lanes] = result
    mixed_low[own, lanes] = result.astype(low)
    row_stats[h, :, lanes] = jnp.broadcast_to(row_max + jnp.log(row_sum), (8, result.shape[1]))


def forward_kernel(
    length_ref, rows_ref, weight_ref, bias_ref, q_x, k_t, k_wide, v_wide, mixed, mixed_low, row_stats, v_x
):
    project_heads(length_ref[0], rows_ref, weight_ref, bias_ref, q_x, k_t, v_x, k_wide, v_wide)
    heads = q_x.shape[0]
    block = 512
    blocks = q_x.shape[2] // block

    def step(index, carry):
        h = index // blocks
        start = pl.multiple_of(lax.rem(index, blocks) * block, block)
        attend_block(h, pl.ds(start, block), q_x, k_wide, v_x, mixed, mixed_low, row_stats)
        return carry

    lax.fori_loop(0, heads * blocks, step, 0)


def attention_forward(length, rows, weight, bias):
    slot_rows = rows.shape[0]
    head_cols = weight.shape[1] // 3
    heads = head_cols // HEAD
    vmem = pl.BlockSpec(memory_space=pltpu.VMEM)
    return pl.pallas_call(
        forward_kernel,
        in_specs=[pl.BlockSpec(memory_space=pltpu.SMEM), vmem, vmem, vmem],
        out_specs=[vmem] * 7,
        out_shape=[
            jax.ShapeDtypeStruct((heads, WIDE, slot_rows), low),
            jax.ShapeDtypeStruct((head_cols, slot_rows), low),
            jax.ShapeDtypeStruct((heads, slot_rows, WIDE), low),
            jax.ShapeDtypeStruct((heads, slot_rows, WIDE), low),
            jax.ShapeDtypeStruct((head_cols, slot_rows), full),
            jax.ShapeDtypeStruct((head_cols, slot_rows), low),
            jax.ShapeDtypeStruct((heads, 8, slot_rows), full),
        ],
        scratch_shapes=[pltpu.VMEM((heads, WIDE, slot_rows), low)],
        compiler_params=pltpu.CompilerParams(vmem_limit_bytes=VMEM_BYTES),
        name="attention_forward",
    )(length, rows, weight, bias)


def prepare_backward(h, q_x, do_x, grad_t, mixed, row_stats):
    slot_rows = grad_t.shape[1]
    own = slice(h * HEAD, (h + 1) * HEAD)
    grad = grad_t[own, :]
    delta = jnp.sum(grad.astype(full) * mixed[own, :], axis=0, keepdims=True)
    parts = [part.astype(full) for part in three_parts(-delta)]
    do_x[h, :HEAD, :] = grad
    do_x[h, HEAD:, :] = stack_rows(parts, slot_rows)
    parts = [part.astype(full) for part in three_parts(-row_stats[h, 0:1, :])]
    q_x[h, HEAD:, :] = stack_rows([jnp.ones((1, slot_rows), full)] + parts, slot_rows)


def attend_back_block(h, lanes, first, q_x, do_x, k_t, k_wide, v_wide, grad_q, grad_k, grad_v):
    own = pl.ds(h * HEAD, HEAD)
    probs = jnp.exp(mul(k_wide[h], q_x[h, :, lanes]))
    grad_scores = (probs * mul(v_wide[h], do_x[h, :, lanes])).astype(low)
    value_part = mul(do_x[h, :HEAD, lanes], probs.astype(low), NT)
    key_part = mul(q_x[h, :HEAD, lanes], grad_scores, NT)

    @pl.when(first)
    def _():
        grad_v[...] = value_part
        grad_k[...] = key_part

    @pl.when(jnp.logical_not(first))
    def _():
        grad_v[...] += value_part
        grad_k[...] += key_part

    grad_q[own, lanes] = (mul(k_t[own, :], grad_scores) * HEAD**-0.5).astype(low)


def backward_kernel(
    q_in, k_t, k_wide, v_wide, mixed, row_stats, grad_t, rows_ref, weight_ref,
    partial_out, weight_out, sums_out, q_x, do_x, grads, grad_k, grad_v,
):
    heads, _, slot_rows = q_in.shape
    head_cols = heads * HEAD
    q_x[:, :HEAD, :] = q_in[:, :HEAD, :]
    for h in range(heads):
        prepare_backward(h, q_x, do_x, grad_t, mixed, row_stats)
    block = 512
    blocks = slot_rows // block

    def step(index, carry):
        h = index // blocks
        turn = lax.rem(index, blocks)
        start = pl.multiple_of(turn * block, block)
        attend_back_block(
            h, pl.ds(start, block), turn == 0, q_x, do_x, k_t, k_wide, v_wide,
            grads, grad_k, grad_v,
        )

        @pl.when(turn == blocks - 1)
        def _():
            grads[pl.ds(head_cols + h * HEAD, HEAD), :] = grad_k[...].astype(low)
            grads[pl.ds(2 * head_cols + h * HEAD, HEAD), :] = grad_v[...].astype(low)

        return carry

    lax.fori_loop(0, heads * blocks, step, 0)
    for start in range(0, slot_rows, block):
        partial_out[start : start + block, :] = mul(
            grads[:, start : start + block], weight_ref[...], TT
        ).astype(partial_out.dtype)
    weight_out[...] = jnp.transpose(mul(grads[...], rows_ref[...])).astype(weight_out.dtype)
    sums_out[...] = jnp.broadcast_to(
        jnp.sum(grads[...].astype(full), axis=1, keepdims=True), sums_out.shape
    )


def attention_backward(q_x, k_t, k_wide, v_wide, mixed, row_stats, grad_t, rows, weight):
    heads, _, slot_rows = q_x.shape
    width, all_cols = weight.shape
    vmem = pl.BlockSpec(memory_space=pltpu.VMEM)
    return pl.pallas_call(
        backward_kernel,
        in_specs=[vmem] * 9,
        out_specs=[vmem] * 3,
        out_shape=[
            jax.ShapeDtypeStruct((slot_rows, width), low),
            jax.ShapeDtypeStruct((width, all_cols), low),
            jax.ShapeDtypeStruct((all_cols, WIDE), full),
        ],
        scratch_shapes=[
            pltpu.VMEM((heads, WIDE, slot_rows), low),
            pltpu.VMEM((heads, WIDE, slot_rows), low),
            pltpu.VMEM((all_cols, slot_rows), low),
            pltpu.VMEM((HEAD, slot_rows), full),
            pltpu.VMEM((HEAD, slot_rows), full),
        ],
        compiler_params=pltpu.CompilerParams(vmem_limit_bytes=VMEM_BYTES),
        name="attention_backward",
    )(q_x, k_t, k_wide, v_wide, mixed, row_stats, grad_t, rows, weight)


MESH = pl.DeviceIdType.MESH
OWN, RELATIONS = 0, 7
UP_W, OUT_W, DOWN_W, QKV_W = 0, 1, 2, 3


def offset_of(relation):
    return (0, -1, -2, -3, 1, 2, 3)[relation]


class Place:
    def __init__(self):
        self.f, self.s = lax.axis_index("fsdp"), lax.axis_index("seq")
        self.z, self.x = self.f // 2, lax.rem(self.f, 2)
        self.y, self.c = self.s // 2, lax.rem(self.s, 2)
        self.core = (self.f, 2 * self.y + 1 - self.c)
        self.across_y = (self.f, 2 * (1 - self.y) + self.c)
        self.diagonal = (self.f, 2 * (1 - self.y) + 1 - self.c)
        self.across_x = (2 * self.z + 1 - self.x, self.s)
        self.above = (self.f + 2, self.s)
        self.below = (self.f - 2, self.s)

    def has(self, relation):
        offset = offset_of(relation)
        return (self.z + offset >= 0) & (self.z + offset <= 3)

    def source(self, relation, column):
        own_column = self.f + 2 * offset_of(relation)
        return own_column if column == 0 else own_column + 1 - 2 * self.x

    def member(self, turn):
        flip_y = 1 - turn // 2
        flip_c = lax.rem(turn, 2) if not isinstance(turn, int) else turn % 2
        flip_c = flip_c + (1 - 2 * flip_c) * (turn // 2)
        return 2 * lax.rem(self.y + flip_y, 2) + lax.rem(self.c + flip_c, 2)


def remote(src, dst, send, recv, where):
    return pltpu.make_async_remote_copy(
        src_ref=src, dst_ref=dst, send_sem=send, recv_sem=recv, device_id=where, device_id_type=MESH
    )


def greet(place, everyone):
    barrier = pltpu.get_barrier_semaphore()
    near = [place.core, place.across_y, place.diagonal, place.across_x]
    for where in near:
        pl.semaphore_signal(barrier, inc=1, device_id=where, device_id_type=MESH)

    @pl.when(place.z > 0)
    def _():
        pl.semaphore_signal(barrier, inc=1, device_id=place.below, device_id_type=MESH)

    @pl.when(place.z < 3)
    def _():
        pl.semaphore_signal(barrier, inc=1, device_id=place.above, device_id_type=MESH)

    ends = jnp.where((place.z == 0) | (place.z == 3), 1, 2)
    pl.semaphore_wait(barrier, len(near) + ends)


class Gather:
    def __init__(self, place, own, whole, sems):
        self.place, self.own, self.whole = place, own, whole
        (self.z_send, self.z_recv, self.x_send, self.x_recv, self.c_send, self.c_recv,
         self.y_send, self.y_recv, self.d_send, self.d_recv) = sems

    def piece(self, array, source, quarter=None):
        c = self.place.c
        ref = self.whole[array]
        if array == QKV_W:
            return ref.at[source]
        if array == DOWN_W:
            rows = ref.shape[0] // 8
            part = rows // 4
            quarter = self.place.s if quarter is None else quarter
            return ref.at[pl.ds(pl.multiple_of(source * rows + quarter * part, part), part)]
        rows, columns = ref.shape[0] // 8, ref.shape[1] // 2
        return ref.at[
            pl.ds(pl.multiple_of(source * rows, rows), rows),
            pl.ds(pl.multiple_of(c * columns, columns), columns),
        ]

    def own_piece(self, array):
        ref = self.own[array]
        if array == QKV_W:
            return ref
        if array == DOWN_W:
            part = ref.shape[0] // 4
            return ref.at[pl.ds(pl.multiple_of(self.place.s * part, part), part)]
        columns = ref.shape[1] // 2
        return ref.at[:, pl.ds(pl.multiple_of(self.place.c * columns, columns), columns)]

    def along_z(self, array, relation, way):
        here = self.piece(array, self.place.source(relation, 0))
        src = self.own_piece(array) if relation == OWN else here
        step = abs(offset_of(relation))
        where = self.place.above if way == 0 else self.place.below
        return remote(src, here, self.z_send.at[array, way, step], self.z_recv.at[array, way, step], where)

    def z_ways(self, relation):
        place = self.place
        ways = []
        if offset_of(relation) <= 0:
            ways.append((0, place.has(relation) & (place.z < 3)))
        if offset_of(relation) >= 0:
            ways.append((1, place.has(relation) & (place.z > 0)))
        return ways

    def wait_z(self, array, relation):
        way = 0 if offset_of(relation) < 0 else 1
        step = abs(offset_of(relation)) - 1
        here = self.piece(array, self.place.source(relation, 0))
        where = self.place.below if way == 0 else self.place.above
        remote(
            here, here, self.z_send.at[array, way, step], self.z_recv.at[array, way, step], where
        ).wait_recv()

    def over_x(self, array, relation):
        here = self.piece(array, self.place.source(relation, 0))
        src = self.own_piece(array) if relation == OWN else here
        return remote(
            src, here, self.x_send.at[array, relation], self.x_recv.at[array, relation], self.place.across_x
        )

    def from_x(self, array, relation):
        here = self.piece(array, self.place.source(relation, 1))
        return remote(
            here, here, self.x_send.at[array, relation], self.x_recv.at[array, relation], self.place.across_x
        )

    def to_core(self, array, relation, column):
        here = self.piece(array, self.place.source(relation, column))
        return remote(
            here, here, self.c_send.at[array, relation, column], self.c_recv.at[array, relation, column],
            self.place.core,
        )

    def over_y(self, relation, column):
        here = self.piece(DOWN_W, self.place.source(relation, column))
        return remote(
            here, here, self.y_send.at[relation, column], self.y_recv.at[relation, column], self.place.across_y
        )

    def far_quarter(self, relation, column):
        return self.piece(
            DOWN_W, self.place.source(relation, column), 2 * (1 - self.place.y) + self.place.c
        )

    def from_y(self, relation, column):
        here = self.far_quarter(relation, column)
        return remote(
            here, here, self.y_send.at[relation, column], self.y_recv.at[relation, column], self.place.across_y
        )

    def far_to_core(self, relation, column):
        here = self.far_quarter(relation, column)
        return remote(
            here, here, self.d_send.at[relation, column], self.d_recv.at[relation, column], self.place.core
        )

    def when(self, relation, action):
        if relation == OWN:
            action()
        else:
            pl.when(self.place.has(relation))(action)

    def arrive_z(self, array, relation):
        def action():
            if relation != OWN:
                self.wait_z(array, relation)
            for way, holds in self.z_ways(relation):
                pl.when(holds)(lambda way=way: self.along_z(array, relation, way).start())
            self.over_x(array, relation).start()
            if array != QKV_W and relation != OWN:
                self.to_core(array, relation, 0).start()
                if array == DOWN_W:
                    self.over_y(relation, 0).start()

        self.when(relation, action)

    def arrive_x(self, array, relation):
        def action():
            self.from_x(array, relation).wait_recv()
            if array != QKV_W:
                self.to_core(array, relation, 1).start()
                if array == DOWN_W:
                    self.over_y(relation, 1).start()

        self.when(relation, action)

    def arrive_y(self, relation, column):
        def action():
            self.from_y(relation, column).wait_recv()
            self.far_to_core(relation, column).start()

        if (relation, column) != (OWN, 0):
            self.when(relation, action)

    def finish(self, array):
        for relation in range(RELATIONS):
            def action():
                self.over_x(array, relation).wait_send()
                for way, holds in self.z_ways(relation):
                    pl.when(holds)(lambda way=way: self.along_z(array, relation, way).wait_send())
                if array == QKV_W:
                    return
                for column in range(2):
                    if (relation, column) == (OWN, 0):
                        continue
                    self.to_core(array, relation, column).wait()
                    if array == DOWN_W:
                        self.over_y(relation, column).wait_send()
                        self.far_to_core(relation, column).wait()

            self.when(relation, action)


def front_kernel(
    length_ref, rows_in, qkv_in, up_in, down_in, out_in,
    rows_ref, weight_ref, pieces, q_x, k_t, k_wide, v_wide, mixed, row_stats, up_full, down_full, out_full,
    attended,
    v_x, mixed_low, row_send, row_recv, far_send, far_recv, mix_send, mix_recv, local_sem, *gather_sems,
):
    place = Place()
    slot_rows, width = rows_ref.shape
    local_rows = rows_in.shape[0]
    head_cols = k_t.shape[0]
    heads = head_cols // HEAD
    own_shards = {UP_W: up_in, DOWN_W: down_in, OUT_W: out_in, QKV_W: qkv_in}
    whole = {UP_W: up_full, DOWN_W: down_full, OUT_W: out_full, QKV_W: pieces}
    gather = Gather(place, own_shards, whole, gather_sems)
    greet(place, None)

    halves = 2
    part = local_rows // halves

    def rows_of(member, half):
        return pl.ds(pl.multiple_of(member * local_rows + half * part, part), part)

    def send_rows(half, index):
        where = (place.core, place.across_y)[index]
        return remote(
            rows_in.at[pl.ds(half * part, part)], rows_ref.at[rows_of(place.s, half)],
            row_send.at[index, half], row_recv.at[index, half], where,
        )

    def rows_from(half, index):
        member = (2 * place.y + 1 - place.c, 2 * (1 - place.y) + place.c)[index]
        here = rows_ref.at[rows_of(member, half)]
        where = (place.core, place.across_y)[index]
        return remote(here, here, row_send.at[index, half], row_recv.at[index, half], where)

    def pass_rows(half, arriving):
        flip = place.c if not arriving else 1 - place.c
        here = rows_ref.at[rows_of(2 * (1 - place.y) + flip, half)]
        return remote(here, here, far_send.at[half], far_recv.at[half], place.core)

    for half in range(halves):
        send_rows(half, 1).start()
        send_rows(half, 0).start()
    gather.arrive_z(QKV_W, OWN)

    def own_copies():
        copies = []
        for index, array in enumerate((UP_W, DOWN_W, OUT_W)):
            rows = own_shards[array].shape[0]
            copies.append(pltpu.make_async_copy(
                own_shards[array], whole[array].at[pl.ds(pl.multiple_of(place.f * rows, rows), rows)],
                local_sem.at[index],
            ))
        copies.append(pltpu.make_async_copy(qkv_in, pieces.at[place.f], local_sem.at[3]))
        copies.append(pltpu.make_async_copy(
            rows_in, rows_ref.at[pl.ds(pl.multiple_of(place.s * local_rows, local_rows), local_rows)],
            local_sem.at[4],
        ))
        return copies

    for copy in own_copies():
        copy.start()

    for relation in (1, 4):
        gather.arrive_z(QKV_W, relation)
    gather.arrive_z(UP_W, OWN)
    for relation in (2, 5):
        gather.arrive_z(QKV_W, relation)
    gather.arrive_z(OUT_W, OWN)
    gather.arrive_z(DOWN_W, OWN)
    rows_from(0, 1).wait_recv()
    pass_rows(0, False).start()
    for relation in (3, 6):
        gather.arrive_z(QKV_W, relation)
    for relation in (1, 4):
        gather.arrive_z(UP_W, relation)
    for relation in range(RELATIONS):
        gather.arrive_x(QKV_W, relation)
    for copy in own_copies()[3:]:
        copy.wait()

    shard = weight_ref.shape[0] // 8
    for source in range(8):
        weight_ref[source * shard : (source + 1) * shard, :] = pieces[source, :shard, :]
    bias_q = jnp.transpose(pieces[place.s, shard : shard + 16, :].astype(full))[:head_cols, 0:1]
    bias_v = jnp.transpose(pieces[4 + place.s, shard : shard + 16, :].astype(full))[:head_cols, 0:1]
    length = length_ref[0]

    def project(member):
        start = pl.multiple_of(member * local_rows, local_rows)
        project_block(
            start, length, rows_ref, weight_ref, bias_q, bias_v, q_x, k_t, v_x, k_wide, v_wide, local_rows
        )

    project(place.s)
    for half in range(halves):
        rows_from(half, 0).wait_recv()
    project(2 * place.y + 1 - place.c)
    rows_from(1, 1).wait_recv()
    pass_rows(1, False).start()
    project(2 * (1 - place.y) + place.c)
    for relation in (1, 4):
        gather.arrive_z(OUT_W, relation)
        gather.arrive_z(DOWN_W, relation)
    for half in range(halves):
        pass_rows(half, True).wait_recv()
    project(2 * (1 - place.y) + 1 - place.c)

    def chores(step):
        if step == 0:
            gather.arrive_x(UP_W, OWN)
            for relation in (2, 5):
                gather.arrive_z(UP_W, relation)
        elif step == 2:
            for relation in (2, 5):
                gather.arrive_z(OUT_W, relation)
                gather.arrive_z(DOWN_W, relation)
            gather.arrive_x(OUT_W, OWN)
            gather.arrive_x(DOWN_W, OWN)
        elif step == 4:
            for relation in (1, 4):
                gather.arrive_x(UP_W, relation)
                gather.arrive_y(relation, 0)
            gather.arrive_y(OWN, 1)
        elif step == 6:
            for relation in (3, 6):
                gather.arrive_z(UP_W, relation)
            for relation in (1, 4):
                gather.arrive_x(OUT_W, relation)
                gather.arrive_x(DOWN_W, relation)
        elif step == 8:
            for relation in (3, 6):
                gather.arrive_z(OUT_W, relation)
                gather.arrive_z(DOWN_W, relation)
            for relation in (2, 5):
                gather.arrive_x(UP_W, relation)
                gather.arrive_y(relation, 0)
        elif step == 10:
            for relation in (2, 5):
                gather.arrive_x(OUT_W, relation)
                gather.arrive_x(DOWN_W, relation)
            for relation in (1, 4):
                gather.arrive_y(relation, 1)

    def send_mixed(h, turn, arriving=False):
        member = place.member(turn)
        own = pl.ds(pl.multiple_of(h * HEAD, HEAD), HEAD)
        lanes = pl.ds(pl.multiple_of(member * local_rows, local_rows), local_rows)
        owner = member if arriving else place.s
        there = attended.at[pl.ds(pl.multiple_of(owner * head_cols + h * HEAD, HEAD), HEAD)]
        return remote(
            mixed_low.at[own, lanes], there, mix_send.at[h, turn], mix_recv.at[h, turn], (place.f, member)
        )

    def keep_mixed(h):
        own = pl.ds(pl.multiple_of(h * HEAD, HEAD), HEAD)
        lanes = pl.ds(pl.multiple_of(place.s * local_rows, local_rows), local_rows)
        there = attended.at[pl.ds(pl.multiple_of(place.s * head_cols + h * HEAD, HEAD), HEAD)]
        return pltpu.make_async_copy(mixed_low.at[own, lanes], there, mix_send.at[h, 3])

    turns = slot_rows // local_rows

    def pass_on(index):
        h, turn = index // turns, lax.rem(index, turns)

        @pl.when(turn < turns - 1)
        def _():
            send_mixed(h, turn).start()

        @pl.when(turn == turns - 1)
        def _():
            keep_mixed(h).start()

    def step(index, carry):
        for when in range(0, 12, 2):
            pl.when(index == when)(lambda when=when: chores(when))
        h, turn = index // turns, lax.rem(index, turns)
        start = pl.multiple_of(place.member(turn) * local_rows, local_rows)
        attend_block(h, pl.ds(start, local_rows), q_x, k_wide, v_x, mixed, mixed_low, row_stats)

        @pl.when(index > 0)
        def _():
            pass_on(index - 1)

        return carry

    lax.fori_loop(0, heads * turns, step, 0)
    pass_on(heads * turns - 1)
    for relation in (3, 6):
        gather.arrive_x(UP_W, relation)
        gather.arrive_x(OUT_W, relation)
        gather.arrive_x(DOWN_W, relation)
    for relation in (3, 6):
        gather.arrive_y(relation, 0)
    for relation in (2, 5, 3, 6):
        gather.arrive_y(relation, 1)
    for array in (UP_W, OUT_W, DOWN_W, QKV_W):
        gather.finish(array)
    for copy in own_copies()[:3]:
        copy.wait()
    for half in range(halves):
        for index in range(2):
            send_rows(half, index).wait_send()
        pass_rows(half, False).wait_send()
    for h in range(heads):
        for turn in range(turns - 1):
            send_mixed(h, turn).wait_send()
            send_mixed(h, turn, True).wait_recv()
        keep_mixed(h).wait()


def front(lengths, layer_in, qkv_piece, up_weight, down_weight, out_weight):
    local_rows, width = layer_in.shape
    slot_rows = local_rows * 4
    head_cols = width // 4
    heads = head_cols // HEAD
    vmem = pl.BlockSpec(memory_space=pltpu.VMEM)
    anywhere = pl.BlockSpec(memory_space=pl.ANY)
    dma = pltpu.SemaphoreType.DMA
    hidden = up_weight.shape[1]
    return pl.pallas_call(
        front_kernel,
        in_specs=[pl.BlockSpec(memory_space=pltpu.SMEM)] + [vmem] * 5,
        out_specs=[vmem] * 9 + [anywhere] * 4,
        out_shape=[
            jax.ShapeDtypeStruct((slot_rows, width), low),
            jax.ShapeDtypeStruct((width, 3 * head_cols), low),
            jax.ShapeDtypeStruct((8,) + qkv_piece.shape, low),
            jax.ShapeDtypeStruct((heads, WIDE, slot_rows), low),
            jax.ShapeDtypeStruct((head_cols, slot_rows), low),
            jax.ShapeDtypeStruct((heads, slot_rows, WIDE), low),
            jax.ShapeDtypeStruct((heads, slot_rows, WIDE), low),
            jax.ShapeDtypeStruct((head_cols, slot_rows), full),
            jax.ShapeDtypeStruct((heads, 8, slot_rows), full),
            jax.ShapeDtypeStruct((width, hidden), low),
            jax.ShapeDtypeStruct((hidden, width), low),
            jax.ShapeDtypeStruct((width, width), low),
            jax.ShapeDtypeStruct((width, local_rows), low),
        ],
        scratch_shapes=[
            pltpu.VMEM((heads, WIDE, slot_rows), low),
            pltpu.VMEM((head_cols, slot_rows), low),
            dma((2, 2)), dma((2, 2)), dma((2,)), dma((2,)), dma((heads, 4)), dma((heads, 4)), dma((5,)),
            dma((4, 2, 3)), dma((4, 2, 3)), dma((4, 7)), dma((4, 7)), dma((3, 7, 2)), dma((3, 7, 2)),
            dma((7, 2)), dma((7, 2)), dma((7, 2)), dma((7, 2)),
        ],
        compiler_params=pltpu.CompilerParams(
            vmem_limit_bytes=VMEM_BYTES, collective_id=0, has_side_effects=True
        ),
        name="front",
    )(lengths, layer_in, qkv_piece, up_weight, down_weight, out_weight)


def normalize(values, gain_vec, shift_vec):
    centre = values - jnp.mean(values, axis=-1, keepdims=True)
    factor = lax.rsqrt(jnp.mean(centre * centre, axis=-1, keepdims=True) + norm_epsilon)
    return centre * factor * gain_vec + shift_vec


def column_sums(values):
    return jnp.sum(values, axis=0, dtype=full)


def per_device(
    tokens, read_memory, write_memory, lengths, qkv_weight, qv_bias, out_weight, out_bias, norm1_gain,
    norm1_bias, up_weight, up_bias, down_weight, down_bias, norm2_gain, norm2_bias, cotangent,
):
    seq_count = lax.axis_size("seq")
    fsdp_count = lax.axis_size("fsdp")
    seq_place = lax.axis_index("seq")
    local_rows, width = tokens.shape
    head_cols = width // seq_count
    shard = width // fsdp_count
    length = lengths[0]
    places = seq_place * local_rows + jnp.arange(local_rows, dtype=jnp.int32)
    in_slot = (places < length)[:, None]
    memory_slots = jnp.arange(MEM, dtype=jnp.int32)
    pick_read = places[:, None] == memory_slots[None, :]
    pick_write = places[:, None] == length - MEM + memory_slots[None, :]
    is_memory = jnp.any(pick_read | pick_write, axis=1)[:, None]
    picks = jnp.concatenate([pick_read, pick_write], axis=1).astype(full)
    memory = jnp.concatenate([read_memory[0], write_memory[0]], axis=0)
    layer_in = jnp.where(is_memory, mul(picks.astype(low), memory).astype(low), tokens)

    own_shard = lax.dynamic_slice_in_dim(
        qkv_weight.reshape(shard, 3, seq_count, head_cols), seq_place, 1, 2
    ).reshape(shard, 3 * head_cols)
    vectors = (qv_bias, out_bias, norm1_gain, norm1_bias, up_bias, down_bias, norm2_gain, norm2_bias)
    packed = jnp.concatenate(vectors)
    on_block = (fsdp_count, seq_count) == (8, 4)
    if on_block:
        spare = jnp.zeros((14, 3 * head_cols), low)
        piece = jnp.concatenate([own_shard, packed.reshape(2, -1), spare], axis=0)
        (rows, weight, pieces, q_x, k_t, k_wide, v_wide, mixed, row_stats, up_full, down_full, out_full,
         attended) = front(lengths, layer_in, piece, up_weight, down_weight, out_weight)
        packed = pieces[:, shard : shard + 2].reshape(fsdp_count, -1).astype(full)
    else:
        rows = lax.all_gather(layer_in, "seq", axis=0, tiled=True)
        weight = lax.all_gather(own_shard, "fsdp", axis=0, tiled=True)
        packed = lax.all_gather(packed.reshape(1, -1), "fsdp", axis=0, tiled=True).astype(full)
    whole, start = [], 0
    for vector in vectors:
        whole.append(packed[:, start : start + vector.shape[0]].reshape(-1))
        start += vector.shape[0]
    qv_vec, out_vec, gain_one, shift_one, up_vec, down_vec, gain_two, shift_two = whole
    if not on_block:
        own_qv = lax.dynamic_slice_in_dim(qv_vec.reshape(2, seq_count, head_cols), seq_place, 1, 1)
        bias = jnp.concatenate(
            [own_qv[0, 0], jnp.zeros((head_cols,), full), own_qv[1, 0], jnp.zeros((-3 * head_cols % WIDE,), full)]
        )
        bias = jnp.broadcast_to(bias, (8, bias.shape[0]))
        out_full = lax.all_gather(out_weight, "fsdp", axis=0, tiled=True)
        up_full = lax.all_gather(up_weight, "fsdp", axis=0, tiled=True)
        down_full = lax.all_gather(down_weight, "fsdp", axis=0, tiled=True)
        q_x, k_t, k_wide, v_wide, mixed, mixed_low, row_stats = attention_forward(lengths, rows, weight, bias)
        attended = lax.all_to_all(mixed_low, "seq", split_axis=1, concat_axis=0, tiled=True)
    resid_one = layer_in.astype(full) + mul(attended, out_full, TN) + out_vec
    middle, norm_one_back = jax.vjp(normalize, resid_one, gain_one, shift_one)
    middle_low = middle.astype(low)
    up_pre = mul(middle_low, up_full) + up_vec
    gelu_out, gelu_back = jax.vjp(partial(jax.nn.gelu, approximate=False), up_pre)
    hidden = gelu_out.astype(low)
    down_pre = mul(hidden, down_full) + down_vec
    final, norm_two_back = jax.vjp(normalize, middle + down_pre, gain_two, shift_two)
    output = jnp.where(in_slot, final, 0.0).astype(low)
    grad_final = jnp.where(in_slot, cotangent.astype(full), 0.0)
    grad_resid_two, grad_gain_two, grad_shift_two = norm_two_back(grad_final)
    grad_down = grad_resid_two.astype(low)
    grad_down_weight = mul(hidden, grad_down, TN)
    (grad_up_pre,) = gelu_back(mul(grad_down, down_full, NT))
    grad_up = grad_up_pre.astype(low)
    grad_up_weight = mul(middle_low, grad_up, TN)
    grad_middle = grad_resid_two + mul(grad_up, up_full, NT)
    grad_resid_one, grad_gain_one, grad_shift_one = norm_one_back(grad_middle)
    grad_branch = grad_resid_one.astype(low)
    grad_out_weight = mul(attended, grad_branch)
    grad_attended = mul(out_full, grad_branch, NT).astype(low)
    grad_t = lax.all_to_all(grad_attended, "seq", split_axis=0, concat_axis=1, tiled=True)
    partial_in, weight_part, sums = attention_backward(
        q_x, k_t, k_wide, v_wide, mixed, row_stats, grad_t, rows, weight
    )
    from_heads = lax.psum_scatter(partial_in, "seq", scatter_dimension=0, tiled=True).astype(full)
    grad_layer_in = grad_resid_one + from_heads
    input_grad = jnp.where(is_memory, 0.0, grad_layer_in)
    grad_memory = lax.dot_general(
        picks, grad_layer_in, TN, precision=lax.Precision.HIGHEST, preferred_element_type=full
    )
    grad_memory = lax.psum(grad_memory.astype(low), "seq").astype(full)

    sums = sums[:, 0]
    own_sums = jnp.stack([sums[:head_cols], sums[2 * head_cols :]])[:, None]
    zero_qv = jnp.zeros((2, seq_count, head_cols), full)
    qv_grad = lax.dynamic_update_slice_in_dim(zero_qv, own_sums, seq_place, 1).reshape(-1)
    vector_grads = [
        qv_grad, column_sums(grad_branch), grad_gain_one, grad_shift_one, column_sums(grad_up),
        column_sums(grad_down), grad_gain_two, grad_shift_two,
    ]
    packed_grad = jnp.concatenate([v.reshape(fsdp_count, -1) for v in vector_grads], axis=1)
    packed_sum = lax.psum(packed_grad, ("fsdp", "seq"))
    own_vectors = lax.dynamic_index_in_dim(packed_sum, lax.axis_index("fsdp"), 0, False)
    vector_outs, start = [], 0
    for vector in vectors:
        vector_outs.append(own_vectors[start : start + vector.shape[0]])
        start += vector.shape[0]
    qv_out, out_b_out, gain_one_out, shift_one_out, up_b_out, down_b_out, gain_two_out, shift_two_out = vector_outs

    def both_axes(part):
        piece = lax.psum_scatter(part.astype(low), "fsdp", scatter_dimension=0, tiled=True)
        return lax.psum(piece, "seq").astype(full)

    qkv_piece = lax.psum_scatter(weight_part, "fsdp", scatter_dimension=0, tiled=True)
    qkv_parts = lax.all_gather(qkv_piece, "seq", axis=0).reshape(seq_count, shard, 3, head_cols)
    qkv_out = jnp.transpose(qkv_parts, (1, 2, 0, 3)).reshape(shard, 3 * width).astype(full)
    return (
        output, input_grad, grad_memory[None, :MEM], grad_memory[None, MEM:], qkv_out, qv_out,
        both_axes(grad_out_weight), out_b_out, gain_one_out, shift_one_out,
        both_axes(grad_up_weight), up_b_out, both_axes(grad_down_weight), down_b_out,
        gain_two_out, shift_two_out,
    )


def solution(mesh):
    rows, piece = P(("fsdp", "seq"), None), P("fsdp")
    matrix, memory = P("fsdp", None), P("fsdp", None, None)
    in_specs = (
        rows, memory, memory, piece, matrix, piece, matrix, piece, piece, piece, matrix, piece, matrix,
        piece, piece, piece, rows,
    )
    out_specs = (
        rows, rows, memory, memory, matrix, piece, matrix, piece, piece, piece, matrix, piece, matrix,
        piece, piece, piece,
    )
    return jax.shard_map(per_device, mesh=mesh, in_specs=in_specs, out_specs=out_specs, check_vma=False)
```

```python
from functools import partial

import jax
import jax.numpy as jnp
from jax import lax
from jax.experimental import pallas as pl
from jax.experimental.pallas import tpu as pltpu
from jax.sharding import PartitionSpec as P

HEAD = 64
MEM = 10
WIDE = 128
VMEM_BYTES = 64000 * 1024

norm_epsilon = 1e-06
masked_score = -1e30
low = jnp.bfloat16
full = jnp.float32

NN = (((1,), (0,)), ((), ()))
NT = (((1,), (1,)), ((), ()))
TN = (((0,), (0,)), ((), ()))
TT = (((0,), (1,)), ((), ()))


def mul(left, right, dims=NN):
    return lax.dot_general(left, right, dims, preferred_element_type=full)


def three_parts(value):
    high = value.astype(low)
    rest = value - high.astype(full)
    middle = rest.astype(low)
    return high, middle, (rest - middle.astype(full)).astype(low)


def stack_rows(rows, columns):
    place = lax.broadcasted_iota(jnp.int32, (HEAD, columns), 0)
    block = jnp.zeros((HEAD, columns), full)
    for index, row in enumerate(rows):
        block = jnp.where(place == index, row, block)
    return block.astype(low)


def project_block(start, length, rows_ref, weight_ref, bias_q, bias_v, q_x, k_t, v_x, k_wide, v_wide, step):
    head_cols = k_t.shape[0]
    lanes = pl.ds(start, step)
    made = mul(weight_ref[...], rows_ref[lanes, :], TT)
    place = start + lax.broadcasted_iota(jnp.int32, (1, step), 1)
    key_bias = jnp.where(place < length, 0.0, masked_score)
    one = jnp.ones((1, step), full)
    query_extra = stack_rows([one], step)
    key_extra = stack_rows([key_bias, one, one, one], step)
    value_extra = stack_rows([one, one, one], step)
    for h in range(head_cols // HEAD):
        own = slice(h * HEAD, (h + 1) * HEAD)
        base = 3 * h * HEAD
        query = (made[base : base + HEAD] + bias_q[own]).astype(low)
        q_x[h, :HEAD, lanes] = query * jnp.asarray(HEAD**-0.5, low)
        q_x[h, HEAD:, lanes] = query_extra
        k_t[own, lanes] = made[base + HEAD : base + 2 * HEAD].astype(low)
        v_x[h, :HEAD, lanes] = (made[base + 2 * HEAD : base + 3 * HEAD] + bias_v[own]).astype(low)
        v_x[h, HEAD:, lanes] = value_extra
        k_wide[h, lanes, :] = jnp.transpose(jnp.concatenate([k_t[own, lanes], key_extra], axis=0))
        v_wide[h, lanes, :] = jnp.transpose(v_x[h, :, lanes])


def project_heads(length, rows_ref, weight_ref, bias_ref, q_x, k_t, v_x, k_wide, v_wide):
    head_cols = k_t.shape[0]
    bias = jnp.transpose(bias_ref[...])[:, 0:1]
    for start in range(0, rows_ref.shape[0], 512):
        project_block(
            start, length, rows_ref, weight_ref, bias[:head_cols], bias[head_cols:],
            q_x, k_t, v_x, k_wide, v_wide, 512,
        )


def attend_block(h, lanes, q_x, k_wide, v_x, mixed, mixed_low, row_stats):
    scores = mul(k_wide[h], q_x[h, :, lanes])
    row_max = jnp.max(scores, axis=0, keepdims=True)
    probs = jnp.exp(scores - row_max).astype(low)
    total = mul(v_x[h, : HEAD + 16], probs)
    row_sum = total[HEAD : HEAD + 1]
    own = pl.ds(h * HEAD, HEAD)
    result = total[:HEAD] / row_sum
    mixed[own, lanes] = result
    mixed_low[own, lanes] = result.astype(low)
    row_stats[h, :, lanes] = jnp.broadcast_to(row_max + jnp.log(row_sum), (8, result.shape[1]))


def forward_kernel(
    length_ref, rows_ref, weight_ref, bias_ref, q_x, k_t, k_wide, v_wide, mixed, mixed_low, row_stats, v_x
):
    project_heads(length_ref[0], rows_ref, weight_ref, bias_ref, q_x, k_t, v_x, k_wide, v_wide)
    heads = q_x.shape[0]
    block = 512
    blocks = q_x.shape[2] // block

    def step(index, carry):
        h = index // blocks
        start = pl.multiple_of(lax.rem(index, blocks) * block, block)
        attend_block(h, pl.ds(start, block), q_x, k_wide, v_x, mixed, mixed_low, row_stats)
        return carry

    lax.fori_loop(0, heads * blocks, step, 0)


def attention_forward(length, rows, weight, bias):
    slot_rows = rows.shape[0]
    head_cols = weight.shape[1] // 3
    heads = head_cols // HEAD
    vmem = pl.BlockSpec(memory_space=pltpu.VMEM)
    return pl.pallas_call(
        forward_kernel,
        in_specs=[pl.BlockSpec(memory_space=pltpu.SMEM), vmem, vmem, vmem],
        out_specs=[vmem] * 7,
        out_shape=[
            jax.ShapeDtypeStruct((heads, WIDE, slot_rows), low),
            jax.ShapeDtypeStruct((head_cols, slot_rows), low),
            jax.ShapeDtypeStruct((heads, slot_rows, WIDE), low),
            jax.ShapeDtypeStruct((heads, slot_rows, WIDE), low),
            jax.ShapeDtypeStruct((head_cols, slot_rows), full),
            jax.ShapeDtypeStruct((head_cols, slot_rows), low),
            jax.ShapeDtypeStruct((heads, 8, slot_rows), full),
        ],
        scratch_shapes=[pltpu.VMEM((heads, WIDE, slot_rows), low)],
        compiler_params=pltpu.CompilerParams(vmem_limit_bytes=VMEM_BYTES),
        name="attention_forward",
    )(length, rows, weight, bias)


def attend_back(h, lanes, q_x, q_here, do_x, grad_t, mixed, row_stats, k_t, k_wide, v_wide, grads, grad_k, grad_v, first):
    own = pl.ds(pl.multiple_of(h * HEAD, HEAD), HEAD)
    grad = grad_t[own, lanes]
    columns = grad.shape[1]
    delta = jnp.sum(grad.astype(full) * mixed[own, lanes], axis=0, keepdims=True)
    parts = [part.astype(full) for part in three_parts(-delta)]
    do_x[:HEAD, :] = grad
    do_x[HEAD:, :] = stack_rows(parts, columns)
    parts = [part.astype(full) for part in three_parts(-row_stats[h, 0:1, lanes])]
    q_here[:HEAD, :] = q_x[h, :HEAD, lanes]
    q_here[HEAD:, :] = stack_rows([jnp.ones((1, columns), full)] + parts, columns)
    probs = jnp.exp(mul(k_wide[h], q_here[...]))
    grad_scores = (probs * mul(v_wide[h], do_x[...])).astype(low)
    value_part = mul(grad, probs.astype(low), NT)
    key_part = mul(q_here[:HEAD, :], grad_scores, NT)

    @pl.when(first)
    def _():
        grad_v[...] = value_part
        grad_k[...] = key_part

    @pl.when(jnp.logical_not(first))
    def _():
        grad_v[...] += value_part
        grad_k[...] += key_part

    query_part = mul(k_t[own, :], grad_scores) * HEAD**-0.5
    grads[pl.ds(pl.multiple_of(3 * h * HEAD, HEAD), HEAD), lanes] = query_part.astype(low)


def backward_kernel(
    q_in, k_t, k_wide, v_wide, mixed, row_stats, grad_t, rows_ref, weight_ref,
    partial_out, weight_out, sums_out, q_here, do_x, grads, grad_k, grad_v,
):
    heads, _, slot_rows = q_in.shape
    block = 512
    blocks = slot_rows // block

    def step(index, carry):
        h = index // blocks
        turn = lax.rem(index, blocks)
        start = pl.multiple_of(turn * block, block)
        attend_back(
            h, pl.ds(start, block), q_in, q_here, do_x, grad_t, mixed, row_stats, k_t, k_wide, v_wide, grads, grad_k,
            grad_v, turn == 0,
        )

        @pl.when(turn == blocks - 1)
        def _():
            base = pl.multiple_of(3 * h * HEAD, HEAD)
            grads[pl.ds(base + HEAD, HEAD), :] = grad_k[...].astype(low)
            grads[pl.ds(base + 2 * HEAD, HEAD), :] = grad_v[...].astype(low)

        return carry

    lax.fori_loop(0, heads * blocks, step, 0)
    for start in range(0, slot_rows, block):
        partial_out[start : start + block, :] = mul(
            grads[:, start : start + block], weight_ref[...], TT
        ).astype(partial_out.dtype)
    weight_out[...] = jnp.transpose(mul(grads[...], rows_ref[...])).astype(weight_out.dtype)
    sums_out[...] = jnp.broadcast_to(
        jnp.sum(grads[...].astype(full), axis=1, keepdims=True), sums_out.shape
    )


def attention_backward(q_x, k_t, k_wide, v_wide, mixed, row_stats, grad_t, rows, weight):
    heads, _, slot_rows = q_x.shape
    width, all_cols = weight.shape
    vmem = pl.BlockSpec(memory_space=pltpu.VMEM)
    return pl.pallas_call(
        backward_kernel,
        in_specs=[vmem] * 9,
        out_specs=[vmem] * 3,
        out_shape=[
            jax.ShapeDtypeStruct((slot_rows, width), low),
            jax.ShapeDtypeStruct((width, all_cols), low),
            jax.ShapeDtypeStruct((all_cols, WIDE), full),
        ],
        scratch_shapes=[
            pltpu.VMEM((WIDE, 512), low),
            pltpu.VMEM((WIDE, 512), low),
            pltpu.VMEM((all_cols, slot_rows), low),
            pltpu.VMEM((HEAD, slot_rows), full),
            pltpu.VMEM((HEAD, slot_rows), full),
        ],
        compiler_params=pltpu.CompilerParams(vmem_limit_bytes=VMEM_BYTES),
        name="attention_backward",
    )(q_x, k_t, k_wide, v_wide, mixed, row_stats, grad_t, rows, weight)


MESH = pl.DeviceIdType.MESH
OWN, RELATIONS = 0, 7
UP_W, OUT_W, DOWN_W, QKV_W = 0, 1, 2, 3


def offset_of(relation):
    return (0, -1, -2, -3, 1, 2, 3)[relation]


class Place:
    def __init__(self):
        self.f, self.s = lax.axis_index("fsdp"), lax.axis_index("seq")
        self.z, self.x = self.f // 2, lax.rem(self.f, 2)
        self.y, self.c = self.s // 2, lax.rem(self.s, 2)
        self.core = (self.f, 2 * self.y + 1 - self.c)
        self.across_y = (self.f, 2 * (1 - self.y) + self.c)
        self.diagonal = (self.f, 2 * (1 - self.y) + 1 - self.c)
        self.across_x = (2 * self.z + 1 - self.x, self.s)
        self.above = (self.f + 2, self.s)
        self.below = (self.f - 2, self.s)

    def has(self, relation):
        offset = offset_of(relation)
        return (self.z + offset >= 0) & (self.z + offset <= 3)

    def source(self, relation, column):
        own_column = self.f + 2 * offset_of(relation)
        return own_column if column == 0 else own_column + 1 - 2 * self.x

    def member(self, turn):
        flip_y = 1 - turn // 2
        flip_c = lax.rem(turn, 2) if not isinstance(turn, int) else turn % 2
        flip_c = flip_c + (1 - 2 * flip_c) * (turn // 2)
        return 2 * lax.rem(self.y + flip_y, 2) + lax.rem(self.c + flip_c, 2)


def remote(src, dst, send, recv, where):
    return pltpu.make_async_remote_copy(
        src_ref=src, dst_ref=dst, send_sem=send, recv_sem=recv, device_id=where, device_id_type=MESH
    )


def greet(place, everyone):
    barrier = pltpu.get_barrier_semaphore()
    near = [place.core, place.across_y, place.diagonal, place.across_x]
    for where in near:
        pl.semaphore_signal(barrier, inc=1, device_id=where, device_id_type=MESH)

    @pl.when(place.z > 0)
    def _():
        pl.semaphore_signal(barrier, inc=1, device_id=place.below, device_id_type=MESH)

    @pl.when(place.z < 3)
    def _():
        pl.semaphore_signal(barrier, inc=1, device_id=place.above, device_id_type=MESH)

    ends = jnp.where((place.z == 0) | (place.z == 3), 1, 2)
    pl.semaphore_wait(barrier, len(near) + ends)


class Gather:
    def __init__(self, place, own, whole, sems):
        self.place, self.own, self.whole = place, own, whole
        (self.z_send, self.z_recv, self.x_send, self.x_recv, self.c_send, self.c_recv,
         self.y_send, self.y_recv, self.d_send, self.d_recv) = sems

    def piece(self, array, source, quarter=None):
        c = self.place.c
        ref = self.whole[array]
        if array == QKV_W:
            return ref.at[source]
        if array == DOWN_W:
            rows = ref.shape[0] // 8
            part = rows // 4
            quarter = self.place.s if quarter is None else quarter
            return ref.at[pl.ds(pl.multiple_of(source * rows + quarter * part, part), part)]
        rows, columns = ref.shape[0] // 8, ref.shape[1] // 2
        return ref.at[
            pl.ds(pl.multiple_of(source * rows, rows), rows),
            pl.ds(pl.multiple_of(c * columns, columns), columns),
        ]

    def own_piece(self, array):
        ref = self.own[array]
        if array == QKV_W:
            return ref
        if array == DOWN_W:
            part = ref.shape[0] // 4
            return ref.at[pl.ds(pl.multiple_of(self.place.s * part, part), part)]
        columns = ref.shape[1] // 2
        return ref.at[:, pl.ds(pl.multiple_of(self.place.c * columns, columns), columns)]

    def along_z(self, array, relation, way):
        here = self.piece(array, self.place.source(relation, 0))
        src = self.own_piece(array) if relation == OWN else here
        step = abs(offset_of(relation))
        where = self.place.above if way == 0 else self.place.below
        return remote(src, here, self.z_send.at[array, way, step], self.z_recv.at[array, way, step], where)

    def z_ways(self, relation):
        place = self.place
        ways = []
        if offset_of(relation) <= 0:
            ways.append((0, place.has(relation) & (place.z < 3)))
        if offset_of(relation) >= 0:
            ways.append((1, place.has(relation) & (place.z > 0)))
        return ways

    def wait_z(self, array, relation):
        way = 0 if offset_of(relation) < 0 else 1
        step = abs(offset_of(relation)) - 1
        here = self.piece(array, self.place.source(relation, 0))
        where = self.place.below if way == 0 else self.place.above
        remote(
            here, here, self.z_send.at[array, way, step], self.z_recv.at[array, way, step], where
        ).wait_recv()

    def over_x(self, array, relation):
        here = self.piece(array, self.place.source(relation, 0))
        src = self.own_piece(array) if relation == OWN else here
        return remote(
            src, here, self.x_send.at[array, relation], self.x_recv.at[array, relation], self.place.across_x
        )

    def from_x(self, array, relation):
        here = self.piece(array, self.place.source(relation, 1))
        return remote(
            here, here, self.x_send.at[array, relation], self.x_recv.at[array, relation], self.place.across_x
        )

    def to_core(self, array, relation, column):
        here = self.piece(array, self.place.source(relation, column))
        return remote(
            here, here, self.c_send.at[array, relation, column], self.c_recv.at[array, relation, column],
            self.place.core,
        )

    def over_y(self, relation, column):
        here = self.piece(DOWN_W, self.place.source(relation, column))
        return remote(
            here, here, self.y_send.at[relation, column], self.y_recv.at[relation, column], self.place.across_y
        )

    def far_quarter(self, relation, column):
        return self.piece(
            DOWN_W, self.place.source(relation, column), 2 * (1 - self.place.y) + self.place.c
        )

    def from_y(self, relation, column):
        here = self.far_quarter(relation, column)
        return remote(
            here, here, self.y_send.at[relation, column], self.y_recv.at[relation, column], self.place.across_y
        )

    def far_to_core(self, relation, column):
        here = self.far_quarter(relation, column)
        return remote(
            here, here, self.d_send.at[relation, column], self.d_recv.at[relation, column], self.place.core
        )

    def when(self, relation, action):
        if relation == OWN:
            action()
        else:
            pl.when(self.place.has(relation))(action)

    def arrive_z(self, array, relation):
        def action():
            if relation != OWN:
                self.wait_z(array, relation)
            for way, holds in self.z_ways(relation):
                pl.when(holds)(lambda way=way: self.along_z(array, relation, way).start())
            self.over_x(array, relation).start()
            if array != QKV_W and relation != OWN:
                self.to_core(array, relation, 0).start()
                if array == DOWN_W:
                    self.over_y(relation, 0).start()

        self.when(relation, action)

    def arrive_x(self, array, relation):
        def action():
            self.from_x(array, relation).wait_recv()
            if array != QKV_W:
                self.to_core(array, relation, 1).start()
                if array == DOWN_W:
                    self.over_y(relation, 1).start()

        self.when(relation, action)

    def arrive_y(self, relation, column):
        def action():
            self.from_y(relation, column).wait_recv()
            self.far_to_core(relation, column).start()

        if (relation, column) != (OWN, 0):
            self.when(relation, action)

    def finish(self, array):
        for relation in range(RELATIONS):
            def action():
                self.over_x(array, relation).wait_send()
                for way, holds in self.z_ways(relation):
                    pl.when(holds)(lambda way=way: self.along_z(array, relation, way).wait_send())
                if array == QKV_W:
                    return
                for column in range(2):
                    if (relation, column) == (OWN, 0):
                        continue
                    self.to_core(array, relation, column).wait()
                    if array == DOWN_W:
                        self.over_y(relation, column).wait_send()
                        self.far_to_core(relation, column).wait()

            self.when(relation, action)


def front_kernel(
    length_ref, rows_in, qkv_in, up_in, down_in, out_in,
    rows_ref, weight_ref, pieces, q_x, k_t, k_wide, v_wide, mixed, row_stats, up_full, down_full, out_full,
    attended,
    v_x, mixed_low, row_send, row_recv, far_send, far_recv, mix_send, mix_recv, local_sem, *gather_sems,
):
    place = Place()
    slot_rows, width = rows_ref.shape
    local_rows = rows_in.shape[0]
    head_cols = k_t.shape[0]
    heads = head_cols // HEAD
    own_shards = {UP_W: up_in, DOWN_W: down_in, OUT_W: out_in, QKV_W: qkv_in}
    whole = {UP_W: up_full, DOWN_W: down_full, OUT_W: out_full, QKV_W: pieces}
    gather = Gather(place, own_shards, whole, gather_sems)
    greet(place, None)

    halves = 2
    part = local_rows // halves

    def rows_of(member, half):
        return pl.ds(pl.multiple_of(member * local_rows + half * part, part), part)

    def send_rows(half, index):
        where = (place.core, place.across_y)[index]
        return remote(
            rows_in.at[pl.ds(half * part, part)], rows_ref.at[rows_of(place.s, half)],
            row_send.at[index, half], row_recv.at[index, half], where,
        )

    def rows_from(half, index):
        member = (2 * place.y + 1 - place.c, 2 * (1 - place.y) + place.c)[index]
        here = rows_ref.at[rows_of(member, half)]
        where = (place.core, place.across_y)[index]
        return remote(here, here, row_send.at[index, half], row_recv.at[index, half], where)

    def pass_rows(half, arriving):
        flip = place.c if not arriving else 1 - place.c
        here = rows_ref.at[rows_of(2 * (1 - place.y) + flip, half)]
        return remote(here, here, far_send.at[half], far_recv.at[half], place.core)

    for half in range(halves):
        send_rows(half, 1).start()
        send_rows(half, 0).start()
    gather.arrive_z(QKV_W, OWN)

    def own_copies():
        copies = []
        for index, array in enumerate((UP_W, DOWN_W, OUT_W)):
            rows = own_shards[array].shape[0]
            copies.append(pltpu.make_async_copy(
                own_shards[array], whole[array].at[pl.ds(pl.multiple_of(place.f * rows, rows), rows)],
                local_sem.at[index],
            ))
        copies.append(pltpu.make_async_copy(qkv_in, pieces.at[place.f], local_sem.at[3]))
        copies.append(pltpu.make_async_copy(
            rows_in, rows_ref.at[pl.ds(pl.multiple_of(place.s * local_rows, local_rows), local_rows)],
            local_sem.at[4],
        ))
        return copies

    for copy in own_copies():
        copy.start()

    for relation in (1, 4):
        gather.arrive_z(QKV_W, relation)
    gather.arrive_z(UP_W, OWN)
    for relation in (2, 5):
        gather.arrive_z(QKV_W, relation)
    gather.arrive_z(OUT_W, OWN)
    gather.arrive_z(DOWN_W, OWN)
    rows_from(0, 1).wait_recv()
    pass_rows(0, False).start()
    for relation in (3, 6):
        gather.arrive_z(QKV_W, relation)
    for relation in (1, 4):
        gather.arrive_z(UP_W, relation)
    for relation in range(RELATIONS):
        gather.arrive_x(QKV_W, relation)
    for copy in own_copies()[3:]:
        copy.wait()

    shard = weight_ref.shape[0] // 8
    for source in range(8):
        weight_ref[source * shard : (source + 1) * shard, :] = pieces[source, :shard, :]
    bias_q = jnp.transpose(pieces[place.s, shard : shard + 16, :].astype(full))[:head_cols, 0:1]
    bias_v = jnp.transpose(pieces[4 + place.s, shard : shard + 16, :].astype(full))[:head_cols, 0:1]
    length = length_ref[0]

    def project(member):
        start = pl.multiple_of(member * local_rows, local_rows)
        project_block(
            start, length, rows_ref, weight_ref, bias_q, bias_v, q_x, k_t, v_x, k_wide, v_wide, local_rows
        )

    project(place.s)
    for half in range(halves):
        rows_from(half, 0).wait_recv()
    project(2 * place.y + 1 - place.c)
    rows_from(1, 1).wait_recv()
    pass_rows(1, False).start()
    project(2 * (1 - place.y) + place.c)
    for relation in (1, 4):
        gather.arrive_z(OUT_W, relation)
        gather.arrive_z(DOWN_W, relation)
    for half in range(halves):
        pass_rows(half, True).wait_recv()
    project(2 * (1 - place.y) + 1 - place.c)

    def chores(step):
        if step == 0:
            gather.arrive_x(UP_W, OWN)
            for relation in (2, 5):
                gather.arrive_z(UP_W, relation)
        elif step == 2:
            for relation in (2, 5):
                gather.arrive_z(OUT_W, relation)
                gather.arrive_z(DOWN_W, relation)
            gather.arrive_x(OUT_W, OWN)
            gather.arrive_x(DOWN_W, OWN)
        elif step == 4:
            for relation in (1, 4):
                gather.arrive_x(UP_W, relation)
                gather.arrive_y(relation, 0)
            gather.arrive_y(OWN, 1)
        elif step == 6:
            for relation in (3, 6):
                gather.arrive_z(UP_W, relation)
            for relation in (1, 4):
                gather.arrive_x(OUT_W, relation)
                gather.arrive_x(DOWN_W, relation)
        elif step == 8:
            for relation in (3, 6):
                gather.arrive_z(OUT_W, relation)
                gather.arrive_z(DOWN_W, relation)
            for relation in (2, 5):
                gather.arrive_x(UP_W, relation)
                gather.arrive_y(relation, 0)
        elif step == 10:
            for relation in (2, 5):
                gather.arrive_x(OUT_W, relation)
                gather.arrive_x(DOWN_W, relation)
            for relation in (1, 4):
                gather.arrive_y(relation, 1)

    def send_mixed(h, turn, arriving=False):
        member = place.member(turn)
        own = pl.ds(pl.multiple_of(h * HEAD, HEAD), HEAD)
        lanes = pl.ds(pl.multiple_of(member * local_rows, local_rows), local_rows)
        owner = member if arriving else place.s
        there = attended.at[pl.ds(pl.multiple_of(owner * head_cols + h * HEAD, HEAD), HEAD)]
        return remote(
            mixed_low.at[own, lanes], there, mix_send.at[h, turn], mix_recv.at[h, turn], (place.f, member)
        )

    def keep_mixed(h):
        own = pl.ds(pl.multiple_of(h * HEAD, HEAD), HEAD)
        lanes = pl.ds(pl.multiple_of(place.s * local_rows, local_rows), local_rows)
        there = attended.at[pl.ds(pl.multiple_of(place.s * head_cols + h * HEAD, HEAD), HEAD)]
        return pltpu.make_async_copy(mixed_low.at[own, lanes], there, mix_send.at[h, 3])

    turns = slot_rows // local_rows

    def pass_on(index):
        h, turn = index // turns, lax.rem(index, turns)

        @pl.when(turn < turns - 1)
        def _():
            send_mixed(h, turn).start()

        @pl.when(turn == turns - 1)
        def _():
            keep_mixed(h).start()

    def step(index, carry):
        for when in range(0, 12, 2):
            pl.when(index == when)(lambda when=when: chores(when))
        h, turn = index // turns, lax.rem(index, turns)
        start = pl.multiple_of(place.member(turn) * local_rows, local_rows)
        attend_block(h, pl.ds(start, local_rows), q_x, k_wide, v_x, mixed, mixed_low, row_stats)

        @pl.when(index > 0)
        def _():
            pass_on(index - 1)

        return carry

    lax.fori_loop(0, heads * turns, step, 0)
    pass_on(heads * turns - 1)
    for relation in (3, 6):
        gather.arrive_x(UP_W, relation)
        gather.arrive_x(OUT_W, relation)
        gather.arrive_x(DOWN_W, relation)
    for relation in (3, 6):
        gather.arrive_y(relation, 0)
    for relation in (2, 5, 3, 6):
        gather.arrive_y(relation, 1)
    for array in (UP_W, OUT_W, DOWN_W, QKV_W):
        gather.finish(array)
    for copy in own_copies()[:3]:
        copy.wait()
    for half in range(halves):
        for index in range(2):
            send_rows(half, index).wait_send()
        pass_rows(half, False).wait_send()
    for h in range(heads):
        for turn in range(turns - 1):
            send_mixed(h, turn).wait_send()
            send_mixed(h, turn, True).wait_recv()
        keep_mixed(h).wait()


def front(lengths, layer_in, qkv_piece, up_weight, down_weight, out_weight):
    local_rows, width = layer_in.shape
    slot_rows = local_rows * 4
    head_cols = width // 4
    heads = head_cols // HEAD
    vmem = pl.BlockSpec(memory_space=pltpu.VMEM)
    anywhere = pl.BlockSpec(memory_space=pl.ANY)
    dma = pltpu.SemaphoreType.DMA
    hidden = up_weight.shape[1]
    return pl.pallas_call(
        front_kernel,
        in_specs=[pl.BlockSpec(memory_space=pltpu.SMEM)] + [vmem] * 5,
        out_specs=[vmem] * 9 + [anywhere] * 4,
        out_shape=[
            jax.ShapeDtypeStruct((slot_rows, width), low),
            jax.ShapeDtypeStruct((width, 3 * head_cols), low),
            jax.ShapeDtypeStruct((8,) + qkv_piece.shape, low),
            jax.ShapeDtypeStruct((heads, WIDE, slot_rows), low),
            jax.ShapeDtypeStruct((head_cols, slot_rows), low),
            jax.ShapeDtypeStruct((heads, slot_rows, WIDE), low),
            jax.ShapeDtypeStruct((heads, slot_rows, WIDE), low),
            jax.ShapeDtypeStruct((head_cols, slot_rows), full),
            jax.ShapeDtypeStruct((heads, 8, slot_rows), full),
            jax.ShapeDtypeStruct((width, hidden), low),
            jax.ShapeDtypeStruct((hidden, width), low),
            jax.ShapeDtypeStruct((width, width), low),
            jax.ShapeDtypeStruct((width, local_rows), low),
        ],
        scratch_shapes=[
            pltpu.VMEM((heads, WIDE, slot_rows), low),
            pltpu.VMEM((head_cols, slot_rows), low),
            dma((2, 2)), dma((2, 2)), dma((2,)), dma((2,)), dma((heads, 4)), dma((heads, 4)), dma((5,)),
            dma((4, 2, 3)), dma((4, 2, 3)), dma((4, 7)), dma((4, 7)), dma((3, 7, 2)), dma((3, 7, 2)),
            dma((7, 2)), dma((7, 2)), dma((7, 2)), dma((7, 2)),
        ],
        compiler_params=pltpu.CompilerParams(
            vmem_limit_bytes=VMEM_BYTES, collective_id=0, has_side_effects=True
        ),
        name="front",
    )(lengths, layer_in, qkv_piece, up_weight, down_weight, out_weight)


DW_FIRST = 3
LINES = (3, 0, 2, 1)


def add_low(left, right):
    return (left.astype(full) + right.astype(full)).astype(low)


class Reduce:
    def __init__(self, place, given, mine, sums, from_y, from_x, from_z, sems):
        self.place, self.given, self.mine, self.sums = place, given, mine, sums
        self.from_y, self.from_x, self.from_z = from_y, from_x, from_z
        (self.c_send, self.c_recv, self.y_send, self.y_recv, self.x_send, self.x_recv, self.z_send,
         self.z_recv) = sems

    def dest(self, column, line):
        x = self.place.x
        return 2 * line + (x if column == 0 else 1 - x)

    def part_of(self, ref, array, column, line, core, far):
        dest = self.dest(column, line)
        if array == DOWN_W:
            rows = ref.shape[0] // 8
            part = rows // 4
            y = self.place.y if not far else 1 - self.place.y
            return ref.at[pl.ds(pl.multiple_of(dest * rows + (2 * y + core) * part, part), part)]
        rows, columns = ref.shape[0] // 8, ref.shape[1] // 2
        return ref.at[
            pl.ds(pl.multiple_of(dest * rows, rows), rows), pl.ds(pl.multiple_of(core * columns, columns), columns)
        ]

    def slot(self, array, column, line, far=0):
        if array >= DW_FIRST:
            return self.sums[array].at[self.dest(column, line)]
        if array == DOWN_W:
            return self.sums[array].at[column, line, far]
        return self.sums[array].at[column, line]

    def load_mine(self, array, column, line, far, sem):
        target = self.mine[array].at[column, line, far] if array == DOWN_W else self.mine[array].at[column, line]
        return pltpu.make_async_copy(
            self.part_of(self.given[array], array, column, line, self.place.c, far), target, sem
        )

    def to_core(self, array, column, line, far=0):
        index = array + far
        return remote(
            self.part_of(self.given[array], array, column, line, 1 - self.place.c, far),
            self.slot(array, column, line, far),
            self.c_send.at[index, column, line], self.c_recv.at[index, column, line], self.place.core,
        )

    def add_core(self, array, column, line, far=0):
        self.to_core(array, column, line, far).wait_recv()
        slot = self.slot(array, column, line, far)
        own = self.mine[array].at[column, line, far] if array == DOWN_W else self.mine[array].at[column, line]
        slot[...] = add_low(slot[...], own[...])

    def over_y(self, column, line):
        return remote(
            self.slot(DOWN_W, column, line, 1), self.from_y.at[column, line],
            self.y_send.at[column, line], self.y_recv.at[column, line], self.place.across_y,
        )

    def add_y(self, column, line):
        self.over_y(column, line).wait_recv()
        slot = self.slot(DOWN_W, column, line, 0)
        slot[...] = add_low(slot[...], self.from_y[column, line])

    def over_x(self, array, line):
        return remote(
            self.slot(array, 1, line), self.from_x[array].at[line],
            self.x_send.at[array, line], self.x_recv.at[array, line], self.place.across_x,
        )

    def add_x(self, array, line):
        self.over_x(array, line).wait_recv()
        slot = self.slot(array, 0, line)
        slot[...] = add_low(slot[...], self.from_x[array][line])

    def along_z(self, array, way, line):
        return remote(
            self.slot(array, 0, line), self.from_z[array].at[way, line],
            self.z_send.at[array, way, line], self.z_recv.at[array, way, line],
            self.place.above if way == 0 else self.place.below,
        )

    def add_z(self, array, way, line):
        self.along_z(array, way, line).wait_recv()
        slot = self.slot(array, 0, line)
        slot[...] = add_low(slot[...], self.from_z[array][way, line])

    def hop(self, array, level):
        @pl.when(self.place.z == level)
        def _():
            for line in range(3, level, -1):
                if level > 0:
                    self.add_z(array, 0, line)
                self.along_z(array, 0, line).start()

        @pl.when(self.place.z == 3 - level)
        def _():
            for line in range(0, 3 - level):
                if level > 0:
                    self.add_z(array, 1, line)
                self.along_z(array, 1, line).start()

    def settle(self, array):
        for line in range(4):

            @pl.when(self.place.z == line)
            def _(line=line):
                if line > 0:
                    self.add_z(array, 0, line)
                if line < 3:
                    self.add_z(array, 1, line)

    def finish(self, array):
        for line in range(4):
            self.over_x(array, line).wait_send()
            pl.when(self.place.z < line)(lambda line=line: self.along_z(array, 0, line).wait_send())
            pl.when(self.place.z > line)(lambda line=line: self.along_z(array, 1, line).wait_send())
            if array >= DW_FIRST:
                continue
            for column in range(2):
                for far in range(2 if array == DOWN_W else 1):
                    self.to_core(array, column, line, far).wait_send()
                if array == DOWN_W:
                    self.over_y(column, line).wait_send()


def back_kernel(
    length_ref, grad_own, q_x, k_t, k_wide, v_wide, mixed, row_stats, vectors_in,
    rows_in, weight_in, resid_in, up_given, down_given, out_given,
    input_out, read_out, write_out, qkv_out, vector_out, up_out, down_out, out_out,
    grad_t, q_here, do_x, grads, grad_k, grad_v, rows_ref, weight_ref, resid_ref, up_mine, out_mine, down_mine,
    up_sum, out_sum, down_sum, dw, down_y, up_x, out_x, down_x, dw_x, up_z, out_z, down_z, dw_z,
    up_last, out_last, up_other, out_other, down_all, dw_all,
    near_send, near_recv, near_own, far_sum, far_recv, memory_all,
    mix_send, mix_recv, local_sem, mine_sem, share_send, share_recv, near_s, near_r, far_s, far_r, memory_s,
    memory_r, *sems,
):
    place = Place()
    heads, _, slot_rows = q_x.shape
    width, local_rows = grad_own.shape
    head_cols = heads * HEAD
    last = DW_FIRST + heads - 1
    given = {UP_W: up_given, OUT_W: out_given, DOWN_W: down_given}
    mine = {UP_W: up_mine, OUT_W: out_mine, DOWN_W: down_mine}
    sums = {UP_W: up_sum, OUT_W: out_sum, DOWN_W: down_sum}
    from_x = {UP_W: up_x, OUT_W: out_x, DOWN_W: down_x}
    from_z = {UP_W: up_z, OUT_W: out_z, DOWN_W: down_z}
    for h in range(heads):
        sums[DW_FIRST + h], from_x[DW_FIRST + h] = dw.at[h], dw_x.at[h]
        from_z[DW_FIRST + h] = dw_z.at[h]
    reduce = Reduce(place, given, mine, sums, down_y, from_x, from_z, sems)
    greet(place, None)

    peers = (place.across_y, place.diagonal, place.core)

    def member_rows(turn):
        member = place.member(turn)
        return member, pl.ds(pl.multiple_of(member * local_rows, local_rows), local_rows)

    def send_grad(turn, arriving=False):
        member, lanes = member_rows(turn)
        own_lanes = pl.ds(pl.multiple_of(place.s * local_rows, local_rows), local_rows)
        src = grad_own.at[pl.ds(pl.multiple_of(member * head_cols, head_cols), head_cols)]
        return remote(
            src, grad_t.at[:, lanes if arriving else own_lanes], mix_send.at[turn], mix_recv.at[turn], peers[turn]
        )

    for turn in range(3):
        send_grad(turn).start()
    loads = []
    for index, (src, dst) in enumerate(((rows_in, rows_ref), (weight_in, weight_ref), (resid_in, resid_ref))):
        loads.append(pltpu.make_async_copy(src, dst, local_sem.at[index]))
    order = (
        (UP_W, 1, 0), (DOWN_W, 1, 1), (DOWN_W, 0, 1), (UP_W, 0, 0), (OUT_W, 1, 0), (OUT_W, 0, 0), (DOWN_W, 1, 0),
        (DOWN_W, 0, 0),
    )
    for array, column, far in order:
        for line in LINES:
            reduce.to_core(array, column, line, far).start()
            reduce.load_mine(array, column, line, far, mine_sem.at[array + far, column, line]).start()
    for load in loads:
        load.start()

    def gather_core(array, column, far=0):
        for line in LINES:
            reduce.load_mine(array, column, line, far, mine_sem.at[array + far, column, line]).wait()
            reduce.add_core(array, column, line, far)

    own_lanes = pl.ds(pl.multiple_of(place.s * local_rows, local_rows), local_rows)
    grad_t[:, own_lanes] = grad_own[pl.ds(pl.multiple_of(place.s * head_cols, head_cols), head_cols), :]

    def send_x(array):
        for line in LINES:
            reduce.over_x(array, line).start()

    def take_x(array):
        for line in LINES:
            reduce.add_x(array, line)

    turns = slot_rows // local_rows

    def weight_part(h):
        if h == 0:
            loads[0].wait()
        base = 3 * h * HEAD
        part = jnp.transpose(mul(grads[base : base + 3 * HEAD, :], rows_ref[...])).astype(low)
        shard = width // 8
        for dest in range(8):
            dw[h, dest, :shard, :] = part[dest * shard : (dest + 1) * shard]
            if h == heads - 1:
                dw[h, dest, shard:, :] = vectors_in[dest].astype(low)
            else:
                dw[h, dest, shard:, :] = jnp.zeros((16, 3 * HEAD), low)
        if h == heads - 1:
            total = jnp.sum(grads[...].astype(full), axis=1, keepdims=True)
            spread = jnp.transpose(jnp.broadcast_to(total, (total.shape[0], WIDE)))[0:1]
            for kind, first_dest in ((0, 0), (2, 4)):
                for head in range(heads):
                    start = (3 * head + kind) * HEAD
                    dw[h, first_dest + place.s, shard : shard + 1, head * HEAD : (head + 1) * HEAD] = spread[
                        :, start : start + HEAD
                    ].astype(low)
        send_x(DW_FIRST + h)

    def chores(index):
        if index == 1:
            send_grad(2, True).wait_recv()
            gather_core(UP_W, 1)
            send_x(UP_W)
        elif index == 2:
            send_grad(1, True).wait_recv()
            for column in (1, 0):
                gather_core(DOWN_W, column, 1)
                for line in LINES:
                    reduce.over_y(column, line).start()
        elif index == 3:
            send_grad(0, True).wait_recv()
            gather_core(OUT_W, 1)
            send_x(OUT_W)
            gather_core(OUT_W, 0)
        elif index == 4:
            weight_part(0)
            gather_core(UP_W, 0)
        elif index == 5:
            gather_core(DOWN_W, 1)
            gather_core(DOWN_W, 0)
        elif index == 6:
            for line in LINES:
                reduce.add_y(1, line)
            send_x(DOWN_W)
        elif index == 7:
            take_x(UP_W)
            reduce.hop(UP_W, 0)
        elif index == 8:
            weight_part(1)
            take_x(OUT_W)
            reduce.hop(OUT_W, 0)
            take_x(DW_FIRST)
            reduce.hop(DW_FIRST, 0)
        elif index == 9:
            for line in LINES:
                reduce.add_y(0, line)
        elif index == 10:
            reduce.hop(UP_W, 1)
            reduce.hop(DW_FIRST, 1)
        elif index == 11:
            take_x(DOWN_W)
            reduce.hop(DOWN_W, 0)
            reduce.hop(OUT_W, 1)
            reduce.hop(DW_FIRST, 2)

    def step(index, carry):
        for when in range(1, 12):
            pl.when(index == when)(lambda when=when: chores(when))
        h, turn = index // turns, lax.rem(index, turns)
        _, lanes = member_rows(turns - 1 - turn)
        attend_back(
            h, lanes, q_x, q_here, do_x, grad_t, mixed, row_stats, k_t, k_wide, v_wide, grads, grad_k, grad_v, turn == 0
        )

        @pl.when(turn == turns - 1)
        def _():
            base = pl.multiple_of(3 * h * HEAD, HEAD)
            grads[pl.ds(base + HEAD, HEAD), :] = grad_k[...].astype(low)
            grads[pl.ds(base + 2 * HEAD, HEAD), :] = grad_v[...].astype(low)

        return carry

    lax.fori_loop(0, heads * turns, step, 0)

    weight_part(heads - 1)
    loads[1].wait()

    def part_for(turn):
        _, lanes = member_rows(turn)
        return mul(grads[:, lanes], weight_ref[...], TT)

    def share_near(index):
        return remote(
            near_send.at[index], near_recv.at[index], near_s.at[index], near_r.at[index], place.core
        )

    def share_far():
        return remote(far_sum, far_recv, far_s.at[0], far_r.at[0], place.across_y)

    near_send[0] = part_for(1).astype(low)
    share_near(0).start()
    near_own[...] = part_for(0).astype(low)
    share_near(0).wait_recv()
    far_sum[...] = add_low(near_own[...], near_recv[0])
    share_far().start()
    take_x(last)
    reduce.hop(last, 0)
    near_send[1] = part_for(2).astype(low)
    share_near(1).start()
    take_x(last - 1)
    reduce.hop(last - 1, 0)
    loads[2].wait()
    resid_ref[...] += part_for(3)
    reduce.hop(last, 1)
    reduce.hop(last - 1, 1)
    reduce.hop(UP_W, 2)
    reduce.hop(OUT_W, 2)
    reduce.hop(DOWN_W, 1)
    reduce.hop(last, 2)
    reduce.hop(last - 1, 2)
    reduce.hop(DOWN_W, 2)

    share = {UP_W: (up_last, up_other), OUT_W: (out_last, out_other)}

    def sum_y(array):
        mine_now = sums[array].at[0, place.z]
        return remote(mine_now, share[array][0], share_send.at[array, 0], share_recv.at[array, 0], place.across_y)

    def half_to_core(array):
        mine_now = sums[array].at[0, place.z]
        return remote(mine_now, share[array][1], share_send.at[array, 1], share_recv.at[array, 1], place.core)

    def quarter_to(turn, arriving=False):
        member = place.member(turn) if arriving else place.s
        return remote(
            down_sum.at[0, place.z, 0], down_all.at[member], share_send.at[2, turn], share_recv.at[2, turn], peers[turn]
        )

    def dw_to(h, turn, arriving=False):
        member = place.member(turn) if arriving else place.s
        return remote(
            dw.at[h, place.f], dw_all.at[h, member], share_send.at[DW_FIRST + h, turn],
            share_recv.at[DW_FIRST + h, turn], peers[turn],
        )

    reduce.settle(UP_W)
    sum_y(UP_W).start()
    reduce.settle(OUT_W)
    sum_y(OUT_W).start()
    for h in range(heads):
        reduce.settle(DW_FIRST + h)
        for turn in range(3):
            dw_to(h, turn).start()
    reduce.settle(DOWN_W)
    for turn in range(3):
        quarter_to(turn).start()
    for array in (UP_W, OUT_W):
        sum_y(array).wait()
        slot = sums[array].at[0, place.z]
        slot[...] = add_low(slot[...], share[array][0][...])
        half_to_core(array).start()

    share_near(1).wait_recv()
    share_far().wait_recv()
    grad_layer = resid_ref[...] + near_recv[1].astype(full) + far_recv[...].astype(full)
    length = length_ref[0]
    rows_at = place.s * local_rows + lax.broadcasted_iota(jnp.int32, (local_rows, 1), 0)
    in_read = rows_at < MEM
    in_write = (rows_at >= length - MEM) & (rows_at < length)
    input_out[...] = jnp.where(in_read | in_write, 0.0, grad_layer)
    line_at = lax.broadcasted_iota(jnp.int32, (32, local_rows), 0)
    row_at = place.s * local_rows + lax.broadcasted_iota(jnp.int32, (32, local_rows), 1)
    wanted = jnp.where(line_at < 16, line_at, length - MEM + line_at - 16)
    used = (line_at < MEM) | ((line_at >= 16) & (line_at < 16 + MEM))
    pick = jnp.where(used & (wanted == row_at), 1.0, 0.0).astype(low)
    memory_all[place.s] = mul(pick, grad_layer.astype(low)).astype(low)

    def memory_to(turn, arriving=False):
        member = place.member(turn) if arriving else place.s
        return remote(
            memory_all.at[place.s], memory_all.at[member], memory_s.at[turn], memory_r.at[turn], peers[turn]
        )

    for turn in range(3):
        memory_to(turn).start()

    for array, out in ((UP_W, up_out), (OUT_W, out_out)):
        columns = out.shape[1] // 2
        out[:, pl.ds(pl.multiple_of(place.c * columns, columns), columns)] = sums[array][0, place.z].astype(full)
        half_to_core(array).wait()
        out[:, pl.ds(pl.multiple_of((1 - place.c) * columns, columns), columns)] = share[array][1][...].astype(full)
    down_all[place.s] = down_sum[0, place.z, 0]
    for turn in range(3):
        quarter_to(turn).wait_send()
        quarter_to(turn, True).wait_recv()
    quarter = down_out.shape[0] // 4
    for member in range(4):
        down_out[member * quarter : (member + 1) * quarter, :] = down_all[member].astype(full)
    shard = qkv_out.shape[0]
    for h in range(heads):
        dw_all[h, place.s] = dw[h, place.f]
        for turn in range(3):
            dw_to(h, turn).wait_send()
            dw_to(h, turn, True).wait_recv()
        for member in range(4):
            for kind in range(3):
                start = kind * width + (member * heads + h) * HEAD
                qkv_out[:, start : start + HEAD] = dw_all[
                    h, member, :shard, kind * HEAD : (kind + 1) * HEAD
                ].astype(full)
    vector_sum = dw_all[heads - 1, 0, shard:, :].astype(full)
    for member in range(1, 4):
        vector_sum = vector_sum + dw_all[heads - 1, member, shard:, :].astype(full)
    vector_out[...] = vector_sum
    for turn in range(3):
        memory_to(turn).wait_send()
        memory_to(turn, True).wait_recv()
    memory = memory_all[0].astype(full)
    for member in range(1, 4):
        memory = memory + memory_all[member].astype(full)
    read_out[...] = memory[:MEM]
    write_out[...] = memory[16 : 16 + MEM]
    for array in range(DW_FIRST + heads):
        reduce.finish(array)
    for turn in range(3):
        send_grad(turn).wait_send()
    for index in range(2):
        share_near(index).wait_send()
    share_far().wait_send()


def back(lengths, grad_own, saved, vectors, rows, weight, resid, up_given, down_given, out_given):
    q_x, k_t, k_wide, v_wide, mixed, row_stats = saved
    heads, _, slot_rows = q_x.shape
    width, local_rows = grad_own.shape
    hidden = up_given.shape[1]
    shard, head_cols = width // 8, heads * HEAD
    half, small, piece = hidden // 2, width // 2, hidden // 32
    vmem = pl.BlockSpec(memory_space=pltpu.VMEM)
    anywhere = pl.BlockSpec(memory_space=pl.ANY)
    dma = pltpu.SemaphoreType.DMA
    arrays = DW_FIRST + heads

    def held(*shape, kind=low):
        return pltpu.VMEM(shape, kind)

    tall = (shard + 16, 3 * HEAD)
    return pl.pallas_call(
        back_kernel,
        in_specs=[pl.BlockSpec(memory_space=pltpu.SMEM)] + [vmem] * 8 + [anywhere] * 6,
        out_specs=[vmem] * 8,
        out_shape=[
            jax.ShapeDtypeStruct((local_rows, width), full),
            jax.ShapeDtypeStruct((MEM, width), full),
            jax.ShapeDtypeStruct((MEM, width), full),
            jax.ShapeDtypeStruct((shard, 3 * width), full),
            jax.ShapeDtypeStruct((16, 3 * HEAD), full),
            jax.ShapeDtypeStruct((shard, hidden), full),
            jax.ShapeDtypeStruct((hidden // 8, width), full),
            jax.ShapeDtypeStruct((shard, width), full),
        ],
        scratch_shapes=[
            held(head_cols, slot_rows), held(WIDE, local_rows), held(WIDE, local_rows), held(3 * head_cols, slot_rows),
            held(HEAD, slot_rows, kind=full), held(HEAD, slot_rows, kind=full),
            held(slot_rows, width), held(width, 3 * head_cols), held(local_rows, width, kind=full),
            held(2, 4, shard, half), held(2, 4, shard, small), held(2, 4, 2, piece, width),
            held(2, 4, shard, half), held(2, 4, shard, small), held(2, 4, 2, piece, width),
            held(heads, 8, *tall), held(2, 4, piece, width),
            held(4, shard, half), held(4, shard, small), held(4, piece, width), held(heads, 4, *tall),
            held(2, 4, shard, half), held(2, 4, shard, small), held(2, 4, piece, width), held(heads, 2, 4, *tall),
            held(shard, half), held(shard, small), held(shard, half), held(shard, small),
            held(4, piece, width), held(heads, 4, *tall),
            held(2, local_rows, width), held(2, local_rows, width), held(local_rows, width),
            held(local_rows, width), held(local_rows, width), held(4, 32, width),
            dma((3,)), dma((3,)), dma((3,)), dma((4, 2, 4)), dma((arrays, 3)), dma((arrays, 3)),
            dma((2,)), dma((2,)), dma((1,)), dma((1,)), dma((3,)), dma((3,)),
            dma((4, 2, 4)), dma((4, 2, 4)), dma((2, 4)), dma((2, 4)), dma((arrays, 4)), dma((arrays, 4)),
            dma((arrays, 2, 4)), dma((arrays, 2, 4)),
        ],
        compiler_params=pltpu.CompilerParams(
            vmem_limit_bytes=VMEM_BYTES, collective_id=1, has_side_effects=True
        ),
        name="back",
    )(
        lengths, grad_own, q_x, k_t, k_wide, v_wide, mixed, row_stats, vectors, rows, weight, resid,
        up_given, down_given, out_given,
    )


def normalize(values, gain_vec, shift_vec):
    centre = values - jnp.mean(values, axis=-1, keepdims=True)
    factor = lax.rsqrt(jnp.mean(centre * centre, axis=-1, keepdims=True) + norm_epsilon)
    return centre * factor * gain_vec + shift_vec


def column_sums(values):
    return jnp.sum(values, axis=0, dtype=full)


def per_device(
    tokens, read_memory, write_memory, lengths, qkv_weight, qv_bias, out_weight, out_bias, norm1_gain,
    norm1_bias, up_weight, up_bias, down_weight, down_bias, norm2_gain, norm2_bias, cotangent,
):
    seq_count = lax.axis_size("seq")
    fsdp_count = lax.axis_size("fsdp")
    seq_place = lax.axis_index("seq")
    local_rows, width = tokens.shape
    head_cols = width // seq_count
    shard = width // fsdp_count
    length = lengths[0]
    places = seq_place * local_rows + jnp.arange(local_rows, dtype=jnp.int32)
    in_slot = (places < length)[:, None]
    memory_slots = jnp.arange(MEM, dtype=jnp.int32)
    pick_read = places[:, None] == memory_slots[None, :]
    pick_write = places[:, None] == length - MEM + memory_slots[None, :]
    is_memory = jnp.any(pick_read | pick_write, axis=1)[:, None]
    picks = jnp.concatenate([pick_read, pick_write], axis=1).astype(full)
    memory = jnp.concatenate([read_memory[0], write_memory[0]], axis=0)
    layer_in = jnp.where(is_memory, mul(picks.astype(low), memory).astype(low), tokens)

    heads = head_cols // HEAD
    own_shard = lax.dynamic_slice_in_dim(
        qkv_weight.reshape(shard, 3, seq_count, heads, HEAD), seq_place, 1, 2
    )
    own_shard = jnp.transpose(own_shard[:, :, 0], (0, 2, 1, 3)).reshape(shard, 3 * head_cols)
    vectors = (qv_bias, out_bias, norm1_gain, norm1_bias, up_bias, down_bias, norm2_gain, norm2_bias)
    packed = jnp.concatenate(vectors)
    on_block = (fsdp_count, seq_count) == (8, 4)
    if on_block:
        spare = jnp.zeros((14, 3 * head_cols), low)
        piece = jnp.concatenate([own_shard, packed.reshape(2, -1), spare], axis=0)
        (rows, weight, pieces, q_x, k_t, k_wide, v_wide, mixed, row_stats, up_full, down_full, out_full,
         attended) = front(lengths, layer_in, piece, up_weight, down_weight, out_weight)
        packed = pieces[:, shard : shard + 2].reshape(fsdp_count, -1).astype(full)
    else:
        rows = lax.all_gather(layer_in, "seq", axis=0, tiled=True)
        weight = lax.all_gather(own_shard, "fsdp", axis=0, tiled=True)
        packed = lax.all_gather(packed.reshape(1, -1), "fsdp", axis=0, tiled=True).astype(full)
    whole, start = [], 0
    for vector in vectors:
        whole.append(packed[:, start : start + vector.shape[0]].reshape(-1))
        start += vector.shape[0]
    qv_vec, out_vec, gain_one, shift_one, up_vec, down_vec, gain_two, shift_two = whole
    if not on_block:
        own_qv = lax.dynamic_slice_in_dim(qv_vec.reshape(2, seq_count, head_cols), seq_place, 1, 1)
        bias = jnp.concatenate([own_qv[0, 0], own_qv[1, 0]])
        bias = jnp.broadcast_to(bias, (8, bias.shape[0]))
        out_full = lax.all_gather(out_weight, "fsdp", axis=0, tiled=True)
        up_full = lax.all_gather(up_weight, "fsdp", axis=0, tiled=True)
        down_full = lax.all_gather(down_weight, "fsdp", axis=0, tiled=True)
        q_x, k_t, k_wide, v_wide, mixed, mixed_low, row_stats = attention_forward(lengths, rows, weight, bias)
        attended = lax.all_to_all(mixed_low, "seq", split_axis=1, concat_axis=0, tiled=True)
    resid_one = layer_in.astype(full) + mul(attended, out_full, TN) + out_vec
    middle, norm_one_back = jax.vjp(normalize, resid_one, gain_one, shift_one)
    middle_low = middle.astype(low)
    up_pre = mul(middle_low, up_full) + up_vec
    gelu_out, gelu_back = jax.vjp(partial(jax.nn.gelu, approximate=False), up_pre)
    hidden = gelu_out.astype(low)
    down_pre = mul(hidden, down_full) + down_vec
    final, norm_two_back = jax.vjp(normalize, middle + down_pre, gain_two, shift_two)
    output = jnp.where(in_slot, final, 0.0).astype(low)
    grad_final = jnp.where(in_slot, cotangent.astype(full), 0.0)
    grad_resid_two, grad_gain_two, grad_shift_two = norm_two_back(grad_final)
    grad_down = grad_resid_two.astype(low)
    grad_down_weight = mul(hidden, grad_down, TN)
    (grad_up_pre,) = gelu_back(mul(grad_down, down_full, NT))
    grad_up = grad_up_pre.astype(low)
    grad_up_weight = mul(middle_low, grad_up, TN)
    grad_middle = grad_resid_two + mul(grad_up, up_full, NT)
    grad_resid_one, grad_gain_one, grad_shift_one = norm_one_back(grad_middle)
    grad_branch = grad_resid_one.astype(low)
    grad_out_weight = mul(attended, grad_branch)
    grad_attended = mul(out_full, grad_branch, NT).astype(low)
    vector_grads = [
        column_sums(grad_branch), grad_gain_one, grad_shift_one, column_sums(grad_up),
        column_sums(grad_down), grad_gain_two, grad_shift_two,
    ]
    packed_grad = jnp.concatenate([v.reshape(fsdp_count, -1) for v in vector_grads], axis=1)
    saved = (q_x, k_t, k_wide, v_wide, mixed, row_stats)
    if on_block:
        packed_grad = jnp.pad(
            packed_grad.reshape(fsdp_count, 5, head_cols), ((0, 0), (1, 10), (0, 0))
        )
        (input_grad, grad_read, grad_write, qkv_out, vector_sum, up_out, down_out, out_out) = back(
            lengths, grad_attended, saved, packed_grad, rows, weight, grad_resid_one,
            grad_up_weight.astype(low), grad_down_weight.astype(low), grad_out_weight.astype(low),
        )
        own_vectors = vector_sum[:6].reshape(-1)
    else:
        grad_t = lax.all_to_all(grad_attended, "seq", split_axis=0, concat_axis=1, tiled=True)
        partial_in, weight_part, sums = attention_backward(*saved, grad_t, rows, weight)
        from_heads = lax.psum_scatter(partial_in, "seq", scatter_dimension=0, tiled=True).astype(full)
        grad_layer_in = grad_resid_one + from_heads
        input_grad = jnp.where(is_memory, 0.0, grad_layer_in)
        grad_memory = lax.dot_general(
            picks, grad_layer_in, TN, precision=lax.Precision.HIGHEST, preferred_element_type=full
        )
        grad_memory = lax.psum(grad_memory.astype(low), "seq").astype(full)
        grad_read, grad_write = grad_memory[:MEM], grad_memory[MEM:]
        sums = sums[:, 0].reshape(heads, 3, HEAD)
        own_sums = jnp.stack([sums[:, 0].reshape(-1), sums[:, 2].reshape(-1)])[:, None]
        zero_qv = jnp.zeros((2, seq_count, head_cols), full)
        qv_grad = lax.dynamic_update_slice_in_dim(zero_qv, own_sums, seq_place, 1)
        packed_grad = jnp.concatenate([qv_grad.reshape(fsdp_count, -1), packed_grad], axis=1)
        packed_sum = lax.psum(packed_grad, ("fsdp", "seq"))
        own_vectors = lax.dynamic_index_in_dim(packed_sum, lax.axis_index("fsdp"), 0, False)

        def both_axes(part):
            piece = lax.psum_scatter(part.astype(low), "fsdp", scatter_dimension=0, tiled=True)
            return lax.psum(piece, "seq").astype(full)

        qkv_piece = lax.psum_scatter(weight_part, "fsdp", scatter_dimension=0, tiled=True)
        qkv_parts = lax.all_gather(qkv_piece, "seq", axis=0).reshape(seq_count, shard, heads, 3, HEAD)
        qkv_out = jnp.transpose(qkv_parts, (1, 3, 0, 2, 4)).reshape(shard, 3 * width).astype(full)
        up_out, down_out, out_out = both_axes(grad_up_weight), both_axes(grad_down_weight), both_axes(grad_out_weight)
    vector_outs, start = [], 0
    for vector in vectors:
        vector_outs.append(own_vectors[start : start + vector.shape[0]])
        start += vector.shape[0]
    qv_out, out_b_out, gain_one_out, shift_one_out, up_b_out, down_b_out, gain_two_out, shift_two_out = vector_outs
    return (
        output, input_grad, grad_read[None], grad_write[None], qkv_out, qv_out, out_out, out_b_out, gain_one_out,
        shift_one_out, up_out, up_b_out, down_out, down_b_out, gain_two_out, shift_two_out,
    )


def solution(mesh):
    rows, piece = P(("fsdp", "seq"), None), P("fsdp")
    matrix, memory = P("fsdp", None), P("fsdp", None, None)
    in_specs = (
        rows, memory, memory, piece, matrix, piece, matrix, piece, piece, piece, matrix, piece, matrix,
        piece, piece, piece, rows,
    )
    out_specs = (
        rows, rows, memory, memory, matrix, piece, matrix, piece, piece, piece, matrix, piece, matrix,
        piece, piece, piece,
    )
    return jax.shard_map(per_device, mesh=mesh, in_specs=in_specs, out_specs=out_specs, check_vma=False)
```

```python
from functools import partial

import jax
import jax.numpy as jnp
from jax import lax
from jax.experimental import pallas as pl
from jax.experimental.pallas import tpu as pltpu
from jax.sharding import PartitionSpec as P

HEAD = 64
MEM = 10
WIDE = 128
VMEM_BYTES = 64000 * 1024

norm_epsilon = 1e-06
masked_score = -1e30
low = jnp.bfloat16
full = jnp.float32

NN = (((1,), (0,)), ((), ()))
NT = (((1,), (1,)), ((), ()))
TN = (((0,), (0,)), ((), ()))
TT = (((0,), (1,)), ((), ()))


def mul(left, right, dims=NN):
    return lax.dot_general(left, right, dims, preferred_element_type=full)


def three_parts(value):
    high = value.astype(low)
    rest = value - high.astype(full)
    middle = rest.astype(low)
    return high, middle, (rest - middle.astype(full)).astype(low)


def stack_rows(rows, columns):
    place = lax.broadcasted_iota(jnp.int32, (HEAD, columns), 0)
    block = jnp.zeros((HEAD, columns), full)
    for index, row in enumerate(rows):
        block = jnp.where(place == index, row, block)
    return block.astype(low)


def project_block(start, length, rows_ref, weight_ref, bias_q, bias_v, q_x, k_t, v_x, k_wide, v_wide, step):
    head_cols = k_t.shape[0]
    lanes = pl.ds(start, step)
    made = mul(weight_ref[...], rows_ref[lanes, :], TT)
    place = start + lax.broadcasted_iota(jnp.int32, (1, step), 1)
    key_bias = jnp.where(place < length, 0.0, masked_score)
    one = jnp.ones((1, step), full)
    query_extra = stack_rows([one], step)
    key_extra = stack_rows([key_bias, one, one, one], step)
    value_extra = stack_rows([one, one, one], step)
    for h in range(head_cols // HEAD):
        own = slice(h * HEAD, (h + 1) * HEAD)
        base = 3 * h * HEAD
        query = (made[base : base + HEAD] + bias_q[own]).astype(low)
        q_x[h, :HEAD, lanes] = query * jnp.asarray(HEAD**-0.5, low)
        q_x[h, HEAD:, lanes] = query_extra
        k_t[own, lanes] = made[base + HEAD : base + 2 * HEAD].astype(low)
        v_x[h, :HEAD, lanes] = (made[base + 2 * HEAD : base + 3 * HEAD] + bias_v[own]).astype(low)
        v_x[h, HEAD:, lanes] = value_extra
        k_wide[h, lanes, :] = jnp.transpose(jnp.concatenate([k_t[own, lanes], key_extra], axis=0))
        v_wide[h, lanes, :] = jnp.transpose(v_x[h, :, lanes])


def project_heads(length, rows_ref, weight_ref, bias_ref, q_x, k_t, v_x, k_wide, v_wide):
    head_cols = k_t.shape[0]
    bias = jnp.transpose(bias_ref[...])[:, 0:1]
    for start in range(0, rows_ref.shape[0], 512):
        project_block(
            start, length, rows_ref, weight_ref, bias[:head_cols], bias[head_cols:],
            q_x, k_t, v_x, k_wide, v_wide, 512,
        )


def attend_block(h, lanes, q_x, k_wide, v_x, mixed, mixed_low, row_stats):
    scores = mul(k_wide[h], q_x[h, :, lanes])
    row_max = jnp.max(scores, axis=0, keepdims=True)
    probs = jnp.exp(scores - row_max).astype(low)
    total = mul(v_x[h, : HEAD + 16], probs)
    row_sum = total[HEAD : HEAD + 1]
    own = pl.ds(h * HEAD, HEAD)
    result = total[:HEAD] / row_sum
    mixed[own, lanes] = result
    mixed_low[own, lanes] = result.astype(low)
    row_stats[h, :, lanes] = jnp.broadcast_to(row_max + jnp.log(row_sum), (8, result.shape[1]))


def forward_kernel(
    length_ref, rows_ref, weight_ref, bias_ref, q_x, k_t, k_wide, v_wide, mixed, mixed_low, row_stats, v_x
):
    project_heads(length_ref[0], rows_ref, weight_ref, bias_ref, q_x, k_t, v_x, k_wide, v_wide)
    heads = q_x.shape[0]
    block = 512
    blocks = q_x.shape[2] // block

    def step(index, carry):
        h = index // blocks
        start = pl.multiple_of(lax.rem(index, blocks) * block, block)
        attend_block(h, pl.ds(start, block), q_x, k_wide, v_x, mixed, mixed_low, row_stats)
        return carry

    lax.fori_loop(0, heads * blocks, step, 0)


def attention_forward(length, rows, weight, bias):
    slot_rows = rows.shape[0]
    head_cols = weight.shape[1] // 3
    heads = head_cols // HEAD
    vmem = pl.BlockSpec(memory_space=pltpu.VMEM)
    return pl.pallas_call(
        forward_kernel,
        in_specs=[pl.BlockSpec(memory_space=pltpu.SMEM), vmem, vmem, vmem],
        out_specs=[vmem] * 7,
        out_shape=[
            jax.ShapeDtypeStruct((heads, WIDE, slot_rows), low),
            jax.ShapeDtypeStruct((head_cols, slot_rows), low),
            jax.ShapeDtypeStruct((heads, slot_rows, WIDE), low),
            jax.ShapeDtypeStruct((heads, slot_rows, WIDE), low),
            jax.ShapeDtypeStruct((head_cols, slot_rows), full),
            jax.ShapeDtypeStruct((head_cols, slot_rows), low),
            jax.ShapeDtypeStruct((heads, 8, slot_rows), full),
        ],
        scratch_shapes=[pltpu.VMEM((heads, WIDE, slot_rows), low)],
        compiler_params=pltpu.CompilerParams(vmem_limit_bytes=VMEM_BYTES),
        name="attention_forward",
    )(length, rows, weight, bias)


def attend_back(h, lanes, q_x, q_here, do_x, grad_t, mixed, row_stats, k_t, k_wide, v_wide, grads, grad_k, grad_v, first):
    own = pl.ds(pl.multiple_of(h * HEAD, HEAD), HEAD)
    grad = grad_t[own, lanes]
    columns = grad.shape[1]
    delta = jnp.sum(grad.astype(full) * mixed[own, lanes], axis=0, keepdims=True)
    parts = [part.astype(full) for part in three_parts(-delta)]
    do_x[:HEAD, :] = grad
    do_x[HEAD:, :] = stack_rows(parts, columns)
    parts = [part.astype(full) for part in three_parts(-row_stats[h, 0:1, lanes])]
    q_here[:HEAD, :] = q_x[h, :HEAD, lanes]
    q_here[HEAD:, :] = stack_rows([jnp.ones((1, columns), full)] + parts, columns)
    probs = jnp.exp(mul(k_wide[h], q_here[...]))
    grad_scores = (probs * mul(v_wide[h], do_x[...])).astype(low)
    value_part = mul(grad, probs.astype(low), NT)
    key_part = mul(q_here[:HEAD, :], grad_scores, NT)

    @pl.when(first)
    def _():
        grad_v[...] = value_part
        grad_k[...] = key_part

    @pl.when(jnp.logical_not(first))
    def _():
        grad_v[...] += value_part
        grad_k[...] += key_part

    query_part = mul(k_t[own, :], grad_scores) * HEAD**-0.5
    grads[pl.ds(pl.multiple_of(3 * h * HEAD, HEAD), HEAD), lanes] = query_part.astype(low)


def backward_kernel(
    q_in, k_t, k_wide, v_wide, mixed, row_stats, grad_t, rows_ref, weight_ref,
    partial_out, weight_out, sums_out, q_here, do_x, grads, grad_k, grad_v,
):
    heads, _, slot_rows = q_in.shape
    block = 512
    blocks = slot_rows // block

    def step(index, carry):
        h = index // blocks
        turn = lax.rem(index, blocks)
        start = pl.multiple_of(turn * block, block)
        attend_back(
            h, pl.ds(start, block), q_in, q_here, do_x, grad_t, mixed, row_stats, k_t, k_wide, v_wide, grads, grad_k,
            grad_v, turn == 0,
        )

        @pl.when(turn == blocks - 1)
        def _():
            base = pl.multiple_of(3 * h * HEAD, HEAD)
            grads[pl.ds(base + HEAD, HEAD), :] = grad_k[...].astype(low)
            grads[pl.ds(base + 2 * HEAD, HEAD), :] = grad_v[...].astype(low)

        return carry

    lax.fori_loop(0, heads * blocks, step, 0)
    for start in range(0, slot_rows, block):
        partial_out[start : start + block, :] = mul(
            grads[:, start : start + block], weight_ref[...], TT
        ).astype(partial_out.dtype)
    weight_out[...] = jnp.transpose(mul(grads[...], rows_ref[...])).astype(weight_out.dtype)
    sums_out[...] = jnp.broadcast_to(
        jnp.sum(grads[...].astype(full), axis=1, keepdims=True), sums_out.shape
    )


def attention_backward(q_x, k_t, k_wide, v_wide, mixed, row_stats, grad_t, rows, weight):
    heads, _, slot_rows = q_x.shape
    width, all_cols = weight.shape
    vmem = pl.BlockSpec(memory_space=pltpu.VMEM)
    return pl.pallas_call(
        backward_kernel,
        in_specs=[vmem] * 9,
        out_specs=[vmem] * 3,
        out_shape=[
            jax.ShapeDtypeStruct((slot_rows, width), low),
            jax.ShapeDtypeStruct((width, all_cols), low),
            jax.ShapeDtypeStruct((all_cols, WIDE), full),
        ],
        scratch_shapes=[
            pltpu.VMEM((WIDE, 512), low),
            pltpu.VMEM((WIDE, 512), low),
            pltpu.VMEM((all_cols, slot_rows), low),
            pltpu.VMEM((HEAD, slot_rows), full),
            pltpu.VMEM((HEAD, slot_rows), full),
        ],
        compiler_params=pltpu.CompilerParams(vmem_limit_bytes=VMEM_BYTES),
        name="attention_backward",
    )(q_x, k_t, k_wide, v_wide, mixed, row_stats, grad_t, rows, weight)


MESH = pl.DeviceIdType.MESH
OWN, RELATIONS = 0, 7
UP_W, OUT_W, DOWN_W, QKV_W = 0, 1, 2, 3


def offset_of(relation):
    return (0, -1, -2, -3, 1, 2, 3)[relation]


class Place:
    def __init__(self):
        self.f, self.s = lax.axis_index("fsdp"), lax.axis_index("seq")
        self.z, self.x = self.f // 2, lax.rem(self.f, 2)
        self.y, self.c = self.s // 2, lax.rem(self.s, 2)
        self.core = (self.f, 2 * self.y + 1 - self.c)
        self.across_y = (self.f, 2 * (1 - self.y) + self.c)
        self.diagonal = (self.f, 2 * (1 - self.y) + 1 - self.c)
        self.across_x = (2 * self.z + 1 - self.x, self.s)
        self.above = (self.f + 2, self.s)
        self.below = (self.f - 2, self.s)

    def has(self, relation):
        offset = offset_of(relation)
        return (self.z + offset >= 0) & (self.z + offset <= 3)

    def source(self, relation, column):
        own_column = self.f + 2 * offset_of(relation)
        return own_column if column == 0 else own_column + 1 - 2 * self.x

    def member(self, turn):
        flip_y = 1 - turn // 2
        flip_c = lax.rem(turn, 2) if not isinstance(turn, int) else turn % 2
        flip_c = flip_c + (1 - 2 * flip_c) * (turn // 2)
        return 2 * lax.rem(self.y + flip_y, 2) + lax.rem(self.c + flip_c, 2)


def remote(src, dst, send, recv, where):
    return pltpu.make_async_remote_copy(
        src_ref=src, dst_ref=dst, send_sem=send, recv_sem=recv, device_id=where, device_id_type=MESH
    )


def greet(place, everyone):
    barrier = pltpu.get_barrier_semaphore()
    near = [place.core, place.across_y, place.diagonal, place.across_x]
    for where in near:
        pl.semaphore_signal(barrier, inc=1, device_id=where, device_id_type=MESH)

    @pl.when(place.z > 0)
    def _():
        pl.semaphore_signal(barrier, inc=1, device_id=place.below, device_id_type=MESH)

    @pl.when(place.z < 3)
    def _():
        pl.semaphore_signal(barrier, inc=1, device_id=place.above, device_id_type=MESH)

    ends = jnp.where((place.z == 0) | (place.z == 3), 1, 2)
    pl.semaphore_wait(barrier, len(near) + ends)


class Gather:
    def __init__(self, place, own, whole, sems):
        self.place, self.own, self.whole = place, own, whole
        (self.z_send, self.z_recv, self.x_send, self.x_recv, self.c_send, self.c_recv,
         self.y_send, self.y_recv, self.d_send, self.d_recv) = sems

    def piece(self, array, source, quarter=None):
        c = self.place.c
        ref = self.whole[array]
        if array == QKV_W:
            return ref.at[source]
        if array == DOWN_W:
            rows = ref.shape[0] // 8
            part = rows // 4
            quarter = self.place.s if quarter is None else quarter
            return ref.at[pl.ds(pl.multiple_of(source * rows + quarter * part, part), part)]
        rows, columns = ref.shape[0] // 8, ref.shape[1] // 2
        return ref.at[
            pl.ds(pl.multiple_of(source * rows, rows), rows),
            pl.ds(pl.multiple_of(c * columns, columns), columns),
        ]

    def own_piece(self, array):
        ref = self.own[array]
        if array == QKV_W:
            return ref
        if array == DOWN_W:
            part = ref.shape[0] // 4
            return ref.at[pl.ds(pl.multiple_of(self.place.s * part, part), part)]
        columns = ref.shape[1] // 2
        return ref.at[:, pl.ds(pl.multiple_of(self.place.c * columns, columns), columns)]

    def along_z(self, array, relation, way):
        here = self.piece(array, self.place.source(relation, 0))
        src = self.own_piece(array) if relation == OWN else here
        step = abs(offset_of(relation))
        where = self.place.above if way == 0 else self.place.below
        return remote(src, here, self.z_send.at[array, way, step], self.z_recv.at[array, way, step], where)

    def z_ways(self, relation):
        place = self.place
        ways = []
        if offset_of(relation) <= 0:
            ways.append((0, place.has(relation) & (place.z < 3)))
        if offset_of(relation) >= 0:
            ways.append((1, place.has(relation) & (place.z > 0)))
        return ways

    def wait_z(self, array, relation):
        way = 0 if offset_of(relation) < 0 else 1
        step = abs(offset_of(relation)) - 1
        here = self.piece(array, self.place.source(relation, 0))
        where = self.place.below if way == 0 else self.place.above
        remote(
            here, here, self.z_send.at[array, way, step], self.z_recv.at[array, way, step], where
        ).wait_recv()

    def over_x(self, array, relation):
        here = self.piece(array, self.place.source(relation, 0))
        src = self.own_piece(array) if relation == OWN else here
        return remote(
            src, here, self.x_send.at[array, relation], self.x_recv.at[array, relation], self.place.across_x
        )

    def from_x(self, array, relation):
        here = self.piece(array, self.place.source(relation, 1))
        return remote(
            here, here, self.x_send.at[array, relation], self.x_recv.at[array, relation], self.place.across_x
        )

    def to_core(self, array, relation, column):
        here = self.piece(array, self.place.source(relation, column))
        return remote(
            here, here, self.c_send.at[array, relation, column], self.c_recv.at[array, relation, column],
            self.place.core,
        )

    def over_y(self, relation, column):
        here = self.piece(DOWN_W, self.place.source(relation, column))
        return remote(
            here, here, self.y_send.at[relation, column], self.y_recv.at[relation, column], self.place.across_y
        )

    def far_quarter(self, relation, column):
        return self.piece(
            DOWN_W, self.place.source(relation, column), 2 * (1 - self.place.y) + self.place.c
        )

    def from_y(self, relation, column):
        here = self.far_quarter(relation, column)
        return remote(
            here, here, self.y_send.at[relation, column], self.y_recv.at[relation, column], self.place.across_y
        )

    def far_to_core(self, relation, column):
        here = self.far_quarter(relation, column)
        return remote(
            here, here, self.d_send.at[relation, column], self.d_recv.at[relation, column], self.place.core
        )

    def when(self, relation, action):
        if relation == OWN:
            action()
        else:
            pl.when(self.place.has(relation))(action)

    def arrive_z(self, array, relation):
        def action():
            if relation != OWN:
                self.wait_z(array, relation)
            for way, holds in self.z_ways(relation):
                pl.when(holds)(lambda way=way: self.along_z(array, relation, way).start())
            self.over_x(array, relation).start()
            if array != QKV_W and relation != OWN:
                self.to_core(array, relation, 0).start()
                if array == DOWN_W:
                    self.over_y(relation, 0).start()

        self.when(relation, action)

    def arrive_x(self, array, relation):
        def action():
            self.from_x(array, relation).wait_recv()
            if array != QKV_W:
                self.to_core(array, relation, 1).start()
                if array == DOWN_W:
                    self.over_y(relation, 1).start()

        self.when(relation, action)

    def arrive_y(self, relation, column):
        def action():
            self.from_y(relation, column).wait_recv()
            self.far_to_core(relation, column).start()

        if (relation, column) != (OWN, 0):
            self.when(relation, action)

    def finish(self, array):
        for relation in range(RELATIONS):
            def action():
                self.over_x(array, relation).wait_send()
                for way, holds in self.z_ways(relation):
                    pl.when(holds)(lambda way=way: self.along_z(array, relation, way).wait_send())
                if array == QKV_W:
                    return
                for column in range(2):
                    if (relation, column) == (OWN, 0):
                        continue
                    self.to_core(array, relation, column).wait()
                    if array == DOWN_W:
                        self.over_y(relation, column).wait_send()
                        self.far_to_core(relation, column).wait()

            self.when(relation, action)


def front_kernel(
    length_ref, rows_in, qkv_in, up_in, down_in, out_in,
    rows_ref, weight_ref, pieces, q_x, k_t, k_wide, v_wide, mixed, row_stats, up_full, down_full, out_full,
    attended,
    v_x, mixed_low, row_send, row_recv, far_send, far_recv, mix_send, mix_recv, local_sem, *gather_sems,
):
    place = Place()
    slot_rows, width = rows_ref.shape
    local_rows = rows_in.shape[0]
    head_cols = k_t.shape[0]
    heads = head_cols // HEAD
    own_shards = {UP_W: up_in, DOWN_W: down_in, OUT_W: out_in, QKV_W: qkv_in}
    whole = {UP_W: up_full, DOWN_W: down_full, OUT_W: out_full, QKV_W: pieces}
    gather = Gather(place, own_shards, whole, gather_sems)
    greet(place, None)

    halves = 2
    part = local_rows // halves

    def rows_of(member, half):
        return pl.ds(pl.multiple_of(member * local_rows + half * part, part), part)

    def send_rows(half, index):
        where = (place.core, place.across_y)[index]
        return remote(
            rows_in.at[pl.ds(half * part, part)], rows_ref.at[rows_of(place.s, half)],
            row_send.at[index, half], row_recv.at[index, half], where,
        )

    def rows_from(half, index):
        member = (2 * place.y + 1 - place.c, 2 * (1 - place.y) + place.c)[index]
        here = rows_ref.at[rows_of(member, half)]
        where = (place.core, place.across_y)[index]
        return remote(here, here, row_send.at[index, half], row_recv.at[index, half], where)

    def pass_rows(half, arriving):
        flip = place.c if not arriving else 1 - place.c
        here = rows_ref.at[rows_of(2 * (1 - place.y) + flip, half)]
        return remote(here, here, far_send.at[half], far_recv.at[half], place.core)

    for half in range(halves):
        send_rows(half, 1).start()
        send_rows(half, 0).start()
    gather.arrive_z(QKV_W, OWN)

    def own_copies():
        copies = []
        for index, array in enumerate((UP_W, DOWN_W, OUT_W)):
            rows = own_shards[array].shape[0]
            copies.append(pltpu.make_async_copy(
                own_shards[array], whole[array].at[pl.ds(pl.multiple_of(place.f * rows, rows), rows)],
                local_sem.at[index],
            ))
        copies.append(pltpu.make_async_copy(qkv_in, pieces.at[place.f], local_sem.at[3]))
        copies.append(pltpu.make_async_copy(
            rows_in, rows_ref.at[pl.ds(pl.multiple_of(place.s * local_rows, local_rows), local_rows)],
            local_sem.at[4],
        ))
        return copies

    for copy in own_copies():
        copy.start()

    for relation in (1, 4):
        gather.arrive_z(QKV_W, relation)
    gather.arrive_z(UP_W, OWN)
    for relation in (2, 5):
        gather.arrive_z(QKV_W, relation)
    gather.arrive_z(OUT_W, OWN)
    gather.arrive_z(DOWN_W, OWN)
    rows_from(0, 1).wait_recv()
    pass_rows(0, False).start()
    for relation in (3, 6):
        gather.arrive_z(QKV_W, relation)
    for relation in (1, 4):
        gather.arrive_z(UP_W, relation)
    for relation in range(RELATIONS):
        gather.arrive_x(QKV_W, relation)
    for copy in own_copies()[3:]:
        copy.wait()

    shard = weight_ref.shape[0] // 8
    for source in range(8):
        weight_ref[source * shard : (source + 1) * shard, :] = pieces[source, :shard, :]
    bias_q = jnp.transpose(pieces[place.s, shard : shard + 16, :].astype(full))[:head_cols, 0:1]
    bias_v = jnp.transpose(pieces[4 + place.s, shard : shard + 16, :].astype(full))[:head_cols, 0:1]
    length = length_ref[0]

    def project(member):
        start = pl.multiple_of(member * local_rows, local_rows)
        project_block(
            start, length, rows_ref, weight_ref, bias_q, bias_v, q_x, k_t, v_x, k_wide, v_wide, local_rows
        )

    project(place.s)
    for half in range(halves):
        rows_from(half, 0).wait_recv()
    project(2 * place.y + 1 - place.c)
    rows_from(1, 1).wait_recv()
    pass_rows(1, False).start()
    project(2 * (1 - place.y) + place.c)
    for relation in (1, 4):
        gather.arrive_z(OUT_W, relation)
        gather.arrive_z(DOWN_W, relation)
    for half in range(halves):
        pass_rows(half, True).wait_recv()
    project(2 * (1 - place.y) + 1 - place.c)

    def chores(step):
        if step == 0:
            gather.arrive_x(UP_W, OWN)
            for relation in (2, 5):
                gather.arrive_z(UP_W, relation)
        elif step == 2:
            for relation in (2, 5):
                gather.arrive_z(OUT_W, relation)
                gather.arrive_z(DOWN_W, relation)
            gather.arrive_x(OUT_W, OWN)
            gather.arrive_x(DOWN_W, OWN)
        elif step == 4:
            for relation in (1, 4):
                gather.arrive_x(UP_W, relation)
                gather.arrive_y(relation, 0)
            gather.arrive_y(OWN, 1)
        elif step == 6:
            for relation in (3, 6):
                gather.arrive_z(UP_W, relation)
            for relation in (1, 4):
                gather.arrive_x(OUT_W, relation)
                gather.arrive_x(DOWN_W, relation)
        elif step == 8:
            for relation in (3, 6):
                gather.arrive_z(OUT_W, relation)
                gather.arrive_z(DOWN_W, relation)
            for relation in (2, 5):
                gather.arrive_x(UP_W, relation)
                gather.arrive_y(relation, 0)
        elif step == 10:
            for relation in (2, 5):
                gather.arrive_x(OUT_W, relation)
                gather.arrive_x(DOWN_W, relation)
            for relation in (1, 4):
                gather.arrive_y(relation, 1)

    def send_mixed(h, turn, arriving=False):
        member = place.member(turn)
        own = pl.ds(pl.multiple_of(h * HEAD, HEAD), HEAD)
        lanes = pl.ds(pl.multiple_of(member * local_rows, local_rows), local_rows)
        owner = member if arriving else place.s
        there = attended.at[pl.ds(pl.multiple_of(owner * head_cols + h * HEAD, HEAD), HEAD)]
        return remote(
            mixed_low.at[own, lanes], there, mix_send.at[h, turn], mix_recv.at[h, turn], (place.f, member)
        )

    def keep_mixed(h):
        own = pl.ds(pl.multiple_of(h * HEAD, HEAD), HEAD)
        lanes = pl.ds(pl.multiple_of(place.s * local_rows, local_rows), local_rows)
        there = attended.at[pl.ds(pl.multiple_of(place.s * head_cols + h * HEAD, HEAD), HEAD)]
        return pltpu.make_async_copy(mixed_low.at[own, lanes], there, mix_send.at[h, 3])

    turns = slot_rows // local_rows

    def pass_on(index):
        h, turn = index // turns, lax.rem(index, turns)

        @pl.when(turn < turns - 1)
        def _():
            send_mixed(h, turn).start()

        @pl.when(turn == turns - 1)
        def _():
            keep_mixed(h).start()

    def step(index, carry):
        for when in range(0, 12, 2):
            pl.when(index == when)(lambda when=when: chores(when))
        h, turn = index // turns, lax.rem(index, turns)
        start = pl.multiple_of(place.member(turn) * local_rows, local_rows)
        attend_block(h, pl.ds(start, local_rows), q_x, k_wide, v_x, mixed, mixed_low, row_stats)

        @pl.when(index > 0)
        def _():
            pass_on(index - 1)

        return carry

    lax.fori_loop(0, heads * turns, step, 0)
    pass_on(heads * turns - 1)
    for relation in (3, 6):
        gather.arrive_x(UP_W, relation)
        gather.arrive_x(OUT_W, relation)
        gather.arrive_x(DOWN_W, relation)
    for relation in (3, 6):
        gather.arrive_y(relation, 0)
    for relation in (2, 5, 3, 6):
        gather.arrive_y(relation, 1)
    for array in (UP_W, OUT_W, DOWN_W, QKV_W):
        gather.finish(array)
    for copy in own_copies()[:3]:
        copy.wait()
    for half in range(halves):
        for index in range(2):
            send_rows(half, index).wait_send()
        pass_rows(half, False).wait_send()
    for h in range(heads):
        for turn in range(turns - 1):
            send_mixed(h, turn).wait_send()
            send_mixed(h, turn, True).wait_recv()
        keep_mixed(h).wait()


def front(lengths, layer_in, qkv_piece, up_weight, down_weight, out_weight):
    local_rows, width = layer_in.shape
    slot_rows = local_rows * 4
    head_cols = width // 4
    heads = head_cols // HEAD
    vmem = pl.BlockSpec(memory_space=pltpu.VMEM)
    anywhere = pl.BlockSpec(memory_space=pl.ANY)
    dma = pltpu.SemaphoreType.DMA
    hidden = up_weight.shape[1]
    return pl.pallas_call(
        front_kernel,
        in_specs=[pl.BlockSpec(memory_space=pltpu.SMEM)] + [vmem] * 5,
        out_specs=[vmem] * 9 + [anywhere] * 4,
        out_shape=[
            jax.ShapeDtypeStruct((slot_rows, width), low),
            jax.ShapeDtypeStruct((width, 3 * head_cols), low),
            jax.ShapeDtypeStruct((8,) + qkv_piece.shape, low),
            jax.ShapeDtypeStruct((heads, WIDE, slot_rows), low),
            jax.ShapeDtypeStruct((head_cols, slot_rows), low),
            jax.ShapeDtypeStruct((heads, slot_rows, WIDE), low),
            jax.ShapeDtypeStruct((heads, slot_rows, WIDE), low),
            jax.ShapeDtypeStruct((head_cols, slot_rows), full),
            jax.ShapeDtypeStruct((heads, 8, slot_rows), full),
            jax.ShapeDtypeStruct((width, hidden), low),
            jax.ShapeDtypeStruct((hidden, width), low),
            jax.ShapeDtypeStruct((width, width), low),
            jax.ShapeDtypeStruct((width, local_rows), low),
        ],
        scratch_shapes=[
            pltpu.VMEM((heads, WIDE, slot_rows), low),
            pltpu.VMEM((head_cols, slot_rows), low),
            dma((2, 2)), dma((2, 2)), dma((2,)), dma((2,)), dma((heads, 4)), dma((heads, 4)), dma((5,)),
            dma((4, 2, 3)), dma((4, 2, 3)), dma((4, 7)), dma((4, 7)), dma((3, 7, 2)), dma((3, 7, 2)),
            dma((7, 2)), dma((7, 2)), dma((7, 2)), dma((7, 2)),
        ],
        compiler_params=pltpu.CompilerParams(
            vmem_limit_bytes=VMEM_BYTES, collective_id=0, has_side_effects=True
        ),
        name="front",
    )(lengths, layer_in, qkv_piece, up_weight, down_weight, out_weight)


DW_FIRST = 3
LINES = (3, 0, 2, 1)


def add_low(left, right):
    return (left.astype(full) + right.astype(full)).astype(low)


class Reduce:
    def __init__(self, place, given, sums, from_y, from_x, from_z, sems):
        self.place, self.given, self.sums = place, given, sums
        self.from_y, self.from_x, self.from_z = from_y, from_x, from_z
        self.y_send, self.y_recv, self.x_send, self.x_recv, self.z_send, self.z_recv = sems

    def dest(self, column, line):
        x = self.place.x
        return 2 * line + (x if column == 0 else 1 - x)

    def slot(self, array, column, line, far=0):
        if array >= DW_FIRST:
            return self.sums[array].at[self.dest(column, line)]
        if array == DOWN_W:
            return self.sums[array].at[column, line, far]
        return self.sums[array].at[column, line]

    def load(self, array, column, line, sem):
        target, source = self.sums[array].at[column, line], self.given[array].at[column, line]
        if array == DOWN_W:
            target, source = target.at[0], source.at[0]
        return pltpu.make_async_copy(source, target, sem)

    def over_y(self, column, line):
        return remote(
            self.given[DOWN_W].at[column, line, 1], self.from_y.at[column, line],
            self.y_send.at[column, line], self.y_recv.at[column, line], self.place.across_y,
        )

    def add_y(self, column, line):
        self.over_y(column, line).wait_recv()
        slot = self.slot(DOWN_W, column, line, 0)
        slot[...] = add_low(slot[...], self.from_y[column, line])

    def over_x(self, array, line):
        start = self.given[array].at[1, line] if array in (UP_W, OUT_W) else self.slot(array, 1, line)
        return remote(
            start, self.from_x[array].at[line],
            self.x_send.at[array, line], self.x_recv.at[array, line], self.place.across_x,
        )

    def add_x(self, array, line):
        self.over_x(array, line).wait_recv()
        slot = self.slot(array, 0, line)
        slot[...] = add_low(slot[...], self.from_x[array][line])

    def along_z(self, array, way, line):
        return remote(
            self.slot(array, 0, line), self.from_z[array].at[way, line],
            self.z_send.at[array, way, line], self.z_recv.at[array, way, line],
            self.place.above if way == 0 else self.place.below,
        )

    def add_z(self, array, way, line):
        self.along_z(array, way, line).wait_recv()
        slot = self.slot(array, 0, line)
        slot[...] = add_low(slot[...], self.from_z[array][way, line])

    def hop(self, array, level, lines=(0, 1, 2, 3)):
        @pl.when(self.place.z == level)
        def _():
            for line in range(3, level, -1):
                if line in lines:
                    if level > 0:
                        self.add_z(array, 0, line)
                    self.along_z(array, 0, line).start()

        @pl.when(self.place.z == 3 - level)
        def _():
            for line in range(0, 3 - level):
                if line in lines:
                    if level > 0:
                        self.add_z(array, 1, line)
                    self.along_z(array, 1, line).start()

    def settle(self, array):
        for line in range(4):

            @pl.when(self.place.z == line)
            def _(line=line):
                if line > 0:
                    self.add_z(array, 0, line)
                if line < 3:
                    self.add_z(array, 1, line)

    def finish(self, array):
        for line in range(4):
            self.over_x(array, line).wait_send()
            pl.when(self.place.z < line)(lambda line=line: self.along_z(array, 0, line).wait_send())
            pl.when(self.place.z > line)(lambda line=line: self.along_z(array, 1, line).wait_send())
            if array == DOWN_W:
                for column in range(2):
                    self.over_y(column, line).wait_send()


class Spread:
    def __init__(self, place, blocks, source, send, recv):
        self.place, self.blocks, self.source, self.send, self.recv = place, blocks, source, send, recv
        self.near = 2 * place.y + 1 - place.c
        self.far = 2 * (1 - place.y) + place.c
        self.last = 2 * (1 - place.y) + 1 - place.c

    def copy(self, kind, arriving=False):
        place = self.place
        if kind == 2:
            here = self.blocks.at[self.last if arriving else self.far]
            return remote(here, here, self.send.at[2], self.recv.at[2], place.core)
        member = (self.near, self.far)[kind] if arriving else place.s
        return remote(
            self.source, self.blocks.at[member], self.send.at[kind], self.recv.at[kind],
            (place.core, place.across_y)[kind],
        )

    def start(self):
        self.copy(1).start()
        self.copy(0).start()

    def pass_on(self):
        self.copy(1, True).wait_recv()
        self.copy(2).start()

    def finish(self):
        self.blocks[self.place.s] = self.source[...]
        self.copy(0, True).wait_recv()
        self.copy(2, True).wait_recv()
        for kind in range(3):
            self.copy(kind).wait_send()


def back_kernel(
    length_ref, grad_own, vectors_in, q_in, k_in, k_wide_in, v_wide_in, mixed_in, stats_in, rows_in, weight_in, resid_in, up_given, down_given, out_given,
    input_out, read_out, write_out, qkv_out, vector_out, up_out, down_out, out_out,
    q_x, k_t, k_wide, v_wide, mixed, row_stats, grad_t, q_here, do_x, grads, grad_k, grad_v, rows_ref, weight_ref, resid_ref,
    up_sum, out_sum, down_sum, dw, down_y, up_x, out_x, down_x, dw_x, up_z, out_z, down_z, dw_z,
    up_last, out_last, up_other, out_other, down_all, dw_all,
    near_send, near_recv, far_sum, far_recv, memory_all, memory_own,
    mix_send, mix_recv, local_sem, saved_sem, mine_sem, share_send, share_recv, near_s, near_r, far_s, far_r,
    *sems,
):
    place = Place()
    heads, _, slot_rows = q_in.shape
    width, local_rows = grad_own.shape
    head_cols = heads * HEAD
    last = DW_FIRST + heads - 1
    given = {UP_W: up_given, OUT_W: out_given, DOWN_W: down_given}
    sums = {UP_W: up_sum, OUT_W: out_sum, DOWN_W: down_sum}
    from_x = {UP_W: up_x, OUT_W: out_x, DOWN_W: down_x}
    from_z = {UP_W: up_z, OUT_W: out_z, DOWN_W: down_z}
    for h in range(heads):
        sums[DW_FIRST + h], from_x[DW_FIRST + h] = dw.at[h], dw_x.at[h]
        from_z[DW_FIRST + h] = dw_z.at[h]
    reduce = Reduce(place, given, sums, down_y, from_x, from_z, sems)
    greet(place, None)

    peers = (place.across_y, place.diagonal, place.core)

    def member_rows(turn):
        member = place.member(turn)
        return member, pl.ds(pl.multiple_of(member * local_rows, local_rows), local_rows)

    def send_grad(turn, arriving=False):
        member, lanes = member_rows(turn)
        own_lanes = pl.ds(pl.multiple_of(place.s * local_rows, local_rows), local_rows)
        src = grad_own.at[pl.ds(pl.multiple_of(member * head_cols, head_cols), head_cols)]
        return remote(
            src, grad_t.at[:, lanes if arriving else own_lanes], mix_send.at[turn], mix_recv.at[turn], peers[turn]
        )

    def saved_loads(h):
        own = pl.ds(h * HEAD, HEAD)
        pairs = (
            (k_wide_in.at[h], k_wide.at[h]), (q_in.at[h, pl.ds(0, HEAD)], q_x.at[h]), (v_wide_in.at[h], v_wide.at[h]),
            (mixed_in.at[own], mixed.at[own]), (stats_in.at[h], row_stats.at[h]), (k_in.at[own], k_t.at[own]),
        )
        return [pltpu.make_async_copy(src, dst, saved_sem.at[h, i]) for i, (src, dst) in enumerate(pairs)]

    for turn in range(3):
        send_grad(turn).start()
    for load in saved_loads(0):
        load.start()
    loads = []
    for index, (src, dst) in enumerate(((rows_in, rows_ref), (weight_in, weight_ref), (resid_in, resid_ref))):
        loads.append(pltpu.make_async_copy(src, dst, local_sem.at[index]))

    def sum_loads(array):
        columns = (0, 1) if array == DOWN_W else (0,)
        return [
            reduce.load(array, column, line, mine_sem.at[array, column, line]) for column in columns for line in LINES
        ]

    def send_x(array, lines=LINES):
        for line in lines:
            reduce.over_x(array, line).start()

    send_x(UP_W)
    for column in (1, 0):
        for line in LINES:
            reduce.over_y(column, line).start()
    send_x(OUT_W)
    for array in (UP_W, DOWN_W, OUT_W):
        for load in sum_loads(array):
            load.start()
    for load in loads:
        load.start()

    for h in range(1, heads):
        for load in saved_loads(h):
            load.start()

    own_lanes = pl.ds(pl.multiple_of(place.s * local_rows, local_rows), local_rows)
    grad_t[:, own_lanes] = grad_own[pl.ds(pl.multiple_of(place.s * head_cols, head_cols), head_cols), :]

    def take_x(array, lines=LINES):
        for line in lines:
            reduce.add_x(array, line)

    turns = slot_rows // local_rows

    def weight_part(h):
        if h == 0:
            loads[0].wait()
        base = 3 * h * HEAD
        part = jnp.transpose(mul(grads[base : base + 3 * HEAD, :], rows_ref[...])).astype(low)
        shard = width // 8
        for dest in range(8):
            dw[h, dest, :shard, :] = part[dest * shard : (dest + 1) * shard]
            if h == heads - 1:
                dw[h, dest, shard:, :] = vectors_in[dest].astype(low)
            else:
                dw[h, dest, shard:, :] = jnp.zeros((16, 3 * HEAD), low)
        if h == heads - 1:
            total = jnp.sum(grads[...].astype(full), axis=1, keepdims=True)
            spread = jnp.transpose(jnp.broadcast_to(total, (total.shape[0], WIDE)))[0:1]
            for kind, first_dest in ((0, 0), (2, 4)):
                for head in range(heads):
                    start = (3 * head + kind) * HEAD
                    dw[h, first_dest + place.s, shard : shard + 1, head * HEAD : (head + 1) * HEAD] = spread[
                        :, start : start + HEAD
                    ].astype(low)
        send_x(DW_FIRST + h)

    share = {UP_W: (up_last, up_other), OUT_W: (out_last, out_other)}

    def sum_y(array):
        mine_now = sums[array].at[0, place.z]
        return remote(mine_now, share[array][0], share_send.at[array, 0], share_recv.at[array, 0], place.across_y)

    def half_to_core(array):
        mine_now = sums[array].at[0, place.z]
        return remote(mine_now, share[array][1], share_send.at[array, 1], share_recv.at[array, 1], place.core)

    def spread_of(array):
        if array == DOWN_W:
            return Spread(place, down_all, down_sum.at[0, place.z, 0], share_send.at[2], share_recv.at[2])
        h = array - DW_FIRST
        return Spread(place, dw_all.at[h], dw.at[h, place.f], share_send.at[array], share_recv.at[array])

    def add_last(array):
        sum_y(array).wait()
        slot = sums[array].at[0, place.z]
        slot[...] = add_low(slot[...], share[array][0][...])
        half_to_core(array).start()

    first, second = DW_FIRST, DW_FIRST + 1

    def add_y(column):
        for line in LINES:
            reduce.add_y(column, line)

    def chores(index):
        if index == 1:
            send_grad(2, True).wait_recv()
        elif index == 2:
            send_grad(1, True).wait_recv()
            for array in (UP_W, DOWN_W, OUT_W):
                for load in sum_loads(array):
                    load.wait()
        elif index == 3:
            send_grad(0, True).wait_recv()
            take_x(UP_W, (3,))
            reduce.hop(UP_W, 0, (3,))
        elif index == 4:
            for load in saved_loads(1):
                load.wait()
            weight_part(0)
            take_x(UP_W, (0,))
            reduce.hop(UP_W, 0, (0,))
        elif index == 5:
            add_y(1)
            send_x(DOWN_W)
            take_x(UP_W, (2,))
            reduce.hop(UP_W, 0, (2,))
        elif index == 6:
            reduce.hop(UP_W, 1, (3, 0))
            take_x(UP_W, (1,))
            reduce.hop(UP_W, 0, (1,))
        elif index == 7:
            take_x(OUT_W)
            reduce.hop(OUT_W, 0)
            reduce.hop(UP_W, 1, (2, 1))
        elif index == 8:
            for load in saved_loads(2):
                load.wait()
            weight_part(1)
            reduce.hop(UP_W, 2)
            add_y(0)
        elif index == 9:
            take_x(DOWN_W, (3, 0))
            reduce.hop(DOWN_W, 0, (3, 0))
            reduce.hop(OUT_W, 1)
        elif index == 10:
            reduce.settle(UP_W)
            sum_y(UP_W).start()
            take_x(DOWN_W, (2, 1))
            reduce.hop(DOWN_W, 0, (2, 1))
        elif index == 11:
            reduce.hop(OUT_W, 2)
            reduce.hop(DOWN_W, 1)
            take_x(first)
            reduce.hop(first, 0)

    def step(index, carry):
        for when in range(1, 12):
            pl.when(index == when)(lambda when=when: chores(when))
        h, turn = index // turns, lax.rem(index, turns)
        _, lanes = member_rows(turns - 1 - turn)
        attend_back(
            h, lanes, q_x, q_here, do_x, grad_t, mixed, row_stats, k_t, k_wide, v_wide, grads, grad_k, grad_v, turn == 0
        )

        @pl.when(turn == turns - 1)
        def _():
            base = pl.multiple_of(3 * h * HEAD, HEAD)
            grads[pl.ds(base + HEAD, HEAD), :] = grad_k[...].astype(low)
            grads[pl.ds(base + 2 * HEAD, HEAD), :] = grad_v[...].astype(low)

        return carry

    for load in saved_loads(0):
        load.wait()
    lax.fori_loop(0, heads * turns, step, 0)

    weight_part(heads - 1)
    loads[1].wait()
    loads[2].wait()

    halves, part = 2, local_rows // 2
    length = length_ref[0]

    def memory_pick(rows, start):
        line = lax.broadcasted_iota(jnp.int32, (32, rows), 0)
        row = start + lax.broadcasted_iota(jnp.int32, (32, rows), 1)
        wanted = jnp.where(line < 16, line, length - MEM + line - 16)
        used = (line < MEM) | ((line >= 16) & (line < 16 + MEM))
        return jnp.where(used & (wanted == row), 1.0, 0.0).astype(low)

    def part_for(turn, half):
        start = pl.multiple_of(place.member(turn) * local_rows + half * part, part)
        return mul(grads[:, pl.ds(start, part)], weight_ref[...], TT)

    def share_near(index, half):
        rows = pl.ds(half * part, part)
        return remote(
            near_send.at[index, rows], near_recv.at[index, rows], near_s.at[index, half], near_r.at[index, half],
            place.core,
        )

    def share_far(half):
        rows = pl.ds(half * part, part)
        return remote(far_sum.at[rows], far_recv.at[rows], far_s.at[half], far_r.at[half], place.across_y)

    for half in range(halves):
        rows = slice(half * part, (half + 1) * part)
        near_send[0, rows, :] = part_for(1, half).astype(low)
        share_near(0, half).start()
        far_sum[rows, :] = part_for(0, half).astype(low)
        if half == 0:
            taken = mul(memory_pick(slot_rows, 0), grads[...], NT).astype(low)
            own_part = mul(memory_pick(local_rows, place.s * local_rows), resid_ref[...].astype(low))
            memory_own[...] = (mul(taken, weight_ref[...], NT) + own_part).astype(low)
        share_near(0, half).wait_recv()
        far_sum[rows, :] = add_low(far_sum[rows, :], near_recv[0, rows, :])
        share_far(half).start()
    memory = Spread(place, memory_all, memory_own, share_send.at[DW_FIRST + heads], share_recv.at[DW_FIRST + heads])
    memory.start()
    take_x(second)
    reduce.hop(second, 0)
    take_x(last)
    reduce.hop(last, 0)
    reduce.hop(first, 1)
    for half in range(halves):
        rows = slice(half * part, (half + 1) * part)
        near_send[1, rows, :] = part_for(2, half).astype(low)
        share_near(1, half).start()
    reduce.hop(last, 1)
    reduce.hop(second, 1)
    reduce.hop(DOWN_W, 2)
    reduce.hop(first, 2)
    for half in range(halves):
        resid_ref[half * part : (half + 1) * part, :] += part_for(3, half)
    reduce.hop(last, 2)
    reduce.hop(second, 2)
    reduce.settle(OUT_W)
    sum_y(OUT_W).start()
    for h in (heads - 1, 0, 1):
        reduce.settle(DW_FIRST + h)
        spread_of(DW_FIRST + h).start()
    reduce.settle(DOWN_W)
    spread_of(DOWN_W).start()
    add_last(UP_W)
    add_last(OUT_W)
    memory.pass_on()
    for h in (heads - 1, 0, 1):
        spread_of(DW_FIRST + h).pass_on()
    spread_of(DOWN_W).pass_on()
    for array, out in ((UP_W, up_out), (OUT_W, out_out)):
        columns = out.shape[1] // 2
        out[:, pl.ds(pl.multiple_of(place.c * columns, columns), columns)] = sums[array][0, place.z]
        half_to_core(array).wait()
        out[:, pl.ds(pl.multiple_of((1 - place.c) * columns, columns), columns)] = share[array][1][...]
    for h in range(heads):
        spread_of(DW_FIRST + h).finish()
    spread_of(DOWN_W).finish()
    quarter = down_out.shape[0] // 4
    for member in range(4):
        down_out[member * quarter : (member + 1) * quarter, :] = down_all[member]
    shard = qkv_out.shape[0]
    for kind in range(3):
        for member in range(4):
            for h in range(heads):
                start = kind * width + (member * heads + h) * HEAD
                qkv_out[:, start : start + HEAD] = dw_all[h, member, :shard, kind * HEAD : (kind + 1) * HEAD]
    vector_sum = dw_all[heads - 1, 0, shard:, :].astype(full)
    for member in range(1, 4):
        vector_sum = vector_sum + dw_all[heads - 1, member, shard:, :].astype(full)
    vector_out[...] = vector_sum
    memory.finish()
    total = memory_all[0].astype(full)
    for member in range(1, 4):
        total = total + memory_all[member].astype(full)
    read_out[...] = total[:MEM]
    write_out[...] = total[16 : 16 + MEM]
    for half in range(halves):
        rows = slice(half * part, (half + 1) * part)
        share_near(1, half).wait_recv()
        share_far(half).wait_recv()
        grad_layer = resid_ref[rows, :] + near_recv[1, rows, :].astype(full) + far_recv[rows, :].astype(full)
        rows_at = place.s * local_rows + half * part + lax.broadcasted_iota(jnp.int32, (part, 1), 0)
        in_write = (rows_at >= length - MEM) & (rows_at < length)
        input_out[rows, :] = jnp.where((rows_at < MEM) | in_write, 0.0, grad_layer)
    for array in range(DW_FIRST + heads):
        reduce.finish(array)
    for turn in range(3):
        send_grad(turn).wait_send()
    for half in range(halves):
        for index in range(2):
            share_near(index, half).wait_send()
        share_far(half).wait_send()


def back(lengths, grad_own, saved, vectors, rows, weight, resid, up_given, down_given, out_given):
    q_x, k_t, k_wide, v_wide, mixed, row_stats = saved
    heads, _, slot_rows = q_x.shape
    width, local_rows = grad_own.shape
    hidden = 2 * up_given.shape[3]
    shard, head_cols = width // 8, heads * HEAD
    half, small, piece = hidden // 2, width // 2, hidden // 32
    vmem = pl.BlockSpec(memory_space=pltpu.VMEM)
    anywhere = pl.BlockSpec(memory_space=pl.ANY)
    dma = pltpu.SemaphoreType.DMA
    arrays = DW_FIRST + heads

    def held(*shape, kind=low):
        return pltpu.VMEM(shape, kind)

    tall = (shard + 16, 3 * HEAD)
    return pl.pallas_call(
        back_kernel,
        in_specs=[pl.BlockSpec(memory_space=pltpu.SMEM)] + [vmem] * 2 + [anywhere] * 12,
        out_specs=[vmem] * 8,
        out_shape=[
            jax.ShapeDtypeStruct((local_rows, width), full),
            jax.ShapeDtypeStruct((MEM, width), full),
            jax.ShapeDtypeStruct((MEM, width), full),
            jax.ShapeDtypeStruct((shard, 3 * width), low),
            jax.ShapeDtypeStruct((16, 3 * HEAD), full),
            jax.ShapeDtypeStruct((shard, hidden), low),
            jax.ShapeDtypeStruct((hidden // 8, width), low),
            jax.ShapeDtypeStruct((shard, width), low),
        ],
        scratch_shapes=[
            held(heads, HEAD, slot_rows), held(head_cols, slot_rows), held(heads, slot_rows, WIDE),
            held(heads, slot_rows, WIDE), held(head_cols, slot_rows, kind=full), held(heads, 8, slot_rows, kind=full),
            held(head_cols, slot_rows), held(WIDE, local_rows), held(WIDE, local_rows), held(3 * head_cols, slot_rows),
            held(HEAD, slot_rows, kind=full), held(HEAD, slot_rows, kind=full),
            held(slot_rows, width), held(width, 3 * head_cols), held(local_rows, width, kind=full),
            held(2, 4, shard, half), held(2, 4, shard, small), held(2, 4, 2, piece, width),
            held(heads, 8, *tall), held(2, 4, piece, width),
            held(4, shard, half), held(4, shard, small), held(4, piece, width), held(heads, 4, *tall),
            held(2, 4, shard, half), held(2, 4, shard, small), held(2, 4, piece, width), held(heads, 2, 4, *tall),
            held(shard, half), held(shard, small), held(shard, half), held(shard, small),
            held(4, piece, width), held(heads, 4, *tall),
            held(2, local_rows, width), held(2, local_rows, width), held(local_rows, width),
            held(local_rows, width), held(4, 32, width), held(32, width),
            dma((3,)), dma((3,)), dma((3,)), dma((heads, 6)), dma((3, 2, 4)), dma((arrays + 1, 3)),
            dma((arrays + 1, 3)), dma((2, 2)), dma((2, 2)), dma((2,)), dma((2,)),
            dma((2, 4)), dma((2, 4)), dma((arrays, 4)), dma((arrays, 4)),
            dma((arrays, 2, 4)), dma((arrays, 2, 4)),
        ],
        compiler_params=pltpu.CompilerParams(
            vmem_limit_bytes=VMEM_BYTES, collective_id=1, has_side_effects=True
        ),
        name="back",
    )(
        lengths, grad_own, vectors, q_x, k_t, k_wide, v_wide, mixed, row_stats, rows, weight, resid,
        up_given, down_given, out_given,
    )


VECTOR_ROWS = ((1, 0), (1, 1), (2, 0), (4, 1), (5, 0), (5, 1))


def phi_parts(value):
    normal = 0.5 * (1.0 + lax.erf(value * (0.5**0.5)))
    density = jnp.exp(-0.5 * value * value) * (0.5 * 2.0**0.5 * 3.141592653589793**-0.5)
    return normal, normal + value * density


def statistics(values):
    centre = values - jnp.mean(values, axis=1, keepdims=True)
    factor = lax.rsqrt(jnp.mean(centre * centre, axis=1, keepdims=True) + norm_epsilon)
    return centre * factor, factor


def norm_back(grad, gain, normed, factor):
    scaled = grad * gain
    first = jnp.mean(scaled, axis=1, keepdims=True)
    second = jnp.mean(scaled * normed, axis=1, keepdims=True)
    return factor * (scaled - first - normed * second)


def column_total(values):
    return jnp.sum(values, axis=0, keepdims=True)


def middle_kernel(
    length_ref, layer_in, cotangent, pieces, attended_in, up_in, down_in, out_in,
    output, resid_out, grad_own, vector_out, up_out, down_out, out_out,
    attended, up_w, down_w, out_w, vectors, small, up_bias, hidden, slope, normed_one, middle_low, grad_down,
    grad_two, grad_mid, totals, up_total, up_grad, down_grad, out_grad, up_sum, down_sum, out_sum,
    load_sem, save_sem, c_send, c_recv,
):
    place = Place()
    rows, width = layer_in.shape
    ff = up_w.shape[1]
    chunk = ff // 4
    shard = width // 8
    barrier = pltpu.get_barrier_semaphore()
    pl.semaphore_signal(barrier, inc=1, device_id=place.core, device_id_type=MESH)

    def chunk_lanes(j):
        return pl.ds(pl.multiple_of(j * chunk, chunk), chunk)

    def up_load(j):
        return pltpu.make_async_copy(up_in.at[:, chunk_lanes(j)], up_w.at[:, chunk_lanes(j)], load_sem.at[j])

    def down_load(j):
        return pltpu.make_async_copy(down_in.at[chunk_lanes(j)], down_w.at[chunk_lanes(j)], load_sem.at[4 + j])

    first_loads = [
        pltpu.make_async_copy(pieces.at[:, pl.ds(shard, 16)], vectors, load_sem.at[8]),
        pltpu.make_async_copy(attended_in, attended, load_sem.at[9]),
        pltpu.make_async_copy(out_in, out_w, load_sem.at[10]),
    ]
    for load in first_loads:
        load.start()
    for j in range(4):
        up_load(j).start()
        down_load(j).start()
    first_loads[0].wait()
    spots = ((0, 192), (0, 288), (0, 384), (1, 288), (1, 384), (1, 480))
    for source in range(8):
        for index, (line, start) in enumerate(spots):
            small[index : index + 1, source * shard : (source + 1) * shard] = vectors[
                source, line : line + 1, start : start + shard
            ].astype(full)
        base = source * 4 * shard
        up_bias[0:1, base : base + shard] = vectors[source, 0:1, 480:576].astype(full)
        up_bias[0:1, base + shard : base + 4 * shard] = vectors[source, 1:2, 0:288].astype(full)
    out_bias, gain_one, shift_one = small[0:1, :], small[1:2, :], small[2:3, :]
    down_bias, gain_two, shift_two = small[3:4, :], small[4:5, :], small[5:6, :]
    first_loads[1].wait()
    first_loads[2].wait()

    branch = mul(attended[...], out_w[...], TN)
    normed, factor_one = statistics(layer_in[...].astype(full) + branch + out_bias)
    normed_one[...] = normed
    middle_low[...] = (normed * gain_one + shift_one).astype(low)
    grad_mid[...] = jnp.zeros_like(grad_mid)

    def forward_chunk(j, carry):
        up_load(j).wait()
        lanes = chunk_lanes(j)
        value = mul(middle_low[...], up_w[:, lanes]) + up_bias[0:1, lanes]
        normal, slope_here = phi_parts(value)
        hidden[:, lanes] = (value * normal).astype(low)
        slope[:, lanes] = slope_here
        down_load(j).wait()
        grad_mid[...] += mul(hidden[:, lanes], down_w[lanes, :])
        return carry

    lax.fori_loop(0, 4, forward_chunk, 0)
    middle = normed_one[...] * gain_one + shift_one
    normed_two, factor_two = statistics(middle + grad_mid[...] + down_bias)
    places = place.s * rows + lax.broadcasted_iota(jnp.int32, (rows, 1), 0)
    in_slot = places < length_ref[0]
    output[...] = jnp.where(in_slot, normed_two * gain_two + shift_two, 0.0).astype(low)
    grad_final = jnp.where(in_slot, cotangent[...].astype(full), 0.0)
    totals[4:5, :] = column_total(grad_final * normed_two)
    totals[5:6, :] = column_total(grad_final)
    grad_resid = norm_back(grad_final, gain_two, normed_two, factor_two)
    grad_two[...] = grad_resid
    grad_down[...] = grad_resid.astype(low)
    totals[3:4, :] = column_total(grad_down[...].astype(full))
    pl.semaphore_wait(barrier, 1)

    def down_piece(ref, line, column, far, core):
        dest = 2 * line + (place.x if column == 0 else 1 - place.x)
        y = place.y if far == 0 else 1 - place.y
        return ref.at[pl.ds(pl.multiple_of(dest * 4 * shard + (2 * y + core) * shard, shard), shard)]

    def side_piece(ref, line, column, core):
        dest = 2 * line + (place.x if column == 0 else 1 - place.x)
        half = ref.shape[1] // 2
        return ref.at[
            pl.ds(pl.multiple_of(dest * shard, shard), shard), pl.ds(pl.multiple_of(core * half, half), half)
        ]

    def down_share(line, column, far):
        return remote(
            down_piece(down_grad, line, column, far, 1 - place.c), down_sum.at[column, line, far],
            c_send.at[2 + far, column, line], c_recv.at[2 + far, column, line], place.core,
        )

    def side_share(array, line, column):
        grad, total = ((up_grad, up_sum), (out_grad, out_sum))[array]
        return remote(
            side_piece(grad, line, column, 1 - place.c), total.at[column, line],
            c_send.at[array, column, line], c_recv.at[array, column, line], place.core,
        )

    def down_save(column, line):
        return pltpu.make_async_copy(down_sum.at[column, line], down_out.at[column, line], save_sem.at[2, column, line])

    def side_save(array, column, line):
        total, out = ((up_sum, up_out), (out_sum, out_out))[array]
        return pltpu.make_async_copy(total.at[column, line], out.at[column, line], save_sem.at[array, column, line])

    def down_chunk(line, carry):
        lanes = chunk_lanes(line)
        down_grad[lanes, :] = mul(hidden[:, lanes], grad_down[...], TN).astype(low)
        for column in range(2):
            for far in range(2):
                down_share(line, column, far).start()
        return carry

    lax.fori_loop(0, 4, down_chunk, 0)
    grad_mid[...] = grad_two[...]

    def back_chunk(turn, carry):
        j = lax.rem(2 * (1 - place.c) + turn, 4)
        lanes = chunk_lanes(j)
        grad_up = (mul(grad_down[...], down_w[lanes, :], NT) * slope[:, lanes]).astype(low)
        up_total[0:1, lanes] = column_total(grad_up.astype(full))
        up_grad[:, lanes] = mul(middle_low[...], grad_up, TN).astype(low)
        grad_mid[...] += mul(grad_up, up_w[:, lanes], NT)

        @pl.when(turn == 1)
        def _():
            for column in (1, 0):
                for line in LINES:
                    side_share(0, line, column).start()

        return carry

    lax.fori_loop(0, 4, back_chunk, 0)
    grad_middle = grad_mid[...]
    normed = normed_one[...]
    totals[1:2, :] = column_total(grad_middle * normed)
    totals[2:3, :] = column_total(grad_middle)
    grad_one = norm_back(grad_middle, gain_one, normed, factor_one)
    resid_out[...] = grad_one
    grad_branch = grad_one.astype(low)
    totals[0:1, :] = column_total(grad_branch.astype(full))
    out_grad[...] = mul(attended[...], grad_branch).astype(low)
    for column in (1, 0):
        for line in LINES:
            side_share(1, line, column).start()
    grad_own[...] = mul(out_w[...], grad_branch, NT).astype(low)

    def add_down(column, line):
        for far in range(2):
            down_share(line, column, far).wait_recv()
            down_sum[column, line, far] = add_low(
                down_sum[column, line, far], down_piece(down_grad, line, column, far, place.c)[...]
            )
        down_save(column, line).start()

    def add_side(array, column, line):
        grad, total = ((up_grad, up_sum), (out_grad, out_sum))[array]
        side_share(array, line, column).wait_recv()
        total[column, line] = add_low(total[column, line], side_piece(grad, line, column, place.c)[...])
        side_save(array, column, line).start()

    for column in range(2):
        for line in range(4):
            add_side(0, column, line)
            add_down(column, line)
    vector_out[...] = jnp.zeros_like(vector_out)
    half = 3 * HEAD // 2
    for dest in range(8):
        for index, (line, side) in enumerate(VECTOR_ROWS):
            vector_out[dest, line : line + 1, side * half : (side + 1) * half] = totals[
                index : index + 1, dest * shard : (dest + 1) * shard
            ]
        base = dest * 4 * shard
        vector_out[dest, 2:3, half:] = up_total[0:1, base : base + shard]
        vector_out[dest, 3:4, :] = up_total[0:1, base + shard : base + 3 * shard]
        vector_out[dest, 4:5, :half] = up_total[0:1, base + 3 * shard : base + 4 * shard]
    for column in range(2):
        for line in range(4):
            add_side(1, column, line)
    for column in range(2):
        for line in range(4):
            for array in range(2):
                side_share(array, line, column).wait_send()
                side_save(array, column, line).wait()
            for far in range(2):
                down_share(line, column, far).wait_send()
            down_save(column, line).wait()


def middle_part(lengths, layer_in, cotangent, pieces, attended, up_full, down_full, out_full):
    rows, width = layer_in.shape
    ff = up_full.shape[1]
    shard = width // 8
    vmem = pl.BlockSpec(memory_space=pltpu.VMEM)
    anywhere = pl.BlockSpec(memory_space=pl.ANY)
    dma = pltpu.SemaphoreType.DMA

    def held(*shape, kind=low):
        return pltpu.VMEM(shape, kind)

    def shaped(*shape, kind=low):
        return jax.ShapeDtypeStruct(shape, kind)

    up_parts, down_parts, out_parts = (2, 4, shard, ff // 2), (2, 4, 2, ff // 32, width), (2, 4, shard, width // 2)
    return pl.pallas_call(
        middle_kernel,
        in_specs=[pl.BlockSpec(memory_space=pltpu.SMEM)] + [vmem] * 2 + [anywhere] * 5,
        out_specs=[vmem] * 4 + [anywhere] * 3,
        out_shape=[
            shaped(rows, width), shaped(rows, width, kind=full), shaped(width, rows),
            shaped(8, 16, 3 * HEAD, kind=full), shaped(*up_parts), shaped(*down_parts), shaped(*out_parts),
        ],
        scratch_shapes=[
            held(width, rows), held(width, ff), held(ff, width), held(width, width), held(8, 16, 9 * HEAD),
            held(8, width, kind=full), held(8, ff, kind=full), held(rows, ff), held(rows, ff, kind=full),
            held(rows, width, kind=full), held(rows, width), held(rows, width), held(rows, width, kind=full),
            held(rows, width, kind=full), held(8, width, kind=full), held(8, ff, kind=full),
            held(width, ff), held(ff, width), held(width, width), held(*up_parts), held(*down_parts),
            held(*out_parts), dma((11,)), dma((3, 2, 4)), dma((4, 2, 4)), dma((4, 2, 4)),
        ],
        compiler_params=pltpu.CompilerParams(
            vmem_limit_bytes=VMEM_BYTES, collective_id=2, has_side_effects=True
        ),
        name="middle",
    )(lengths, layer_in, cotangent, pieces, attended, up_full, down_full, out_full)


def normalize(values, gain_vec, shift_vec):
    centre = values - jnp.mean(values, axis=-1, keepdims=True)
    factor = lax.rsqrt(jnp.mean(centre * centre, axis=-1, keepdims=True) + norm_epsilon)
    return centre * factor * gain_vec + shift_vec


def column_sums(values):
    return jnp.sum(values, axis=0, dtype=full)


def per_device(
    tokens, read_memory, write_memory, lengths, qkv_weight, qv_bias, out_weight, out_bias, norm1_gain,
    norm1_bias, up_weight, up_bias, down_weight, down_bias, norm2_gain, norm2_bias, cotangent,
):
    seq_count = lax.axis_size("seq")
    fsdp_count = lax.axis_size("fsdp")
    seq_place = lax.axis_index("seq")
    local_rows, width = tokens.shape
    head_cols = width // seq_count
    shard = width // fsdp_count
    length = lengths[0]
    places = seq_place * local_rows + jnp.arange(local_rows, dtype=jnp.int32)
    in_slot = (places < length)[:, None]
    memory_slots = jnp.arange(MEM, dtype=jnp.int32)
    pick_read = places[:, None] == memory_slots[None, :]
    pick_write = places[:, None] == length - MEM + memory_slots[None, :]
    is_memory = jnp.any(pick_read | pick_write, axis=1)[:, None]
    picks = jnp.concatenate([pick_read, pick_write], axis=1).astype(full)
    memory = jnp.concatenate([read_memory[0], write_memory[0]], axis=0)
    layer_in = jnp.where(is_memory, mul(picks.astype(low), memory).astype(low), tokens)

    heads = head_cols // HEAD
    own_shard = lax.dynamic_slice_in_dim(
        qkv_weight.reshape(shard, 3, seq_count, heads, HEAD), seq_place, 1, 2
    )
    own_shard = jnp.transpose(own_shard[:, :, 0], (0, 2, 1, 3)).reshape(shard, 3 * head_cols)
    vectors = (qv_bias, out_bias, norm1_gain, norm1_bias, up_bias, down_bias, norm2_gain, norm2_bias)
    packed = jnp.concatenate(vectors)
    on_block = (fsdp_count, seq_count) == (8, 4)
    if on_block:
        spare = jnp.zeros((14, 3 * head_cols), low)
        piece = jnp.concatenate([own_shard, packed.reshape(2, -1), spare], axis=0)
        (rows, weight, pieces, q_x, k_t, k_wide, v_wide, mixed, row_stats, up_full, down_full, out_full,
         attended) = front(lengths, layer_in, piece, up_weight, down_weight, out_weight)
    else:
        rows = lax.all_gather(layer_in, "seq", axis=0, tiled=True)
        weight = lax.all_gather(own_shard, "fsdp", axis=0, tiled=True)
        packed = lax.all_gather(packed.reshape(1, -1), "fsdp", axis=0, tiled=True).astype(full)
    if not on_block:
        whole, start = [], 0
        for vector in vectors:
            whole.append(packed[:, start : start + vector.shape[0]].reshape(-1))
            start += vector.shape[0]
        qv_vec, out_vec, gain_one, shift_one, up_vec, down_vec, gain_two, shift_two = whole
        own_qv = lax.dynamic_slice_in_dim(qv_vec.reshape(2, seq_count, head_cols), seq_place, 1, 1)
        bias = jnp.concatenate([own_qv[0, 0], own_qv[1, 0]])
        bias = jnp.broadcast_to(bias, (8, bias.shape[0]))
        out_full = lax.all_gather(out_weight, "fsdp", axis=0, tiled=True)
        up_full = lax.all_gather(up_weight, "fsdp", axis=0, tiled=True)
        down_full = lax.all_gather(down_weight, "fsdp", axis=0, tiled=True)
        q_x, k_t, k_wide, v_wide, mixed, mixed_low, row_stats = attention_forward(lengths, rows, weight, bias)
        attended = lax.all_to_all(mixed_low, "seq", split_axis=1, concat_axis=0, tiled=True)
    if on_block:
        (output, grad_resid_one, grad_attended, packed_grad, grad_up_weight, grad_down_weight, grad_out_weight) = (
            middle_part(lengths, layer_in, cotangent, pieces, attended, up_full, down_full, out_full)
        )
    else:
        resid_one = layer_in.astype(full) + mul(attended, out_full, TN) + out_vec
        middle, norm_one_back = jax.vjp(normalize, resid_one, gain_one, shift_one)
        middle_low = middle.astype(low)
        up_pre = mul(middle_low, up_full) + up_vec
        gelu_out, gelu_back = jax.vjp(partial(jax.nn.gelu, approximate=False), up_pre)
        hidden = gelu_out.astype(low)
        down_pre = mul(hidden, down_full) + down_vec
        final, norm_two_back = jax.vjp(normalize, middle + down_pre, gain_two, shift_two)
        output = jnp.where(in_slot, final, 0.0).astype(low)
        grad_final = jnp.where(in_slot, cotangent.astype(full), 0.0)
        grad_resid_two, grad_gain_two, grad_shift_two = norm_two_back(grad_final)
        grad_down = grad_resid_two.astype(low)
        grad_down_weight = mul(hidden, grad_down, TN)
        (grad_up_pre,) = gelu_back(mul(grad_down, down_full, NT))
        grad_up = grad_up_pre.astype(low)
        grad_up_weight = mul(middle_low, grad_up, TN)
        grad_middle = grad_resid_two + mul(grad_up, up_full, NT)
        grad_resid_one, grad_gain_one, grad_shift_one = norm_one_back(grad_middle)
        grad_branch = grad_resid_one.astype(low)
        grad_out_weight = mul(attended, grad_branch)
        grad_attended = mul(out_full, grad_branch, NT).astype(low)
        vector_grads = [
            column_sums(grad_branch), grad_gain_one, grad_shift_one, column_sums(grad_up),
            column_sums(grad_down), grad_gain_two, grad_shift_two,
        ]
        packed_grad = jnp.concatenate([v.reshape(fsdp_count, -1) for v in vector_grads], axis=1)
    saved = (q_x, k_t, k_wide, v_wide, mixed, row_stats)
    if on_block:
        (input_grad, grad_read, grad_write, qkv_out, vector_sum, up_out, down_out, out_out) = back(
            lengths, grad_attended, saved, packed_grad, rows, weight, grad_resid_one,
            grad_up_weight, grad_down_weight, grad_out_weight,
        )
        own_vectors = vector_sum[:6].reshape(-1)
        qkv_out, up_out, down_out, out_out = (g.astype(full) for g in (qkv_out, up_out, down_out, out_out))
    else:
        grad_t = lax.all_to_all(grad_attended, "seq", split_axis=0, concat_axis=1, tiled=True)
        partial_in, weight_part, sums = attention_backward(*saved, grad_t, rows, weight)
        from_heads = lax.psum_scatter(partial_in, "seq", scatter_dimension=0, tiled=True).astype(full)
        grad_layer_in = grad_resid_one + from_heads
        input_grad = jnp.where(is_memory, 0.0, grad_layer_in)
        grad_memory = lax.dot_general(
            picks, grad_layer_in, TN, precision=lax.Precision.HIGHEST, preferred_element_type=full
        )
        grad_memory = lax.psum(grad_memory.astype(low), "seq").astype(full)
        grad_read, grad_write = grad_memory[:MEM], grad_memory[MEM:]
        sums = sums[:, 0].reshape(heads, 3, HEAD)
        own_sums = jnp.stack([sums[:, 0].reshape(-1), sums[:, 2].reshape(-1)])[:, None]
        zero_qv = jnp.zeros((2, seq_count, head_cols), full)
        qv_grad = lax.dynamic_update_slice_in_dim(zero_qv, own_sums, seq_place, 1)
        packed_grad = jnp.concatenate([qv_grad.reshape(fsdp_count, -1), packed_grad], axis=1)
        packed_sum = lax.psum(packed_grad, ("fsdp", "seq"))
        own_vectors = lax.dynamic_index_in_dim(packed_sum, lax.axis_index("fsdp"), 0, False)

        def both_axes(part):
            piece = lax.psum_scatter(part.astype(low), "fsdp", scatter_dimension=0, tiled=True)
            return lax.psum(piece, "seq").astype(full)

        qkv_piece = lax.psum_scatter(weight_part, "fsdp", scatter_dimension=0, tiled=True)
        qkv_parts = lax.all_gather(qkv_piece, "seq", axis=0).reshape(seq_count, shard, heads, 3, HEAD)
        qkv_out = jnp.transpose(qkv_parts, (1, 3, 0, 2, 4)).reshape(shard, 3 * width).astype(full)
        up_out, down_out, out_out = both_axes(grad_up_weight), both_axes(grad_down_weight), both_axes(grad_out_weight)
    vector_outs, start = [], 0
    for vector in vectors:
        vector_outs.append(own_vectors[start : start + vector.shape[0]])
        start += vector.shape[0]
    qv_out, out_b_out, gain_one_out, shift_one_out, up_b_out, down_b_out, gain_two_out, shift_two_out = vector_outs
    return (
        output, input_grad, grad_read[None], grad_write[None], qkv_out, qv_out, out_out, out_b_out, gain_one_out,
        shift_one_out, up_out, up_b_out, down_out, down_b_out, gain_two_out, shift_two_out,
    )


def solution(mesh):
    rows, piece = P(("fsdp", "seq"), None), P("fsdp")
    matrix, memory = P("fsdp", None), P("fsdp", None, None)
    in_specs = (
        rows, memory, memory, piece, matrix, piece, matrix, piece, piece, piece, matrix, piece, matrix,
        piece, piece, piece, rows,
    )
    out_specs = (
        rows, rows, memory, memory, matrix, piece, matrix, piece, piece, piece, matrix, piece, matrix,
        piece, piece, piece,
    )
    return jax.shard_map(per_device, mesh=mesh, in_specs=in_specs, out_specs=out_specs, check_vma=False)
```

```python
from functools import partial

import jax
import jax.numpy as jnp
from jax import lax
from jax.experimental import pallas as pl
from jax.experimental.pallas import tpu as pltpu
from jax.sharding import PartitionSpec as P

HEAD = 64
MEM = 10
WIDE = 128
VMEM_BYTES = 64000 * 1024

norm_epsilon = 1e-06
masked_score = -1e30
low = jnp.bfloat16
full = jnp.float32

NN = (((1,), (0,)), ((), ()))
NT = (((1,), (1,)), ((), ()))
TN = (((0,), (0,)), ((), ()))
TT = (((0,), (1,)), ((), ()))


def mul(left, right, dims=NN):
    return lax.dot_general(left, right, dims, preferred_element_type=full)


def three_parts(value):
    high = value.astype(low)
    rest = value - high.astype(full)
    middle = rest.astype(low)
    return high, middle, (rest - middle.astype(full)).astype(low)


def stack_rows(rows, columns):
    place = lax.broadcasted_iota(jnp.int32, (HEAD, columns), 0)
    block = jnp.zeros((HEAD, columns), full)
    for index, row in enumerate(rows):
        block = jnp.where(place == index, row, block)
    return block.astype(low)


def project_block(start, length, rows_ref, weight_ref, bias_q, bias_v, q_x, k_t, v_x, k_wide, v_wide, step):
    head_cols = k_t.shape[0]
    lanes = pl.ds(start, step)
    made = mul(weight_ref[...], rows_ref[lanes, :], TT)
    place = start + lax.broadcasted_iota(jnp.int32, (1, step), 1)
    key_bias = jnp.where(place < length, 0.0, masked_score)
    one = jnp.ones((1, step), full)
    query_extra = stack_rows([one], step)
    key_extra = stack_rows([key_bias, one, one, one], step)
    value_extra = stack_rows([one, one, one], step)
    for h in range(head_cols // HEAD):
        own = slice(h * HEAD, (h + 1) * HEAD)
        base = 3 * h * HEAD
        query = (made[base : base + HEAD] + bias_q[own]).astype(low)
        q_x[h, :HEAD, lanes] = query * jnp.asarray(HEAD**-0.5, low)
        q_x[h, HEAD:, lanes] = query_extra
        k_t[own, lanes] = made[base + HEAD : base + 2 * HEAD].astype(low)
        v_x[h, :HEAD, lanes] = (made[base + 2 * HEAD : base + 3 * HEAD] + bias_v[own]).astype(low)
        v_x[h, HEAD:, lanes] = value_extra
        k_wide[h, lanes, :] = jnp.transpose(jnp.concatenate([k_t[own, lanes], key_extra], axis=0))
        v_wide[h, lanes, :] = jnp.transpose(v_x[h, :, lanes])


def project_heads(length, rows_ref, weight_ref, bias_ref, q_x, k_t, v_x, k_wide, v_wide):
    head_cols = k_t.shape[0]
    bias = jnp.transpose(bias_ref[...])[:, 0:1]
    for start in range(0, rows_ref.shape[0], 512):
        project_block(
            start, length, rows_ref, weight_ref, bias[:head_cols], bias[head_cols:],
            q_x, k_t, v_x, k_wide, v_wide, 512,
        )


def attend_block(h, lanes, q_x, k_wide, v_x, mixed, mixed_low, row_stats):
    scores = mul(k_wide[h], q_x[h, :, lanes])
    row_max = jnp.max(scores, axis=0, keepdims=True)
    probs = jnp.exp(scores - row_max).astype(low)
    total = mul(v_x[h, : HEAD + 16], probs)
    row_sum = total[HEAD : HEAD + 1]
    own = pl.ds(h * HEAD, HEAD)
    result = total[:HEAD] / row_sum
    mixed[own, lanes] = result
    mixed_low[own, lanes] = result.astype(low)
    row_stats[h, :, lanes] = jnp.broadcast_to(row_max + jnp.log(row_sum), (8, result.shape[1]))


def forward_kernel(
    length_ref, rows_ref, weight_ref, bias_ref, q_x, k_t, k_wide, v_wide, mixed, mixed_low, row_stats, v_x
):
    project_heads(length_ref[0], rows_ref, weight_ref, bias_ref, q_x, k_t, v_x, k_wide, v_wide)
    heads = q_x.shape[0]
    block = 512
    blocks = q_x.shape[2] // block

    def step(index, carry):
        h = index // blocks
        start = pl.multiple_of(lax.rem(index, blocks) * block, block)
        attend_block(h, pl.ds(start, block), q_x, k_wide, v_x, mixed, mixed_low, row_stats)
        return carry

    lax.fori_loop(0, heads * blocks, step, 0)


def attention_forward(length, rows, weight, bias):
    slot_rows = rows.shape[0]
    head_cols = weight.shape[1] // 3
    heads = head_cols // HEAD
    vmem = pl.BlockSpec(memory_space=pltpu.VMEM)
    return pl.pallas_call(
        forward_kernel,
        in_specs=[pl.BlockSpec(memory_space=pltpu.SMEM), vmem, vmem, vmem],
        out_specs=[vmem] * 7,
        out_shape=[
            jax.ShapeDtypeStruct((heads, WIDE, slot_rows), low),
            jax.ShapeDtypeStruct((head_cols, slot_rows), low),
            jax.ShapeDtypeStruct((heads, slot_rows, WIDE), low),
            jax.ShapeDtypeStruct((heads, slot_rows, WIDE), low),
            jax.ShapeDtypeStruct((head_cols, slot_rows), full),
            jax.ShapeDtypeStruct((head_cols, slot_rows), low),
            jax.ShapeDtypeStruct((heads, 8, slot_rows), full),
        ],
        scratch_shapes=[pltpu.VMEM((heads, WIDE, slot_rows), low)],
        compiler_params=pltpu.CompilerParams(vmem_limit_bytes=VMEM_BYTES),
        name="attention_forward",
    )(length, rows, weight, bias)


def attend_back(h, lanes, q_x, q_here, do_x, grad_t, mixed, row_stats, k_t, k_wide, v_wide, grads, grad_k, grad_v, first):
    own = pl.ds(pl.multiple_of(h * HEAD, HEAD), HEAD)
    grad = grad_t[own, lanes]
    columns = grad.shape[1]
    delta = jnp.sum(grad.astype(full) * mixed[own, lanes], axis=0, keepdims=True)
    parts = [part.astype(full) for part in three_parts(-delta)]
    do_x[:HEAD, :] = grad
    do_x[HEAD:, :] = stack_rows(parts, columns)
    parts = [part.astype(full) for part in three_parts(-row_stats[h, 0:1, lanes])]
    q_here[:HEAD, :] = q_x[h, :HEAD, lanes]
    q_here[HEAD:, :] = stack_rows([jnp.ones((1, columns), full)] + parts, columns)
    probs = jnp.exp(mul(k_wide[h], q_here[...]))
    grad_scores = (probs * mul(v_wide[h], do_x[...])).astype(low)
    value_part = mul(grad, probs.astype(low), NT)
    key_part = mul(q_here[:HEAD, :], grad_scores, NT)

    @pl.when(first)
    def _():
        grad_v[...] = value_part
        grad_k[...] = key_part

    @pl.when(jnp.logical_not(first))
    def _():
        grad_v[...] += value_part
        grad_k[...] += key_part

    query_part = mul(k_t[own, :], grad_scores) * HEAD**-0.5
    grads[pl.ds(pl.multiple_of(3 * h * HEAD, HEAD), HEAD), lanes] = query_part.astype(low)


def backward_kernel(
    q_in, k_t, k_wide, v_wide, mixed, row_stats, grad_t, rows_ref, weight_ref,
    partial_out, weight_out, sums_out, q_here, do_x, grads, grad_k, grad_v,
):
    heads, _, slot_rows = q_in.shape
    block = 512
    blocks = slot_rows // block

    def step(index, carry):
        h = index // blocks
        turn = lax.rem(index, blocks)
        start = pl.multiple_of(turn * block, block)
        attend_back(
            h, pl.ds(start, block), q_in, q_here, do_x, grad_t, mixed, row_stats, k_t, k_wide, v_wide, grads, grad_k,
            grad_v, turn == 0,
        )

        @pl.when(turn == blocks - 1)
        def _():
            base = pl.multiple_of(3 * h * HEAD, HEAD)
            grads[pl.ds(base + HEAD, HEAD), :] = grad_k[...].astype(low)
            grads[pl.ds(base + 2 * HEAD, HEAD), :] = grad_v[...].astype(low)

        return carry

    lax.fori_loop(0, heads * blocks, step, 0)
    for start in range(0, slot_rows, block):
        partial_out[start : start + block, :] = mul(
            grads[:, start : start + block], weight_ref[...], TT
        ).astype(partial_out.dtype)
    weight_out[...] = jnp.transpose(mul(grads[...], rows_ref[...])).astype(weight_out.dtype)
    sums_out[...] = jnp.broadcast_to(
        jnp.sum(grads[...].astype(full), axis=1, keepdims=True), sums_out.shape
    )


def attention_backward(q_x, k_t, k_wide, v_wide, mixed, row_stats, grad_t, rows, weight):
    heads, _, slot_rows = q_x.shape
    width, all_cols = weight.shape
    vmem = pl.BlockSpec(memory_space=pltpu.VMEM)
    return pl.pallas_call(
        backward_kernel,
        in_specs=[vmem] * 9,
        out_specs=[vmem] * 3,
        out_shape=[
            jax.ShapeDtypeStruct((slot_rows, width), low),
            jax.ShapeDtypeStruct((width, all_cols), low),
            jax.ShapeDtypeStruct((all_cols, WIDE), full),
        ],
        scratch_shapes=[
            pltpu.VMEM((WIDE, 512), low),
            pltpu.VMEM((WIDE, 512), low),
            pltpu.VMEM((all_cols, slot_rows), low),
            pltpu.VMEM((HEAD, slot_rows), full),
            pltpu.VMEM((HEAD, slot_rows), full),
        ],
        compiler_params=pltpu.CompilerParams(vmem_limit_bytes=VMEM_BYTES),
        name="attention_backward",
    )(q_x, k_t, k_wide, v_wide, mixed, row_stats, grad_t, rows, weight)


MESH = pl.DeviceIdType.MESH
OWN, RELATIONS = 0, 7
UP_W, OUT_W, DOWN_W, QKV_W = 0, 1, 2, 3


def offset_of(relation):
    return (0, -1, -2, -3, 1, 2, 3)[relation]


class Place:
    def __init__(self):
        self.f, self.s = lax.axis_index("fsdp"), lax.axis_index("seq")
        self.z, self.x = self.f // 2, lax.rem(self.f, 2)
        self.y, self.c = self.s // 2, lax.rem(self.s, 2)
        self.core = (self.f, 2 * self.y + 1 - self.c)
        self.across_y = (self.f, 2 * (1 - self.y) + self.c)
        self.diagonal = (self.f, 2 * (1 - self.y) + 1 - self.c)
        self.across_x = (2 * self.z + 1 - self.x, self.s)
        self.above = (self.f + 2, self.s)
        self.below = (self.f - 2, self.s)

    def has(self, relation):
        offset = offset_of(relation)
        return (self.z + offset >= 0) & (self.z + offset <= 3)

    def source(self, relation, column):
        own_column = self.f + 2 * offset_of(relation)
        return own_column if column == 0 else own_column + 1 - 2 * self.x

    def member(self, turn):
        flip_y = 1 - turn // 2
        flip_c = lax.rem(turn, 2) if not isinstance(turn, int) else turn % 2
        flip_c = flip_c + (1 - 2 * flip_c) * (turn // 2)
        return 2 * lax.rem(self.y + flip_y, 2) + lax.rem(self.c + flip_c, 2)


def remote(src, dst, send, recv, where):
    return pltpu.make_async_remote_copy(
        src_ref=src, dst_ref=dst, send_sem=send, recv_sem=recv, device_id=where, device_id_type=MESH
    )


def greet(place, everyone):
    barrier = pltpu.get_barrier_semaphore()
    near = [place.core, place.across_y, place.diagonal, place.across_x]
    for where in near:
        pl.semaphore_signal(barrier, inc=1, device_id=where, device_id_type=MESH)

    @pl.when(place.z > 0)
    def _():
        pl.semaphore_signal(barrier, inc=1, device_id=place.below, device_id_type=MESH)

    @pl.when(place.z < 3)
    def _():
        pl.semaphore_signal(barrier, inc=1, device_id=place.above, device_id_type=MESH)

    ends = jnp.where((place.z == 0) | (place.z == 3), 1, 2)
    pl.semaphore_wait(barrier, len(near) + ends)


class Gather:
    def __init__(self, place, own, whole, sems):
        self.place, self.own, self.whole = place, own, whole
        (self.z_send, self.z_recv, self.x_send, self.x_recv, self.c_send, self.c_recv,
         self.y_send, self.y_recv, self.d_send, self.d_recv) = sems

    def piece(self, array, source, quarter=None):
        c = self.place.c
        ref = self.whole[array]
        if array == QKV_W:
            return ref.at[source]
        if array == DOWN_W:
            rows = ref.shape[0] // 8
            part = rows // 4
            quarter = self.place.s if quarter is None else quarter
            return ref.at[pl.ds(pl.multiple_of(source * rows + quarter * part, part), part)]
        rows, columns = ref.shape[0] // 8, ref.shape[1] // 2
        return ref.at[
            pl.ds(pl.multiple_of(source * rows, rows), rows),
            pl.ds(pl.multiple_of(c * columns, columns), columns),
        ]

    def own_piece(self, array):
        ref = self.own[array]
        if array == QKV_W:
            return ref
        if array == DOWN_W:
            part = ref.shape[0] // 4
            return ref.at[pl.ds(pl.multiple_of(self.place.s * part, part), part)]
        columns = ref.shape[1] // 2
        return ref.at[:, pl.ds(pl.multiple_of(self.place.c * columns, columns), columns)]

    def along_z(self, array, relation, way):
        here = self.piece(array, self.place.source(relation, 0))
        src = self.own_piece(array) if relation == OWN else here
        step = abs(offset_of(relation))
        where = self.place.above if way == 0 else self.place.below
        return remote(src, here, self.z_send.at[array, way, step], self.z_recv.at[array, way, step], where)

    def z_ways(self, relation):
        place = self.place
        ways = []
        if offset_of(relation) <= 0:
            ways.append((0, place.has(relation) & (place.z < 3)))
        if offset_of(relation) >= 0:
            ways.append((1, place.has(relation) & (place.z > 0)))
        return ways

    def wait_z(self, array, relation):
        way = 0 if offset_of(relation) < 0 else 1
        step = abs(offset_of(relation)) - 1
        here = self.piece(array, self.place.source(relation, 0))
        where = self.place.below if way == 0 else self.place.above
        remote(
            here, here, self.z_send.at[array, way, step], self.z_recv.at[array, way, step], where
        ).wait_recv()

    def over_x(self, array, relation):
        here = self.piece(array, self.place.source(relation, 0))
        src = self.own_piece(array) if relation == OWN else here
        return remote(
            src, here, self.x_send.at[array, relation], self.x_recv.at[array, relation], self.place.across_x
        )

    def from_x(self, array, relation):
        here = self.piece(array, self.place.source(relation, 1))
        return remote(
            here, here, self.x_send.at[array, relation], self.x_recv.at[array, relation], self.place.across_x
        )

    def to_core(self, array, relation, column):
        here = self.piece(array, self.place.source(relation, column))
        return remote(
            here, here, self.c_send.at[array, relation, column], self.c_recv.at[array, relation, column],
            self.place.core,
        )

    def over_y(self, relation, column):
        here = self.piece(DOWN_W, self.place.source(relation, column))
        return remote(
            here, here, self.y_send.at[relation, column], self.y_recv.at[relation, column], self.place.across_y
        )

    def far_quarter(self, relation, column):
        return self.piece(
            DOWN_W, self.place.source(relation, column), 2 * (1 - self.place.y) + self.place.c
        )

    def from_y(self, relation, column):
        here = self.far_quarter(relation, column)
        return remote(
            here, here, self.y_send.at[relation, column], self.y_recv.at[relation, column], self.place.across_y
        )

    def far_to_core(self, relation, column):
        here = self.far_quarter(relation, column)
        return remote(
            here, here, self.d_send.at[relation, column], self.d_recv.at[relation, column], self.place.core
        )

    def when(self, relation, action):
        if relation == OWN:
            action()
        else:
            pl.when(self.place.has(relation))(action)

    def arrive_z(self, array, relation):
        def action():
            if relation != OWN:
                self.wait_z(array, relation)
            for way, holds in self.z_ways(relation):
                pl.when(holds)(lambda way=way: self.along_z(array, relation, way).start())
            self.over_x(array, relation).start()
            if array != QKV_W and relation != OWN:
                self.to_core(array, relation, 0).start()
                if array == DOWN_W:
                    self.over_y(relation, 0).start()

        self.when(relation, action)

    def arrive_x(self, array, relation):
        def action():
            self.from_x(array, relation).wait_recv()
            if array != QKV_W:
                self.to_core(array, relation, 1).start()
                if array == DOWN_W:
                    self.over_y(relation, 1).start()

        self.when(relation, action)

    def arrive_y(self, relation, column):
        def action():
            self.from_y(relation, column).wait_recv()
            self.far_to_core(relation, column).start()

        if (relation, column) != (OWN, 0):
            self.when(relation, action)

    def finish(self, array):
        for relation in range(RELATIONS):
            def action():
                self.over_x(array, relation).wait_send()
                for way, holds in self.z_ways(relation):
                    pl.when(holds)(lambda way=way: self.along_z(array, relation, way).wait_send())
                if array == QKV_W:
                    return
                for column in range(2):
                    if (relation, column) == (OWN, 0):
                        continue
                    self.to_core(array, relation, column).wait()
                    if array == DOWN_W:
                        self.over_y(relation, column).wait_send()
                        self.far_to_core(relation, column).wait()

            self.when(relation, action)


def front_kernel(
    length_ref, rows_in, qkv_in, up_in, down_in, out_in,
    rows_ref, weight_ref, pieces, q_x, k_t, k_wide, v_wide, mixed, row_stats, up_full, down_full, out_full,
    attended,
    v_x, mixed_low, row_send, row_recv, far_send, far_recv, mix_send, mix_recv, local_sem, *gather_sems,
):
    place = Place()
    slot_rows, width = rows_ref.shape
    local_rows = rows_in.shape[0]
    head_cols = k_t.shape[0]
    heads = head_cols // HEAD
    own_shards = {UP_W: up_in, DOWN_W: down_in, OUT_W: out_in, QKV_W: qkv_in}
    whole = {UP_W: up_full, DOWN_W: down_full, OUT_W: out_full, QKV_W: pieces}
    gather = Gather(place, own_shards, whole, gather_sems)
    greet(place, None)

    halves = 2
    part = local_rows // halves

    def rows_of(member, half):
        return pl.ds(pl.multiple_of(member * local_rows + half * part, part), part)

    def send_rows(half, index):
        where = (place.core, place.across_y)[index]
        return remote(
            rows_in.at[pl.ds(half * part, part)], rows_ref.at[rows_of(place.s, half)],
            row_send.at[index, half], row_recv.at[index, half], where,
        )

    def rows_from(half, index):
        member = (2 * place.y + 1 - place.c, 2 * (1 - place.y) + place.c)[index]
        here = rows_ref.at[rows_of(member, half)]
        where = (place.core, place.across_y)[index]
        return remote(here, here, row_send.at[index, half], row_recv.at[index, half], where)

    def pass_rows(half, arriving):
        flip = place.c if not arriving else 1 - place.c
        here = rows_ref.at[rows_of(2 * (1 - place.y) + flip, half)]
        return remote(here, here, far_send.at[half], far_recv.at[half], place.core)

    for half in range(halves):
        send_rows(half, 1).start()
        send_rows(half, 0).start()
    gather.arrive_z(QKV_W, OWN)

    def own_copies():
        copies = []
        for index, array in enumerate((UP_W, DOWN_W, OUT_W)):
            rows = own_shards[array].shape[0]
            copies.append(pltpu.make_async_copy(
                own_shards[array], whole[array].at[pl.ds(pl.multiple_of(place.f * rows, rows), rows)],
                local_sem.at[index],
            ))
        copies.append(pltpu.make_async_copy(qkv_in, pieces.at[place.f], local_sem.at[3]))
        copies.append(pltpu.make_async_copy(
            rows_in, rows_ref.at[pl.ds(pl.multiple_of(place.s * local_rows, local_rows), local_rows)],
            local_sem.at[4],
        ))
        return copies

    for copy in own_copies():
        copy.start()

    for relation in (1, 4):
        gather.arrive_z(QKV_W, relation)
    gather.arrive_z(UP_W, OWN)
    for relation in (2, 5):
        gather.arrive_z(QKV_W, relation)
    gather.arrive_z(OUT_W, OWN)
    gather.arrive_z(DOWN_W, OWN)
    rows_from(0, 1).wait_recv()
    pass_rows(0, False).start()
    for relation in (3, 6):
        gather.arrive_z(QKV_W, relation)
    for relation in (1, 4):
        gather.arrive_z(UP_W, relation)
    for relation in range(RELATIONS):
        gather.arrive_x(QKV_W, relation)
    for copy in own_copies()[3:]:
        copy.wait()

    shard = weight_ref.shape[0] // 8
    for source in range(8):
        weight_ref[source * shard : (source + 1) * shard, :] = pieces[source, :shard, :]
    bias_q = jnp.transpose(pieces[place.s, shard : shard + 16, :].astype(full))[:head_cols, 0:1]
    bias_v = jnp.transpose(pieces[4 + place.s, shard : shard + 16, :].astype(full))[:head_cols, 0:1]
    length = length_ref[0]

    def project(member):
        start = pl.multiple_of(member * local_rows, local_rows)
        project_block(
            start, length, rows_ref, weight_ref, bias_q, bias_v, q_x, k_t, v_x, k_wide, v_wide, local_rows
        )

    project(place.s)
    for half in range(halves):
        rows_from(half, 0).wait_recv()
    project(2 * place.y + 1 - place.c)
    rows_from(1, 1).wait_recv()
    pass_rows(1, False).start()
    project(2 * (1 - place.y) + place.c)
    for relation in (1, 4):
        gather.arrive_z(OUT_W, relation)
        gather.arrive_z(DOWN_W, relation)
    for half in range(halves):
        pass_rows(half, True).wait_recv()
    project(2 * (1 - place.y) + 1 - place.c)

    def chores(step):
        if step == 0:
            gather.arrive_x(UP_W, OWN)
            for relation in (2, 5):
                gather.arrive_z(UP_W, relation)
        elif step == 2:
            for relation in (2, 5):
                gather.arrive_z(OUT_W, relation)
                gather.arrive_z(DOWN_W, relation)
            gather.arrive_x(OUT_W, OWN)
            gather.arrive_x(DOWN_W, OWN)
        elif step == 4:
            for relation in (1, 4):
                gather.arrive_x(UP_W, relation)
                gather.arrive_y(relation, 0)
            gather.arrive_y(OWN, 1)
        elif step == 6:
            for relation in (3, 6):
                gather.arrive_z(UP_W, relation)
            for relation in (1, 4):
                gather.arrive_x(OUT_W, relation)
                gather.arrive_x(DOWN_W, relation)
        elif step == 8:
            for relation in (3, 6):
                gather.arrive_z(OUT_W, relation)
                gather.arrive_z(DOWN_W, relation)
            for relation in (2, 5):
                gather.arrive_x(UP_W, relation)
                gather.arrive_y(relation, 0)
        elif step == 10:
            for relation in (2, 5):
                gather.arrive_x(OUT_W, relation)
                gather.arrive_x(DOWN_W, relation)
            for relation in (1, 4):
                gather.arrive_y(relation, 1)

    def send_mixed(h, turn, arriving=False):
        member = place.member(turn)
        own = pl.ds(pl.multiple_of(h * HEAD, HEAD), HEAD)
        lanes = pl.ds(pl.multiple_of(member * local_rows, local_rows), local_rows)
        owner = member if arriving else place.s
        there = attended.at[pl.ds(pl.multiple_of(owner * head_cols + h * HEAD, HEAD), HEAD)]
        return remote(
            mixed_low.at[own, lanes], there, mix_send.at[h, turn], mix_recv.at[h, turn], (place.f, member)
        )

    def keep_mixed(h):
        own = pl.ds(pl.multiple_of(h * HEAD, HEAD), HEAD)
        lanes = pl.ds(pl.multiple_of(place.s * local_rows, local_rows), local_rows)
        there = attended.at[pl.ds(pl.multiple_of(place.s * head_cols + h * HEAD, HEAD), HEAD)]
        return pltpu.make_async_copy(mixed_low.at[own, lanes], there, mix_send.at[h, 3])

    turns = slot_rows // local_rows

    def pass_on(index):
        h, turn = index // turns, lax.rem(index, turns)

        @pl.when(turn < turns - 1)
        def _():
            send_mixed(h, turn).start()

        @pl.when(turn == turns - 1)
        def _():
            keep_mixed(h).start()

    def step(index, carry):
        for when in range(0, 12, 2):
            pl.when(index == when)(lambda when=when: chores(when))
        h, turn = index // turns, lax.rem(index, turns)
        start = pl.multiple_of(place.member(turn) * local_rows, local_rows)
        attend_block(h, pl.ds(start, local_rows), q_x, k_wide, v_x, mixed, mixed_low, row_stats)

        @pl.when(index > 0)
        def _():
            pass_on(index - 1)

        return carry

    lax.fori_loop(0, heads * turns, step, 0)
    pass_on(heads * turns - 1)
    for relation in (3, 6):
        gather.arrive_x(UP_W, relation)
        gather.arrive_x(OUT_W, relation)
        gather.arrive_x(DOWN_W, relation)
    for relation in (3, 6):
        gather.arrive_y(relation, 0)
    for relation in (2, 5, 3, 6):
        gather.arrive_y(relation, 1)
    for array in (UP_W, OUT_W, DOWN_W, QKV_W):
        gather.finish(array)
    for copy in own_copies()[:3]:
        copy.wait()
    for half in range(halves):
        for index in range(2):
            send_rows(half, index).wait_send()
        pass_rows(half, False).wait_send()
    for h in range(heads):
        for turn in range(turns - 1):
            send_mixed(h, turn).wait_send()
            send_mixed(h, turn, True).wait_recv()
        keep_mixed(h).wait()


def front(lengths, layer_in, qkv_piece, up_weight, down_weight, out_weight):
    local_rows, width = layer_in.shape
    slot_rows = local_rows * 4
    head_cols = width // 4
    heads = head_cols // HEAD
    vmem = pl.BlockSpec(memory_space=pltpu.VMEM)
    anywhere = pl.BlockSpec(memory_space=pl.ANY)
    dma = pltpu.SemaphoreType.DMA
    hidden = up_weight.shape[1]
    return pl.pallas_call(
        front_kernel,
        in_specs=[pl.BlockSpec(memory_space=pltpu.SMEM)] + [vmem] * 5,
        out_specs=[vmem] * 9 + [anywhere] * 4,
        out_shape=[
            jax.ShapeDtypeStruct((slot_rows, width), low),
            jax.ShapeDtypeStruct((width, 3 * head_cols), low),
            jax.ShapeDtypeStruct((8,) + qkv_piece.shape, low),
            jax.ShapeDtypeStruct((heads, WIDE, slot_rows), low),
            jax.ShapeDtypeStruct((head_cols, slot_rows), low),
            jax.ShapeDtypeStruct((heads, slot_rows, WIDE), low),
            jax.ShapeDtypeStruct((heads, slot_rows, WIDE), low),
            jax.ShapeDtypeStruct((head_cols, slot_rows), full),
            jax.ShapeDtypeStruct((heads, 8, slot_rows), full),
            jax.ShapeDtypeStruct((width, hidden), low),
            jax.ShapeDtypeStruct((hidden, width), low),
            jax.ShapeDtypeStruct((width, width), low),
            jax.ShapeDtypeStruct((width, local_rows), low),
        ],
        scratch_shapes=[
            pltpu.VMEM((heads, WIDE, slot_rows), low),
            pltpu.VMEM((head_cols, slot_rows), low),
            dma((2, 2)), dma((2, 2)), dma((2,)), dma((2,)), dma((heads, 4)), dma((heads, 4)), dma((5,)),
            dma((4, 2, 3)), dma((4, 2, 3)), dma((4, 7)), dma((4, 7)), dma((3, 7, 2)), dma((3, 7, 2)),
            dma((7, 2)), dma((7, 2)), dma((7, 2)), dma((7, 2)),
        ],
        compiler_params=pltpu.CompilerParams(
            vmem_limit_bytes=VMEM_BYTES, collective_id=0, has_side_effects=True
        ),
        name="front",
    )(lengths, layer_in, qkv_piece, up_weight, down_weight, out_weight)


DW_FIRST = 3
LINES = (3, 0, 2, 1)


def add_low(left, right):
    return (left.astype(full) + right.astype(full)).astype(low)


class Reduce:
    def __init__(self, place, given, sums, from_y, from_x, from_z, sems):
        self.place, self.given, self.sums = place, given, sums
        self.from_y, self.from_x, self.from_z = from_y, from_x, from_z
        self.last = max(sums)
        self.y_send, self.y_recv, self.x_send, self.x_recv, self.z_send, self.z_recv = sems

    def dest(self, column, line):
        x = self.place.x
        return 2 * line + (x if column == 0 else 1 - x)

    def slot(self, array, line, column=0):
        if array >= DW_FIRST:
            rows = 4 * HEAD if array == self.last else 3 * HEAD
            return self.sums[array].at[self.dest(column, line), pl.ds(0, rows // 4)]
        return self.sums[array].at[line]

    def cut(self, array, ref):
        if DW_FIRST <= array < self.last:
            return ref.at[pl.ds(0, 3 * HEAD // 4)]
        return ref

    def load(self, array, column, line, sem):
        source = self.given[array]
        if array == OUT_W:
            return pltpu.make_async_copy(source.at[line], self.sums[array].at[line], sem)
        source = source.at[column, line, 0] if array == DOWN_W else source.at[column, line]
        return pltpu.make_async_copy(source, self.sums[array].at[line], sem)

    def over_y(self, line):
        return remote(
            self.given[DOWN_W].at[0, line, 1], self.from_y.at[line], self.y_send.at[line], self.y_recv.at[line],
            self.place.across_y,
        )

    def add_y(self, line):
        self.over_y(line).wait_recv()
        slot = self.slot(DOWN_W, line)
        slot[...] = add_low(slot[...], self.from_y[line])

    def over_x(self, array, line):
        if array == OUT_W:
            here = self.sums[array].at[self.place.z]
            return remote(
                here.at[1], self.from_x[array], self.x_send.at[array, 0], self.x_recv.at[array, 0], self.place.across_x
            )
        if array == UP_W:
            start = self.given[array].at[1, line]
        elif array == DOWN_W:
            start = self.given[array].at[1, line, 0]
        else:
            start = self.slot(array, line, 1)
        return remote(
            start, self.cut(array, self.from_x[array].at[line]), self.x_send.at[array, line],
            self.x_recv.at[array, line], self.place.across_x,
        )

    def add_x(self, array, line):
        self.over_x(array, line).wait_recv()
        slot = self.sums[array].at[self.place.z, 0] if array == OUT_W else self.slot(array, line)
        came = self.from_x[array] if array == OUT_W else self.cut(array, self.from_x[array].at[line])
        slot[...] = add_low(slot[...], came[...])

    def along_z(self, array, way, line):
        return remote(
            self.slot(array, line), self.cut(array, self.from_z[array].at[way, line]),
            self.z_send.at[array, way, line], self.z_recv.at[array, way, line],
            self.place.above if way == 0 else self.place.below,
        )

    def add_z(self, array, way, line):
        self.along_z(array, way, line).wait_recv()
        slot = self.slot(array, line)
        slot[...] = add_low(slot[...], self.cut(array, self.from_z[array].at[way, line])[...])

    def hop(self, array, level, lines=(0, 1, 2, 3)):
        @pl.when(self.place.z == level)
        def _():
            for line in range(3, level, -1):
                if line in lines:
                    if level > 0:
                        self.add_z(array, 0, line)
                    self.along_z(array, 0, line).start()

        @pl.when(self.place.z == 3 - level)
        def _():
            for line in range(0, 3 - level):
                if line in lines:
                    if level > 0:
                        self.add_z(array, 1, line)
                    self.along_z(array, 1, line).start()

    def settle(self, array):
        for line in range(4):

            @pl.when(self.place.z == line)
            def _(line=line):
                if line > 0:
                    self.add_z(array, 0, line)
                if line < 3:
                    self.add_z(array, 1, line)

    def finish(self, array):
        for line in range(4):
            if array != OUT_W or line == 0:
                self.over_x(array, line).wait_send()
            pl.when(self.place.z < line)(lambda line=line: self.along_z(array, 0, line).wait_send())
            pl.when(self.place.z > line)(lambda line=line: self.along_z(array, 1, line).wait_send())
            if array == DOWN_W:
                self.over_y(line).wait_send()


class Spread:
    def __init__(self, place, blocks, source, send, recv):
        self.place, self.blocks, self.source, self.send, self.recv = place, blocks, source, send, recv
        self.near = 2 * place.y + 1 - place.c
        self.far = 2 * (1 - place.y) + place.c
        self.last = 2 * (1 - place.y) + 1 - place.c

    def copy(self, kind, arriving=False):
        place = self.place
        if kind == 2:
            here = self.blocks.at[self.last if arriving else self.far]
            return remote(here, here, self.send.at[2], self.recv.at[2], place.core)
        member = (self.near, self.far)[kind] if arriving else place.s
        return remote(
            self.source, self.blocks.at[member], self.send.at[kind], self.recv.at[kind],
            (place.core, place.across_y)[kind],
        )

    def start(self):
        self.copy(1).start()
        self.copy(0).start()

    def pass_on(self):
        self.copy(1, True).wait_recv()
        self.copy(2).start()

    def finish(self):
        self.blocks[self.place.s] = self.source[...]
        self.copy(0, True).wait_recv()
        self.copy(2, True).wait_recv()
        for kind in range(3):
            self.copy(kind).wait_send()


def back_kernel(
    length_ref, grad_own, vectors_in, q_in, k_in, k_wide_in, v_wide_in, mixed_in, stats_in, rows_in, weight_in, resid_in, up_given, down_given, out_given,
    input_out, read_out, write_out, qkv_out, vector_out, up_out, down_out, out_out,
    q_x, k_t, k_wide, v_wide, mixed, row_stats, grad_t, q_here, do_x, grads, grad_k, grad_v, rows_ref, weight_ref, resid_ref,
    up_sum, out_sum, down_sum, dw, down_y, up_x, out_x, down_x, dw_x, up_z, out_z, down_z, dw_z,
    up_last, out_last, up_other, out_other, down_all, dw_all,
    near_send, near_recv, far_sum, far_recv, memory_all, memory_own,
    mix_send, mix_recv, local_sem, saved_sem, mine_sem, share_send, share_recv, near_s, near_r, far_s, far_r,
    *sems,
):
    place = Place()
    heads, _, slot_rows = q_in.shape
    width, local_rows = grad_own.shape
    head_cols = heads * HEAD
    last = DW_FIRST + heads - 1
    given = {UP_W: up_given, OUT_W: out_given, DOWN_W: down_given}
    sums = {UP_W: up_sum, OUT_W: out_sum, DOWN_W: down_sum}
    from_x = {UP_W: up_x, OUT_W: out_x, DOWN_W: down_x}
    from_z = {UP_W: up_z, OUT_W: out_z, DOWN_W: down_z}
    for h in range(heads):
        sums[DW_FIRST + h], from_x[DW_FIRST + h] = dw.at[h], dw_x.at[h]
        from_z[DW_FIRST + h] = dw_z.at[h]
    reduce = Reduce(place, given, sums, down_y, from_x, from_z, sems)
    greet(place, None)

    peers = (place.across_y, place.diagonal, place.core)

    def member_rows(turn):
        member = place.member(turn)
        return member, pl.ds(pl.multiple_of(member * local_rows, local_rows), local_rows)

    def send_grad(turn, arriving=False):
        member, lanes = member_rows(turn)
        own_lanes = pl.ds(pl.multiple_of(place.s * local_rows, local_rows), local_rows)
        src = grad_own.at[pl.ds(pl.multiple_of(member * head_cols, head_cols), head_cols)]
        return remote(
            src, grad_t.at[:, lanes if arriving else own_lanes], mix_send.at[turn], mix_recv.at[turn], peers[turn]
        )

    def saved_loads(h):
        own = pl.ds(h * HEAD, HEAD)
        pairs = (
            (k_wide_in.at[h], k_wide.at[h]), (q_in.at[h, pl.ds(0, HEAD)], q_x.at[h]), (v_wide_in.at[h], v_wide.at[h]),
            (mixed_in.at[own], mixed.at[own]), (stats_in.at[h], row_stats.at[h]), (k_in.at[own], k_t.at[own]),
        )
        return [pltpu.make_async_copy(src, dst, saved_sem.at[h, i]) for i, (src, dst) in enumerate(pairs)]

    for turn in range(3):
        send_grad(turn).start()
    for load in saved_loads(0):
        load.start()
    loads = []
    for index, (src, dst) in enumerate(((rows_in, rows_ref), (weight_in, weight_ref), (resid_in, resid_ref))):
        loads.append(pltpu.make_async_copy(src, dst, local_sem.at[index]))

    def sum_loads(array):
        return [reduce.load(array, 0, line, mine_sem.at[array, line]) for line in LINES]

    def send_x(array, lines=LINES):
        for line in lines:
            reduce.over_x(array, line).start()

    send_x(UP_W)
    for line in LINES:
        reduce.over_y(line).start()
    send_x(DOWN_W)
    for array in (OUT_W, UP_W, DOWN_W):
        for load in sum_loads(array):
            load.start()
    for load in loads:
        load.start()

    for h in range(1, heads):
        for load in saved_loads(h):
            load.start()

    own_lanes = pl.ds(pl.multiple_of(place.s * local_rows, local_rows), local_rows)
    grad_t[:, own_lanes] = grad_own[pl.ds(pl.multiple_of(place.s * head_cols, head_cols), head_cols), :]

    def take_x(array, lines=LINES):
        for line in lines:
            reduce.add_x(array, line)

    turns = slot_rows // local_rows

    def weight_part(h):
        if h == 0:
            loads[0].wait()
        base = 3 * h * HEAD
        part = jnp.transpose(mul(grads[base : base + 3 * HEAD, :], rows_ref[...])).astype(low)
        half = width // 16
        for dest in range(8):
            start = 2 * half * dest
            dw[h, dest, :half, :] = jnp.concatenate(
                [part[start : start + half], part[start + half : start + 2 * half]], axis=1
            )
            if h == heads - 1:
                dw[h, dest, half:, :] = vectors_in[dest].astype(low)
        if h == heads - 1:
            total = jnp.sum(grads[...].astype(full), axis=1, keepdims=True)
            spread = jnp.transpose(jnp.broadcast_to(total, (total.shape[0], WIDE)))[0:1]
            for kind, first_dest in ((0, 0), (2, 4)):
                for head in range(heads):
                    start = (3 * head + kind) * HEAD
                    dw[h, first_dest + place.s, half : half + 1, head * HEAD : (head + 1) * HEAD] = spread[
                        :, start : start + HEAD
                    ].astype(low)
        send_x(DW_FIRST + h)

    share = {UP_W: (up_last, up_other), OUT_W: (out_last, out_other)}

    def settled(array):
        return sums[array].at[place.z, 0] if array == OUT_W else sums[array].at[place.z]

    def sum_y(array):
        mine_now = settled(array)
        return remote(mine_now, share[array][0], share_send.at[array, 0], share_recv.at[array, 0], place.across_y)

    def half_to_core(array):
        mine_now = settled(array)
        return remote(mine_now, share[array][1], share_send.at[array, 1], share_recv.at[array, 1], place.core)

    def spread_of(array):
        if array == DOWN_W:
            return Spread(place, down_all, down_sum.at[place.z], share_send.at[2], share_recv.at[2])
        h = array - DW_FIRST
        return Spread(
            place, dw_all.at[h, :, pl.ds(0, reduce.slot(array, 0).shape[0])], reduce.slot(array, place.z),
            share_send.at[array], share_recv.at[array],
        )

    def add_last(array):
        sum_y(array).wait()
        slot = settled(array)
        slot[...] = add_low(slot[...], share[array][0][...])
        half_to_core(array).start()

    first, second = DW_FIRST, DW_FIRST + 1

    def chores(index):
        if index == 1:
            send_grad(2, True).wait_recv()
            for load in sum_loads(OUT_W):
                load.wait()
            reduce.hop(OUT_W, 0)
        elif index == 2:
            send_grad(1, True).wait_recv()
            for array in (UP_W, DOWN_W):
                for load in sum_loads(array):
                    load.wait()
            take_x(UP_W, (3,))
            reduce.hop(UP_W, 0, (3,))
        elif index == 3:
            send_grad(0, True).wait_recv()
            reduce.hop(OUT_W, 1)
        elif index == 4:
            for load in saved_loads(1):
                load.wait()
            weight_part(0)
            take_x(UP_W, (0,))
            reduce.hop(UP_W, 0, (0,))
        elif index == 5:
            reduce.hop(OUT_W, 2)
        elif index == 6:
            for line in LINES:
                reduce.add_y(line)
            take_x(UP_W, (2,))
            reduce.hop(UP_W, 0, (2,))
            reduce.settle(OUT_W)
            reduce.over_x(OUT_W, 0).start()
        elif index == 7:
            reduce.hop(UP_W, 1, (3, 0))
        elif index == 8:
            for load in saved_loads(2):
                load.wait()
            weight_part(1)
            take_x(UP_W, (1,))
            reduce.hop(UP_W, 0, (1,))
        elif index == 9:
            reduce.hop(UP_W, 2)
            reduce.hop(UP_W, 1, (2,))
            take_x(DOWN_W, (3, 0))
            reduce.hop(DOWN_W, 0, (3, 0))
        elif index == 10:
            reduce.hop(UP_W, 1, (1,))
            take_x(DOWN_W, (2,))
            reduce.hop(DOWN_W, 0, (2,))
        elif index == 11:
            reduce.settle(UP_W)
            sum_y(UP_W).start()
            take_x(DOWN_W, (1,))
            reduce.hop(DOWN_W, 0, (1,))
            reduce.hop(DOWN_W, 1, (3, 0))

    def step(index, carry):
        for when in range(1, 12):
            pl.when(index == when)(lambda when=when: chores(when))
        h, turn = index // turns, lax.rem(index, turns)
        _, lanes = member_rows(turns - 1 - turn)
        attend_back(
            h, lanes, q_x, q_here, do_x, grad_t, mixed, row_stats, k_t, k_wide, v_wide, grads, grad_k, grad_v, turn == 0
        )

        @pl.when(turn == turns - 1)
        def _():
            base = pl.multiple_of(3 * h * HEAD, HEAD)
            grads[pl.ds(base + HEAD, HEAD), :] = grad_k[...].astype(low)
            grads[pl.ds(base + 2 * HEAD, HEAD), :] = grad_v[...].astype(low)

        return carry

    for load in saved_loads(0):
        load.wait()
    lax.fori_loop(0, heads * turns, step, 0)

    weight_part(heads - 1)
    loads[1].wait()
    loads[2].wait()

    halves, part = 2, local_rows // 2
    length = length_ref[0]

    def memory_pick(rows, start):
        line = lax.broadcasted_iota(jnp.int32, (32, rows), 0)
        row = start + lax.broadcasted_iota(jnp.int32, (32, rows), 1)
        wanted = jnp.where(line < 16, line, length - MEM + line - 16)
        used = (line < MEM) | ((line >= 16) & (line < 16 + MEM))
        return jnp.where(used & (wanted == row), 1.0, 0.0).astype(low)

    def part_for(turn, half):
        start = pl.multiple_of(place.member(turn) * local_rows + half * part, part)
        return mul(grads[:, pl.ds(start, part)], weight_ref[...], TT)

    def share_near(index, half):
        rows = pl.ds(half * part, part)
        return remote(
            near_send.at[index, rows], near_recv.at[index, rows], near_s.at[index, half], near_r.at[index, half],
            place.core,
        )

    def share_far(half):
        rows = pl.ds(half * part, part)
        return remote(far_sum.at[rows], far_recv.at[rows], far_s.at[half], far_r.at[half], place.across_y)

    for half in range(halves):
        rows = slice(half * part, (half + 1) * part)
        near_send[0, rows, :] = part_for(1, half).astype(low)
        share_near(0, half).start()
        far_sum[rows, :] = part_for(0, half).astype(low)
        if half == 0:
            taken = mul(memory_pick(slot_rows, 0), grads[...], NT).astype(low)
            own_part = mul(memory_pick(local_rows, place.s * local_rows), resid_ref[...].astype(low))
            memory_own[...] = (mul(taken, weight_ref[...], NT) + own_part).astype(low)
        share_near(0, half).wait_recv()
        far_sum[rows, :] = add_low(far_sum[rows, :], near_recv[0, rows, :])
        share_far(half).start()
    memory = Spread(place, memory_all, memory_own, share_send.at[DW_FIRST + heads], share_recv.at[DW_FIRST + heads])
    memory.start()
    take_x(first)
    reduce.hop(first, 0)
    reduce.add_x(OUT_W, 0)
    sum_y(OUT_W).start()
    for half in range(halves):
        rows = slice(half * part, (half + 1) * part)
        near_send[1, rows, :] = part_for(2, half).astype(low)
        share_near(1, half).start()
    reduce.hop(DOWN_W, 1, (2, 1))
    reduce.hop(DOWN_W, 2)
    take_x(second)
    reduce.hop(second, 0)
    take_x(last)
    reduce.hop(last, 0)
    reduce.hop(first, 1)
    add_last(UP_W)
    for half in range(halves):
        resid_ref[half * part : (half + 1) * part, :] += part_for(3, half)
    reduce.hop(second, 1)
    reduce.hop(first, 2)
    reduce.hop(last, 1)
    reduce.settle(DOWN_W)
    spread_of(DOWN_W).start()
    reduce.hop(second, 2)
    reduce.settle(first)
    spread_of(first).start()
    reduce.hop(last, 2)
    reduce.settle(second)
    spread_of(second).start()
    reduce.settle(last)
    spread_of(last).start()
    add_last(OUT_W)
    memory.pass_on()
    for h in (heads - 1, 0, 1):
        spread_of(DW_FIRST + h).pass_on()
    spread_of(DOWN_W).pass_on()
    for array, out in ((UP_W, up_out), (OUT_W, out_out)):
        columns = out.shape[1] // 2
        out[:, pl.ds(pl.multiple_of(place.c * columns, columns), columns)] = settled(array)[...]
        half_to_core(array).wait()
        out[:, pl.ds(pl.multiple_of((1 - place.c) * columns, columns), columns)] = share[array][1][...]
    for h in range(heads):
        spread_of(DW_FIRST + h).finish()
    spread_of(DOWN_W).finish()
    quarter = down_out.shape[0] // 4
    for member in range(4):
        down_out[member * quarter : (member + 1) * quarter, :] = down_all[member]
    half = qkv_out.shape[0] // 2
    for kind in range(3):
        for member in range(4):
            for h in range(heads):
                start = kind * width + (member * heads + h) * HEAD
                for side in range(2):
                    lanes = (3 * side + kind) * HEAD
                    qkv_out[side * half : (side + 1) * half, start : start + HEAD] = dw_all[
                        h, member, :half, lanes : lanes + HEAD
                    ]
    vector_sum = dw_all[heads - 1, 0, half:, :].astype(full)
    for member in range(1, 4):
        vector_sum = vector_sum + dw_all[heads - 1, member, half:, :].astype(full)
    vector_out[...] = vector_sum
    memory.finish()
    total = memory_all[0].astype(full)
    for member in range(1, 4):
        total = total + memory_all[member].astype(full)
    read_out[...] = total[:MEM]
    write_out[...] = total[16 : 16 + MEM]
    for half in range(halves):
        rows = slice(half * part, (half + 1) * part)
        share_near(1, half).wait_recv()
        share_far(half).wait_recv()
        grad_layer = resid_ref[rows, :] + near_recv[1, rows, :].astype(full) + far_recv[rows, :].astype(full)
        rows_at = place.s * local_rows + half * part + lax.broadcasted_iota(jnp.int32, (part, 1), 0)
        in_write = (rows_at >= length - MEM) & (rows_at < length)
        input_out[rows, :] = jnp.where((rows_at < MEM) | in_write, 0.0, grad_layer)
    for array in range(DW_FIRST + heads):
        reduce.finish(array)
    for turn in range(3):
        send_grad(turn).wait_send()
    for half in range(halves):
        for index in range(2):
            share_near(index, half).wait_send()
        share_far(half).wait_send()


def back(lengths, grad_own, saved, vectors, rows, weight, resid, up_given, down_given, out_given):
    q_x, k_t, k_wide, v_wide, mixed, row_stats = saved
    heads, _, slot_rows = q_x.shape
    width, local_rows = grad_own.shape
    hidden = 2 * up_given.shape[3]
    shard, head_cols = width // 8, heads * HEAD
    half, small, piece = hidden // 2, width // 2, hidden // 32
    vmem = pl.BlockSpec(memory_space=pltpu.VMEM)
    anywhere = pl.BlockSpec(memory_space=pl.ANY)
    dma = pltpu.SemaphoreType.DMA
    arrays = DW_FIRST + heads

    def held(*shape, kind=low):
        return pltpu.VMEM(shape, kind)

    tall = (shard // 2 + 16, 6 * HEAD)
    return pl.pallas_call(
        back_kernel,
        in_specs=[pl.BlockSpec(memory_space=pltpu.SMEM)] + [vmem] * 2 + [anywhere] * 12,
        out_specs=[vmem] * 8,
        out_shape=[
            jax.ShapeDtypeStruct((local_rows, width), full),
            jax.ShapeDtypeStruct((MEM, width), full),
            jax.ShapeDtypeStruct((MEM, width), full),
            jax.ShapeDtypeStruct((shard, 3 * width), low),
            jax.ShapeDtypeStruct((16, 6 * HEAD), full),
            jax.ShapeDtypeStruct((shard, hidden), low),
            jax.ShapeDtypeStruct((hidden // 8, width), low),
            jax.ShapeDtypeStruct((shard, width), low),
        ],
        scratch_shapes=[
            held(heads, HEAD, slot_rows), held(head_cols, slot_rows), held(heads, slot_rows, WIDE),
            held(heads, slot_rows, WIDE), held(head_cols, slot_rows, kind=full), held(heads, 8, slot_rows, kind=full),
            held(head_cols, slot_rows), held(WIDE, local_rows), held(WIDE, local_rows), held(3 * head_cols, slot_rows),
            held(HEAD, slot_rows, kind=full), held(HEAD, slot_rows, kind=full),
            held(slot_rows, width), held(width, 3 * head_cols), held(local_rows, width, kind=full),
            held(4, shard, half), held(4, 2, shard, small), held(4, piece, width),
            held(heads, 8, *tall), held(4, piece, width),
            held(4, shard, half), held(shard, small), held(4, piece, width), held(heads, 4, *tall),
            held(2, 4, shard, half), held(2, 4, 2, shard, small), held(2, 4, piece, width), held(heads, 2, 4, *tall),
            held(shard, half), held(shard, small), held(shard, half), held(shard, small),
            held(4, piece, width), held(heads, 4, *tall),
            held(2, local_rows, width), held(2, local_rows, width), held(local_rows, width),
            held(local_rows, width), held(4, 32, width), held(32, width),
            dma((3,)), dma((3,)), dma((3,)), dma((heads, 6)), dma((3, 4)), dma((arrays + 1, 3)),
            dma((arrays + 1, 3)), dma((2, 2)), dma((2, 2)), dma((2,)), dma((2,)),
            dma((4,)), dma((4,)), dma((arrays, 4)), dma((arrays, 4)),
            dma((arrays, 2, 4)), dma((arrays, 2, 4)),
        ],
        compiler_params=pltpu.CompilerParams(
            vmem_limit_bytes=VMEM_BYTES, collective_id=1, has_side_effects=True
        ),
        name="back",
    )(
        lengths, grad_own, vectors, q_x, k_t, k_wide, v_wide, mixed, row_stats, rows, weight, resid,
        up_given, down_given, out_given,
    )


def phi_parts(value):
    normal = 0.5 * (1.0 + lax.erf(value * (0.5**0.5)))
    density = jnp.exp(-0.5 * value * value) * (0.5 * 2.0**0.5 * 3.141592653589793**-0.5)
    return normal, normal + value * density


def statistics(values):
    centre = values - jnp.mean(values, axis=1, keepdims=True)
    factor = lax.rsqrt(jnp.mean(centre * centre, axis=1, keepdims=True) + norm_epsilon)
    return centre * factor, factor


def norm_back(grad, gain, normed, factor):
    scaled = grad * gain
    first = jnp.mean(scaled, axis=1, keepdims=True)
    second = jnp.mean(scaled * normed, axis=1, keepdims=True)
    return factor * (scaled - first - normed * second)


def column_total(values):
    return jnp.sum(values, axis=0, keepdims=True)


def middle_kernel(
    length_ref, layer_in, cotangent, pieces, attended_in, up_in, down_in, out_in,
    output, resid_out, grad_own, vector_out, up_out, down_out, out_out,
    attended, up_w, down_w, out_w, vectors, small, up_bias, hidden, slope, normed_one, middle_low, grad_down,
    grad_two, grad_mid, totals, up_total, up_grad, down_grad, out_grad, up_sum, down_sum, out_sum,
    from_y, load_sem, save_sem, c_send, c_recv, y_send, y_recv,
):
    place = Place()
    rows, width = layer_in.shape
    ff = up_w.shape[1]
    chunk = ff // 4
    shard = width // 8
    barrier = pltpu.get_barrier_semaphore()
    for where in (place.core, place.across_y):
        pl.semaphore_signal(barrier, inc=1, device_id=where, device_id_type=MESH)

    def chunk_lanes(j):
        return pl.ds(pl.multiple_of(j * chunk, chunk), chunk)

    def up_load(j):
        return pltpu.make_async_copy(up_in.at[:, chunk_lanes(j)], up_w.at[:, chunk_lanes(j)], load_sem.at[j])

    def down_load(j):
        return pltpu.make_async_copy(down_in.at[chunk_lanes(j)], down_w.at[chunk_lanes(j)], load_sem.at[4 + j])

    first_loads = [
        pltpu.make_async_copy(pieces.at[:, pl.ds(shard, 16)], vectors, load_sem.at[8]),
        pltpu.make_async_copy(attended_in, attended, load_sem.at[9]),
        pltpu.make_async_copy(out_in, out_w, load_sem.at[10]),
    ]
    for load in first_loads:
        load.start()
    for j in range(4):
        up_load(j).start()
        down_load(j).start()
    first_loads[0].wait()
    spots = ((0, 192), (0, 288), (0, 384), (1, 288), (1, 384), (1, 480))
    for source in range(8):
        for index, (line, start) in enumerate(spots):
            small[index : index + 1, source * shard : (source + 1) * shard] = vectors[
                source, line : line + 1, start : start + shard
            ].astype(full)
        base = source * 4 * shard
        up_bias[0:1, base : base + shard] = vectors[source, 0:1, 480:576].astype(full)
        up_bias[0:1, base + shard : base + 4 * shard] = vectors[source, 1:2, 0:288].astype(full)
    out_bias, gain_one, shift_one = small[0:1, :], small[1:2, :], small[2:3, :]
    down_bias, gain_two, shift_two = small[3:4, :], small[4:5, :], small[5:6, :]
    first_loads[1].wait()
    first_loads[2].wait()

    branch = mul(attended[...], out_w[...], TN)
    normed, factor_one = statistics(layer_in[...].astype(full) + branch + out_bias)
    normed_one[...] = normed
    middle_low[...] = (normed * gain_one + shift_one).astype(low)
    grad_mid[...] = jnp.zeros_like(grad_mid)

    def forward_chunk(j, carry):
        up_load(j).wait()
        lanes = chunk_lanes(j)
        value = mul(middle_low[...], up_w[:, lanes]) + up_bias[0:1, lanes]
        normal, slope_here = phi_parts(value)
        hidden[:, lanes] = (value * normal).astype(low)
        slope[:, lanes] = slope_here
        down_load(j).wait()
        grad_mid[...] += mul(hidden[:, lanes], down_w[lanes, :])
        return carry

    lax.fori_loop(0, 4, forward_chunk, 0)
    middle = normed_one[...] * gain_one + shift_one
    normed_two, factor_two = statistics(middle + grad_mid[...] + down_bias)
    places = place.s * rows + lax.broadcasted_iota(jnp.int32, (rows, 1), 0)
    in_slot = places < length_ref[0]
    output[...] = jnp.where(in_slot, normed_two * gain_two + shift_two, 0.0).astype(low)
    grad_final = jnp.where(in_slot, cotangent[...].astype(full), 0.0)
    totals[4:5, :] = column_total(grad_final * normed_two)
    totals[5:6, :] = column_total(grad_final)
    grad_resid = norm_back(grad_final, gain_two, normed_two, factor_two)
    grad_two[...] = grad_resid
    grad_down[...] = grad_resid.astype(low)
    totals[3:4, :] = column_total(grad_down[...].astype(full))
    pl.semaphore_wait(barrier, 2)

    def down_piece(ref, line, column, far, core):
        dest = 2 * line + (place.x if column == 0 else 1 - place.x)
        y = place.y if far == 0 else 1 - place.y
        return ref.at[pl.ds(pl.multiple_of(dest * 4 * shard + (2 * y + core) * shard, shard), shard)]

    def side_piece(ref, line, column, core):
        dest = 2 * line + (place.x if column == 0 else 1 - place.x)
        half = ref.shape[1] // 2
        return ref.at[
            pl.ds(pl.multiple_of(dest * shard, shard), shard), pl.ds(pl.multiple_of(core * half, half), half)
        ]

    def down_share(line, column, far):
        return remote(
            down_piece(down_grad, line, column, far, 1 - place.c), down_sum.at[column, line, far],
            c_send.at[2 + far, column, line], c_recv.at[2 + far, column, line], place.core,
        )

    def side_slot(array, line, column):
        return out_sum.at[line, column] if array == 1 else up_sum.at[column, line]

    def over_y(line):
        return remote(down_sum.at[1, line, 1], from_y.at[line], y_send.at[line], y_recv.at[line], place.across_y)

    def side_share(array, line, column):
        grad = (up_grad, out_grad)[array]
        return remote(
            side_piece(grad, line, column, 1 - place.c), side_slot(array, line, column),
            c_send.at[array, column, line], c_recv.at[array, column, line], place.core,
        )

    def down_save(column, line):
        return pltpu.make_async_copy(down_sum.at[column, line], down_out.at[column, line], save_sem.at[2, column, line])

    def side_save(array, column, line):
        out = out_out.at[line, column] if array == 1 else up_out.at[column, line]
        return pltpu.make_async_copy(side_slot(array, line, column), out, save_sem.at[array, column, line])

    def add_far(column, line):
        down_share(line, column, 1).wait_recv()
        down_sum[column, line, 1] = add_low(
            down_sum[column, line, 1], down_piece(down_grad, line, column, 1, place.c)[...]
        )

    def down_chunk(line, carry):
        lanes = chunk_lanes(line)
        down_grad[lanes, :] = mul(hidden[:, lanes], grad_down[...], TN).astype(low)
        for column in range(2):
            for far in range(2):
                down_share(line, column, far).start()
        return carry

    lax.fori_loop(0, 4, down_chunk, 0)
    grad_mid[...] = grad_two[...]

    def back_chunk(turn, carry):
        j = lax.rem(2 * (1 - place.c) + turn, 4)
        lanes = chunk_lanes(j)
        grad_up = (mul(grad_down[...], down_w[lanes, :], NT) * slope[:, lanes]).astype(low)
        up_total[0:1, lanes] = column_total(grad_up.astype(full))
        up_grad[:, lanes] = mul(middle_low[...], grad_up, TN).astype(low)
        grad_mid[...] += mul(grad_up, up_w[:, lanes], NT)

        @pl.when(turn == 0)
        def _():
            for line in LINES:
                add_far(1, line)
                over_y(line).start()

        @pl.when(turn == 1)
        def _():
            for column in (1, 0):
                for line in LINES:
                    side_share(0, line, column).start()

        return carry

    lax.fori_loop(0, 4, back_chunk, 0)
    grad_middle = grad_mid[...]
    normed = normed_one[...]
    totals[1:2, :] = column_total(grad_middle * normed)
    totals[2:3, :] = column_total(grad_middle)
    grad_one = norm_back(grad_middle, gain_one, normed, factor_one)
    resid_out[...] = grad_one
    grad_branch = grad_one.astype(low)
    totals[0:1, :] = column_total(grad_branch.astype(full))
    out_grad[...] = mul(attended[...], grad_branch).astype(low)
    for column in (1, 0):
        for line in LINES:
            side_share(1, line, column).start()
    grad_own[...] = mul(out_w[...], grad_branch, NT).astype(low)

    def add_down(column, line):
        down_share(line, column, 0).wait_recv()
        down_sum[column, line, 0] = add_low(
            down_sum[column, line, 0], down_piece(down_grad, line, column, 0, place.c)[...]
        )
        if column == 0:
            add_far(column, line)
        else:
            over_y(line).wait()
            down_sum[column, line, 0] = add_low(down_sum[column, line, 0], from_y[line])
        down_save(column, line).start()

    def add_side(array, column, line):
        slot = side_slot(array, line, column)
        side_share(array, line, column).wait_recv()
        slot[...] = add_low(slot[...], side_piece((up_grad, out_grad)[array], line, column, place.c)[...])
        side_save(array, column, line).start()

    for line in LINES:
        add_down(0, line)
    for column in (1, 0):
        for line in LINES:
            add_side(0, column, line)
    vector_out[...] = jnp.zeros_like(vector_out)
    for dest in range(8):
        for index, (line, start) in enumerate(((0, 2), (0, 3), (1, 0), (2, 1), (2, 2), (2, 3))):
            vector_out[dest, line : line + 1, start * shard : (start + 1) * shard] = totals[
                index : index + 1, dest * shard : (dest + 1) * shard
            ]
        base = dest * 4 * shard
        vector_out[dest, 1:2, shard:] = up_total[0:1, base : base + 3 * shard]
        vector_out[dest, 2:3, :shard] = up_total[0:1, base + 3 * shard : base + 4 * shard]
    for column in range(2):
        for line in range(4):
            add_side(1, column, line)
    for line in LINES:
        add_down(1, line)
    for column in range(2):
        for line in range(4):
            for array in range(2):
                side_share(array, line, column).wait_send()
                side_save(array, column, line).wait()
            for far in range(2):
                down_share(line, column, far).wait_send()
            down_save(column, line).wait()


def middle_part(lengths, layer_in, cotangent, pieces, attended, up_full, down_full, out_full):
    rows, width = layer_in.shape
    ff = up_full.shape[1]
    shard = width // 8
    vmem = pl.BlockSpec(memory_space=pltpu.VMEM)
    anywhere = pl.BlockSpec(memory_space=pl.ANY)
    dma = pltpu.SemaphoreType.DMA

    def held(*shape, kind=low):
        return pltpu.VMEM(shape, kind)

    def shaped(*shape, kind=low):
        return jax.ShapeDtypeStruct(shape, kind)

    up_parts, down_parts, out_parts = (2, 4, shard, ff // 2), (2, 4, 2, ff // 32, width), (4, 2, shard, width // 2)
    return pl.pallas_call(
        middle_kernel,
        in_specs=[pl.BlockSpec(memory_space=pltpu.SMEM)] + [vmem] * 2 + [anywhere] * 5,
        out_specs=[vmem] * 4 + [anywhere] * 3,
        out_shape=[
            shaped(rows, width), shaped(rows, width, kind=full), shaped(width, rows),
            shaped(8, 16, 4 * shard, kind=full), shaped(*up_parts), shaped(*down_parts), shaped(*out_parts),
        ],
        scratch_shapes=[
            held(width, rows), held(width, ff), held(ff, width), held(width, width), held(8, 16, 9 * HEAD),
            held(8, width, kind=full), held(8, ff, kind=full), held(rows, ff), held(rows, ff, kind=full),
            held(rows, width, kind=full), held(rows, width), held(rows, width), held(rows, width, kind=full),
            held(rows, width, kind=full), held(8, width, kind=full), held(8, ff, kind=full),
            held(width, ff), held(ff, width), held(width, width), held(*up_parts), held(*down_parts),
            held(*out_parts), held(4, ff // 32, width), dma((11,)), dma((3, 2, 4)), dma((4, 2, 4)),
            dma((4, 2, 4)), dma((4,)), dma((4,)),
        ],
        compiler_params=pltpu.CompilerParams(
            vmem_limit_bytes=VMEM_BYTES, collective_id=2, has_side_effects=True
        ),
        name="middle",
    )(lengths, layer_in, cotangent, pieces, attended, up_full, down_full, out_full)


def normalize(values, gain_vec, shift_vec):
    centre = values - jnp.mean(values, axis=-1, keepdims=True)
    factor = lax.rsqrt(jnp.mean(centre * centre, axis=-1, keepdims=True) + norm_epsilon)
    return centre * factor * gain_vec + shift_vec


def column_sums(values):
    return jnp.sum(values, axis=0, dtype=full)


def per_device(
    tokens, read_memory, write_memory, lengths, qkv_weight, qv_bias, out_weight, out_bias, norm1_gain,
    norm1_bias, up_weight, up_bias, down_weight, down_bias, norm2_gain, norm2_bias, cotangent,
):
    seq_count = lax.axis_size("seq")
    fsdp_count = lax.axis_size("fsdp")
    seq_place = lax.axis_index("seq")
    local_rows, width = tokens.shape
    head_cols = width // seq_count
    shard = width // fsdp_count
    length = lengths[0]
    places = seq_place * local_rows + jnp.arange(local_rows, dtype=jnp.int32)
    in_slot = (places < length)[:, None]
    memory_slots = jnp.arange(MEM, dtype=jnp.int32)
    pick_read = places[:, None] == memory_slots[None, :]
    pick_write = places[:, None] == length - MEM + memory_slots[None, :]
    is_memory = jnp.any(pick_read | pick_write, axis=1)[:, None]
    picks = jnp.concatenate([pick_read, pick_write], axis=1).astype(full)
    memory = jnp.concatenate([read_memory[0], write_memory[0]], axis=0)
    layer_in = jnp.where(is_memory, mul(picks.astype(low), memory).astype(low), tokens)

    heads = head_cols // HEAD
    own_shard = lax.dynamic_slice_in_dim(
        qkv_weight.reshape(shard, 3, seq_count, heads, HEAD), seq_place, 1, 2
    )
    own_shard = jnp.transpose(own_shard[:, :, 0], (0, 2, 1, 3)).reshape(shard, 3 * head_cols)
    vectors = (qv_bias, out_bias, norm1_gain, norm1_bias, up_bias, down_bias, norm2_gain, norm2_bias)
    packed = jnp.concatenate(vectors)
    on_block = (fsdp_count, seq_count) == (8, 4)
    if on_block:
        spare = jnp.zeros((14, 3 * head_cols), low)
        piece = jnp.concatenate([own_shard, packed.reshape(2, -1), spare], axis=0)
        (rows, weight, pieces, q_x, k_t, k_wide, v_wide, mixed, row_stats, up_full, down_full, out_full,
         attended) = front(lengths, layer_in, piece, up_weight, down_weight, out_weight)
    else:
        rows = lax.all_gather(layer_in, "seq", axis=0, tiled=True)
        weight = lax.all_gather(own_shard, "fsdp", axis=0, tiled=True)
        packed = lax.all_gather(packed.reshape(1, -1), "fsdp", axis=0, tiled=True).astype(full)
    if not on_block:
        whole, start = [], 0
        for vector in vectors:
            whole.append(packed[:, start : start + vector.shape[0]].reshape(-1))
            start += vector.shape[0]
        qv_vec, out_vec, gain_one, shift_one, up_vec, down_vec, gain_two, shift_two = whole
        own_qv = lax.dynamic_slice_in_dim(qv_vec.reshape(2, seq_count, head_cols), seq_place, 1, 1)
        bias = jnp.concatenate([own_qv[0, 0], own_qv[1, 0]])
        bias = jnp.broadcast_to(bias, (8, bias.shape[0]))
        out_full = lax.all_gather(out_weight, "fsdp", axis=0, tiled=True)
        up_full = lax.all_gather(up_weight, "fsdp", axis=0, tiled=True)
        down_full = lax.all_gather(down_weight, "fsdp", axis=0, tiled=True)
        q_x, k_t, k_wide, v_wide, mixed, mixed_low, row_stats = attention_forward(lengths, rows, weight, bias)
        attended = lax.all_to_all(mixed_low, "seq", split_axis=1, concat_axis=0, tiled=True)
    if on_block:
        (output, grad_resid_one, grad_attended, packed_grad, grad_up_weight, grad_down_weight, grad_out_weight) = (
            middle_part(lengths, layer_in, cotangent, pieces, attended, up_full, down_full, out_full)
        )
    else:
        resid_one = layer_in.astype(full) + mul(attended, out_full, TN) + out_vec
        middle, norm_one_back = jax.vjp(normalize, resid_one, gain_one, shift_one)
        middle_low = middle.astype(low)
        up_pre = mul(middle_low, up_full) + up_vec
        gelu_out, gelu_back = jax.vjp(partial(jax.nn.gelu, approximate=False), up_pre)
        hidden = gelu_out.astype(low)
        down_pre = mul(hidden, down_full) + down_vec
        final, norm_two_back = jax.vjp(normalize, middle + down_pre, gain_two, shift_two)
        output = jnp.where(in_slot, final, 0.0).astype(low)
        grad_final = jnp.where(in_slot, cotangent.astype(full), 0.0)
        grad_resid_two, grad_gain_two, grad_shift_two = norm_two_back(grad_final)
        grad_down = grad_resid_two.astype(low)
        grad_down_weight = mul(hidden, grad_down, TN)
        (grad_up_pre,) = gelu_back(mul(grad_down, down_full, NT))
        grad_up = grad_up_pre.astype(low)
        grad_up_weight = mul(middle_low, grad_up, TN)
        grad_middle = grad_resid_two + mul(grad_up, up_full, NT)
        grad_resid_one, grad_gain_one, grad_shift_one = norm_one_back(grad_middle)
        grad_branch = grad_resid_one.astype(low)
        grad_out_weight = mul(attended, grad_branch)
        grad_attended = mul(out_full, grad_branch, NT).astype(low)
        vector_grads = [
            column_sums(grad_branch), grad_gain_one, grad_shift_one, column_sums(grad_up),
            column_sums(grad_down), grad_gain_two, grad_shift_two,
        ]
        packed_grad = jnp.concatenate([v.reshape(fsdp_count, -1) for v in vector_grads], axis=1)
    saved = (q_x, k_t, k_wide, v_wide, mixed, row_stats)
    if on_block:
        (input_grad, grad_read, grad_write, qkv_out, vector_sum, up_out, down_out, out_out) = back(
            lengths, grad_attended, saved, packed_grad, rows, weight, grad_resid_one,
            grad_up_weight, grad_down_weight, grad_out_weight,
        )
        own_vectors = vector_sum[:3].reshape(-1)
        qkv_out, up_out, down_out, out_out = (g.astype(full) for g in (qkv_out, up_out, down_out, out_out))
    else:
        grad_t = lax.all_to_all(grad_attended, "seq", split_axis=0, concat_axis=1, tiled=True)
        partial_in, weight_part, sums = attention_backward(*saved, grad_t, rows, weight)
        from_heads = lax.psum_scatter(partial_in, "seq", scatter_dimension=0, tiled=True).astype(full)
        grad_layer_in = grad_resid_one + from_heads
        input_grad = jnp.where(is_memory, 0.0, grad_layer_in)
        grad_memory = lax.dot_general(
            picks, grad_layer_in, TN, precision=lax.Precision.HIGHEST, preferred_element_type=full
        )
        grad_memory = lax.psum(grad_memory.astype(low), "seq").astype(full)
        grad_read, grad_write = grad_memory[:MEM], grad_memory[MEM:]
        sums = sums[:, 0].reshape(heads, 3, HEAD)
        own_sums = jnp.stack([sums[:, 0].reshape(-1), sums[:, 2].reshape(-1)])[:, None]
        zero_qv = jnp.zeros((2, seq_count, head_cols), full)
        qv_grad = lax.dynamic_update_slice_in_dim(zero_qv, own_sums, seq_place, 1)
        packed_grad = jnp.concatenate([qv_grad.reshape(fsdp_count, -1), packed_grad], axis=1)
        packed_sum = lax.psum(packed_grad, ("fsdp", "seq"))
        own_vectors = lax.dynamic_index_in_dim(packed_sum, lax.axis_index("fsdp"), 0, False)

        def both_axes(part):
            piece = lax.psum_scatter(part.astype(low), "fsdp", scatter_dimension=0, tiled=True)
            return lax.psum(piece, "seq").astype(full)

        qkv_piece = lax.psum_scatter(weight_part, "fsdp", scatter_dimension=0, tiled=True)
        qkv_parts = lax.all_gather(qkv_piece, "seq", axis=0).reshape(seq_count, shard, heads, 3, HEAD)
        qkv_out = jnp.transpose(qkv_parts, (1, 3, 0, 2, 4)).reshape(shard, 3 * width).astype(full)
        up_out, down_out, out_out = both_axes(grad_up_weight), both_axes(grad_down_weight), both_axes(grad_out_weight)
    vector_outs, start = [], 0
    for vector in vectors:
        vector_outs.append(own_vectors[start : start + vector.shape[0]])
        start += vector.shape[0]
    qv_out, out_b_out, gain_one_out, shift_one_out, up_b_out, down_b_out, gain_two_out, shift_two_out = vector_outs
    return (
        output, input_grad, grad_read[None], grad_write[None], qkv_out, qv_out, out_out, out_b_out, gain_one_out,
        shift_one_out, up_out, up_b_out, down_out, down_b_out, gain_two_out, shift_two_out,
    )


def solution(mesh):
    rows, piece = P(("fsdp", "seq"), None), P("fsdp")
    matrix, memory = P("fsdp", None), P("fsdp", None, None)
    in_specs = (
        rows, memory, memory, piece, matrix, piece, matrix, piece, piece, piece, matrix, piece, matrix,
        piece, piece, piece, rows,
    )
    out_specs = (
        rows, rows, memory, memory, matrix, piece, matrix, piece, piece, piece, matrix, piece, matrix,
        piece, piece, piece,
    )
    return jax.shard_map(per_device, mesh=mesh, in_specs=in_specs, out_specs=out_specs, check_vma=False)
```

```python
from functools import partial

import jax
import jax.numpy as jnp
from jax import lax
from jax.experimental import pallas as pl
from jax.experimental.pallas import tpu as pltpu
from jax.sharding import PartitionSpec as P

HEAD = 64
MEM = 10
WIDE = 128
VMEM_BYTES = 64000 * 1024

norm_epsilon = 1e-06
masked_score = -1e30
low = jnp.bfloat16
full = jnp.float32

NN = (((1,), (0,)), ((), ()))
NT = (((1,), (1,)), ((), ()))
TN = (((0,), (0,)), ((), ()))
TT = (((0,), (1,)), ((), ()))


def mul(left, right, dims=NN):
    return lax.dot_general(left, right, dims, preferred_element_type=full)


def three_parts(value):
    high = value.astype(low)
    rest = value - high.astype(full)
    middle = rest.astype(low)
    return high, middle, (rest - middle.astype(full)).astype(low)


def stack_rows(rows, columns):
    place = lax.broadcasted_iota(jnp.int32, (HEAD, columns), 0)
    block = jnp.zeros((HEAD, columns), full)
    for index, row in enumerate(rows):
        block = jnp.where(place == index, row, block)
    return block.astype(low)


def project_block(start, length, rows_ref, weight_ref, bias_q, bias_v, q_x, k_t, v_x, k_wide, v_wide, step):
    head_cols = k_t.shape[0]
    lanes = pl.ds(start, step)
    made = mul(weight_ref[...], rows_ref[lanes, :], TT)
    place = start + lax.broadcasted_iota(jnp.int32, (1, step), 1)
    key_bias = jnp.where(place < length, 0.0, masked_score)
    one = jnp.ones((1, step), full)
    query_extra = stack_rows([one], step)
    key_extra = stack_rows([key_bias, one, one, one], step)
    value_extra = stack_rows([one, one, one], step)
    for h in range(head_cols // HEAD):
        own = slice(h * HEAD, (h + 1) * HEAD)
        base = 3 * h * HEAD
        query = (made[base : base + HEAD] + bias_q[own]).astype(low)
        q_x[h, :HEAD, lanes] = query * jnp.asarray(HEAD**-0.5, low)
        q_x[h, HEAD:, lanes] = query_extra
        k_t[own, lanes] = made[base + HEAD : base + 2 * HEAD].astype(low)
        v_x[h, :HEAD, lanes] = (made[base + 2 * HEAD : base + 3 * HEAD] + bias_v[own]).astype(low)
        v_x[h, HEAD:, lanes] = value_extra
        k_wide[h, lanes, :] = jnp.transpose(jnp.concatenate([k_t[own, lanes], key_extra], axis=0))
        v_wide[h, lanes, :] = jnp.transpose(v_x[h, :, lanes])


def project_heads(length, rows_ref, weight_ref, bias_ref, q_x, k_t, v_x, k_wide, v_wide):
    head_cols = k_t.shape[0]
    bias = jnp.transpose(bias_ref[...])[:, 0:1]
    for start in range(0, rows_ref.shape[0], 512):
        project_block(
            start, length, rows_ref, weight_ref, bias[:head_cols], bias[head_cols:],
            q_x, k_t, v_x, k_wide, v_wide, 512,
        )


def attend_block(h, lanes, q_x, k_wide, v_x, mixed, mixed_low, row_stats):
    scores = mul(k_wide[h], q_x[h, :, lanes])
    row_max = jnp.max(scores, axis=0, keepdims=True)
    probs = jnp.exp(scores - row_max).astype(low)
    total = mul(v_x[h, : HEAD + 16], probs)
    row_sum = total[HEAD : HEAD + 1]
    own = pl.ds(h * HEAD, HEAD)
    result = total[:HEAD] / row_sum
    mixed[own, lanes] = result
    mixed_low[own, lanes] = result.astype(low)
    row_stats[h, :, lanes] = jnp.broadcast_to(row_max + jnp.log(row_sum), (8, result.shape[1]))


def forward_kernel(
    length_ref, rows_ref, weight_ref, bias_ref, q_x, k_t, k_wide, v_wide, mixed, mixed_low, row_stats, v_x
):
    project_heads(length_ref[0], rows_ref, weight_ref, bias_ref, q_x, k_t, v_x, k_wide, v_wide)
    heads = q_x.shape[0]
    block = 512
    blocks = q_x.shape[2] // block

    def step(index, carry):
        h = index // blocks
        start = pl.multiple_of(lax.rem(index, blocks) * block, block)
        attend_block(h, pl.ds(start, block), q_x, k_wide, v_x, mixed, mixed_low, row_stats)
        return carry

    lax.fori_loop(0, heads * blocks, step, 0)


def attention_forward(length, rows, weight, bias):
    slot_rows = rows.shape[0]
    head_cols = weight.shape[1] // 3
    heads = head_cols // HEAD
    vmem = pl.BlockSpec(memory_space=pltpu.VMEM)
    return pl.pallas_call(
        forward_kernel,
        in_specs=[pl.BlockSpec(memory_space=pltpu.SMEM), vmem, vmem, vmem],
        out_specs=[vmem] * 7,
        out_shape=[
            jax.ShapeDtypeStruct((heads, WIDE, slot_rows), low),
            jax.ShapeDtypeStruct((head_cols, slot_rows), low),
            jax.ShapeDtypeStruct((heads, slot_rows, WIDE), low),
            jax.ShapeDtypeStruct((heads, slot_rows, WIDE), low),
            jax.ShapeDtypeStruct((head_cols, slot_rows), full),
            jax.ShapeDtypeStruct((head_cols, slot_rows), low),
            jax.ShapeDtypeStruct((heads, 8, slot_rows), full),
        ],
        scratch_shapes=[pltpu.VMEM((heads, WIDE, slot_rows), low)],
        compiler_params=pltpu.CompilerParams(vmem_limit_bytes=VMEM_BYTES),
        name="attention_forward",
    )(length, rows, weight, bias)


def attend_back(h, lanes, q_x, q_here, do_x, grad_t, mixed, row_stats, k_t, k_wide, v_wide, grads, grad_k, grad_v, first):
    own = pl.ds(pl.multiple_of(h * HEAD, HEAD), HEAD)
    grad = grad_t[own, lanes]
    columns = grad.shape[1]
    delta = jnp.sum(grad.astype(full) * mixed[own, lanes], axis=0, keepdims=True)
    parts = [part.astype(full) for part in three_parts(-delta)]
    do_x[:HEAD, :] = grad
    do_x[HEAD:, :] = stack_rows(parts, columns)
    parts = [part.astype(full) for part in three_parts(-row_stats[h, 0:1, lanes])]
    q_here[:HEAD, :] = q_x[h, :HEAD, lanes]
    q_here[HEAD:, :] = stack_rows([jnp.ones((1, columns), full)] + parts, columns)
    probs = jnp.exp(mul(k_wide[h], q_here[...]))
    grad_scores = (probs * mul(v_wide[h], do_x[...])).astype(low)
    value_part = mul(grad, probs.astype(low), NT)
    key_part = mul(q_here[:HEAD, :], grad_scores, NT)

    @pl.when(first)
    def _():
        grad_v[...] = value_part
        grad_k[...] = key_part

    @pl.when(jnp.logical_not(first))
    def _():
        grad_v[...] += value_part
        grad_k[...] += key_part

    query_part = mul(k_t[own, :], grad_scores) * HEAD**-0.5
    grads[pl.ds(pl.multiple_of(3 * h * HEAD, HEAD), HEAD), lanes] = query_part.astype(low)


def backward_kernel(
    q_in, k_t, k_wide, v_wide, mixed, row_stats, grad_t, rows_ref, weight_ref,
    partial_out, weight_out, sums_out, q_here, do_x, grads, grad_k, grad_v,
):
    heads, _, slot_rows = q_in.shape
    block = 512
    blocks = slot_rows // block

    def step(index, carry):
        h = index // blocks
        turn = lax.rem(index, blocks)
        start = pl.multiple_of(turn * block, block)
        attend_back(
            h, pl.ds(start, block), q_in, q_here, do_x, grad_t, mixed, row_stats, k_t, k_wide, v_wide, grads, grad_k,
            grad_v, turn == 0,
        )

        @pl.when(turn == blocks - 1)
        def _():
            base = pl.multiple_of(3 * h * HEAD, HEAD)
            grads[pl.ds(base + HEAD, HEAD), :] = grad_k[...].astype(low)
            grads[pl.ds(base + 2 * HEAD, HEAD), :] = grad_v[...].astype(low)

        return carry

    lax.fori_loop(0, heads * blocks, step, 0)
    for start in range(0, slot_rows, block):
        partial_out[start : start + block, :] = mul(
            grads[:, start : start + block], weight_ref[...], TT
        ).astype(partial_out.dtype)
    weight_out[...] = jnp.transpose(mul(grads[...], rows_ref[...])).astype(weight_out.dtype)
    sums_out[...] = jnp.broadcast_to(
        jnp.sum(grads[...].astype(full), axis=1, keepdims=True), sums_out.shape
    )


def attention_backward(q_x, k_t, k_wide, v_wide, mixed, row_stats, grad_t, rows, weight):
    heads, _, slot_rows = q_x.shape
    width, all_cols = weight.shape
    vmem = pl.BlockSpec(memory_space=pltpu.VMEM)
    return pl.pallas_call(
        backward_kernel,
        in_specs=[vmem] * 9,
        out_specs=[vmem] * 3,
        out_shape=[
            jax.ShapeDtypeStruct((slot_rows, width), low),
            jax.ShapeDtypeStruct((width, all_cols), low),
            jax.ShapeDtypeStruct((all_cols, WIDE), full),
        ],
        scratch_shapes=[
            pltpu.VMEM((WIDE, 512), low),
            pltpu.VMEM((WIDE, 512), low),
            pltpu.VMEM((all_cols, slot_rows), low),
            pltpu.VMEM((HEAD, slot_rows), full),
            pltpu.VMEM((HEAD, slot_rows), full),
        ],
        compiler_params=pltpu.CompilerParams(vmem_limit_bytes=VMEM_BYTES),
        name="attention_backward",
    )(q_x, k_t, k_wide, v_wide, mixed, row_stats, grad_t, rows, weight)


MESH = pl.DeviceIdType.MESH
OWN, RELATIONS = 0, 7
UP_W, OUT_W, DOWN_W, QKV_W = 0, 1, 2, 3


def offset_of(relation):
    return (0, -1, -2, -3, 1, 2, 3)[relation]


class Place:
    def __init__(self):
        self.f, self.s = lax.axis_index("fsdp"), lax.axis_index("seq")
        self.z, self.x = self.f // 2, lax.rem(self.f, 2)
        self.y, self.c = self.s // 2, lax.rem(self.s, 2)
        self.core = (self.f, 2 * self.y + 1 - self.c)
        self.across_y = (self.f, 2 * (1 - self.y) + self.c)
        self.diagonal = (self.f, 2 * (1 - self.y) + 1 - self.c)
        self.across_x = (2 * self.z + 1 - self.x, self.s)
        self.above = (self.f + 2, self.s)
        self.below = (self.f - 2, self.s)

    def has(self, relation):
        offset = offset_of(relation)
        return (self.z + offset >= 0) & (self.z + offset <= 3)

    def source(self, relation, column):
        own_column = self.f + 2 * offset_of(relation)
        return own_column if column == 0 else own_column + 1 - 2 * self.x

    def member(self, turn):
        flip_y = 1 - turn // 2
        flip_c = lax.rem(turn, 2) if not isinstance(turn, int) else turn % 2
        flip_c = flip_c + (1 - 2 * flip_c) * (turn // 2)
        return 2 * lax.rem(self.y + flip_y, 2) + lax.rem(self.c + flip_c, 2)


def remote(src, dst, send, recv, where):
    return pltpu.make_async_remote_copy(
        src_ref=src, dst_ref=dst, send_sem=send, recv_sem=recv, device_id=where, device_id_type=MESH
    )


def greet(place, all_lines):
    barrier = pltpu.get_barrier_semaphore()
    near = [place.core, place.across_y, place.diagonal, place.across_x]
    for where in near:
        pl.semaphore_signal(barrier, inc=1, device_id=where, device_id_type=MESH)
    for line in range(4):
        gap = place.z - line
        meets = gap != 0 if all_lines else (gap == 1) | (gap == -1)

        @pl.when(meets)
        def _(line=line):
            pl.semaphore_signal(
                barrier, inc=1, device_id=(2 * line + place.x, place.s), device_id_type=MESH
            )

    ends = 3 if all_lines else jnp.where((place.z == 0) | (place.z == 3), 1, 2)
    pl.semaphore_wait(barrier, len(near) + ends)


class Gather:
    def __init__(self, place, own, whole, sems):
        self.place, self.own, self.whole = place, own, whole
        (self.z_send, self.z_recv, self.x_send, self.x_recv, self.c_send, self.c_recv,
         self.y_send, self.y_recv, self.d_send, self.d_recv) = sems

    def piece(self, array, source, quarter=None, pair=False):
        c = self.place.c
        ref = self.whole[array]
        if array == QKV_W:
            return ref.at[source]
        if array == DOWN_W:
            rows = ref.shape[0] // 8
            part = rows // 4
            quarter = self.place.s if quarter is None else quarter
            return ref.at[pl.ds(pl.multiple_of(source * rows + quarter * part, part), part)]
        rows, columns = ref.shape[0] // 8, ref.shape[1] // 2
        count = 2 if pair else 1
        return ref.at[
            pl.ds(pl.multiple_of(source * rows, rows), count * rows),
            pl.ds(pl.multiple_of(c * columns, columns), columns),
        ]

    def own_piece(self, array):
        if array == QKV_W:
            return self.piece(array, self.place.f)
        ref = self.own[array]
        if array == DOWN_W:
            part = ref.shape[0] // 4
            return ref.at[pl.ds(pl.multiple_of(self.place.s * part, part), part)]
        columns = ref.shape[1] // 2
        return ref.at[:, pl.ds(pl.multiple_of(self.place.c * columns, columns), columns)]

    def z_piece(self, array, relation):
        source = self.place.source(relation, 0)
        if array == OUT_W:
            return self.piece(array, source - self.place.x, pair=True)
        return self.piece(array, source)

    def along_z(self, array, relation, way):
        here = self.z_piece(array, relation)
        src = self.own_piece(array) if relation == OWN and array != OUT_W else here
        step = abs(offset_of(relation))
        where = self.place.above if way == 0 else self.place.below
        return remote(src, here, self.z_send.at[array, way, step], self.z_recv.at[array, way, step], where)

    def z_ways(self, relation):
        place = self.place
        ways = []
        if offset_of(relation) <= 0:
            ways.append((0, place.has(relation) & (place.z < 3)))
        if offset_of(relation) >= 0:
            ways.append((1, place.has(relation) & (place.z > 0)))
        return ways

    def wait_z(self, array, relation):
        way = 0 if offset_of(relation) < 0 else 1
        step = abs(offset_of(relation)) - 1
        here = self.z_piece(array, relation)
        where = self.place.below if way == 0 else self.place.above
        remote(
            here, here, self.z_send.at[array, way, step], self.z_recv.at[array, way, step], where
        ).wait_recv()

    def over_x(self, array, relation):
        here = self.piece(array, self.place.source(relation, 0))
        src = self.own_piece(array) if relation == OWN else here
        return remote(
            src, here, self.x_send.at[array, relation], self.x_recv.at[array, relation], self.place.across_x
        )

    def from_x(self, array, relation):
        here = self.piece(array, self.place.source(relation, 1))
        return remote(
            here, here, self.x_send.at[array, relation], self.x_recv.at[array, relation], self.place.across_x
        )

    def to_core(self, array, relation, column):
        if array == OUT_W and relation != OWN:
            here = self.z_piece(array, relation)
        else:
            here = self.piece(array, self.place.source(relation, column))
        return remote(
            here, here, self.c_send.at[array, relation, column], self.c_recv.at[array, relation, column],
            self.place.core,
        )

    def over_y(self, relation, column):
        here = self.piece(DOWN_W, self.place.source(relation, column))
        return remote(
            here, here, self.y_send.at[relation, column], self.y_recv.at[relation, column], self.place.across_y
        )

    def far_quarter(self, relation, column):
        return self.piece(
            DOWN_W, self.place.source(relation, column), 2 * (1 - self.place.y) + self.place.c
        )

    def from_y(self, relation, column):
        here = self.far_quarter(relation, column)
        return remote(
            here, here, self.y_send.at[relation, column], self.y_recv.at[relation, column], self.place.across_y
        )

    def far_to_core(self, relation, column):
        here = self.far_quarter(relation, column)
        return remote(
            here, here, self.d_send.at[relation, column], self.d_recv.at[relation, column], self.place.core
        )

    def when(self, relation, action):
        if relation == OWN:
            action()
        else:
            pl.when(self.place.has(relation))(action)

    def arrive_z(self, array, relation):
        def action():
            if relation != OWN:
                self.wait_z(array, relation)
            for way, holds in self.z_ways(relation):
                pl.when(holds)(lambda way=way: self.along_z(array, relation, way).start())
            if array != OUT_W:
                self.over_x(array, relation).start()
            if array != QKV_W and relation != OWN:
                self.to_core(array, relation, 0).start()
                if array == DOWN_W:
                    self.over_y(relation, 0).start()

        self.when(relation, action)

    def cross_out(self):
        self.over_x(OUT_W, OWN).start()

    def pair_out(self, own_copy):
        own_copy.wait()
        self.from_x(OUT_W, OWN).wait_recv()
        self.to_core(OUT_W, OWN, 1).start()
        for way, holds in self.z_ways(OWN):
            pl.when(holds)(lambda way=way: self.along_z(OUT_W, OWN, way).start())

    def arrive_x(self, array, relation):
        def action():
            self.from_x(array, relation).wait_recv()
            if array != QKV_W:
                self.to_core(array, relation, 1).start()
                if array == DOWN_W:
                    self.over_y(relation, 1).start()

        self.when(relation, action)

    def arrive_y(self, relation, column):
        def action():
            self.from_y(relation, column).wait_recv()
            self.far_to_core(relation, column).start()

        if (relation, column) != (OWN, 0):
            self.when(relation, action)

    def finish(self, array):
        for relation in range(RELATIONS):
            def action():
                if array != OUT_W or relation == OWN:
                    self.over_x(array, relation).wait_send()
                for way, holds in self.z_ways(relation):
                    pl.when(holds)(lambda way=way: self.along_z(array, relation, way).wait_send())
                if array == QKV_W:
                    return
                for column in range(2):
                    if (relation, column) == (OWN, 0) or (array == OUT_W and relation != OWN and column == 1):
                        continue
                    self.to_core(array, relation, column).wait()
                    if array == DOWN_W:
                        self.over_y(relation, column).wait_send()
                        self.far_to_core(relation, column).wait()

            self.when(relation, action)


def front_kernel(
    length_ref, tokens, read_rows, write_rows, qkv_in, vectors_in, up_in, down_in, out_in,
    small, up_bias, rows_out, weight_out, q_out, k_out, k_wide_out, v_wide_out, mixed_out, stats_out, up_full,
    down_full, out_full, attended,
    rows_ref, weight_ref, pieces, memory, q_x, k_t, k_wide, v_wide, v_x, mixed, mixed_low, row_stats,
    row_send, row_recv, far_send, far_recv, mix_send, mix_recv, local_sem, save_sem, head_sem, *gather_sems,
):
    place = Place()
    slot_rows, width = rows_ref.shape
    local_rows = tokens.shape[0]
    head_cols = k_t.shape[0]
    heads = head_cols // HEAD
    shard = width // 8
    length = length_ref[0]
    own_shards = {UP_W: up_in, DOWN_W: down_in, OUT_W: out_in}
    whole = {UP_W: up_full, DOWN_W: down_full, OUT_W: out_full, QKV_W: pieces}
    gather = Gather(place, own_shards, whole, gather_sems)

    memory[...] = jnp.zeros_like(memory)
    memory[:MEM, :] = read_rows[...]
    memory[16 : 16 + MEM, :] = write_rows[...]
    line = lax.broadcasted_iota(jnp.int32, (local_rows, 32), 1)
    at = place.s * local_rows + lax.broadcasted_iota(jnp.int32, (local_rows, 32), 0)
    wanted = jnp.where(line < 16, line, length - MEM + line - 16)
    used = (line < MEM) | ((line >= 16) & (line < 16 + MEM))
    pick = jnp.where(used & (wanted == at), 1.0, 0.0)
    taken = mul(pick.astype(low), memory[...]).astype(low)
    is_memory = jnp.sum(pick, axis=1, keepdims=True) > 0.5
    own_start = pl.multiple_of(place.s * local_rows, local_rows)
    rows_ref[pl.ds(own_start, local_rows), :] = jnp.where(is_memory, taken, tokens[...])
    for member in range(4):

        @pl.when(place.s == member)
        def _(member=member):
            for h in range(heads):
                for kind in range(3):
                    start = kind * width + (member * heads + h) * HEAD
                    to = (3 * h + kind) * HEAD
                    pieces[place.f, :, to : to + HEAD] = qkv_in[:, start : start + HEAD]

    columns = 3 * head_cols
    pieces[place.f, :, columns:] = jnp.zeros((shard, HEAD), low)
    for line in range(18):
        pieces[place.f, line : line + 1, columns:] = vectors_in[:, line * HEAD : (line + 1) * HEAD].astype(low)
    greet(place, False)

    halves = 2
    part = local_rows // halves

    def rows_of(member, half):
        return pl.ds(pl.multiple_of(member * local_rows + half * part, part), part)

    def send_rows(half, index):
        where = (place.core, place.across_y)[index]
        here = rows_ref.at[rows_of(place.s, half)]
        return remote(here, here, row_send.at[index, half], row_recv.at[index, half], where)

    def rows_from(half, index):
        member = (2 * place.y + 1 - place.c, 2 * (1 - place.y) + place.c)[index]
        here = rows_ref.at[rows_of(member, half)]
        where = (place.core, place.across_y)[index]
        return remote(here, here, row_send.at[index, half], row_recv.at[index, half], where)

    def pass_rows(half, arriving):
        flip = place.c if not arriving else 1 - place.c
        here = rows_ref.at[rows_of(2 * (1 - place.y) + flip, half)]
        return remote(here, here, far_send.at[half], far_recv.at[half], place.core)

    def own_copies():
        copies = []
        for index, array in enumerate((UP_W, DOWN_W, OUT_W)):
            rows = own_shards[array].shape[0]
            copies.append(pltpu.make_async_copy(
                own_shards[array], whole[array].at[pl.ds(pl.multiple_of(place.f * rows, rows), rows)],
                local_sem.at[index],
            ))
        return copies

    gather.arrive_z(QKV_W, OWN)
    for half in range(halves):
        send_rows(half, 1).start()
        send_rows(half, 0).start()
    gather.cross_out()
    gather.arrive_z(UP_W, OWN)
    for copy in own_copies():
        copy.start()
    for relation in (1, 4):
        gather.arrive_z(QKV_W, relation)
    gather.pair_out(own_copies()[2])
    rows_from(0, 1).wait_recv()
    pass_rows(0, False).start()
    for relation in (2, 5):
        gather.arrive_z(QKV_W, relation)
    gather.arrive_z(DOWN_W, OWN)
    for relation in (1, 4):
        gather.arrive_z(UP_W, relation)
    for relation in (3, 6):
        gather.arrive_z(QKV_W, relation)
    for relation in range(RELATIONS):
        gather.arrive_x(QKV_W, relation)

    for source in range(8):
        weight_ref[source * shard : (source + 1) * shard, :] = pieces[source, :, :columns]
    tile = slice(columns - HEAD, columns + HEAD)
    bias_q = jnp.transpose(pieces[place.s, 0:16, tile].astype(full))[HEAD:]
    bias_v = jnp.transpose(pieces[4 + place.s, 0:16, tile].astype(full))[HEAD:]
    bias_q = jnp.concatenate([bias_q[:, h : h + 1] for h in range(heads)], axis=0)
    bias_v = jnp.concatenate([bias_v[:, h : h + 1] for h in range(heads)], axis=0)

    def project(member):
        start = pl.multiple_of(member * local_rows, local_rows)
        project_block(
            start, length, rows_ref, weight_ref, bias_q, bias_v, q_x, k_t, v_x, k_wide, v_wide, local_rows
        )

    project(place.s)
    for half in range(halves):
        rows_from(half, 0).wait_recv()
    project(2 * place.y + 1 - place.c)
    rows_from(1, 1).wait_recv()
    pass_rows(1, False).start()
    project(2 * (1 - place.y) + place.c)
    for relation in (1, 4):
        gather.arrive_z(OUT_W, relation)
        gather.arrive_z(DOWN_W, relation)

    def scatter_vector(target, index, size, first):
        for source in range(8):
            done = 0
            while done < size:
                line, lane = divmod(first + done, HEAD)
                count = min(HEAD - lane, size - done)
                target[index : index + 1, source * size + done : source * size + done + count] = pieces[
                    source, line : line + 1, columns + lane : columns + lane + count
                ].astype(full)
                done += count

    for index, first in enumerate((2, 3, 4, 9, 10, 11)):
        scatter_vector(small, index, shard, first * shard)
    scatter_vector(up_bias, 0, 4 * shard, 5 * shard)
    for half in range(halves):
        pass_rows(half, True).wait_recv()
    project(2 * (1 - place.y) + 1 - place.c)

    def saves():
        pairs = [(rows_ref, rows_out), (weight_ref, weight_out), (k_t, k_out), (k_wide, k_wide_out), (v_wide, v_wide_out)]
        pairs += [(q_x.at[h, pl.ds(0, HEAD)], q_out.at[h]) for h in range(heads)]
        return [pltpu.make_async_copy(src, dst, save_sem.at[index]) for index, (src, dst) in enumerate(pairs)]

    for save in saves():
        save.start()

    def head_saves(h):
        own = pl.ds(h * HEAD, HEAD)
        return [
            pltpu.make_async_copy(mixed.at[own], mixed_out.at[own], head_sem.at[h, 0]),
            pltpu.make_async_copy(row_stats.at[h], stats_out.at[h], head_sem.at[h, 1]),
        ]

    def chores(step):
        if step == 0:
            for relation in (2, 5):
                gather.arrive_z(UP_W, relation)
        elif step == 1:
            gather.arrive_x(UP_W, OWN)
            gather.arrive_x(DOWN_W, OWN)
        elif step == 3:
            for relation in (2, 5):
                gather.arrive_z(OUT_W, relation)
                gather.arrive_z(DOWN_W, relation)
        elif step == 4:
            for relation in (1, 4):
                gather.arrive_x(UP_W, relation)
                gather.arrive_y(relation, 0)
            for save in head_saves(0):
                save.start()
        elif step == 5:
            gather.arrive_y(OWN, 1)
        elif step == 6:
            for relation in (3, 6):
                gather.arrive_z(UP_W, relation)
        elif step == 7:
            for relation in (1, 4):
                gather.arrive_x(DOWN_W, relation)
        elif step == 8:
            for relation in (2, 5):
                gather.arrive_x(UP_W, relation)
            for save in head_saves(1):
                save.start()
        elif step == 9:
            for relation in (3, 6):
                gather.arrive_z(OUT_W, relation)
                gather.arrive_z(DOWN_W, relation)
            for relation in (2, 5):
                gather.arrive_y(relation, 0)
        elif step == 10:
            for relation in (2, 5):
                gather.arrive_x(DOWN_W, relation)
        elif step == 11:
            for relation in (3, 6):
                gather.arrive_x(UP_W, relation)
            for relation in (1, 4):
                gather.arrive_y(relation, 1)

    def send_mixed(h, turn, arriving=False):
        member = place.member(turn)
        own = pl.ds(pl.multiple_of(h * HEAD, HEAD), HEAD)
        lanes = pl.ds(pl.multiple_of(member * local_rows, local_rows), local_rows)
        owner = member if arriving else place.s
        there = attended.at[pl.ds(pl.multiple_of(owner * head_cols + h * HEAD, HEAD), HEAD)]
        return remote(
            mixed_low.at[own, lanes], there, mix_send.at[h, turn], mix_recv.at[h, turn], (place.f, member)
        )

    def keep_mixed(h):
        own = pl.ds(pl.multiple_of(h * HEAD, HEAD), HEAD)
        lanes = pl.ds(pl.multiple_of(place.s * local_rows, local_rows), local_rows)
        there = attended.at[pl.ds(pl.multiple_of(place.s * head_cols + h * HEAD, HEAD), HEAD)]
        return pltpu.make_async_copy(mixed_low.at[own, lanes], there, mix_send.at[h, 3])

    turns = slot_rows // local_rows

    def pass_on(index):
        h, turn = index // turns, lax.rem(index, turns)

        @pl.when(turn < turns - 1)
        def _():
            send_mixed(h, turn).start()

        @pl.when(turn == turns - 1)
        def _():
            keep_mixed(h).start()

    def step(index, carry):
        for when in range(12):
            pl.when(index == when)(lambda when=when: chores(when))
        h, turn = index // turns, lax.rem(index, turns)
        start = pl.multiple_of(place.member(turn) * local_rows, local_rows)
        attend_block(h, pl.ds(start, local_rows), q_x, k_wide, v_x, mixed, mixed_low, row_stats)

        @pl.when(index > 0)
        def _():
            pass_on(index - 1)

        return carry

    lax.fori_loop(0, heads * turns, step, 0)
    pass_on(heads * turns - 1)
    for save in head_saves(2):
        save.start()
    for relation in (3, 6):
        gather.arrive_x(DOWN_W, relation)
    for relation in (2, 5):
        gather.arrive_y(relation, 1)
    for column in range(2):
        for relation in (3, 6):
            gather.arrive_y(relation, column)
    for array in (UP_W, OUT_W, DOWN_W, QKV_W):
        gather.finish(array)
    for copy in own_copies()[:2]:
        copy.wait()
    for half in range(halves):
        for index in range(2):
            send_rows(half, index).wait_send()
        pass_rows(half, False).wait_send()
    for h in range(heads):
        for turn in range(turns - 1):
            send_mixed(h, turn).wait_send()
            send_mixed(h, turn, True).wait_recv()
        keep_mixed(h).wait()
        for save in head_saves(h):
            save.wait()
    for save in saves():
        save.wait()


def front(lengths, tokens, read_rows, write_rows, qkv_shard, vectors, up_weight, down_weight, out_weight):
    local_rows, width = tokens.shape
    slot_rows = local_rows * 4
    head_cols = width // 4
    heads = head_cols // HEAD
    shard = width // 8
    vmem = pl.BlockSpec(memory_space=pltpu.VMEM)
    anywhere = pl.BlockSpec(memory_space=pl.ANY)
    dma = pltpu.SemaphoreType.DMA
    hidden = up_weight.shape[1]

    def held(*shape, kind=low):
        return pltpu.VMEM(shape, kind)

    def shaped(*shape, kind=low):
        return jax.ShapeDtypeStruct(shape, kind)

    return pl.pallas_call(
        front_kernel,
        in_specs=[pl.BlockSpec(memory_space=pltpu.SMEM)] + [vmem] * 8,
        out_specs=[vmem] * 2 + [anywhere] * 12,
        out_shape=[
            shaped(8, width, kind=full), shaped(8, hidden, kind=full),
            shaped(slot_rows, width), shaped(width, 3 * head_cols), shaped(heads, HEAD, slot_rows),
            shaped(head_cols, slot_rows), shaped(heads, slot_rows, WIDE), shaped(heads, slot_rows, WIDE),
            shaped(head_cols, slot_rows, kind=full), shaped(heads, 8, slot_rows, kind=full),
            shaped(width, hidden), shaped(hidden, width), shaped(width, width), shaped(width, local_rows),
        ],
        scratch_shapes=[
            held(slot_rows, width), held(width, 3 * head_cols), held(8, shard, 3 * head_cols + HEAD),
            held(32, width), held(heads, WIDE, slot_rows), held(head_cols, slot_rows),
            held(heads, slot_rows, WIDE), held(heads, slot_rows, WIDE), held(heads, WIDE, slot_rows),
            held(head_cols, slot_rows, kind=full), held(head_cols, slot_rows), held(heads, 8, slot_rows, kind=full),
            dma((2, 2)), dma((2, 2)), dma((2,)), dma((2,)), dma((heads, 4)), dma((heads, 4)), dma((3,)),
            dma((5 + heads,)), dma((heads, 2)),
            dma((4, 2, 3)), dma((4, 2, 3)), dma((4, 7)), dma((4, 7)), dma((3, 7, 2)), dma((3, 7, 2)),
            dma((7, 2)), dma((7, 2)), dma((7, 2)), dma((7, 2)),
        ],
        compiler_params=pltpu.CompilerParams(
            vmem_limit_bytes=VMEM_BYTES, collective_id=0, has_side_effects=True
        ),
        name="front",
    )(lengths, tokens, read_rows, write_rows, qkv_shard, vectors, up_weight, down_weight, out_weight)


DW_FIRST = 3
LINES = (3, 0, 2, 1)


def add_low(left, right):
    return (left.astype(full) + right.astype(full)).astype(low)


class Reduce:
    def __init__(self, place, given, sums, from_y, from_x, from_z, sems):
        self.place, self.given, self.sums = place, given, sums
        self.from_y, self.from_x, self.from_z = from_y, from_x, from_z
        self.last = max(sums)
        self.y_send, self.y_recv, self.x_send, self.x_recv, self.z_send, self.z_recv = sems

    def dest(self, column, line):
        x = self.place.x
        return 2 * line + (x if column == 0 else 1 - x)

    def slot(self, array, line, column=0):
        if array >= DW_FIRST:
            rows = 4 * HEAD if array == self.last else 3 * HEAD
            return self.sums[array].at[self.dest(column, line), pl.ds(0, rows // 4)]
        return self.sums[array].at[line]

    def cut(self, array, ref):
        if DW_FIRST <= array < self.last:
            return ref.at[pl.ds(0, 3 * HEAD // 4)]
        return ref

    def load(self, array, column, line, sem):
        source = self.given[array]
        if array == OUT_W:
            return pltpu.make_async_copy(source.at[line], self.sums[array].at[line], sem)
        source = source.at[column, line, 0] if array == DOWN_W else source.at[column, line]
        return pltpu.make_async_copy(source, self.sums[array].at[line], sem)

    def over_y(self, line):
        return remote(
            self.given[DOWN_W].at[0, line, 1], self.from_y.at[line], self.y_send.at[line], self.y_recv.at[line],
            self.place.across_y,
        )

    def add_y(self, line):
        self.over_y(line).wait_recv()
        slot = self.slot(DOWN_W, line)
        slot[...] = add_low(slot[...], self.from_y[line])

    def over_x(self, array, line):
        if array == OUT_W:
            here = self.sums[array].at[self.place.z]
            return remote(
                here.at[1], self.from_x[array], self.x_send.at[array, 0], self.x_recv.at[array, 0], self.place.across_x
            )
        if array == UP_W:
            start = self.given[array].at[1, line]
        elif array == DOWN_W:
            start = self.given[array].at[1, line, 0]
        else:
            start = self.slot(array, line, 1)
        return remote(
            start, self.cut(array, self.from_x[array].at[line]), self.x_send.at[array, line],
            self.x_recv.at[array, line], self.place.across_x,
        )

    def add_x(self, array, line):
        self.over_x(array, line).wait_recv()
        slot = self.sums[array].at[self.place.z, 0] if array == OUT_W else self.slot(array, line)
        came = self.from_x[array] if array == OUT_W else self.cut(array, self.from_x[array].at[line])
        slot[...] = add_low(slot[...], came[...])

    def along_z(self, array, way, line):
        return remote(
            self.slot(array, line), self.cut(array, self.from_z[array].at[way, line]),
            self.z_send.at[array, way, line], self.z_recv.at[array, way, line],
            self.place.above if way == 0 else self.place.below,
        )

    def add_z(self, array, way, line):
        self.along_z(array, way, line).wait_recv()
        slot = self.slot(array, line)
        slot[...] = add_low(slot[...], self.cut(array, self.from_z[array].at[way, line])[...])

    def hop(self, array, level, lines=(0, 1, 2, 3)):
        @pl.when(self.place.z == level)
        def _():
            for line in range(3, level, -1):
                if line in lines:
                    if level > 0:
                        self.add_z(array, 0, line)
                    self.along_z(array, 0, line).start()

        @pl.when(self.place.z == 3 - level)
        def _():
            for line in range(0, 3 - level):
                if line in lines:
                    if level > 0:
                        self.add_z(array, 1, line)
                    self.along_z(array, 1, line).start()

    def to_line(self, array, line):
        where = (2 * line + self.place.x, self.place.s)
        return remote(
            self.slot(array, line), self.cut(array, self.from_z[array].at[self.place.z]),
            self.z_send.at[array, 0, line], self.z_recv.at[array, 0, self.place.z], where,
        )

    def fling(self, array, lines=LINES):
        for line in lines:
            pl.when(self.place.z != line)(lambda line=line: self.to_line(array, line).start())

    def settle(self, array):
        if array >= DOWN_W:
            slot = self.slot(array, self.place.z)
            for line in range(4):

                @pl.when(self.place.z != line)
                def _(line=line):
                    came = self.cut(array, self.from_z[array].at[line])
                    remote(
                        came, came, self.z_send.at[array, 0, line], self.z_recv.at[array, 0, line], self.place.core
                    ).wait_recv()
                    slot[...] = add_low(slot[...], came[...])

            return
        for line in range(4):

            @pl.when(self.place.z == line)
            def _(line=line):
                if line > 0:
                    self.add_z(array, 0, line)
                if line < 3:
                    self.add_z(array, 1, line)

    def finish(self, array):
        for line in range(4):
            if array != OUT_W or line == 0:
                self.over_x(array, line).wait_send()
            if array >= DOWN_W:
                pl.when(self.place.z != line)(lambda line=line: self.to_line(array, line).wait_send())
            else:
                pl.when(self.place.z < line)(lambda line=line: self.along_z(array, 0, line).wait_send())
                pl.when(self.place.z > line)(lambda line=line: self.along_z(array, 1, line).wait_send())
            if array == DOWN_W:
                self.over_y(line).wait_send()


class Spread:
    def __init__(self, place, blocks, source, send, recv):
        self.place, self.blocks, self.source, self.send, self.recv = place, blocks, source, send, recv
        self.near = 2 * place.y + 1 - place.c
        self.far = 2 * (1 - place.y) + place.c
        self.last = 2 * (1 - place.y) + 1 - place.c

    def copy(self, kind, arriving=False):
        place = self.place
        if kind == 2:
            here = self.blocks.at[self.last if arriving else self.far]
            return remote(here, here, self.send.at[2], self.recv.at[2], place.core)
        member = (self.near, self.far)[kind] if arriving else place.s
        return remote(
            self.source, self.blocks.at[member], self.send.at[kind], self.recv.at[kind],
            (place.core, place.across_y)[kind],
        )

    def start(self):
        self.copy(1).start()
        self.copy(0).start()

    def pass_on(self):
        self.copy(1, True).wait_recv()
        self.copy(2).start()

    def finish(self):
        self.blocks[self.place.s] = self.source[...]
        self.copy(0, True).wait_recv()
        self.copy(2, True).wait_recv()
        for kind in range(3):
            self.copy(kind).wait_send()


def back_kernel(
    length_ref, grad_own, vectors_in, q_in, k_in, k_wide_in, v_wide_in, mixed_in, stats_in, rows_in, weight_in, resid_in, up_given, down_given, out_given,
    input_out, read_out, write_out, qkv_out, vector_out, up_out, down_out, out_out,
    q_x, k_t, k_wide, v_wide, mixed, row_stats, grad_t, q_here, do_x, grads, grad_k, grad_v, rows_ref, weight_ref, resid_ref,
    up_sum, out_sum, down_sum, dw, down_y, up_x, out_x, down_x, dw_x, up_z, out_z, down_z, dw_z,
    up_last, out_last, up_other, out_other, down_all, dw_all,
    near_send, near_recv, far_sum, far_recv, memory_all, memory_own,
    mix_send, mix_recv, local_sem, saved_sem, mine_sem, share_send, share_recv, near_s, near_r, far_s, far_r,
    *sems,
):
    place = Place()
    heads, _, slot_rows = q_in.shape
    width, local_rows = grad_own.shape
    head_cols = heads * HEAD
    last = DW_FIRST + heads - 1
    given = {UP_W: up_given, OUT_W: out_given, DOWN_W: down_given}
    sums = {UP_W: up_sum, OUT_W: out_sum, DOWN_W: down_sum}
    from_x = {UP_W: up_x, OUT_W: out_x, DOWN_W: down_x}
    from_z = {UP_W: up_z, OUT_W: out_z, DOWN_W: down_z}
    for h in range(heads):
        sums[DW_FIRST + h], from_x[DW_FIRST + h] = dw.at[h], dw_x.at[h]
        from_z[DW_FIRST + h] = dw_z.at[h]
    reduce = Reduce(place, given, sums, down_y, from_x, from_z, sems)
    greet(place, True)

    peers = (place.across_y, place.diagonal, place.core)

    def member_rows(turn):
        member = place.member(turn)
        return member, pl.ds(pl.multiple_of(member * local_rows, local_rows), local_rows)

    def send_grad(turn, arriving=False):
        member, lanes = member_rows(turn)
        own_lanes = pl.ds(pl.multiple_of(place.s * local_rows, local_rows), local_rows)
        src = grad_own.at[pl.ds(pl.multiple_of(member * head_cols, head_cols), head_cols)]
        return remote(
            src, grad_t.at[:, lanes if arriving else own_lanes], mix_send.at[turn], mix_recv.at[turn], peers[turn]
        )

    def saved_loads(h):
        own = pl.ds(h * HEAD, HEAD)
        pairs = (
            (k_wide_in.at[h], k_wide.at[h]), (q_in.at[h], q_x.at[h]), (v_wide_in.at[h], v_wide.at[h]),
            (mixed_in.at[own], mixed.at[own]), (stats_in.at[h], row_stats.at[h]), (k_in.at[own], k_t.at[own]),
        )
        return [pltpu.make_async_copy(src, dst, saved_sem.at[h, i]) for i, (src, dst) in enumerate(pairs)]

    def sum_loads(array):
        return [reduce.load(array, 0, line, mine_sem.at[array, line]) for line in LINES]

    for turn in range(3):
        send_grad(turn).start()
    for load in sum_loads(OUT_W):
        load.start()
    for load in saved_loads(0):
        load.start()
    loads = []
    for index, (src, dst) in enumerate(((rows_in, rows_ref), (weight_in, weight_ref), (resid_in, resid_ref))):
        loads.append(pltpu.make_async_copy(src, dst, local_sem.at[index]))

    def send_x(array, lines=LINES):
        for line in lines:
            reduce.over_x(array, line).start()

    send_x(UP_W)
    for line in LINES:
        reduce.over_y(line).start()
    send_x(DOWN_W)
    for array in (UP_W, DOWN_W):
        for load in sum_loads(array):
            load.start()
    for load in loads:
        load.start()

    for h in range(1, heads):
        for load in saved_loads(h):
            load.start()

    own_lanes = pl.ds(pl.multiple_of(place.s * local_rows, local_rows), local_rows)
    grad_t[:, own_lanes] = grad_own[pl.ds(pl.multiple_of(place.s * head_cols, head_cols), head_cols), :]

    def take_x(array, lines=LINES):
        for line in lines:
            reduce.add_x(array, line)

    turns = slot_rows // local_rows

    def weight_part(h):
        if h == 0:
            loads[0].wait()
        base = 3 * h * HEAD
        part = jnp.transpose(mul(grads[base : base + 3 * HEAD, :], rows_ref[...])).astype(low)
        half = width // 16
        for dest in range(8):
            start = 2 * half * dest
            dw[h, dest, :half, :] = jnp.concatenate(
                [part[start : start + half], part[start + half : start + 2 * half]], axis=1
            )
            if h == heads - 1:
                dw[h, dest, half:, :] = vectors_in[dest].astype(low)
        if h == heads - 1:
            total = jnp.sum(grads[...].astype(full), axis=1, keepdims=True)
            spread = jnp.transpose(jnp.broadcast_to(total, (total.shape[0], WIDE)))[0:1]
            for kind, first_dest in ((0, 0), (2, 4)):
                for head in range(heads):
                    start = (3 * head + kind) * HEAD
                    dw[h, first_dest + place.s, half : half + 1, head * HEAD : (head + 1) * HEAD] = spread[
                        :, start : start + HEAD
                    ].astype(low)
        send_x(DW_FIRST + h)

    share = {UP_W: (up_last, up_other), OUT_W: (out_last, out_other)}

    def settled(array):
        return sums[array].at[place.z, 0] if array == OUT_W else sums[array].at[place.z]

    def sum_y(array):
        mine_now = settled(array)
        return remote(mine_now, share[array][0], share_send.at[array, 0], share_recv.at[array, 0], place.across_y)

    def half_to_core(array):
        mine_now = settled(array)
        return remote(mine_now, share[array][1], share_send.at[array, 1], share_recv.at[array, 1], place.core)

    def spread_of(array):
        if array == DOWN_W:
            return Spread(place, down_all, down_sum.at[place.z], share_send.at[2], share_recv.at[2])
        h = array - DW_FIRST
        return Spread(
            place, dw_all.at[h, :, pl.ds(0, reduce.slot(array, 0).shape[0])], reduce.slot(array, place.z),
            share_send.at[array], share_recv.at[array],
        )

    def add_last(array):
        sum_y(array).wait()
        slot = settled(array)
        slot[...] = add_low(slot[...], share[array][0][...])
        half_to_core(array).start()

    first, second = DW_FIRST, DW_FIRST + 1

    def chores(index):
        if index == 1:
            send_grad(2, True).wait_recv()
        elif index == 2:
            send_grad(1, True).wait_recv()
            for array in (UP_W, DOWN_W):
                for load in sum_loads(array):
                    load.wait()
            take_x(UP_W, (3,))
            reduce.hop(UP_W, 0, (3,))
            reduce.hop(OUT_W, 1, (3, 0))
        elif index == 3:
            send_grad(0, True).wait_recv()
            reduce.hop(OUT_W, 1, (2, 1))
        elif index == 4:
            for load in saved_loads(1):
                load.wait()
            weight_part(0)
            take_x(UP_W, (0,))
            reduce.hop(UP_W, 0, (0,))
            reduce.hop(OUT_W, 2)
        elif index == 5:
            reduce.hop(UP_W, 1, (3,))
        elif index == 6:
            for line in LINES:
                reduce.add_y(line)
            take_x(UP_W, (2,))
            reduce.hop(UP_W, 0, (2,))
            reduce.settle(OUT_W)
            reduce.over_x(OUT_W, 0).start()
        elif index == 7:
            reduce.hop(UP_W, 1, (0,))
            take_x(UP_W, (1,))
            reduce.hop(UP_W, 0, (1,))
        elif index == 8:
            for load in saved_loads(2):
                load.wait()
            weight_part(1)
            reduce.hop(UP_W, 2, (3,))
        elif index == 9:
            reduce.hop(UP_W, 2, (0,))
            reduce.hop(UP_W, 1, (2, 1))
            take_x(DOWN_W, (3, 0))
            reduce.fling(DOWN_W, (3, 0))
        elif index == 10:
            take_x(DOWN_W, (2,))
            reduce.fling(DOWN_W, (2,))
        elif index == 11:
            take_x(DOWN_W, (1,))
            reduce.fling(DOWN_W, (1,))
            reduce.settle(UP_W)
            sum_y(UP_W).start()

    def step(index, carry):
        for when in range(1, 12):
            pl.when(index == when)(lambda when=when: chores(when))
        h, turn = index // turns, lax.rem(index, turns)
        _, lanes = member_rows(turns - 1 - turn)
        attend_back(
            h, lanes, q_x, q_here, do_x, grad_t, mixed, row_stats, k_t, k_wide, v_wide, grads, grad_k, grad_v, turn == 0
        )

        @pl.when(turn == turns - 1)
        def _():
            base = pl.multiple_of(3 * h * HEAD, HEAD)
            grads[pl.ds(base + HEAD, HEAD), :] = grad_k[...].astype(low)
            grads[pl.ds(base + 2 * HEAD, HEAD), :] = grad_v[...].astype(low)

        return carry

    for load in sum_loads(OUT_W):
        load.wait()
    reduce.hop(OUT_W, 0)
    for load in saved_loads(0):
        load.wait()
    lax.fori_loop(0, heads * turns, step, 0)

    weight_part(heads - 1)
    loads[1].wait()
    loads[2].wait()

    halves, part = 2, local_rows // 2
    length = length_ref[0]

    def memory_pick(rows, start):
        line = lax.broadcasted_iota(jnp.int32, (32, rows), 0)
        row = start + lax.broadcasted_iota(jnp.int32, (32, rows), 1)
        wanted = jnp.where(line < 16, line, length - MEM + line - 16)
        used = (line < MEM) | ((line >= 16) & (line < 16 + MEM))
        return jnp.where(used & (wanted == row), 1.0, 0.0).astype(low)

    def part_for(turn, half):
        start = pl.multiple_of(place.member(turn) * local_rows + half * part, part)
        return mul(grads[:, pl.ds(start, part)], weight_ref[...], TT)

    def share_near(index, half):
        rows = pl.ds(half * part, part)
        return remote(
            near_send.at[index, rows], near_recv.at[index, rows], near_s.at[index, half], near_r.at[index, half],
            place.core,
        )

    def share_far(half):
        rows = pl.ds(half * part, part)
        return remote(far_sum.at[rows], far_recv.at[rows], far_s.at[half], far_r.at[half], place.across_y)

    for half in range(halves):
        rows = slice(half * part, (half + 1) * part)
        near_send[0, rows, :] = part_for(1, half).astype(low)
        share_near(0, half).start()
        far_sum[rows, :] = part_for(0, half).astype(low)
        if half == 0:
            taken = mul(memory_pick(slot_rows, 0), grads[...], NT).astype(low)
            own_part = mul(memory_pick(local_rows, place.s * local_rows), resid_ref[...].astype(low))
            memory_own[...] = (mul(taken, weight_ref[...], NT) + own_part).astype(low)
        share_near(0, half).wait_recv()
        far_sum[rows, :] = add_low(far_sum[rows, :], near_recv[0, rows, :])
        share_far(half).start()
    memory = Spread(place, memory_all, memory_own, share_send.at[DW_FIRST + heads], share_recv.at[DW_FIRST + heads])
    memory.start()
    take_x(first)
    reduce.fling(first)
    reduce.add_x(OUT_W, 0)
    sum_y(OUT_W).start()
    for half in range(halves):
        rows = slice(half * part, (half + 1) * part)
        near_send[1, rows, :] = part_for(2, half).astype(low)
        share_near(1, half).start()
    take_x(second)
    reduce.fling(second)
    reduce.settle(DOWN_W)
    spread_of(DOWN_W).start()
    take_x(last)
    reduce.fling(last)
    add_last(UP_W)
    for half in range(halves):
        resid_ref[half * part : (half + 1) * part, :] += part_for(3, half)
    for array in (first, second, last):
        reduce.settle(array)
        spread_of(array).start()
    add_last(OUT_W)
    memory.pass_on()
    for h in (heads - 1, 0, 1):
        spread_of(DW_FIRST + h).pass_on()
    spread_of(DOWN_W).pass_on()
    for array, out in ((UP_W, up_out), (OUT_W, out_out)):
        columns = out.shape[1] // 2
        out[:, pl.ds(pl.multiple_of(place.c * columns, columns), columns)] = settled(array)[...]
        half_to_core(array).wait()
        out[:, pl.ds(pl.multiple_of((1 - place.c) * columns, columns), columns)] = share[array][1][...]
    for h in range(heads):
        spread_of(DW_FIRST + h).finish()
    spread_of(DOWN_W).finish()
    quarter = down_out.shape[0] // 4
    for member in range(4):
        down_out[member * quarter : (member + 1) * quarter, :] = down_all[member]
    half = qkv_out.shape[0] // 2
    for kind in range(3):
        for member in range(4):
            for h in range(heads):
                start = kind * width + (member * heads + h) * HEAD
                for side in range(2):
                    lanes = (3 * side + kind) * HEAD
                    qkv_out[side * half : (side + 1) * half, start : start + HEAD] = dw_all[
                        h, member, :half, lanes : lanes + HEAD
                    ]
    vector_sum = dw_all[heads - 1, 0, half:, :].astype(full)
    for member in range(1, 4):
        vector_sum = vector_sum + dw_all[heads - 1, member, half:, :].astype(full)
    vector_out[...] = vector_sum
    memory.finish()
    total = memory_all[0].astype(full)
    for member in range(1, 4):
        total = total + memory_all[member].astype(full)
    read_out[...] = total[:MEM]
    write_out[...] = total[16 : 16 + MEM]
    for half in range(halves):
        rows = slice(half * part, (half + 1) * part)
        share_near(1, half).wait_recv()
        share_far(half).wait_recv()
        grad_layer = resid_ref[rows, :] + near_recv[1, rows, :].astype(full) + far_recv[rows, :].astype(full)
        rows_at = place.s * local_rows + half * part + lax.broadcasted_iota(jnp.int32, (part, 1), 0)
        in_write = (rows_at >= length - MEM) & (rows_at < length)
        input_out[rows, :] = jnp.where((rows_at < MEM) | in_write, 0.0, grad_layer)
    for array in range(DW_FIRST + heads):
        reduce.finish(array)
    for turn in range(3):
        send_grad(turn).wait_send()
    for half in range(halves):
        for index in range(2):
            share_near(index, half).wait_send()
        share_far(half).wait_send()


def back(lengths, grad_own, saved, vectors, rows, weight, resid, up_given, down_given, out_given):
    q_x, k_t, k_wide, v_wide, mixed, row_stats = saved
    heads, _, slot_rows = q_x.shape
    width, local_rows = grad_own.shape
    hidden = 2 * up_given.shape[3]
    shard, head_cols = width // 8, heads * HEAD
    half, small, piece = hidden // 2, width // 2, hidden // 32
    vmem = pl.BlockSpec(memory_space=pltpu.VMEM)
    anywhere = pl.BlockSpec(memory_space=pl.ANY)
    dma = pltpu.SemaphoreType.DMA
    arrays = DW_FIRST + heads

    def held(*shape, kind=low):
        return pltpu.VMEM(shape, kind)

    tall = (shard // 2 + 16, 6 * HEAD)
    return pl.pallas_call(
        back_kernel,
        in_specs=[pl.BlockSpec(memory_space=pltpu.SMEM)] + [vmem] * 2 + [anywhere] * 12,
        out_specs=[vmem] * 8,
        out_shape=[
            jax.ShapeDtypeStruct((local_rows, width), full),
            jax.ShapeDtypeStruct((MEM, width), full),
            jax.ShapeDtypeStruct((MEM, width), full),
            jax.ShapeDtypeStruct((shard, 3 * width), low),
            jax.ShapeDtypeStruct((16, 6 * HEAD), full),
            jax.ShapeDtypeStruct((shard, hidden), low),
            jax.ShapeDtypeStruct((hidden // 8, width), low),
            jax.ShapeDtypeStruct((shard, width), low),
        ],
        scratch_shapes=[
            held(heads, HEAD, slot_rows), held(head_cols, slot_rows), held(heads, slot_rows, WIDE),
            held(heads, slot_rows, WIDE), held(head_cols, slot_rows, kind=full), held(heads, 8, slot_rows, kind=full),
            held(head_cols, slot_rows), held(WIDE, local_rows), held(WIDE, local_rows), held(3 * head_cols, slot_rows),
            held(HEAD, slot_rows, kind=full), held(HEAD, slot_rows, kind=full),
            held(slot_rows, width), held(width, 3 * head_cols), held(local_rows, width, kind=full),
            held(4, shard, half), held(4, 2, shard, small), held(4, piece, width),
            held(heads, 8, *tall), held(4, piece, width),
            held(4, shard, half), held(shard, small), held(4, piece, width), held(heads, 4, *tall),
            held(2, 4, shard, half), held(2, 4, 2, shard, small), held(4, piece, width), held(heads, 4, *tall),
            held(shard, half), held(shard, small), held(shard, half), held(shard, small),
            held(4, piece, width), held(heads, 4, *tall),
            held(2, local_rows, width), held(2, local_rows, width), held(local_rows, width),
            held(local_rows, width), held(4, 32, width), held(32, width),
            dma((3,)), dma((3,)), dma((3,)), dma((heads, 6)), dma((3, 4)), dma((arrays + 1, 3)),
            dma((arrays + 1, 3)), dma((2, 2)), dma((2, 2)), dma((2,)), dma((2,)),
            dma((4,)), dma((4,)), dma((arrays, 4)), dma((arrays, 4)),
            dma((arrays, 2, 4)), dma((arrays, 2, 4)),
        ],
        compiler_params=pltpu.CompilerParams(
            vmem_limit_bytes=VMEM_BYTES, collective_id=1, has_side_effects=True
        ),
        name="back",
    )(
        lengths, grad_own, vectors, q_x, k_t, k_wide, v_wide, mixed, row_stats, rows, weight, resid,
        up_given, down_given, out_given,
    )


def phi_parts(value):
    normal = 0.5 * (1.0 + lax.erf(value * (0.5**0.5)))
    density = jnp.exp(-0.5 * value * value) * (0.5 * 2.0**0.5 * 3.141592653589793**-0.5)
    return normal, normal + value * density


def statistics(values):
    centre = values - jnp.mean(values, axis=1, keepdims=True)
    factor = lax.rsqrt(jnp.mean(centre * centre, axis=1, keepdims=True) + norm_epsilon)
    return centre * factor, factor


def norm_back(grad, gain, normed, factor):
    scaled = grad * gain
    first = jnp.mean(scaled, axis=1, keepdims=True)
    second = jnp.mean(scaled * normed, axis=1, keepdims=True)
    return factor * (scaled - first - normed * second)


def column_total(values):
    return jnp.sum(values, axis=0, keepdims=True)


def middle_kernel(
    length_ref, cotangent, small, up_bias, rows_in, attended_in, up_in, down_in, out_in,
    output, resid_out, grad_own, vector_out, up_out, down_out, out_out,
    layer_in, attended, up_w, down_w, out_w, hidden, slope, normed_one, middle_low, grad_down,
    grad_two, grad_mid, totals, up_total, up_grad, down_grad, out_grad, up_sum, down_sum, out_sum,
    from_y, load_sem, save_sem, c_send, c_recv, y_send, y_recv,
):
    place = Place()
    rows, width = cotangent.shape
    ff = up_w.shape[1]
    chunk = ff // 4
    shard = width // 8
    barrier = pltpu.get_barrier_semaphore()
    for where in (place.core, place.across_y):
        pl.semaphore_signal(barrier, inc=1, device_id=where, device_id_type=MESH)

    def chunk_lanes(j):
        return pl.ds(pl.multiple_of(j * chunk, chunk), chunk)

    def up_load(j):
        return pltpu.make_async_copy(up_in.at[:, chunk_lanes(j)], up_w.at[:, chunk_lanes(j)], load_sem.at[j])

    def down_load(j):
        return pltpu.make_async_copy(down_in.at[chunk_lanes(j)], down_w.at[chunk_lanes(j)], load_sem.at[4 + j])

    first_loads = [
        pltpu.make_async_copy(
            rows_in.at[pl.ds(pl.multiple_of(place.s * rows, rows), rows)], layer_in, load_sem.at[8]
        ),
        pltpu.make_async_copy(attended_in, attended, load_sem.at[9]),
        pltpu.make_async_copy(out_in, out_w, load_sem.at[10]),
    ]
    for load in first_loads:
        load.start()
    for j in range(4):
        up_load(j).start()
        down_load(j).start()
    out_bias, gain_one, shift_one = small[0:1, :], small[1:2, :], small[2:3, :]
    down_bias, gain_two, shift_two = small[3:4, :], small[4:5, :], small[5:6, :]
    for load in first_loads:
        load.wait()

    branch = mul(attended[...], out_w[...], TN)
    normed, factor_one = statistics(layer_in[...].astype(full) + branch + out_bias)
    normed_one[...] = normed
    middle_low[...] = (normed * gain_one + shift_one).astype(low)
    grad_mid[...] = jnp.zeros_like(grad_mid)

    def forward_chunk(j, carry):
        up_load(j).wait()
        lanes = chunk_lanes(j)
        value = mul(middle_low[...], up_w[:, lanes]) + up_bias[0:1, lanes]
        normal, slope_here = phi_parts(value)
        hidden[:, lanes] = (value * normal).astype(low)
        slope[:, lanes] = slope_here
        down_load(j).wait()
        grad_mid[...] += mul(hidden[:, lanes], down_w[lanes, :])
        return carry

    lax.fori_loop(0, 4, forward_chunk, 0)
    middle = normed_one[...] * gain_one + shift_one
    normed_two, factor_two = statistics(middle + grad_mid[...] + down_bias)
    places = place.s * rows + lax.broadcasted_iota(jnp.int32, (rows, 1), 0)
    in_slot = places < length_ref[0]
    output[...] = jnp.where(in_slot, normed_two * gain_two + shift_two, 0.0).astype(low)
    grad_final = jnp.where(in_slot, cotangent[...].astype(full), 0.0)
    totals[4:5, :] = column_total(grad_final * normed_two)
    totals[5:6, :] = column_total(grad_final)
    grad_resid = norm_back(grad_final, gain_two, normed_two, factor_two)
    grad_two[...] = grad_resid
    grad_down[...] = grad_resid.astype(low)
    totals[3:4, :] = column_total(grad_down[...].astype(full))
    pl.semaphore_wait(barrier, 2)

    def down_piece(ref, line, column, far, core):
        dest = 2 * line + (place.x if column == 0 else 1 - place.x)
        y = place.y if far == 0 else 1 - place.y
        return ref.at[pl.ds(pl.multiple_of(dest * 4 * shard + (2 * y + core) * shard, shard), shard)]

    def side_piece(ref, line, column, core):
        dest = 2 * line + (place.x if column == 0 else 1 - place.x)
        half = ref.shape[1] // 2
        return ref.at[
            pl.ds(pl.multiple_of(dest * shard, shard), shard), pl.ds(pl.multiple_of(core * half, half), half)
        ]

    def down_share(line, column, far):
        return remote(
            down_piece(down_grad, line, column, far, 1 - place.c), down_sum.at[column, line, far],
            c_send.at[2 + far, column, line], c_recv.at[2 + far, column, line], place.core,
        )

    def side_slot(array, line, column):
        return out_sum.at[line, column] if array == 1 else up_sum.at[column, line]

    def over_y(line):
        return remote(down_sum.at[1, line, 1], from_y.at[line], y_send.at[line], y_recv.at[line], place.across_y)

    def side_share(array, line, column):
        grad = (up_grad, out_grad)[array]
        return remote(
            side_piece(grad, line, column, 1 - place.c), side_slot(array, line, column),
            c_send.at[array, column, line], c_recv.at[array, column, line], place.core,
        )

    def down_save(column, line):
        return pltpu.make_async_copy(down_sum.at[column, line], down_out.at[column, line], save_sem.at[2, column, line])

    def side_save(array, column, line):
        out = out_out.at[line, column] if array == 1 else up_out.at[column, line]
        return pltpu.make_async_copy(side_slot(array, line, column), out, save_sem.at[array, column, line])

    def add_far(column, line):
        down_share(line, column, 1).wait_recv()
        down_sum[column, line, 1] = add_low(
            down_sum[column, line, 1], down_piece(down_grad, line, column, 1, place.c)[...]
        )

    def down_chunk(line, carry):
        lanes = chunk_lanes(line)
        down_grad[lanes, :] = mul(hidden[:, lanes], grad_down[...], TN).astype(low)
        for column in range(2):
            for far in range(2):
                down_share(line, column, far).start()
        return carry

    lax.fori_loop(0, 4, down_chunk, 0)
    grad_mid[...] = grad_two[...]

    def back_chunk(turn, carry):
        j = lax.rem(2 * (1 - place.c) + turn, 4)
        lanes = chunk_lanes(j)
        grad_up = (mul(grad_down[...], down_w[lanes, :], NT) * slope[:, lanes]).astype(low)
        up_total[0:1, lanes] = column_total(grad_up.astype(full))
        up_grad[:, lanes] = mul(middle_low[...], grad_up, TN).astype(low)
        grad_mid[...] += mul(grad_up, up_w[:, lanes], NT)

        @pl.when(turn == 0)
        def _():
            for line in LINES:
                add_far(1, line)
                over_y(line).start()

        @pl.when(turn == 1)
        def _():
            for column in (1, 0):
                for line in LINES:
                    side_share(0, line, column).start()

        return carry

    lax.fori_loop(0, 4, back_chunk, 0)
    grad_middle = grad_mid[...]
    normed = normed_one[...]
    totals[1:2, :] = column_total(grad_middle * normed)
    totals[2:3, :] = column_total(grad_middle)
    grad_one = norm_back(grad_middle, gain_one, normed, factor_one)
    resid_out[...] = grad_one
    grad_branch = grad_one.astype(low)
    totals[0:1, :] = column_total(grad_branch.astype(full))
    out_grad[...] = mul(attended[...], grad_branch).astype(low)
    for column in (1, 0):
        for line in LINES:
            side_share(1, line, column).start()
    grad_own[...] = mul(out_w[...], grad_branch, NT).astype(low)

    def add_down(column, line):
        down_share(line, column, 0).wait_recv()
        down_sum[column, line, 0] = add_low(
            down_sum[column, line, 0], down_piece(down_grad, line, column, 0, place.c)[...]
        )
        if column == 0:
            add_far(column, line)
        else:
            over_y(line).wait()
            down_sum[column, line, 0] = add_low(down_sum[column, line, 0], from_y[line])
        down_save(column, line).start()

    def add_side(array, column, line):
        slot = side_slot(array, line, column)
        side_share(array, line, column).wait_recv()
        slot[...] = add_low(slot[...], side_piece((up_grad, out_grad)[array], line, column, place.c)[...])
        side_save(array, column, line).start()

    for line in LINES:
        add_down(0, line)
    for column in (1, 0):
        for line in LINES:
            add_side(0, column, line)
    vector_out[...] = jnp.zeros_like(vector_out)
    for dest in range(8):
        for index, (line, start) in enumerate(((0, 2), (0, 3), (1, 0), (2, 1), (2, 2), (2, 3))):
            vector_out[dest, line : line + 1, start * shard : (start + 1) * shard] = totals[
                index : index + 1, dest * shard : (dest + 1) * shard
            ]
        base = dest * 4 * shard
        vector_out[dest, 1:2, shard:] = up_total[0:1, base : base + 3 * shard]
        vector_out[dest, 2:3, :shard] = up_total[0:1, base + 3 * shard : base + 4 * shard]
    for column in range(2):
        for line in range(4):
            add_side(1, column, line)
    for line in LINES:
        add_down(1, line)
    for column in range(2):
        for line in range(4):
            for array in range(2):
                side_share(array, line, column).wait_send()
                side_save(array, column, line).wait()
            for far in range(2):
                down_share(line, column, far).wait_send()
            down_save(column, line).wait()


def middle_part(lengths, cotangent, small, up_bias, rows_full, attended, up_full, down_full, out_full):
    rows, width = cotangent.shape
    ff = up_full.shape[1]
    shard = width // 8
    vmem = pl.BlockSpec(memory_space=pltpu.VMEM)
    anywhere = pl.BlockSpec(memory_space=pl.ANY)
    dma = pltpu.SemaphoreType.DMA

    def held(*shape, kind=low):
        return pltpu.VMEM(shape, kind)

    def shaped(*shape, kind=low):
        return jax.ShapeDtypeStruct(shape, kind)

    up_parts, down_parts, out_parts = (2, 4, shard, ff // 2), (2, 4, 2, ff // 32, width), (4, 2, shard, width // 2)
    return pl.pallas_call(
        middle_kernel,
        in_specs=[pl.BlockSpec(memory_space=pltpu.SMEM)] + [vmem] * 3 + [anywhere] * 5,
        out_specs=[vmem] * 4 + [anywhere] * 3,
        out_shape=[
            shaped(rows, width), shaped(rows, width, kind=full), shaped(width, rows),
            shaped(8, 16, 4 * shard, kind=full), shaped(*up_parts), shaped(*down_parts), shaped(*out_parts),
        ],
        scratch_shapes=[
            held(rows, width), held(width, rows), held(width, ff), held(ff, width), held(width, width), held(rows, ff), held(rows, ff, kind=full),
            held(rows, width, kind=full), held(rows, width), held(rows, width), held(rows, width, kind=full),
            held(rows, width, kind=full), held(8, width, kind=full), held(8, ff, kind=full),
            held(width, ff), held(ff, width), held(width, width), held(*up_parts), held(*down_parts),
            held(*out_parts), held(4, ff // 32, width), dma((11,)), dma((3, 2, 4)), dma((4, 2, 4)),
            dma((4, 2, 4)), dma((4,)), dma((4,)),
        ],
        compiler_params=pltpu.CompilerParams(
            vmem_limit_bytes=VMEM_BYTES, collective_id=2, has_side_effects=True
        ),
        name="middle",
    )(lengths, cotangent, small, up_bias, rows_full, attended, up_full, down_full, out_full)


def finish_kernel(
    output_in, input_in, qkv_in, vector_in, up_in, down_in, out_in, read_in, write_in,
    output, input_out, read_out, write_out, qkv_out, qv_out, out_out, out_b, gain_one, shift_one, up_out, up_b,
    down_out, down_b, gain_two, shift_two,
):
    shard = qkv_out.shape[0]
    output[...] = output_in[...]
    input_out[...] = input_in[...]
    read_out[...] = read_in[...]
    write_out[...] = write_in[...]
    for given, out in ((qkv_in, qkv_out), (up_in, up_out), (down_in, down_out), (out_in, out_out)):
        out[...] = given[...].astype(full)
    qv_out[...] = vector_in[0:1, : 2 * shard]
    out_b[...] = vector_in[0:1, 2 * shard : 3 * shard]
    gain_one[...] = vector_in[0:1, 3 * shard :]
    shift_one[...] = vector_in[1:2, :shard]
    up_b[:, : 3 * shard] = vector_in[1:2, shard:]
    up_b[:, 3 * shard :] = vector_in[2:3, :shard]
    down_b[...] = vector_in[2:3, shard : 2 * shard]
    gain_two[...] = vector_in[2:3, 2 * shard : 3 * shard]
    shift_two[...] = vector_in[2:3, 3 * shard :]


def finish(output, input_grad, qkv_grad, vectors, up_grad, down_grad, out_grad, grad_read, grad_write):
    shard = qkv_grad.shape[0]

    def shaped(*shape, kind=full):
        return jax.ShapeDtypeStruct(shape, kind)

    line = shaped(1, shard)
    return pl.pallas_call(
        finish_kernel,
        out_shape=[
            shaped(*output.shape, kind=low), shaped(*input_grad.shape), shaped(*grad_read.shape),
            shaped(*grad_write.shape), shaped(*qkv_grad.shape), shaped(1, 2 * shard), shaped(*out_grad.shape),
            line, line, line, shaped(*up_grad.shape), shaped(1, 4 * shard), shaped(*down_grad.shape), line, line, line,
        ],
        compiler_params=pltpu.CompilerParams(vmem_limit_bytes=VMEM_BYTES),
        name="finish",
    )(output, input_grad, qkv_grad, vectors, up_grad, down_grad, out_grad, grad_read, grad_write)


def normalize(values, gain_vec, shift_vec):
    centre = values - jnp.mean(values, axis=-1, keepdims=True)
    factor = lax.rsqrt(jnp.mean(centre * centre, axis=-1, keepdims=True) + norm_epsilon)
    return centre * factor * gain_vec + shift_vec


def column_sums(values):
    return jnp.sum(values, axis=0, dtype=full)


def on_block(
    tokens, read_rows, write_rows, lengths, qkv_weight, vectors, out_weight, up_weight, down_weight, cotangent
):
    total = sum(vector.shape[0] for vector in vectors)
    packed, start = jnp.zeros((1, total), full), 0
    for vector in vectors:
        size = vector.shape[0]
        packed = packed + jnp.pad(vector.astype(full).reshape(1, -1), ((0, 0), (start, total - start - size)))
        start += size
    (small, up_bias, rows, weight, q_t, k_t, k_wide, v_wide, mixed, row_stats, up_full, down_full, out_full,
     attended) = front(
        lengths, tokens, read_rows, write_rows, qkv_weight, packed, up_weight, down_weight, out_weight
    )
    output, resid, grad_own, vector_parts, up_parts, down_parts, out_parts = middle_part(
        lengths, cotangent, small, up_bias, rows, attended, up_full, down_full, out_full
    )
    saved = (q_t, k_t, k_wide, v_wide, mixed, row_stats)
    input_grad, grad_read, grad_write, qkv_grad, vector_sum, up_grad, down_grad, out_grad = back(
        lengths, grad_own, saved, vector_parts, rows, weight, resid, up_parts, down_parts, out_parts
    )
    results = finish(
        output, input_grad, qkv_grad, vector_sum, up_grad, down_grad, out_grad, grad_read, grad_write
    )
    shaped = [result[None] if index in (2, 3) else result for index, result in enumerate(results)]
    return tuple(result.reshape(-1) if result.shape[0] == 1 and result.ndim == 2 else result for result in shaped)


def per_device(
    tokens, read_memory, write_memory, lengths, qkv_weight, qv_bias, out_weight, out_bias, norm1_gain,
    norm1_bias, up_weight, up_bias, down_weight, down_bias, norm2_gain, norm2_bias, cotangent,
):
    seq_count = lax.axis_size("seq")
    fsdp_count = lax.axis_size("fsdp")
    seq_place = lax.axis_index("seq")
    local_rows, width = tokens.shape
    head_cols = width // seq_count
    shard = width // fsdp_count
    length = lengths[0]
    heads = head_cols // HEAD
    vectors = (qv_bias, out_bias, norm1_gain, norm1_bias, up_bias, down_bias, norm2_gain, norm2_bias)
    if (fsdp_count, seq_count) == (8, 4):
        return on_block(
            tokens, read_memory[0], write_memory[0], lengths, qkv_weight, vectors, out_weight, up_weight, down_weight,
            cotangent,
        )
    places = seq_place * local_rows + jnp.arange(local_rows, dtype=jnp.int32)
    in_slot = (places < length)[:, None]
    memory_slots = jnp.arange(MEM, dtype=jnp.int32)
    pick_read = places[:, None] == memory_slots[None, :]
    pick_write = places[:, None] == length - MEM + memory_slots[None, :]
    is_memory = jnp.any(pick_read | pick_write, axis=1)[:, None]
    picks = jnp.concatenate([pick_read, pick_write], axis=1).astype(full)
    memory = jnp.concatenate([read_memory[0], write_memory[0]], axis=0)
    layer_in = jnp.where(is_memory, mul(picks.astype(low), memory).astype(low), tokens)

    own_shard = lax.dynamic_slice_in_dim(
        qkv_weight.reshape(shard, 3, seq_count, heads, HEAD), seq_place, 1, 2
    )
    own_shard = jnp.transpose(own_shard[:, :, 0], (0, 2, 1, 3)).reshape(shard, 3 * head_cols)
    packed = jnp.concatenate(vectors)
    rows = lax.all_gather(layer_in, "seq", axis=0, tiled=True)
    weight = lax.all_gather(own_shard, "fsdp", axis=0, tiled=True)
    packed = lax.all_gather(packed.reshape(1, -1), "fsdp", axis=0, tiled=True).astype(full)
    whole, start = [], 0
    for vector in vectors:
        whole.append(packed[:, start : start + vector.shape[0]].reshape(-1))
        start += vector.shape[0]
    qv_vec, out_vec, gain_one, shift_one, up_vec, down_vec, gain_two, shift_two = whole
    own_qv = lax.dynamic_slice_in_dim(qv_vec.reshape(2, seq_count, head_cols), seq_place, 1, 1)
    bias = jnp.concatenate([own_qv[0, 0], own_qv[1, 0]])
    bias = jnp.broadcast_to(bias, (8, bias.shape[0]))
    out_full = lax.all_gather(out_weight, "fsdp", axis=0, tiled=True)
    up_full = lax.all_gather(up_weight, "fsdp", axis=0, tiled=True)
    down_full = lax.all_gather(down_weight, "fsdp", axis=0, tiled=True)
    q_x, k_t, k_wide, v_wide, mixed, mixed_low, row_stats = attention_forward(lengths, rows, weight, bias)
    attended = lax.all_to_all(mixed_low, "seq", split_axis=1, concat_axis=0, tiled=True)
    resid_one = layer_in.astype(full) + mul(attended, out_full, TN) + out_vec
    middle, norm_one_back = jax.vjp(normalize, resid_one, gain_one, shift_one)
    middle_low = middle.astype(low)
    up_pre = mul(middle_low, up_full) + up_vec
    gelu_out, gelu_back = jax.vjp(partial(jax.nn.gelu, approximate=False), up_pre)
    hidden = gelu_out.astype(low)
    down_pre = mul(hidden, down_full) + down_vec
    final, norm_two_back = jax.vjp(normalize, middle + down_pre, gain_two, shift_two)
    output = jnp.where(in_slot, final, 0.0).astype(low)
    grad_final = jnp.where(in_slot, cotangent.astype(full), 0.0)
    grad_resid_two, grad_gain_two, grad_shift_two = norm_two_back(grad_final)
    grad_down = grad_resid_two.astype(low)
    grad_down_weight = mul(hidden, grad_down, TN)
    (grad_up_pre,) = gelu_back(mul(grad_down, down_full, NT))
    grad_up = grad_up_pre.astype(low)
    grad_up_weight = mul(middle_low, grad_up, TN)
    grad_middle = grad_resid_two + mul(grad_up, up_full, NT)
    grad_resid_one, grad_gain_one, grad_shift_one = norm_one_back(grad_middle)
    grad_branch = grad_resid_one.astype(low)
    grad_out_weight = mul(attended, grad_branch)
    grad_attended = mul(out_full, grad_branch, NT).astype(low)
    vector_grads = [
        column_sums(grad_branch), grad_gain_one, grad_shift_one, column_sums(grad_up),
        column_sums(grad_down), grad_gain_two, grad_shift_two,
    ]
    packed_grad = jnp.concatenate([v.reshape(fsdp_count, -1) for v in vector_grads], axis=1)
    saved = (q_x, k_t, k_wide, v_wide, mixed, row_stats)
    grad_t = lax.all_to_all(grad_attended, "seq", split_axis=0, concat_axis=1, tiled=True)
    partial_in, weight_part, sums = attention_backward(*saved, grad_t, rows, weight)
    from_heads = lax.psum_scatter(partial_in, "seq", scatter_dimension=0, tiled=True).astype(full)
    grad_layer_in = grad_resid_one + from_heads
    input_grad = jnp.where(is_memory, 0.0, grad_layer_in)
    grad_memory = lax.dot_general(
        picks, grad_layer_in, TN, precision=lax.Precision.HIGHEST, preferred_element_type=full
    )
    grad_memory = lax.psum(grad_memory.astype(low), "seq").astype(full)
    grad_read, grad_write = grad_memory[:MEM], grad_memory[MEM:]
    sums = sums[:, 0].reshape(heads, 3, HEAD)
    own_sums = jnp.stack([sums[:, 0].reshape(-1), sums[:, 2].reshape(-1)])[:, None]
    zero_qv = jnp.zeros((2, seq_count, head_cols), full)
    qv_grad = lax.dynamic_update_slice_in_dim(zero_qv, own_sums, seq_place, 1)
    packed_grad = jnp.concatenate([qv_grad.reshape(fsdp_count, -1), packed_grad], axis=1)
    packed_sum = lax.psum(packed_grad, ("fsdp", "seq"))
    own_vectors = lax.dynamic_index_in_dim(packed_sum, lax.axis_index("fsdp"), 0, False)

    def both_axes(part):
        piece = lax.psum_scatter(part.astype(low), "fsdp", scatter_dimension=0, tiled=True)
        return lax.psum(piece, "seq").astype(full)

    qkv_piece = lax.psum_scatter(weight_part, "fsdp", scatter_dimension=0, tiled=True)
    qkv_parts = lax.all_gather(qkv_piece, "seq", axis=0).reshape(seq_count, shard, heads, 3, HEAD)
    qkv_out = jnp.transpose(qkv_parts, (1, 3, 0, 2, 4)).reshape(shard, 3 * width).astype(full)
    up_out, down_out, out_out = both_axes(grad_up_weight), both_axes(grad_down_weight), both_axes(grad_out_weight)
    vector_outs, start = [], 0
    for vector in vectors:
        vector_outs.append(own_vectors[start : start + vector.shape[0]])
        start += vector.shape[0]
    qv_out, out_b_out, gain_one_out, shift_one_out, up_b_out, down_b_out, gain_two_out, shift_two_out = vector_outs
    return (
        output, input_grad, grad_read[None], grad_write[None], qkv_out, qv_out, out_out, out_b_out, gain_one_out,
        shift_one_out, up_out, up_b_out, down_out, down_b_out, gain_two_out, shift_two_out,
    )


def solution(mesh):
    rows, piece = P(("fsdp", "seq"), None), P("fsdp")
    matrix, memory = P("fsdp", None), P("fsdp", None, None)
    in_specs = (
        rows, memory, memory, piece, matrix, piece, matrix, piece, piece, piece, matrix, piece, matrix,
        piece, piece, piece, rows,
    )
    out_specs = (
        rows, rows, memory, memory, matrix, piece, matrix, piece, piece, piece, matrix, piece, matrix,
        piece, piece, piece,
    )
    return jax.shard_map(per_device, mesh=mesh, in_specs=in_specs, out_specs=out_specs, check_vma=False)
```

```python
from functools import partial

import jax
import jax.numpy as jnp
from jax import lax
from jax.experimental import pallas as pl
from jax.experimental.pallas import tpu as pltpu
from jax.sharding import PartitionSpec as P

HEAD = 64
MEM = 10
WIDE = 128
VMEM_BYTES = 64000 * 1024

norm_epsilon = 1e-06
masked_score = -1e30
low = jnp.bfloat16
full = jnp.float32

NN = (((1,), (0,)), ((), ()))
NT = (((1,), (1,)), ((), ()))
TN = (((0,), (0,)), ((), ()))
TT = (((0,), (1,)), ((), ()))


def mul(left, right, dims=NN):
    return lax.dot_general(left, right, dims, preferred_element_type=full)


def three_parts(value):
    high = value.astype(low)
    rest = value - high.astype(full)
    middle = rest.astype(low)
    return high, middle, (rest - middle.astype(full)).astype(low)


def stack_rows(rows, columns):
    place = lax.broadcasted_iota(jnp.int32, (HEAD, columns), 0)
    block = jnp.zeros((HEAD, columns), full)
    for index, row in enumerate(rows):
        block = jnp.where(place == index, row, block)
    return block.astype(low)


def project_block(start, length, rows_ref, weight_ref, bias_q, bias_v, q_x, k_t, v_x, k_wide, v_wide, step):
    head_cols = k_t.shape[0]
    lanes = pl.ds(start, step)
    made = mul(weight_ref[...], rows_ref[lanes, :], TT)
    place = start + lax.broadcasted_iota(jnp.int32, (1, step), 1)
    key_bias = jnp.where(place < length, 0.0, masked_score)
    one = jnp.ones((1, step), full)
    query_extra = stack_rows([one], step)
    key_extra = stack_rows([key_bias, one, one, one], step)
    value_extra = stack_rows([one, one, one], step)
    for h in range(head_cols // HEAD):
        own = slice(h * HEAD, (h + 1) * HEAD)
        base = 3 * h * HEAD
        query = (made[base : base + HEAD] + bias_q[own]).astype(low)
        q_x[h, :HEAD, lanes] = query * jnp.asarray(HEAD**-0.5, low)
        q_x[h, HEAD:, lanes] = query_extra
        k_t[own, lanes] = made[base + HEAD : base + 2 * HEAD].astype(low)
        v_x[h, :HEAD, lanes] = (made[base + 2 * HEAD : base + 3 * HEAD] + bias_v[own]).astype(low)
        v_x[h, HEAD:, lanes] = value_extra
        k_wide[h, lanes, :] = jnp.transpose(jnp.concatenate([k_t[own, lanes], key_extra], axis=0))
        v_wide[h, lanes, :] = jnp.transpose(v_x[h, :, lanes])


def project_heads(length, rows_ref, weight_ref, bias_ref, q_x, k_t, v_x, k_wide, v_wide):
    head_cols = k_t.shape[0]
    bias = jnp.transpose(bias_ref[...])[:, 0:1]
    for start in range(0, rows_ref.shape[0], 512):
        project_block(
            start, length, rows_ref, weight_ref, bias[:head_cols], bias[head_cols:],
            q_x, k_t, v_x, k_wide, v_wide, 512,
        )


def attend_block(h, lanes, q_x, k_wide, v_x, mixed, mixed_low, row_stats):
    scores = mul(k_wide[h], q_x[h, :, lanes])
    row_max = jnp.max(scores, axis=0, keepdims=True)
    probs = jnp.exp(scores - row_max).astype(low)
    total = mul(v_x[h, : HEAD + 16], probs)
    row_sum = total[HEAD : HEAD + 1]
    own = pl.ds(h * HEAD, HEAD)
    result = total[:HEAD] / row_sum
    mixed[own, lanes] = result
    mixed_low[own, lanes] = result.astype(low)
    row_stats[h, :, lanes] = jnp.broadcast_to(row_max + jnp.log(row_sum), (8, result.shape[1]))


def forward_kernel(
    length_ref, rows_ref, weight_ref, bias_ref, q_x, k_t, k_wide, v_wide, mixed, mixed_low, row_stats, v_x
):
    project_heads(length_ref[0], rows_ref, weight_ref, bias_ref, q_x, k_t, v_x, k_wide, v_wide)
    heads = q_x.shape[0]
    block = 512
    blocks = q_x.shape[2] // block

    def step(index, carry):
        h = index // blocks
        start = pl.multiple_of(lax.rem(index, blocks) * block, block)
        attend_block(h, pl.ds(start, block), q_x, k_wide, v_x, mixed, mixed_low, row_stats)
        return carry

    lax.fori_loop(0, heads * blocks, step, 0)


def attention_forward(length, rows, weight, bias):
    slot_rows = rows.shape[0]
    head_cols = weight.shape[1] // 3
    heads = head_cols // HEAD
    vmem = pl.BlockSpec(memory_space=pltpu.VMEM)
    return pl.pallas_call(
        forward_kernel,
        in_specs=[pl.BlockSpec(memory_space=pltpu.SMEM), vmem, vmem, vmem],
        out_specs=[vmem] * 7,
        out_shape=[
            jax.ShapeDtypeStruct((heads, WIDE, slot_rows), low),
            jax.ShapeDtypeStruct((head_cols, slot_rows), low),
            jax.ShapeDtypeStruct((heads, slot_rows, WIDE), low),
            jax.ShapeDtypeStruct((heads, slot_rows, WIDE), low),
            jax.ShapeDtypeStruct((head_cols, slot_rows), full),
            jax.ShapeDtypeStruct((head_cols, slot_rows), low),
            jax.ShapeDtypeStruct((heads, 8, slot_rows), full),
        ],
        scratch_shapes=[pltpu.VMEM((heads, WIDE, slot_rows), low)],
        compiler_params=pltpu.CompilerParams(vmem_limit_bytes=VMEM_BYTES),
        name="attention_forward",
    )(length, rows, weight, bias)


def attend_back(h, lanes, q_x, q_here, do_x, grad_t, mixed, row_stats, k_t, k_wide, v_wide, grads, grad_k, grad_v, first):
    own = pl.ds(pl.multiple_of(h * HEAD, HEAD), HEAD)
    grad = grad_t[own, lanes]
    columns = grad.shape[1]
    delta = jnp.sum(grad.astype(full) * mixed[own, lanes], axis=0, keepdims=True)
    parts = [part.astype(full) for part in three_parts(-delta)]
    do_x[:HEAD, :] = grad
    do_x[HEAD:, :] = stack_rows(parts, columns)
    parts = [part.astype(full) for part in three_parts(-row_stats[h, 0:1, lanes])]
    q_here[:HEAD, :] = q_x[h, :HEAD, lanes]
    q_here[HEAD:, :] = stack_rows([jnp.ones((1, columns), full)] + parts, columns)
    probs = jnp.exp(mul(k_wide[h], q_here[...]))
    grad_scores = (probs * mul(v_wide[h], do_x[...])).astype(low)
    value_part = mul(grad, probs.astype(low), NT)
    key_part = mul(q_here[:HEAD, :], grad_scores, NT)

    @pl.when(first)
    def _():
        grad_v[...] = value_part
        grad_k[...] = key_part

    @pl.when(jnp.logical_not(first))
    def _():
        grad_v[...] += value_part
        grad_k[...] += key_part

    query_part = mul(k_t[own, :], grad_scores) * HEAD**-0.5
    grads[pl.ds(pl.multiple_of(3 * h * HEAD, HEAD), HEAD), lanes] = query_part.astype(low)


def backward_kernel(
    q_in, k_t, k_wide, v_wide, mixed, row_stats, grad_t, rows_ref, weight_ref,
    partial_out, weight_out, sums_out, q_here, do_x, grads, grad_k, grad_v,
):
    heads, _, slot_rows = q_in.shape
    block = 512
    blocks = slot_rows // block

    def step(index, carry):
        h = index // blocks
        turn = lax.rem(index, blocks)
        start = pl.multiple_of(turn * block, block)
        attend_back(
            h, pl.ds(start, block), q_in, q_here, do_x, grad_t, mixed, row_stats, k_t, k_wide, v_wide, grads, grad_k,
            grad_v, turn == 0,
        )

        @pl.when(turn == blocks - 1)
        def _():
            base = pl.multiple_of(3 * h * HEAD, HEAD)
            grads[pl.ds(base + HEAD, HEAD), :] = grad_k[...].astype(low)
            grads[pl.ds(base + 2 * HEAD, HEAD), :] = grad_v[...].astype(low)

        return carry

    lax.fori_loop(0, heads * blocks, step, 0)
    for start in range(0, slot_rows, block):
        partial_out[start : start + block, :] = mul(
            grads[:, start : start + block], weight_ref[...], TT
        ).astype(partial_out.dtype)
    weight_out[...] = jnp.transpose(mul(grads[...], rows_ref[...])).astype(weight_out.dtype)
    sums_out[...] = jnp.broadcast_to(
        jnp.sum(grads[...].astype(full), axis=1, keepdims=True), sums_out.shape
    )


def attention_backward(q_x, k_t, k_wide, v_wide, mixed, row_stats, grad_t, rows, weight):
    heads, _, slot_rows = q_x.shape
    width, all_cols = weight.shape
    vmem = pl.BlockSpec(memory_space=pltpu.VMEM)
    return pl.pallas_call(
        backward_kernel,
        in_specs=[vmem] * 9,
        out_specs=[vmem] * 3,
        out_shape=[
            jax.ShapeDtypeStruct((slot_rows, width), low),
            jax.ShapeDtypeStruct((width, all_cols), low),
            jax.ShapeDtypeStruct((all_cols, WIDE), full),
        ],
        scratch_shapes=[
            pltpu.VMEM((WIDE, 512), low),
            pltpu.VMEM((WIDE, 512), low),
            pltpu.VMEM((all_cols, slot_rows), low),
            pltpu.VMEM((HEAD, slot_rows), full),
            pltpu.VMEM((HEAD, slot_rows), full),
        ],
        compiler_params=pltpu.CompilerParams(vmem_limit_bytes=VMEM_BYTES),
        name="attention_backward",
    )(q_x, k_t, k_wide, v_wide, mixed, row_stats, grad_t, rows, weight)


MESH = pl.DeviceIdType.MESH
OWN, RELATIONS = 0, 7
UP_W, OUT_W, DOWN_W, QKV_W = 0, 1, 2, 3


def offset_of(relation):
    return (0, -1, -2, -3, 1, 2, 3)[relation]


class Place:
    def __init__(self):
        self.f, self.s = lax.axis_index("fsdp"), lax.axis_index("seq")
        self.z, self.x = self.f // 2, lax.rem(self.f, 2)
        self.y, self.c = self.s // 2, lax.rem(self.s, 2)
        self.core = (self.f, 2 * self.y + 1 - self.c)
        self.across_y = (self.f, 2 * (1 - self.y) + self.c)
        self.diagonal = (self.f, 2 * (1 - self.y) + 1 - self.c)
        self.across_x = (2 * self.z + 1 - self.x, self.s)
        self.above = (self.f + 2, self.s)
        self.below = (self.f - 2, self.s)

    def has(self, relation):
        offset = offset_of(relation)
        return (self.z + offset >= 0) & (self.z + offset <= 3)

    def source(self, relation, column):
        own_column = self.f + 2 * offset_of(relation)
        return own_column if column == 0 else own_column + 1 - 2 * self.x

    def member(self, turn):
        flip_y = 1 - turn // 2
        flip_c = lax.rem(turn, 2) if not isinstance(turn, int) else turn % 2
        flip_c = flip_c + (1 - 2 * flip_c) * (turn // 2)
        return 2 * lax.rem(self.y + flip_y, 2) + lax.rem(self.c + flip_c, 2)


def remote(src, dst, send, recv, where):
    return pltpu.make_async_remote_copy(
        src_ref=src, dst_ref=dst, send_sem=send, recv_sem=recv, device_id=where, device_id_type=MESH
    )


def greet(place, all_lines):
    barrier = pltpu.get_barrier_semaphore()
    near = [place.core, place.across_y, place.diagonal, place.across_x]
    for where in near:
        pl.semaphore_signal(barrier, inc=1, device_id=where, device_id_type=MESH)
    for line in range(4):
        gap = place.z - line
        meets = gap != 0 if all_lines else (gap == 1) | (gap == -1)

        @pl.when(meets)
        def _(line=line):
            pl.semaphore_signal(
                barrier, inc=1, device_id=(2 * line + place.x, place.s), device_id_type=MESH
            )

    ends = 3 if all_lines else jnp.where((place.z == 0) | (place.z == 3), 1, 2)
    pl.semaphore_wait(barrier, len(near) + ends)


class Gather:
    def __init__(self, place, own, whole, sems):
        self.place, self.own, self.whole = place, own, whole
        (self.z_send, self.z_recv, self.x_send, self.x_recv, self.c_send, self.c_recv,
         self.y_send, self.y_recv, self.d_send, self.d_recv) = sems

    def piece(self, array, source, quarter=None, pair=False):
        c = self.place.c
        ref = self.whole[array]
        if array == QKV_W:
            return ref.at[source]
        if array == DOWN_W:
            rows = ref.shape[0] // 8
            part = rows // 4
            quarter = self.place.s if quarter is None else quarter
            return ref.at[pl.ds(pl.multiple_of(source * rows + quarter * part, part), part)]
        rows, columns = ref.shape[0] // 8, ref.shape[1] // 2
        count = 2 if pair else 1
        return ref.at[
            pl.ds(pl.multiple_of(source * rows, rows), count * rows),
            pl.ds(pl.multiple_of(c * columns, columns), columns),
        ]

    def own_piece(self, array):
        if array == QKV_W:
            return self.piece(array, self.place.f)
        ref = self.own[array]
        if array == DOWN_W:
            part = ref.shape[0] // 4
            return ref.at[pl.ds(pl.multiple_of(self.place.s * part, part), part)]
        columns = ref.shape[1] // 2
        return ref.at[:, pl.ds(pl.multiple_of(self.place.c * columns, columns), columns)]

    def z_piece(self, array, relation):
        source = self.place.source(relation, 0)
        if array == OUT_W:
            return self.piece(array, source - self.place.x, pair=True)
        return self.piece(array, source)

    def along_z(self, array, relation, way):
        here = self.z_piece(array, relation)
        src = self.own_piece(array) if relation == OWN and array != OUT_W else here
        step = abs(offset_of(relation))
        where = self.place.above if way == 0 else self.place.below
        return remote(src, here, self.z_send.at[array, way, step], self.z_recv.at[array, way, step], where)

    def z_ways(self, relation):
        place = self.place
        ways = []
        if offset_of(relation) <= 0:
            ways.append((0, place.has(relation) & (place.z < 3)))
        if offset_of(relation) >= 0:
            ways.append((1, place.has(relation) & (place.z > 0)))
        return ways

    def wait_z(self, array, relation):
        way = 0 if offset_of(relation) < 0 else 1
        step = abs(offset_of(relation)) - 1
        here = self.z_piece(array, relation)
        where = self.place.below if way == 0 else self.place.above
        remote(
            here, here, self.z_send.at[array, way, step], self.z_recv.at[array, way, step], where
        ).wait_recv()

    def over_x(self, array, relation):
        here = self.piece(array, self.place.source(relation, 0))
        src = self.own_piece(array) if relation == OWN else here
        return remote(
            src, here, self.x_send.at[array, relation], self.x_recv.at[array, relation], self.place.across_x
        )

    def from_x(self, array, relation):
        here = self.piece(array, self.place.source(relation, 1))
        return remote(
            here, here, self.x_send.at[array, relation], self.x_recv.at[array, relation], self.place.across_x
        )

    def to_core(self, array, relation, column):
        if array == OUT_W and relation != OWN:
            here = self.z_piece(array, relation)
        else:
            here = self.piece(array, self.place.source(relation, column))
        return remote(
            here, here, self.c_send.at[array, relation, column], self.c_recv.at[array, relation, column],
            self.place.core,
        )

    def over_y(self, relation, column):
        here = self.piece(DOWN_W, self.place.source(relation, column))
        return remote(
            here, here, self.y_send.at[relation, column], self.y_recv.at[relation, column], self.place.across_y
        )

    def far_quarter(self, relation, column):
        return self.piece(
            DOWN_W, self.place.source(relation, column), 2 * (1 - self.place.y) + self.place.c
        )

    def from_y(self, relation, column):
        here = self.far_quarter(relation, column)
        return remote(
            here, here, self.y_send.at[relation, column], self.y_recv.at[relation, column], self.place.across_y
        )

    def far_to_core(self, relation, column):
        here = self.far_quarter(relation, column)
        return remote(
            here, here, self.d_send.at[relation, column], self.d_recv.at[relation, column], self.place.core
        )

    def when(self, relation, action):
        if relation == OWN:
            action()
        else:
            pl.when(self.place.has(relation))(action)

    def arrive_z(self, array, relation, along=True, across=True):
        def action():
            if relation != OWN:
                self.wait_z(array, relation)
            for way, holds in self.z_ways(relation) if along else ():
                pl.when(holds)(lambda way=way: self.along_z(array, relation, way).start())
            if array != OUT_W and across:
                self.over_x(array, relation).start()
            if array != QKV_W and relation != OWN:
                self.to_core(array, relation, 0).start()
                if array == DOWN_W:
                    self.over_y(relation, 0).start()

        self.when(relation, action)

    def cross_out(self):
        self.over_x(OUT_W, OWN).start()

    def pair_out(self, own_copy):
        own_copy.wait()
        self.from_x(OUT_W, OWN).wait_recv()
        self.to_core(OUT_W, OWN, 1).start()
        for way, holds in self.z_ways(OWN):
            pl.when(holds)(lambda way=way: self.along_z(OUT_W, OWN, way).start())

    def arrive_x(self, array, relation):
        def action():
            self.from_x(array, relation).wait_recv()
            if array != QKV_W:
                self.to_core(array, relation, 1).start()
                if array == DOWN_W:
                    self.over_y(relation, 1).start()

        self.when(relation, action)

    def arrive_y(self, relation, column):
        def action():
            self.from_y(relation, column).wait_recv()
            self.far_to_core(relation, column).start()

        if (relation, column) != (OWN, 0):
            self.when(relation, action)

    def finish(self, array):
        for relation in range(RELATIONS):
            def action():
                if array != OUT_W or relation == OWN:
                    self.over_x(array, relation).wait_send()
                for way, holds in self.z_ways(relation):
                    pl.when(holds)(lambda way=way: self.along_z(array, relation, way).wait_send())
                if array == QKV_W:
                    return
                for column in range(2):
                    if (relation, column) == (OWN, 0) or (array == OUT_W and relation != OWN and column == 1):
                        continue
                    self.to_core(array, relation, column).wait()
                    if array == DOWN_W:
                        self.over_y(relation, column).wait_send()
                        self.far_to_core(relation, column).wait()

            self.when(relation, action)


def front_kernel(
    length_ref, tokens, read_rows, write_rows, qkv_in, vectors_in, up_in, down_in, out_in,
    small, up_bias, rows_out, weight_out, q_out, k_out, k_wide_out, v_wide_out, mixed_out, stats_out, up_full,
    down_full, out_full, attended,
    rows_ref, weight_ref, pieces, memory, q_x, k_t, k_wide, v_wide, v_x, mixed, mixed_low, row_stats,
    row_send, row_recv, far_send, far_recv, mix_send, mix_recv, local_sem, save_sem, head_sem, *gather_sems,
):
    place = Place()
    slot_rows, width = rows_ref.shape
    local_rows = tokens.shape[0]
    head_cols = k_t.shape[0]
    heads = head_cols // HEAD
    shard = width // 8
    length = length_ref[0]
    own_shards = {UP_W: up_in, DOWN_W: down_in, OUT_W: out_in}
    whole = {UP_W: up_full, DOWN_W: down_full, OUT_W: out_full, QKV_W: pieces}
    gather = Gather(place, own_shards, whole, gather_sems)

    memory[...] = jnp.zeros_like(memory)
    memory[:MEM, :] = read_rows[...]
    memory[16 : 16 + MEM, :] = write_rows[...]
    line = lax.broadcasted_iota(jnp.int32, (local_rows, 32), 1)
    at = place.s * local_rows + lax.broadcasted_iota(jnp.int32, (local_rows, 32), 0)
    wanted = jnp.where(line < 16, line, length - MEM + line - 16)
    used = (line < MEM) | ((line >= 16) & (line < 16 + MEM))
    pick = jnp.where(used & (wanted == at), 1.0, 0.0)
    taken = mul(pick.astype(low), memory[...]).astype(low)
    is_memory = jnp.sum(pick, axis=1, keepdims=True) > 0.5
    own_start = pl.multiple_of(place.s * local_rows, local_rows)
    rows_ref[pl.ds(own_start, local_rows), :] = jnp.where(is_memory, taken, tokens[...])
    for member in range(4):

        @pl.when(place.s == member)
        def _(member=member):
            for h in range(heads):
                for kind in range(3):
                    start = kind * width + (member * heads + h) * HEAD
                    to = (3 * h + kind) * HEAD
                    pieces[place.f, :, to : to + HEAD] = qkv_in[:, start : start + HEAD]

    columns = 3 * head_cols
    pieces[place.f, :, columns:] = jnp.zeros((shard, HEAD), low)
    for line in range(18):
        pieces[place.f, line : line + 1, columns:] = vectors_in[:, line * HEAD : (line + 1) * HEAD].astype(low)
    greet(place, False)

    halves = 2
    part = local_rows // halves

    def rows_of(member, half):
        return pl.ds(pl.multiple_of(member * local_rows + half * part, part), part)

    def send_rows(half, index):
        where = (place.core, place.across_y)[index]
        here = rows_ref.at[rows_of(place.s, half)]
        return remote(here, here, row_send.at[index, half], row_recv.at[index, half], where)

    def rows_from(half, index):
        member = (2 * place.y + 1 - place.c, 2 * (1 - place.y) + place.c)[index]
        here = rows_ref.at[rows_of(member, half)]
        where = (place.core, place.across_y)[index]
        return remote(here, here, row_send.at[index, half], row_recv.at[index, half], where)

    def pass_rows(half, arriving):
        flip = place.c if not arriving else 1 - place.c
        here = rows_ref.at[rows_of(2 * (1 - place.y) + flip, half)]
        return remote(here, here, far_send.at[half], far_recv.at[half], place.core)

    def own_copies():
        copies = []
        for index, array in enumerate((UP_W, DOWN_W, OUT_W)):
            rows = own_shards[array].shape[0]
            copies.append(pltpu.make_async_copy(
                own_shards[array], whole[array].at[pl.ds(pl.multiple_of(place.f * rows, rows), rows)],
                local_sem.at[index],
            ))
        return copies

    gather.arrive_z(QKV_W, OWN)
    for half in range(halves):
        send_rows(half, 1).start()
        send_rows(half, 0).start()
    gather.cross_out()
    for copy in own_copies():
        copy.start()
    for relation in (1, 4):
        gather.arrive_z(QKV_W, relation)
    gather.pair_out(own_copies()[2])
    for relation in (2, 5):
        gather.arrive_z(QKV_W, relation)
    gather.arrive_z(UP_W, OWN, across=False)
    rows_from(0, 1).wait_recv()
    pass_rows(0, False).start()
    for relation in (3, 6):
        gather.arrive_z(QKV_W, relation)
    gather.arrive_z(UP_W, OWN, along=False)
    gather.arrive_z(DOWN_W, OWN)
    for relation in range(RELATIONS):
        gather.arrive_x(QKV_W, relation)

    for source in range(8):
        weight_ref[source * shard : (source + 1) * shard, :] = pieces[source, :, :columns]
    tile = slice(columns - HEAD, columns + HEAD)
    bias_q = jnp.transpose(pieces[place.s, 0:16, tile].astype(full))[HEAD:]
    bias_v = jnp.transpose(pieces[4 + place.s, 0:16, tile].astype(full))[HEAD:]
    bias_q = jnp.concatenate([bias_q[:, h : h + 1] for h in range(heads)], axis=0)
    bias_v = jnp.concatenate([bias_v[:, h : h + 1] for h in range(heads)], axis=0)

    def project(member):
        start = pl.multiple_of(member * local_rows, local_rows)
        project_block(
            start, length, rows_ref, weight_ref, bias_q, bias_v, q_x, k_t, v_x, k_wide, v_wide, local_rows
        )

    project(place.s)
    for half in range(halves):
        rows_from(half, 0).wait_recv()
    project(2 * place.y + 1 - place.c)
    rows_from(1, 1).wait_recv()
    pass_rows(1, False).start()
    for relation in (1, 4):
        gather.arrive_z(UP_W, relation)
        gather.arrive_z(OUT_W, relation)
    project(2 * (1 - place.y) + place.c)
    for relation in (1, 4):
        gather.arrive_z(DOWN_W, relation)

    def scatter_vector(target, index, size, first):
        for source in range(8):
            done = 0
            while done < size:
                line, lane = divmod(first + done, HEAD)
                count = min(HEAD - lane, size - done)
                target[index : index + 1, source * size + done : source * size + done + count] = pieces[
                    source, line : line + 1, columns + lane : columns + lane + count
                ].astype(full)
                done += count

    for index, first in enumerate((2, 3, 4, 9, 10, 11)):
        scatter_vector(small, index, shard, first * shard)
    scatter_vector(up_bias, 0, 4 * shard, 5 * shard)
    for half in range(halves):
        pass_rows(half, True).wait_recv()
    project(2 * (1 - place.y) + 1 - place.c)

    def saves():
        pairs = [(rows_ref, rows_out), (weight_ref, weight_out), (k_t, k_out), (k_wide, k_wide_out), (v_wide, v_wide_out)]
        pairs += [(q_x.at[h, pl.ds(0, HEAD)], q_out.at[h]) for h in range(heads)]
        return [pltpu.make_async_copy(src, dst, save_sem.at[index]) for index, (src, dst) in enumerate(pairs)]

    for save in saves():
        save.start()

    def head_saves(h):
        own = pl.ds(h * HEAD, HEAD)
        return [
            pltpu.make_async_copy(mixed.at[own], mixed_out.at[own], head_sem.at[h, 0]),
            pltpu.make_async_copy(row_stats.at[h], stats_out.at[h], head_sem.at[h, 1]),
        ]

    def chores(step):
        if step == 1:
            gather.arrive_x(UP_W, OWN)
        elif step == 2:
            for relation in (2, 5):
                gather.arrive_z(UP_W, relation)
            gather.arrive_x(DOWN_W, OWN)
        elif step == 3:
            for relation in (1, 4):
                gather.arrive_y(relation, 0)
        elif step == 4:
            for relation in (2, 5):
                gather.arrive_z(OUT_W, relation)
            for save in head_saves(0):
                save.start()
        elif step == 5:
            for relation in (2, 5):
                gather.arrive_z(DOWN_W, relation)
            gather.arrive_y(OWN, 1)
        elif step == 6:
            for relation in (1, 4):
                gather.arrive_x(UP_W, relation)
        elif step == 8:
            for relation in (2, 5):
                gather.arrive_y(relation, 0)
            for save in head_saves(1):
                save.start()
        elif step == 9:
            for relation in (3, 6):
                gather.arrive_z(UP_W, relation)
            for relation in (2, 5):
                gather.arrive_x(UP_W, relation)
        elif step == 11:
            for relation in (3, 6):
                gather.arrive_z(OUT_W, relation)
                gather.arrive_z(DOWN_W, relation)
            for relation in (1, 4):
                gather.arrive_x(DOWN_W, relation)

    def send_mixed(h, turn, arriving=False):
        member = place.member(turn)
        own = pl.ds(pl.multiple_of(h * HEAD, HEAD), HEAD)
        lanes = pl.ds(pl.multiple_of(member * local_rows, local_rows), local_rows)
        owner = member if arriving else place.s
        there = attended.at[pl.ds(pl.multiple_of(owner * head_cols + h * HEAD, HEAD), HEAD)]
        return remote(
            mixed_low.at[own, lanes], there, mix_send.at[h, turn], mix_recv.at[h, turn], (place.f, member)
        )

    def keep_mixed(h):
        own = pl.ds(pl.multiple_of(h * HEAD, HEAD), HEAD)
        lanes = pl.ds(pl.multiple_of(place.s * local_rows, local_rows), local_rows)
        there = attended.at[pl.ds(pl.multiple_of(place.s * head_cols + h * HEAD, HEAD), HEAD)]
        return pltpu.make_async_copy(mixed_low.at[own, lanes], there, mix_send.at[h, 3])

    turns = slot_rows // local_rows

    def pass_on(index):
        h, turn = index // turns, lax.rem(index, turns)

        @pl.when(turn < turns - 1)
        def _():
            send_mixed(h, turn).start()

        @pl.when(turn == turns - 1)
        def _():
            keep_mixed(h).start()

    def step(index, carry):
        for when in range(12):
            pl.when(index == when)(lambda when=when: chores(when))
        h, turn = index // turns, lax.rem(index, turns)
        start = pl.multiple_of(place.member(turn) * local_rows, local_rows)
        attend_block(h, pl.ds(start, local_rows), q_x, k_wide, v_x, mixed, mixed_low, row_stats)

        @pl.when(index > 0)
        def _():
            pass_on(index - 1)

        return carry

    lax.fori_loop(0, heads * turns, step, 0)
    pass_on(heads * turns - 1)
    for save in head_saves(2):
        save.start()
    for relation in (3, 6):
        gather.arrive_x(UP_W, relation)
    for relation in (2, 5):
        gather.arrive_x(DOWN_W, relation)
    for relation in (1, 4):
        gather.arrive_y(relation, 1)
    for relation in (3, 6):
        gather.arrive_y(relation, 0)
        gather.arrive_x(DOWN_W, relation)
    for relation in (2, 5, 3, 6):
        gather.arrive_y(relation, 1)
    for array in (UP_W, OUT_W, DOWN_W, QKV_W):
        gather.finish(array)
    for copy in own_copies()[:2]:
        copy.wait()
    for half in range(halves):
        for index in range(2):
            send_rows(half, index).wait_send()
        pass_rows(half, False).wait_send()
    for h in range(heads):
        for turn in range(turns - 1):
            send_mixed(h, turn).wait_send()
            send_mixed(h, turn, True).wait_recv()
        keep_mixed(h).wait()
        for save in head_saves(h):
            save.wait()
    for save in saves():
        save.wait()


def front(lengths, tokens, read_rows, write_rows, qkv_shard, vectors, up_weight, down_weight, out_weight):
    local_rows, width = tokens.shape
    slot_rows = local_rows * 4
    head_cols = width // 4
    heads = head_cols // HEAD
    shard = width // 8
    vmem = pl.BlockSpec(memory_space=pltpu.VMEM)
    anywhere = pl.BlockSpec(memory_space=pl.ANY)
    dma = pltpu.SemaphoreType.DMA
    hidden = up_weight.shape[1]

    def held(*shape, kind=low):
        return pltpu.VMEM(shape, kind)

    def shaped(*shape, kind=low):
        return jax.ShapeDtypeStruct(shape, kind)

    return pl.pallas_call(
        front_kernel,
        in_specs=[pl.BlockSpec(memory_space=pltpu.SMEM)] + [vmem] * 8,
        out_specs=[vmem] * 2 + [anywhere] * 12,
        out_shape=[
            shaped(8, width, kind=full), shaped(8, hidden, kind=full),
            shaped(slot_rows, width), shaped(width, 3 * head_cols), shaped(heads, HEAD, slot_rows),
            shaped(head_cols, slot_rows), shaped(heads, slot_rows, WIDE), shaped(heads, slot_rows, WIDE),
            shaped(head_cols, slot_rows, kind=full), shaped(heads, 8, slot_rows, kind=full),
            shaped(width, hidden), shaped(hidden, width), shaped(width, width), shaped(width, local_rows),
        ],
        scratch_shapes=[
            held(slot_rows, width), held(width, 3 * head_cols), held(8, shard, 3 * head_cols + HEAD),
            held(32, width), held(heads, WIDE, slot_rows), held(head_cols, slot_rows),
            held(heads, slot_rows, WIDE), held(heads, slot_rows, WIDE), held(heads, WIDE, slot_rows),
            held(head_cols, slot_rows, kind=full), held(head_cols, slot_rows), held(heads, 8, slot_rows, kind=full),
            dma((2, 2)), dma((2, 2)), dma((2,)), dma((2,)), dma((heads, 4)), dma((heads, 4)), dma((3,)),
            dma((5 + heads,)), dma((heads, 2)),
            dma((4, 2, 3)), dma((4, 2, 3)), dma((4, 7)), dma((4, 7)), dma((3, 7, 2)), dma((3, 7, 2)),
            dma((7, 2)), dma((7, 2)), dma((7, 2)), dma((7, 2)),
        ],
        compiler_params=pltpu.CompilerParams(
            vmem_limit_bytes=VMEM_BYTES, collective_id=0, has_side_effects=True
        ),
        name="front",
    )(lengths, tokens, read_rows, write_rows, qkv_shard, vectors, up_weight, down_weight, out_weight)


DW_FIRST = 3
LINES = (3, 0, 2, 1)


def add_low(left, right):
    return (left.astype(full) + right.astype(full)).astype(low)


class Reduce:
    def __init__(self, place, given, sums, from_y, from_x, from_z, sems):
        self.place, self.given, self.sums = place, given, sums
        self.from_y, self.from_x, self.from_z = from_y, from_x, from_z
        self.last = max(sums)
        self.y_send, self.y_recv, self.x_send, self.x_recv, self.z_send, self.z_recv = sems

    def dest(self, column, line):
        x = self.place.x
        return 2 * line + (x if column == 0 else 1 - x)

    def slot(self, array, line, column=0):
        if array >= DW_FIRST:
            rows = 4 * HEAD if array == self.last else 3 * HEAD
            return self.sums[array].at[self.dest(column, line), pl.ds(0, rows // 4)]
        return self.sums[array].at[line]

    def cut(self, array, ref):
        if DW_FIRST <= array < self.last:
            return ref.at[pl.ds(0, 3 * HEAD // 4)]
        return ref

    def load(self, array, column, line, sem):
        source = self.given[array]
        if array == OUT_W:
            return pltpu.make_async_copy(source.at[line], self.sums[array].at[line], sem)
        source = source.at[column, line, 0] if array == DOWN_W else source.at[column, line]
        return pltpu.make_async_copy(source, self.sums[array].at[line], sem)

    def over_y(self, line):
        return remote(
            self.given[DOWN_W].at[0, line, 1], self.from_y.at[line], self.y_send.at[line], self.y_recv.at[line],
            self.place.across_y,
        )

    def add_y(self, line):
        self.over_y(line).wait_recv()
        slot = self.slot(DOWN_W, line)
        slot[...] = add_low(slot[...], self.from_y[line])

    def over_x(self, array, line):
        if array == OUT_W:
            here = self.sums[array].at[self.place.z]
            return remote(
                here.at[1], self.from_x[array], self.x_send.at[array, 0], self.x_recv.at[array, 0], self.place.across_x
            )
        if array == UP_W:
            start = self.given[array].at[1, line]
        elif array == DOWN_W:
            start = self.given[array].at[1, line, 0]
        else:
            start = self.slot(array, line, 1)
        return remote(
            start, self.cut(array, self.from_x[array].at[line]), self.x_send.at[array, line],
            self.x_recv.at[array, line], self.place.across_x,
        )

    def add_x(self, array, line):
        self.over_x(array, line).wait_recv()
        slot = self.sums[array].at[self.place.z, 0] if array == OUT_W else self.slot(array, line)
        came = self.from_x[array] if array == OUT_W else self.cut(array, self.from_x[array].at[line])
        slot[...] = add_low(slot[...], came[...])

    def along_z(self, array, way, line):
        return remote(
            self.slot(array, line), self.cut(array, self.from_z[array].at[way, line]),
            self.z_send.at[array, way, line], self.z_recv.at[array, way, line],
            self.place.above if way == 0 else self.place.below,
        )

    def add_z(self, array, way, line):
        self.along_z(array, way, line).wait_recv()
        slot = self.slot(array, line)
        slot[...] = add_low(slot[...], self.cut(array, self.from_z[array].at[way, line])[...])

    def hop(self, array, level, lines=(0, 1, 2, 3)):
        @pl.when(self.place.z == level)
        def _():
            for line in range(3, level, -1):
                if line in lines:
                    if level > 0:
                        self.add_z(array, 0, line)
                    self.along_z(array, 0, line).start()

        @pl.when(self.place.z == 3 - level)
        def _():
            for line in range(0, 3 - level):
                if line in lines:
                    if level > 0:
                        self.add_z(array, 1, line)
                    self.along_z(array, 1, line).start()

    def to_line(self, array, line):
        where = (2 * line + self.place.x, self.place.s)
        return remote(
            self.slot(array, line), self.cut(array, self.from_z[array].at[self.place.z]),
            self.z_send.at[array, 0, line], self.z_recv.at[array, 0, self.place.z], where,
        )

    def fling(self, array, lines=LINES):
        for line in lines:
            pl.when(self.place.z != line)(lambda line=line: self.to_line(array, line).start())

    def settle(self, array):
        if array >= DOWN_W:
            slot = self.slot(array, self.place.z)
            for line in range(4):

                @pl.when(self.place.z != line)
                def _(line=line):
                    came = self.cut(array, self.from_z[array].at[line])
                    remote(
                        came, came, self.z_send.at[array, 0, line], self.z_recv.at[array, 0, line], self.place.core
                    ).wait_recv()
                    slot[...] = add_low(slot[...], came[...])

            return
        for line in range(4):

            @pl.when(self.place.z == line)
            def _(line=line):
                if line > 0:
                    self.add_z(array, 0, line)
                if line < 3:
                    self.add_z(array, 1, line)

    def finish(self, array):
        for line in range(4):
            if array != OUT_W or line == 0:
                self.over_x(array, line).wait_send()
            if array >= DOWN_W:
                pl.when(self.place.z != line)(lambda line=line: self.to_line(array, line).wait_send())
            else:
                pl.when(self.place.z < line)(lambda line=line: self.along_z(array, 0, line).wait_send())
                pl.when(self.place.z > line)(lambda line=line: self.along_z(array, 1, line).wait_send())
            if array == DOWN_W:
                self.over_y(line).wait_send()


class Spread:
    def __init__(self, place, blocks, source, send, recv):
        self.place, self.blocks, self.source, self.send, self.recv = place, blocks, source, send, recv
        self.near = 2 * place.y + 1 - place.c
        self.far = 2 * (1 - place.y) + place.c
        self.last = 2 * (1 - place.y) + 1 - place.c

    def copy(self, kind, arriving=False):
        place = self.place
        if kind == 2:
            here = self.blocks.at[self.last if arriving else self.far]
            return remote(here, here, self.send.at[2], self.recv.at[2], place.core)
        member = (self.near, self.far)[kind] if arriving else place.s
        return remote(
            self.source, self.blocks.at[member], self.send.at[kind], self.recv.at[kind],
            (place.core, place.across_y)[kind],
        )

    def start(self):
        self.copy(1).start()
        self.copy(0).start()

    def pass_on(self):
        self.copy(1, True).wait_recv()
        self.copy(2).start()

    def finish(self):
        self.blocks[self.place.s] = self.source[...]
        self.copy(0, True).wait_recv()
        self.copy(2, True).wait_recv()
        for kind in range(3):
            self.copy(kind).wait_send()


def back_kernel(
    length_ref, grad_own, vectors_in, q_in, k_in, k_wide_in, v_wide_in, mixed_in, stats_in, rows_in, weight_in, resid_in, up_given, down_given, out_given,
    input_out, read_out, write_out, qkv_out, vector_out, up_out, down_out, out_out,
    q_x, k_t, k_wide, v_wide, mixed, row_stats, grad_t, q_here, do_x, grads, grad_k, grad_v, rows_ref, weight_ref, resid_ref,
    up_sum, out_sum, down_sum, dw, down_y, up_x, out_x, down_x, dw_x, up_z, out_z, down_z, dw_z,
    up_last, out_last, up_other, out_other, down_all, dw_all,
    near_send, near_recv, far_sum, far_recv, memory_all, memory_own,
    mix_send, mix_recv, local_sem, saved_sem, mine_sem, share_send, share_recv, near_s, near_r, far_s, far_r,
    *sems,
):
    place = Place()
    heads, _, slot_rows = q_in.shape
    width, local_rows = grad_own.shape
    head_cols = heads * HEAD
    last = DW_FIRST + heads - 1
    given = {UP_W: up_given, OUT_W: out_given, DOWN_W: down_given}
    sums = {UP_W: up_sum, OUT_W: out_sum, DOWN_W: down_sum}
    from_x = {UP_W: up_x, OUT_W: out_x, DOWN_W: down_x}
    from_z = {UP_W: up_z, OUT_W: out_z, DOWN_W: down_z}
    for h in range(heads):
        sums[DW_FIRST + h], from_x[DW_FIRST + h] = dw.at[h], dw_x.at[h]
        from_z[DW_FIRST + h] = dw_z.at[h]
    reduce = Reduce(place, given, sums, down_y, from_x, from_z, sems)
    greet(place, True)

    peers = (place.across_y, place.diagonal, place.core)

    def member_rows(turn):
        member = place.member(turn)
        return member, pl.ds(pl.multiple_of(member * local_rows, local_rows), local_rows)

    def send_grad(turn, arriving=False):
        member, lanes = member_rows(turn)
        own_lanes = pl.ds(pl.multiple_of(place.s * local_rows, local_rows), local_rows)
        src = grad_own.at[pl.ds(pl.multiple_of(member * head_cols, head_cols), head_cols)]
        return remote(
            src, grad_t.at[:, lanes if arriving else own_lanes], mix_send.at[turn], mix_recv.at[turn], peers[turn]
        )

    def saved_loads(h):
        own = pl.ds(h * HEAD, HEAD)
        pairs = (
            (k_wide_in.at[h], k_wide.at[h]), (q_in.at[h], q_x.at[h]), (v_wide_in.at[h], v_wide.at[h]),
            (mixed_in.at[own], mixed.at[own]), (stats_in.at[h], row_stats.at[h]), (k_in.at[own], k_t.at[own]),
        )
        return [pltpu.make_async_copy(src, dst, saved_sem.at[h, i]) for i, (src, dst) in enumerate(pairs)]

    def sum_loads(array):
        return [reduce.load(array, 0, line, mine_sem.at[array, line]) for line in LINES]

    for turn in range(3):
        send_grad(turn).start()
    for load in sum_loads(OUT_W):
        load.start()
    for load in saved_loads(0):
        load.start()
    loads = []
    for index, (src, dst) in enumerate(((rows_in, rows_ref), (weight_in, weight_ref), (resid_in, resid_ref))):
        loads.append(pltpu.make_async_copy(src, dst, local_sem.at[index]))

    def send_x(array, lines=LINES):
        for line in lines:
            reduce.over_x(array, line).start()

    send_x(UP_W)
    for line in LINES:
        reduce.over_y(line).start()
    send_x(DOWN_W)
    for array in (UP_W, DOWN_W):
        for load in sum_loads(array):
            load.start()
    for load in loads:
        load.start()

    for h in range(1, heads):
        for load in saved_loads(h):
            load.start()

    own_lanes = pl.ds(pl.multiple_of(place.s * local_rows, local_rows), local_rows)
    grad_t[:, own_lanes] = grad_own[pl.ds(pl.multiple_of(place.s * head_cols, head_cols), head_cols), :]

    def take_x(array, lines=LINES):
        for line in lines:
            reduce.add_x(array, line)

    turns = slot_rows // local_rows

    def weight_part(h):
        if h == 0:
            loads[0].wait()
        base = 3 * h * HEAD
        part = jnp.transpose(mul(grads[base : base + 3 * HEAD, :], rows_ref[...])).astype(low)
        half = width // 16
        for dest in range(8):
            start = 2 * half * dest
            dw[h, dest, :half, :] = jnp.concatenate(
                [part[start : start + half], part[start + half : start + 2 * half]], axis=1
            )
            if h == heads - 1:
                dw[h, dest, half:, :] = vectors_in[dest].astype(low)
        if h == heads - 1:
            total = jnp.sum(grads[...].astype(full), axis=1, keepdims=True)
            spread = jnp.transpose(jnp.broadcast_to(total, (total.shape[0], WIDE)))[0:1]
            for kind, first_dest in ((0, 0), (2, 4)):
                for head in range(heads):
                    start = (3 * head + kind) * HEAD
                    dw[h, first_dest + place.s, half : half + 1, head * HEAD : (head + 1) * HEAD] = spread[
                        :, start : start + HEAD
                    ].astype(low)
        send_x(DW_FIRST + h)

    share = {UP_W: (up_last, up_other), OUT_W: (out_last, out_other)}

    def settled(array):
        return sums[array].at[place.z, 0] if array == OUT_W else sums[array].at[place.z]

    def sum_y(array):
        mine_now = settled(array)
        return remote(mine_now, share[array][0], share_send.at[array, 0], share_recv.at[array, 0], place.across_y)

    def half_to_core(array):
        mine_now = settled(array)
        return remote(mine_now, share[array][1], share_send.at[array, 1], share_recv.at[array, 1], place.core)

    def spread_of(array):
        if array == DOWN_W:
            return Spread(place, down_all, down_sum.at[place.z], share_send.at[2], share_recv.at[2])
        h = array - DW_FIRST
        return Spread(
            place, dw_all.at[h, :, pl.ds(0, reduce.slot(array, 0).shape[0])], reduce.slot(array, place.z),
            share_send.at[array], share_recv.at[array],
        )

    def add_last(array):
        sum_y(array).wait()
        slot = settled(array)
        slot[...] = add_low(slot[...], share[array][0][...])
        half_to_core(array).start()

    first, second = DW_FIRST, DW_FIRST + 1

    def chores(index):
        if index == 1:
            send_grad(2, True).wait_recv()
        elif index == 2:
            send_grad(1, True).wait_recv()
            for array in (UP_W, DOWN_W):
                for load in sum_loads(array):
                    load.wait()
            take_x(UP_W, (3,))
            reduce.hop(UP_W, 0, (3,))
            reduce.hop(OUT_W, 1, (3, 0))
        elif index == 3:
            send_grad(0, True).wait_recv()
            reduce.hop(OUT_W, 1, (2, 1))
        elif index == 4:
            for load in saved_loads(1):
                load.wait()
            weight_part(0)
            take_x(UP_W, (0,))
            reduce.hop(UP_W, 0, (0,))
            reduce.hop(OUT_W, 2)
        elif index == 5:
            reduce.hop(UP_W, 1, (3,))
        elif index == 6:
            for line in LINES:
                reduce.add_y(line)
            take_x(UP_W, (2,))
            reduce.hop(UP_W, 0, (2,))
            reduce.settle(OUT_W)
            reduce.over_x(OUT_W, 0).start()
        elif index == 7:
            reduce.hop(UP_W, 1, (0,))
            take_x(UP_W, (1,))
            reduce.hop(UP_W, 0, (1,))
        elif index == 8:
            for load in saved_loads(2):
                load.wait()
            weight_part(1)
            reduce.hop(UP_W, 2, (3,))
        elif index == 9:
            reduce.hop(UP_W, 2, (0,))
            reduce.hop(UP_W, 1, (2, 1))
            take_x(DOWN_W, (3, 0))
            reduce.fling(DOWN_W, (3, 0))
        elif index == 10:
            take_x(DOWN_W, (2,))
            reduce.fling(DOWN_W, (2,))
        elif index == 11:
            take_x(DOWN_W, (1,))
            reduce.fling(DOWN_W, (1,))

    def step(index, carry):
        for when in range(1, 12):
            pl.when(index == when)(lambda when=when: chores(when))
        h, turn = index // turns, lax.rem(index, turns)
        _, lanes = member_rows(turns - 1 - turn)
        attend_back(
            h, lanes, q_x, q_here, do_x, grad_t, mixed, row_stats, k_t, k_wide, v_wide, grads, grad_k, grad_v, turn == 0
        )

        @pl.when(turn == turns - 1)
        def _():
            base = pl.multiple_of(3 * h * HEAD, HEAD)
            grads[pl.ds(base + HEAD, HEAD), :] = grad_k[...].astype(low)
            grads[pl.ds(base + 2 * HEAD, HEAD), :] = grad_v[...].astype(low)

        return carry

    for load in sum_loads(OUT_W):
        load.wait()
    reduce.hop(OUT_W, 0)
    for load in saved_loads(0):
        load.wait()
    lax.fori_loop(0, heads * turns, step, 0)

    weight_part(heads - 1)
    loads[1].wait()
    loads[2].wait()

    halves, part = 2, local_rows // 2
    length = length_ref[0]

    def memory_pick(rows, start):
        line = lax.broadcasted_iota(jnp.int32, (32, rows), 0)
        row = start + lax.broadcasted_iota(jnp.int32, (32, rows), 1)
        wanted = jnp.where(line < 16, line, length - MEM + line - 16)
        used = (line < MEM) | ((line >= 16) & (line < 16 + MEM))
        return jnp.where(used & (wanted == row), 1.0, 0.0).astype(low)

    def part_for(turn, half):
        start = pl.multiple_of(place.member(turn) * local_rows + half * part, part)
        return mul(grads[:, pl.ds(start, part)], weight_ref[...], TT)

    def share_near(index, half):
        rows = pl.ds(half * part, part)
        return remote(
            near_send.at[index, rows], near_recv.at[index, rows], near_s.at[index, half], near_r.at[index, half],
            place.core,
        )

    def share_far(half):
        rows = pl.ds(half * part, part)
        return remote(far_sum.at[rows], far_recv.at[rows], far_s.at[half], far_r.at[half], place.across_y)

    for half in range(halves):
        rows = slice(half * part, (half + 1) * part)
        near_send[0, rows, :] = part_for(1, half).astype(low)
        share_near(0, half).start()
        far_sum[rows, :] = part_for(0, half).astype(low)
        if half == 0:
            taken = mul(memory_pick(slot_rows, 0), grads[...], NT).astype(low)
            own_part = mul(memory_pick(local_rows, place.s * local_rows), resid_ref[...].astype(low))
            memory_own[...] = (mul(taken, weight_ref[...], NT) + own_part).astype(low)
        share_near(0, half).wait_recv()
        far_sum[rows, :] = add_low(far_sum[rows, :], near_recv[0, rows, :])
        share_far(half).start()
    memory = Spread(place, memory_all, memory_own, share_send.at[DW_FIRST + heads], share_recv.at[DW_FIRST + heads])
    memory.start()
    reduce.settle(UP_W)
    sum_y(UP_W).start()
    take_x(first)
    reduce.fling(first)
    reduce.add_x(OUT_W, 0)
    sum_y(OUT_W).start()
    for half in range(halves):
        rows = slice(half * part, (half + 1) * part)
        near_send[1, rows, :] = part_for(2, half).astype(low)
        share_near(1, half).start()
    take_x(second)
    reduce.fling(second)
    reduce.settle(DOWN_W)
    spread_of(DOWN_W).start()
    take_x(last)
    reduce.fling(last)
    add_last(UP_W)
    for half in range(halves):
        resid_ref[half * part : (half + 1) * part, :] += part_for(3, half)
    for array in (first, second, last):
        reduce.settle(array)
        spread_of(array).start()
    add_last(OUT_W)
    memory.pass_on()
    for h in (heads - 1, 0, 1):
        spread_of(DW_FIRST + h).pass_on()
    spread_of(DOWN_W).pass_on()
    for array, out in ((UP_W, up_out), (OUT_W, out_out)):
        columns = out.shape[1] // 2
        out[:, pl.ds(pl.multiple_of(place.c * columns, columns), columns)] = settled(array)[...]
        half_to_core(array).wait()
        out[:, pl.ds(pl.multiple_of((1 - place.c) * columns, columns), columns)] = share[array][1][...]
    for h in range(heads):
        spread_of(DW_FIRST + h).finish()
    spread_of(DOWN_W).finish()
    quarter = down_out.shape[0] // 4
    for member in range(4):
        down_out[member * quarter : (member + 1) * quarter, :] = down_all[member]
    half = qkv_out.shape[0] // 2
    for kind in range(3):
        for member in range(4):
            for h in range(heads):
                start = kind * width + (member * heads + h) * HEAD
                for side in range(2):
                    lanes = (3 * side + kind) * HEAD
                    qkv_out[side * half : (side + 1) * half, start : start + HEAD] = dw_all[
                        h, member, :half, lanes : lanes + HEAD
                    ]
    vector_sum = dw_all[heads - 1, 0, half:, :].astype(full)
    for member in range(1, 4):
        vector_sum = vector_sum + dw_all[heads - 1, member, half:, :].astype(full)
    vector_out[...] = vector_sum
    memory.finish()
    total = memory_all[0].astype(full)
    for member in range(1, 4):
        total = total + memory_all[member].astype(full)
    read_out[...] = total[:MEM]
    write_out[...] = total[16 : 16 + MEM]
    for half in range(halves):
        rows = slice(half * part, (half + 1) * part)
        share_near(1, half).wait_recv()
        share_far(half).wait_recv()
        grad_layer = resid_ref[rows, :] + near_recv[1, rows, :].astype(full) + far_recv[rows, :].astype(full)
        rows_at = place.s * local_rows + half * part + lax.broadcasted_iota(jnp.int32, (part, 1), 0)
        in_write = (rows_at >= length - MEM) & (rows_at < length)
        input_out[rows, :] = jnp.where((rows_at < MEM) | in_write, 0.0, grad_layer)
    for array in range(DW_FIRST + heads):
        reduce.finish(array)
    for turn in range(3):
        send_grad(turn).wait_send()
    for half in range(halves):
        for index in range(2):
            share_near(index, half).wait_send()
        share_far(half).wait_send()


def back(lengths, grad_own, saved, vectors, rows, weight, resid, up_given, down_given, out_given):
    q_x, k_t, k_wide, v_wide, mixed, row_stats = saved
    heads, _, slot_rows = q_x.shape
    width, local_rows = grad_own.shape
    hidden = 2 * up_given.shape[3]
    shard, head_cols = width // 8, heads * HEAD
    half, small, piece = hidden // 2, width // 2, hidden // 32
    vmem = pl.BlockSpec(memory_space=pltpu.VMEM)
    anywhere = pl.BlockSpec(memory_space=pl.ANY)
    dma = pltpu.SemaphoreType.DMA
    arrays = DW_FIRST + heads

    def held(*shape, kind=low):
        return pltpu.VMEM(shape, kind)

    tall = (shard // 2 + 16, 6 * HEAD)
    return pl.pallas_call(
        back_kernel,
        in_specs=[pl.BlockSpec(memory_space=pltpu.SMEM)] + [vmem] * 2 + [anywhere] * 12,
        out_specs=[vmem] * 8,
        out_shape=[
            jax.ShapeDtypeStruct((local_rows, width), full),
            jax.ShapeDtypeStruct((MEM, width), full),
            jax.ShapeDtypeStruct((MEM, width), full),
            jax.ShapeDtypeStruct((shard, 3 * width), low),
            jax.ShapeDtypeStruct((16, 6 * HEAD), full),
            jax.ShapeDtypeStruct((shard, hidden), low),
            jax.ShapeDtypeStruct((hidden // 8, width), low),
            jax.ShapeDtypeStruct((shard, width), low),
        ],
        scratch_shapes=[
            held(heads, HEAD, slot_rows), held(head_cols, slot_rows), held(heads, slot_rows, WIDE),
            held(heads, slot_rows, WIDE), held(head_cols, slot_rows, kind=full), held(heads, 8, slot_rows, kind=full),
            held(head_cols, slot_rows), held(WIDE, local_rows), held(WIDE, local_rows), held(3 * head_cols, slot_rows),
            held(HEAD, slot_rows, kind=full), held(HEAD, slot_rows, kind=full),
            held(slot_rows, width), held(width, 3 * head_cols), held(local_rows, width, kind=full),
            held(4, shard, half), held(4, 2, shard, small), held(4, piece, width),
            held(heads, 8, *tall), held(4, piece, width),
            held(4, shard, half), held(shard, small), held(4, piece, width), held(heads, 4, *tall),
            held(2, 4, shard, half), held(2, 4, 2, shard, small), held(4, piece, width), held(heads, 4, *tall),
            held(shard, half), held(shard, small), held(shard, half), held(shard, small),
            held(4, piece, width), held(heads, 4, *tall),
            held(2, local_rows, width), held(2, local_rows, width), held(local_rows, width),
            held(local_rows, width), held(4, 32, width), held(32, width),
            dma((3,)), dma((3,)), dma((3,)), dma((heads, 6)), dma((3, 4)), dma((arrays + 1, 3)),
            dma((arrays + 1, 3)), dma((2, 2)), dma((2, 2)), dma((2,)), dma((2,)),
            dma((4,)), dma((4,)), dma((arrays, 4)), dma((arrays, 4)),
            dma((arrays, 2, 4)), dma((arrays, 2, 4)),
        ],
        compiler_params=pltpu.CompilerParams(
            vmem_limit_bytes=VMEM_BYTES, collective_id=1, has_side_effects=True
        ),
        name="back",
    )(
        lengths, grad_own, vectors, q_x, k_t, k_wide, v_wide, mixed, row_stats, rows, weight, resid,
        up_given, down_given, out_given,
    )


def phi_parts(value):
    normal = 0.5 * (1.0 + lax.erf(value * (0.5**0.5)))
    density = jnp.exp(-0.5 * value * value) * (0.5 * 2.0**0.5 * 3.141592653589793**-0.5)
    return normal, normal + value * density


def statistics(values):
    centre = values - jnp.mean(values, axis=1, keepdims=True)
    factor = lax.rsqrt(jnp.mean(centre * centre, axis=1, keepdims=True) + norm_epsilon)
    return centre * factor, factor


def norm_back(grad, gain, normed, factor):
    scaled = grad * gain
    first = jnp.mean(scaled, axis=1, keepdims=True)
    second = jnp.mean(scaled * normed, axis=1, keepdims=True)
    return factor * (scaled - first - normed * second)


def column_total(values):
    return jnp.sum(values, axis=0, keepdims=True)


def middle_kernel(
    length_ref, cotangent, small, up_bias, rows_in, attended_in, up_in, down_in, out_in,
    output, resid_out, grad_own, vector_out, up_out, down_out, out_out,
    layer_in, attended, up_w, down_w, out_w, hidden, slope, normed_one, middle_low, grad_down,
    grad_two, grad_mid, totals, up_total, up_grad, down_grad, out_grad, up_sum, down_sum, out_sum,
    from_y, load_sem, save_sem, c_send, c_recv, y_send, y_recv,
):
    place = Place()
    rows, width = cotangent.shape
    ff = up_w.shape[1]
    chunk = ff // 4
    shard = width // 8
    barrier = pltpu.get_barrier_semaphore()
    for where in (place.core, place.across_y):
        pl.semaphore_signal(barrier, inc=1, device_id=where, device_id_type=MESH)

    def chunk_lanes(j):
        return pl.ds(pl.multiple_of(j * chunk, chunk), chunk)

    def up_load(j):
        return pltpu.make_async_copy(up_in.at[:, chunk_lanes(j)], up_w.at[:, chunk_lanes(j)], load_sem.at[j])

    def down_load(j):
        return pltpu.make_async_copy(down_in.at[chunk_lanes(j)], down_w.at[chunk_lanes(j)], load_sem.at[4 + j])

    first_loads = [
        pltpu.make_async_copy(
            rows_in.at[pl.ds(pl.multiple_of(place.s * rows, rows), rows)], layer_in, load_sem.at[8]
        ),
        pltpu.make_async_copy(attended_in, attended, load_sem.at[9]),
        pltpu.make_async_copy(out_in, out_w, load_sem.at[10]),
    ]
    for load in first_loads:
        load.start()
    for j in range(4):
        up_load(j).start()
        down_load(j).start()
    out_bias, gain_one, shift_one = small[0:1, :], small[1:2, :], small[2:3, :]
    down_bias, gain_two, shift_two = small[3:4, :], small[4:5, :], small[5:6, :]
    for load in first_loads:
        load.wait()

    branch = mul(attended[...], out_w[...], TN)
    normed, factor_one = statistics(layer_in[...].astype(full) + branch + out_bias)
    normed_one[...] = normed
    middle_low[...] = (normed * gain_one + shift_one).astype(low)
    grad_mid[...] = jnp.zeros_like(grad_mid)

    def forward_chunk(j, carry):
        up_load(j).wait()
        lanes = chunk_lanes(j)
        value = mul(middle_low[...], up_w[:, lanes]) + up_bias[0:1, lanes]
        normal, slope_here = phi_parts(value)
        hidden[:, lanes] = (value * normal).astype(low)
        slope[:, lanes] = slope_here
        down_load(j).wait()
        grad_mid[...] += mul(hidden[:, lanes], down_w[lanes, :])
        return carry

    lax.fori_loop(0, 4, forward_chunk, 0)
    middle = normed_one[...] * gain_one + shift_one
    normed_two, factor_two = statistics(middle + grad_mid[...] + down_bias)
    places = place.s * rows + lax.broadcasted_iota(jnp.int32, (rows, 1), 0)
    in_slot = places < length_ref[0]
    output[...] = jnp.where(in_slot, normed_two * gain_two + shift_two, 0.0).astype(low)
    grad_final = jnp.where(in_slot, cotangent[...].astype(full), 0.0)
    totals[4:5, :] = column_total(grad_final * normed_two)
    totals[5:6, :] = column_total(grad_final)
    grad_resid = norm_back(grad_final, gain_two, normed_two, factor_two)
    grad_two[...] = grad_resid
    grad_down[...] = grad_resid.astype(low)
    totals[3:4, :] = column_total(grad_down[...].astype(full))
    pl.semaphore_wait(barrier, 2)

    def down_piece(ref, line, column, far, core):
        dest = 2 * line + (place.x if column == 0 else 1 - place.x)
        y = place.y if far == 0 else 1 - place.y
        return ref.at[pl.ds(pl.multiple_of(dest * 4 * shard + (2 * y + core) * shard, shard), shard)]

    def side_piece(ref, line, column, core):
        dest = 2 * line + (place.x if column == 0 else 1 - place.x)
        half = ref.shape[1] // 2
        return ref.at[
            pl.ds(pl.multiple_of(dest * shard, shard), shard), pl.ds(pl.multiple_of(core * half, half), half)
        ]

    def down_share(line, column, far):
        return remote(
            down_piece(down_grad, line, column, far, 1 - place.c), down_sum.at[column, line, far],
            c_send.at[2 + far, column, line], c_recv.at[2 + far, column, line], place.core,
        )

    def side_slot(array, line, column):
        return out_sum.at[line, column] if array == 1 else up_sum.at[column, line]

    def over_y(line):
        return remote(down_sum.at[1, line, 1], from_y.at[line], y_send.at[line], y_recv.at[line], place.across_y)

    def side_share(array, line, column):
        grad = (up_grad, out_grad)[array]
        return remote(
            side_piece(grad, line, column, 1 - place.c), side_slot(array, line, column),
            c_send.at[array, column, line], c_recv.at[array, column, line], place.core,
        )

    def down_save(column, line):
        return pltpu.make_async_copy(down_sum.at[column, line], down_out.at[column, line], save_sem.at[2, column, line])

    def side_save(array, column, line):
        out = out_out.at[line, column] if array == 1 else up_out.at[column, line]
        return pltpu.make_async_copy(side_slot(array, line, column), out, save_sem.at[array, column, line])

    def add_far(column, line):
        down_share(line, column, 1).wait_recv()
        down_sum[column, line, 1] = add_low(
            down_sum[column, line, 1], down_piece(down_grad, line, column, 1, place.c)[...]
        )

    def down_chunk(line, carry):
        lanes = chunk_lanes(line)
        down_grad[lanes, :] = mul(hidden[:, lanes], grad_down[...], TN).astype(low)
        for column in range(2):
            for far in range(2):
                down_share(line, column, far).start()
        return carry

    lax.fori_loop(0, 4, down_chunk, 0)
    grad_mid[...] = grad_two[...]

    def back_chunk(turn, carry):
        j = lax.rem(2 * (1 - place.c) + turn, 4)
        lanes = chunk_lanes(j)
        grad_up = (mul(grad_down[...], down_w[lanes, :], NT) * slope[:, lanes]).astype(low)
        up_total[0:1, lanes] = column_total(grad_up.astype(full))
        up_grad[:, lanes] = mul(middle_low[...], grad_up, TN).astype(low)
        grad_mid[...] += mul(grad_up, up_w[:, lanes], NT)

        @pl.when(turn == 0)
        def _():
            for line in LINES:
                add_far(1, line)
                over_y(line).start()

        @pl.when(turn == 1)
        def _():
            for column in (1, 0):
                for line in LINES:
                    side_share(0, line, column).start()

        return carry

    lax.fori_loop(0, 4, back_chunk, 0)
    grad_middle = grad_mid[...]
    normed = normed_one[...]
    totals[1:2, :] = column_total(grad_middle * normed)
    totals[2:3, :] = column_total(grad_middle)
    grad_one = norm_back(grad_middle, gain_one, normed, factor_one)
    resid_out[...] = grad_one
    grad_branch = grad_one.astype(low)
    totals[0:1, :] = column_total(grad_branch.astype(full))
    out_grad[...] = mul(attended[...], grad_branch).astype(low)
    for column in (1, 0):
        for line in LINES:
            side_share(1, line, column).start()
    grad_own[...] = mul(out_w[...], grad_branch, NT).astype(low)

    def add_down(column, line):
        down_share(line, column, 0).wait_recv()
        down_sum[column, line, 0] = add_low(
            down_sum[column, line, 0], down_piece(down_grad, line, column, 0, place.c)[...]
        )
        if column == 0:
            add_far(column, line)
        else:
            over_y(line).wait()
            down_sum[column, line, 0] = add_low(down_sum[column, line, 0], from_y[line])
        down_save(column, line).start()

    def add_side(array, column, line):
        slot = side_slot(array, line, column)
        side_share(array, line, column).wait_recv()
        slot[...] = add_low(slot[...], side_piece((up_grad, out_grad)[array], line, column, place.c)[...])
        side_save(array, column, line).start()

    for line in LINES:
        add_down(0, line)
    for column in (1, 0):
        for line in LINES:
            add_side(0, column, line)
    vector_out[...] = jnp.zeros_like(vector_out)
    for dest in range(8):
        for index, (line, start) in enumerate(((0, 2), (0, 3), (1, 0), (2, 1), (2, 2), (2, 3))):
            vector_out[dest, line : line + 1, start * shard : (start + 1) * shard] = totals[
                index : index + 1, dest * shard : (dest + 1) * shard
            ]
        base = dest * 4 * shard
        vector_out[dest, 1:2, shard:] = up_total[0:1, base : base + 3 * shard]
        vector_out[dest, 2:3, :shard] = up_total[0:1, base + 3 * shard : base + 4 * shard]
    for column in range(2):
        for line in range(4):
            add_side(1, column, line)
    for line in LINES:
        add_down(1, line)
    for column in range(2):
        for line in range(4):
            for array in range(2):
                side_share(array, line, column).wait_send()
                side_save(array, column, line).wait()
            for far in range(2):
                down_share(line, column, far).wait_send()
            down_save(column, line).wait()


def middle_part(lengths, cotangent, small, up_bias, rows_full, attended, up_full, down_full, out_full):
    rows, width = cotangent.shape
    ff = up_full.shape[1]
    shard = width // 8
    vmem = pl.BlockSpec(memory_space=pltpu.VMEM)
    anywhere = pl.BlockSpec(memory_space=pl.ANY)
    dma = pltpu.SemaphoreType.DMA

    def held(*shape, kind=low):
        return pltpu.VMEM(shape, kind)

    def shaped(*shape, kind=low):
        return jax.ShapeDtypeStruct(shape, kind)

    up_parts, down_parts, out_parts = (2, 4, shard, ff // 2), (2, 4, 2, ff // 32, width), (4, 2, shard, width // 2)
    return pl.pallas_call(
        middle_kernel,
        in_specs=[pl.BlockSpec(memory_space=pltpu.SMEM)] + [vmem] * 3 + [anywhere] * 5,
        out_specs=[vmem] * 4 + [anywhere] * 3,
        out_shape=[
            shaped(rows, width), shaped(rows, width, kind=full), shaped(width, rows),
            shaped(8, 16, 4 * shard, kind=full), shaped(*up_parts), shaped(*down_parts), shaped(*out_parts),
        ],
        scratch_shapes=[
            held(rows, width), held(width, rows), held(width, ff), held(ff, width), held(width, width), held(rows, ff), held(rows, ff, kind=full),
            held(rows, width, kind=full), held(rows, width), held(rows, width), held(rows, width, kind=full),
            held(rows, width, kind=full), held(8, width, kind=full), held(8, ff, kind=full),
            held(width, ff), held(ff, width), held(width, width), held(*up_parts), held(*down_parts),
            held(*out_parts), held(4, ff // 32, width), dma((11,)), dma((3, 2, 4)), dma((4, 2, 4)),
            dma((4, 2, 4)), dma((4,)), dma((4,)),
        ],
        compiler_params=pltpu.CompilerParams(
            vmem_limit_bytes=VMEM_BYTES, collective_id=2, has_side_effects=True
        ),
        name="middle",
    )(lengths, cotangent, small, up_bias, rows_full, attended, up_full, down_full, out_full)


def finish_kernel(
    output_in, input_in, qkv_in, vector_in, up_in, down_in, out_in, read_in, write_in,
    output, input_out, read_out, write_out, qkv_out, qv_out, out_out, out_b, gain_one, shift_one, up_out, up_b,
    down_out, down_b, gain_two, shift_two,
):
    shard = out_b.shape[1]
    output[...] = output_in[...]
    input_out[...] = input_in[...]
    for given, out in ((read_in, read_out), (write_in, write_out)):
        for line in range(given.shape[0]):
            out[line] = given[line : line + 1]
    for given, out in ((qkv_in, qkv_out), (up_in, up_out), (down_in, down_out), (out_in, out_out)):
        out[...] = given[...].astype(full)
    qv_out[...] = vector_in[0:1, : 2 * shard]
    out_b[...] = vector_in[0:1, 2 * shard : 3 * shard]
    gain_one[...] = vector_in[0:1, 3 * shard :]
    shift_one[...] = vector_in[1:2, :shard]
    up_b[:, : 3 * shard] = vector_in[1:2, shard:]
    up_b[:, 3 * shard :] = vector_in[2:3, :shard]
    down_b[...] = vector_in[2:3, shard : 2 * shard]
    gain_two[...] = vector_in[2:3, 2 * shard : 3 * shard]
    shift_two[...] = vector_in[2:3, 3 * shard :]


def finish(output, input_grad, qkv_grad, vectors, up_grad, down_grad, out_grad, grad_read, grad_write):
    shard = qkv_grad.shape[0]

    def shaped(*shape, kind=full):
        return jax.ShapeDtypeStruct(shape, kind)

    line = shaped(1, shard)
    steps = 2

    def rows(array):
        return pl.BlockSpec((array.shape[0] // steps,) + array.shape[1:], lambda i: (i, 0))

    def once(*shape):
        return pl.BlockSpec(shape, lambda i: (0,) * len(shape))

    lone = once(1, shard)
    memory = (grad_read.shape[0], 1, grad_read.shape[1])
    return pl.pallas_call(
        finish_kernel,
        grid=(steps,),
        in_specs=[
            rows(output), rows(input_grad), rows(qkv_grad), once(*vectors.shape), rows(up_grad), rows(down_grad),
            rows(out_grad), once(*grad_read.shape), once(*grad_write.shape),
        ],
        out_specs=[
            rows(output), rows(input_grad), once(*memory), once(*memory), rows(qkv_grad), once(1, 2 * shard),
            rows(out_grad), lone, lone, lone, rows(up_grad), once(1, 4 * shard), rows(down_grad), lone, lone, lone,
        ],
        out_shape=[
            shaped(*output.shape, kind=low), shaped(*input_grad.shape), shaped(*memory), shaped(*memory),
            shaped(*qkv_grad.shape), shaped(1, 2 * shard), shaped(*out_grad.shape), line, line, line,
            shaped(*up_grad.shape), shaped(1, 4 * shard), shaped(*down_grad.shape), line, line, line,
        ],
        compiler_params=pltpu.CompilerParams(vmem_limit_bytes=VMEM_BYTES),
        name="finish",
    )(output, input_grad, qkv_grad, vectors, up_grad, down_grad, out_grad, grad_read, grad_write)


def normalize(values, gain_vec, shift_vec):
    centre = values - jnp.mean(values, axis=-1, keepdims=True)
    factor = lax.rsqrt(jnp.mean(centre * centre, axis=-1, keepdims=True) + norm_epsilon)
    return centre * factor * gain_vec + shift_vec


def column_sums(values):
    return jnp.sum(values, axis=0, dtype=full)


def on_block(
    tokens, read_rows, write_rows, lengths, qkv_weight, vectors, out_weight, up_weight, down_weight, cotangent
):
    total = sum(vector.shape[0] for vector in vectors)
    packed, start = jnp.zeros((1, total), full), 0
    for vector in vectors:
        size = vector.shape[0]
        packed = packed + jnp.pad(vector.astype(full).reshape(1, -1), ((0, 0), (start, total - start - size)))
        start += size
    (small, up_bias, rows, weight, q_t, k_t, k_wide, v_wide, mixed, row_stats, up_full, down_full, out_full,
     attended) = front(
        lengths, tokens, read_rows, write_rows, qkv_weight, packed, up_weight, down_weight, out_weight
    )
    output, resid, grad_own, vector_parts, up_parts, down_parts, out_parts = middle_part(
        lengths, cotangent, small, up_bias, rows, attended, up_full, down_full, out_full
    )
    saved = (q_t, k_t, k_wide, v_wide, mixed, row_stats)
    input_grad, grad_read, grad_write, qkv_grad, vector_sum, up_grad, down_grad, out_grad = back(
        lengths, grad_own, saved, vector_parts, rows, weight, resid, up_parts, down_parts, out_parts
    )
    results = finish(
        output, input_grad, qkv_grad, vector_sum, up_grad, down_grad, out_grad, grad_read, grad_write
    )
    shaped = [jnp.swapaxes(result, 0, 1) if index in (2, 3) else result for index, result in enumerate(results)]
    return tuple(result.reshape(-1) if result.shape[0] == 1 and result.ndim == 2 else result for result in shaped)


def per_device(
    tokens, read_memory, write_memory, lengths, qkv_weight, qv_bias, out_weight, out_bias, norm1_gain,
    norm1_bias, up_weight, up_bias, down_weight, down_bias, norm2_gain, norm2_bias, cotangent,
):
    seq_count = lax.axis_size("seq")
    fsdp_count = lax.axis_size("fsdp")
    seq_place = lax.axis_index("seq")
    local_rows, width = tokens.shape
    head_cols = width // seq_count
    shard = width // fsdp_count
    length = lengths[0]
    heads = head_cols // HEAD
    vectors = (qv_bias, out_bias, norm1_gain, norm1_bias, up_bias, down_bias, norm2_gain, norm2_bias)
    if (fsdp_count, seq_count) == (8, 4):
        return on_block(
            tokens, read_memory[0], write_memory[0], lengths, qkv_weight, vectors, out_weight, up_weight, down_weight,
            cotangent,
        )
    places = seq_place * local_rows + jnp.arange(local_rows, dtype=jnp.int32)
    in_slot = (places < length)[:, None]
    memory_slots = jnp.arange(MEM, dtype=jnp.int32)
    pick_read = places[:, None] == memory_slots[None, :]
    pick_write = places[:, None] == length - MEM + memory_slots[None, :]
    is_memory = jnp.any(pick_read | pick_write, axis=1)[:, None]
    picks = jnp.concatenate([pick_read, pick_write], axis=1).astype(full)
    memory = jnp.concatenate([read_memory[0], write_memory[0]], axis=0)
    layer_in = jnp.where(is_memory, mul(picks.astype(low), memory).astype(low), tokens)

    own_shard = lax.dynamic_slice_in_dim(
        qkv_weight.reshape(shard, 3, seq_count, heads, HEAD), seq_place, 1, 2
    )
    own_shard = jnp.transpose(own_shard[:, :, 0], (0, 2, 1, 3)).reshape(shard, 3 * head_cols)
    packed = jnp.concatenate(vectors)
    rows = lax.all_gather(layer_in, "seq", axis=0, tiled=True)
    weight = lax.all_gather(own_shard, "fsdp", axis=0, tiled=True)
    packed = lax.all_gather(packed.reshape(1, -1), "fsdp", axis=0, tiled=True).astype(full)
    whole, start = [], 0
    for vector in vectors:
        whole.append(packed[:, start : start + vector.shape[0]].reshape(-1))
        start += vector.shape[0]
    qv_vec, out_vec, gain_one, shift_one, up_vec, down_vec, gain_two, shift_two = whole
    own_qv = lax.dynamic_slice_in_dim(qv_vec.reshape(2, seq_count, head_cols), seq_place, 1, 1)
    bias = jnp.concatenate([own_qv[0, 0], own_qv[1, 0]])
    bias = jnp.broadcast_to(bias, (8, bias.shape[0]))
    out_full = lax.all_gather(out_weight, "fsdp", axis=0, tiled=True)
    up_full = lax.all_gather(up_weight, "fsdp", axis=0, tiled=True)
    down_full = lax.all_gather(down_weight, "fsdp", axis=0, tiled=True)
    q_x, k_t, k_wide, v_wide, mixed, mixed_low, row_stats = attention_forward(lengths, rows, weight, bias)
    attended = lax.all_to_all(mixed_low, "seq", split_axis=1, concat_axis=0, tiled=True)
    resid_one = layer_in.astype(full) + mul(attended, out_full, TN) + out_vec
    middle, norm_one_back = jax.vjp(normalize, resid_one, gain_one, shift_one)
    middle_low = middle.astype(low)
    up_pre = mul(middle_low, up_full) + up_vec
    gelu_out, gelu_back = jax.vjp(partial(jax.nn.gelu, approximate=False), up_pre)
    hidden = gelu_out.astype(low)
    down_pre = mul(hidden, down_full) + down_vec
    final, norm_two_back = jax.vjp(normalize, middle + down_pre, gain_two, shift_two)
    output = jnp.where(in_slot, final, 0.0).astype(low)
    grad_final = jnp.where(in_slot, cotangent.astype(full), 0.0)
    grad_resid_two, grad_gain_two, grad_shift_two = norm_two_back(grad_final)
    grad_down = grad_resid_two.astype(low)
    grad_down_weight = mul(hidden, grad_down, TN)
    (grad_up_pre,) = gelu_back(mul(grad_down, down_full, NT))
    grad_up = grad_up_pre.astype(low)
    grad_up_weight = mul(middle_low, grad_up, TN)
    grad_middle = grad_resid_two + mul(grad_up, up_full, NT)
    grad_resid_one, grad_gain_one, grad_shift_one = norm_one_back(grad_middle)
    grad_branch = grad_resid_one.astype(low)
    grad_out_weight = mul(attended, grad_branch)
    grad_attended = mul(out_full, grad_branch, NT).astype(low)
    vector_grads = [
        column_sums(grad_branch), grad_gain_one, grad_shift_one, column_sums(grad_up),
        column_sums(grad_down), grad_gain_two, grad_shift_two,
    ]
    packed_grad = jnp.concatenate([v.reshape(fsdp_count, -1) for v in vector_grads], axis=1)
    saved = (q_x, k_t, k_wide, v_wide, mixed, row_stats)
    grad_t = lax.all_to_all(grad_attended, "seq", split_axis=0, concat_axis=1, tiled=True)
    partial_in, weight_part, sums = attention_backward(*saved, grad_t, rows, weight)
    from_heads = lax.psum_scatter(partial_in, "seq", scatter_dimension=0, tiled=True).astype(full)
    grad_layer_in = grad_resid_one + from_heads
    input_grad = jnp.where(is_memory, 0.0, grad_layer_in)
    grad_memory = lax.dot_general(
        picks, grad_layer_in, TN, precision=lax.Precision.HIGHEST, preferred_element_type=full
    )
    grad_memory = lax.psum(grad_memory.astype(low), "seq").astype(full)
    grad_read, grad_write = grad_memory[:MEM], grad_memory[MEM:]
    sums = sums[:, 0].reshape(heads, 3, HEAD)
    own_sums = jnp.stack([sums[:, 0].reshape(-1), sums[:, 2].reshape(-1)])[:, None]
    zero_qv = jnp.zeros((2, seq_count, head_cols), full)
    qv_grad = lax.dynamic_update_slice_in_dim(zero_qv, own_sums, seq_place, 1)
    packed_grad = jnp.concatenate([qv_grad.reshape(fsdp_count, -1), packed_grad], axis=1)
    packed_sum = lax.psum(packed_grad, ("fsdp", "seq"))
    own_vectors = lax.dynamic_index_in_dim(packed_sum, lax.axis_index("fsdp"), 0, False)

    def both_axes(part):
        piece = lax.psum_scatter(part.astype(low), "fsdp", scatter_dimension=0, tiled=True)
        return lax.psum(piece, "seq").astype(full)

    qkv_piece = lax.psum_scatter(weight_part, "fsdp", scatter_dimension=0, tiled=True)
    qkv_parts = lax.all_gather(qkv_piece, "seq", axis=0).reshape(seq_count, shard, heads, 3, HEAD)
    qkv_out = jnp.transpose(qkv_parts, (1, 3, 0, 2, 4)).reshape(shard, 3 * width).astype(full)
    up_out, down_out, out_out = both_axes(grad_up_weight), both_axes(grad_down_weight), both_axes(grad_out_weight)
    vector_outs, start = [], 0
    for vector in vectors:
        vector_outs.append(own_vectors[start : start + vector.shape[0]])
        start += vector.shape[0]
    qv_out, out_b_out, gain_one_out, shift_one_out, up_b_out, down_b_out, gain_two_out, shift_two_out = vector_outs
    return (
        output, input_grad, grad_read[None], grad_write[None], qkv_out, qv_out, out_out, out_b_out, gain_one_out,
        shift_one_out, up_out, up_b_out, down_out, down_b_out, gain_two_out, shift_two_out,
    )


def solution(mesh):
    rows, piece = P(("fsdp", "seq"), None), P("fsdp")
    matrix, memory = P("fsdp", None), P("fsdp", None, None)
    in_specs = (
        rows, memory, memory, piece, matrix, piece, matrix, piece, piece, piece, matrix, piece, matrix,
        piece, piece, piece, rows,
    )
    out_specs = (
        rows, rows, memory, memory, matrix, piece, matrix, piece, piece, piece, matrix, piece, matrix,
        piece, piece, piece,
    )
    return jax.shard_map(per_device, mesh=mesh, in_specs=in_specs, out_specs=out_specs, check_vma=False)
```

```python
from functools import partial

import jax
import jax.numpy as jnp
from jax import lax
from jax.experimental import pallas as pl
from jax.experimental.pallas import tpu as pltpu
from jax.sharding import PartitionSpec as P

HEAD = 64
MEM = 10
WIDE = 128
VMEM_BYTES = 64000 * 1024

norm_epsilon = 1e-06
masked_score = -1e30
low = jnp.bfloat16
full = jnp.float32

NN = (((1,), (0,)), ((), ()))
NT = (((1,), (1,)), ((), ()))
TN = (((0,), (0,)), ((), ()))
TT = (((0,), (1,)), ((), ()))


def mul(left, right, dims=NN):
    return lax.dot_general(left, right, dims, preferred_element_type=full)


def three_parts(value):
    high = value.astype(low)
    rest = value - high.astype(full)
    middle = rest.astype(low)
    return high, middle, (rest - middle.astype(full)).astype(low)


def stack_rows(rows, columns):
    place = lax.broadcasted_iota(jnp.int32, (HEAD, columns), 0)
    block = jnp.zeros((HEAD, columns), full)
    for index, row in enumerate(rows):
        block = jnp.where(place == index, row, block)
    return block.astype(low)


def project_block(start, length, rows_ref, weight_ref, bias_q, bias_v, q_x, k_t, v_x, k_wide, v_wide, step):
    head_cols = k_t.shape[0]
    lanes = pl.ds(start, step)
    made = mul(weight_ref[...], rows_ref[lanes, :], TT)
    place = start + lax.broadcasted_iota(jnp.int32, (1, step), 1)
    key_bias = jnp.where(place < length, 0.0, masked_score)
    one = jnp.ones((1, step), full)
    query_extra = stack_rows([one], step)
    key_extra = stack_rows([key_bias, one, one, one], step)
    value_extra = stack_rows([one, one, one], step)
    for h in range(head_cols // HEAD):
        own = slice(h * HEAD, (h + 1) * HEAD)
        base = 3 * h * HEAD
        query = (made[base : base + HEAD] + bias_q[own]).astype(low)
        q_x[h, :HEAD, lanes] = query * jnp.asarray(HEAD**-0.5, low)
        q_x[h, HEAD:, lanes] = query_extra
        k_t[own, lanes] = made[base + HEAD : base + 2 * HEAD].astype(low)
        v_x[h, :HEAD, lanes] = (made[base + 2 * HEAD : base + 3 * HEAD] + bias_v[own]).astype(low)
        v_x[h, HEAD:, lanes] = value_extra
        k_wide[h, lanes, :] = jnp.transpose(jnp.concatenate([k_t[own, lanes], key_extra], axis=0))
        v_wide[h, lanes, :] = jnp.transpose(v_x[h, :, lanes])


def project_heads(length, rows_ref, weight_ref, bias_ref, q_x, k_t, v_x, k_wide, v_wide):
    head_cols = k_t.shape[0]
    bias = jnp.transpose(bias_ref[...])[:, 0:1]
    for start in range(0, rows_ref.shape[0], 512):
        project_block(
            start, length, rows_ref, weight_ref, bias[:head_cols], bias[head_cols:],
            q_x, k_t, v_x, k_wide, v_wide, 512,
        )


def attend_block(h, lanes, q_x, k_wide, v_x, mixed, mixed_low, row_stats):
    scores = mul(k_wide[h], q_x[h, :, lanes])
    row_max = jnp.max(scores, axis=0, keepdims=True)
    probs = jnp.exp(scores - row_max).astype(low)
    total = mul(v_x[h, : HEAD + 16], probs)
    row_sum = total[HEAD : HEAD + 1]
    own = pl.ds(h * HEAD, HEAD)
    result = total[:HEAD] / row_sum
    mixed[own, lanes] = result
    mixed_low[own, lanes] = result.astype(low)
    row_stats[h, :, lanes] = jnp.broadcast_to(row_max + jnp.log(row_sum), (8, result.shape[1]))


def forward_kernel(
    length_ref, rows_ref, weight_ref, bias_ref, q_x, k_t, k_wide, v_wide, mixed, mixed_low, row_stats, v_x
):
    project_heads(length_ref[0], rows_ref, weight_ref, bias_ref, q_x, k_t, v_x, k_wide, v_wide)
    heads = q_x.shape[0]
    block = 512
    blocks = q_x.shape[2] // block

    def step(index, carry):
        h = index // blocks
        start = pl.multiple_of(lax.rem(index, blocks) * block, block)
        attend_block(h, pl.ds(start, block), q_x, k_wide, v_x, mixed, mixed_low, row_stats)
        return carry

    lax.fori_loop(0, heads * blocks, step, 0)


def attention_forward(length, rows, weight, bias):
    slot_rows = rows.shape[0]
    head_cols = weight.shape[1] // 3
    heads = head_cols // HEAD
    vmem = pl.BlockSpec(memory_space=pltpu.VMEM)
    return pl.pallas_call(
        forward_kernel,
        in_specs=[pl.BlockSpec(memory_space=pltpu.SMEM), vmem, vmem, vmem],
        out_specs=[vmem] * 7,
        out_shape=[
            jax.ShapeDtypeStruct((heads, WIDE, slot_rows), low),
            jax.ShapeDtypeStruct((head_cols, slot_rows), low),
            jax.ShapeDtypeStruct((heads, slot_rows, WIDE), low),
            jax.ShapeDtypeStruct((heads, slot_rows, WIDE), low),
            jax.ShapeDtypeStruct((head_cols, slot_rows), full),
            jax.ShapeDtypeStruct((head_cols, slot_rows), low),
            jax.ShapeDtypeStruct((heads, 8, slot_rows), full),
        ],
        scratch_shapes=[pltpu.VMEM((heads, WIDE, slot_rows), low)],
        compiler_params=pltpu.CompilerParams(vmem_limit_bytes=VMEM_BYTES),
        name="attention_forward",
    )(length, rows, weight, bias)


def attend_back(h, lanes, q_x, q_here, do_x, grad_t, mixed, row_stats, k_t, k_wide, v_wide, grads, grad_k, grad_v, first):
    own = pl.ds(pl.multiple_of(h * HEAD, HEAD), HEAD)
    grad = grad_t[own, lanes]
    columns = grad.shape[1]
    delta = jnp.sum(grad.astype(full) * mixed[own, lanes], axis=0, keepdims=True)
    parts = [part.astype(full) for part in three_parts(-delta)]
    do_x[:HEAD, :] = grad
    do_x[HEAD:, :] = stack_rows(parts, columns)
    parts = [part.astype(full) for part in three_parts(-row_stats[h, 0:1, lanes])]
    q_here[:HEAD, :] = q_x[h, :HEAD, lanes]
    q_here[HEAD:, :] = stack_rows([jnp.ones((1, columns), full)] + parts, columns)
    probs = jnp.exp(mul(k_wide[h], q_here[...]))
    grad_scores = (probs * mul(v_wide[h], do_x[...])).astype(low)
    value_part = mul(grad, probs.astype(low), NT)
    key_part = mul(q_here[:HEAD, :], grad_scores, NT)

    @pl.when(first)
    def _():
        grad_v[...] = value_part
        grad_k[...] = key_part

    @pl.when(jnp.logical_not(first))
    def _():
        grad_v[...] += value_part
        grad_k[...] += key_part

    query_part = mul(k_t[own, :], grad_scores) * HEAD**-0.5
    grads[pl.ds(pl.multiple_of(3 * h * HEAD, HEAD), HEAD), lanes] = query_part.astype(low)


def backward_kernel(
    q_in, k_t, k_wide, v_wide, mixed, row_stats, grad_t, rows_ref, weight_ref,
    partial_out, weight_out, sums_out, q_here, do_x, grads, grad_k, grad_v,
):
    heads, _, slot_rows = q_in.shape
    block = 512
    blocks = slot_rows // block

    def step(index, carry):
        h = index // blocks
        turn = lax.rem(index, blocks)
        start = pl.multiple_of(turn * block, block)
        attend_back(
            h, pl.ds(start, block), q_in, q_here, do_x, grad_t, mixed, row_stats, k_t, k_wide, v_wide, grads, grad_k,
            grad_v, turn == 0,
        )

        @pl.when(turn == blocks - 1)
        def _():
            base = pl.multiple_of(3 * h * HEAD, HEAD)
            grads[pl.ds(base + HEAD, HEAD), :] = grad_k[...].astype(low)
            grads[pl.ds(base + 2 * HEAD, HEAD), :] = grad_v[...].astype(low)

        return carry

    lax.fori_loop(0, heads * blocks, step, 0)
    for start in range(0, slot_rows, block):
        partial_out[start : start + block, :] = mul(
            grads[:, start : start + block], weight_ref[...], TT
        ).astype(partial_out.dtype)
    weight_out[...] = jnp.transpose(mul(grads[...], rows_ref[...])).astype(weight_out.dtype)
    sums_out[...] = jnp.broadcast_to(
        jnp.sum(grads[...].astype(full), axis=1, keepdims=True), sums_out.shape
    )


def attention_backward(q_x, k_t, k_wide, v_wide, mixed, row_stats, grad_t, rows, weight):
    heads, _, slot_rows = q_x.shape
    width, all_cols = weight.shape
    vmem = pl.BlockSpec(memory_space=pltpu.VMEM)
    return pl.pallas_call(
        backward_kernel,
        in_specs=[vmem] * 9,
        out_specs=[vmem] * 3,
        out_shape=[
            jax.ShapeDtypeStruct((slot_rows, width), low),
            jax.ShapeDtypeStruct((width, all_cols), low),
            jax.ShapeDtypeStruct((all_cols, WIDE), full),
        ],
        scratch_shapes=[
            pltpu.VMEM((WIDE, 512), low),
            pltpu.VMEM((WIDE, 512), low),
            pltpu.VMEM((all_cols, slot_rows), low),
            pltpu.VMEM((HEAD, slot_rows), full),
            pltpu.VMEM((HEAD, slot_rows), full),
        ],
        compiler_params=pltpu.CompilerParams(vmem_limit_bytes=VMEM_BYTES),
        name="attention_backward",
    )(q_x, k_t, k_wide, v_wide, mixed, row_stats, grad_t, rows, weight)


MESH = pl.DeviceIdType.MESH
OWN, RELATIONS = 0, 7
UP_W, OUT_W, DOWN_W, QKV_W = 0, 1, 2, 3


def offset_of(relation):
    return (0, -1, -2, -3, 1, 2, 3)[relation]


class Place:
    def __init__(self):
        self.f, self.s = lax.axis_index("fsdp"), lax.axis_index("seq")
        self.z, self.x = self.f // 2, lax.rem(self.f, 2)
        self.y, self.c = self.s // 2, lax.rem(self.s, 2)
        self.core = (self.f, 2 * self.y + 1 - self.c)
        self.across_y = (self.f, 2 * (1 - self.y) + self.c)
        self.diagonal = (self.f, 2 * (1 - self.y) + 1 - self.c)
        self.across_x = (2 * self.z + 1 - self.x, self.s)
        self.above = (self.f + 2, self.s)
        self.below = (self.f - 2, self.s)

    def has(self, relation):
        offset = offset_of(relation)
        return (self.z + offset >= 0) & (self.z + offset <= 3)

    def source(self, relation, column):
        own_column = self.f + 2 * offset_of(relation)
        return own_column if column == 0 else own_column + 1 - 2 * self.x

    def member(self, turn):
        flip_y = 1 - turn // 2
        flip_c = lax.rem(turn, 2) if not isinstance(turn, int) else turn % 2
        flip_c = flip_c + (1 - 2 * flip_c) * (turn // 2)
        return 2 * lax.rem(self.y + flip_y, 2) + lax.rem(self.c + flip_c, 2)


def remote(src, dst, send, recv, where):
    return pltpu.make_async_remote_copy(
        src_ref=src, dst_ref=dst, send_sem=send, recv_sem=recv, device_id=where, device_id_type=MESH
    )


def greet(place, all_lines):
    barrier = pltpu.get_barrier_semaphore()
    near = [place.core, place.across_y, place.diagonal, place.across_x]
    for where in near:
        pl.semaphore_signal(barrier, inc=1, device_id=where, device_id_type=MESH)
    for line in range(4):
        gap = place.z - line
        meets = gap != 0 if all_lines else (gap == 1) | (gap == -1)

        @pl.when(meets)
        def _(line=line):
            pl.semaphore_signal(
                barrier, inc=1, device_id=(2 * line + place.x, place.s), device_id_type=MESH
            )

    ends = 3 if all_lines else jnp.where((place.z == 0) | (place.z == 3), 1, 2)
    pl.semaphore_wait(barrier, len(near) + ends)


class Gather:
    def __init__(self, place, own, whole, sems):
        self.place, self.own, self.whole = place, own, whole
        (self.z_send, self.z_recv, self.x_send, self.x_recv, self.c_send, self.c_recv,
         self.y_send, self.y_recv, self.d_send, self.d_recv) = sems

    def piece(self, array, source, quarter=None, pair=False):
        c = self.place.c
        ref = self.whole[array]
        if array == QKV_W:
            return ref.at[source]
        if array == DOWN_W:
            rows = ref.shape[0] // 8
            part = rows // 4
            quarter = self.place.s if quarter is None else quarter
            return ref.at[pl.ds(pl.multiple_of(source * rows + quarter * part, part), part)]
        rows, columns = ref.shape[0] // 8, ref.shape[1] // 2
        count = 2 if pair else 1
        return ref.at[
            pl.ds(pl.multiple_of(source * rows, rows), count * rows),
            pl.ds(pl.multiple_of(c * columns, columns), columns),
        ]

    def own_piece(self, array):
        if array == QKV_W:
            return self.piece(array, self.place.f)
        ref = self.own[array]
        if array == DOWN_W:
            part = ref.shape[0] // 4
            return ref.at[pl.ds(pl.multiple_of(self.place.s * part, part), part)]
        columns = ref.shape[1] // 2
        return ref.at[:, pl.ds(pl.multiple_of(self.place.c * columns, columns), columns)]

    def z_piece(self, array, relation):
        source = self.place.source(relation, 0)
        if array == OUT_W:
            return self.piece(array, source - self.place.x, pair=True)
        return self.piece(array, source)

    def along_z(self, array, relation, way):
        here = self.z_piece(array, relation)
        src = self.own_piece(array) if relation == OWN and array != OUT_W else here
        step = abs(offset_of(relation))
        where = self.place.above if way == 0 else self.place.below
        return remote(src, here, self.z_send.at[array, way, step], self.z_recv.at[array, way, step], where)

    def z_ways(self, relation):
        place = self.place
        ways = []
        if offset_of(relation) <= 0:
            ways.append((0, place.has(relation) & (place.z < 3)))
        if offset_of(relation) >= 0:
            ways.append((1, place.has(relation) & (place.z > 0)))
        return ways

    def wait_z(self, array, relation):
        way = 0 if offset_of(relation) < 0 else 1
        step = abs(offset_of(relation)) - 1
        here = self.z_piece(array, relation)
        where = self.place.below if way == 0 else self.place.above
        remote(
            here, here, self.z_send.at[array, way, step], self.z_recv.at[array, way, step], where
        ).wait_recv()

    def over_x(self, array, relation):
        here = self.piece(array, self.place.source(relation, 0))
        src = self.own_piece(array) if relation == OWN else here
        return remote(
            src, here, self.x_send.at[array, relation], self.x_recv.at[array, relation], self.place.across_x
        )

    def from_x(self, array, relation):
        here = self.piece(array, self.place.source(relation, 1))
        return remote(
            here, here, self.x_send.at[array, relation], self.x_recv.at[array, relation], self.place.across_x
        )

    def to_core(self, array, relation, column):
        if array == OUT_W and relation != OWN:
            here = self.z_piece(array, relation)
        else:
            here = self.piece(array, self.place.source(relation, column))
        return remote(
            here, here, self.c_send.at[array, relation, column], self.c_recv.at[array, relation, column],
            self.place.core,
        )

    def over_y(self, relation, column):
        here = self.piece(DOWN_W, self.place.source(relation, column))
        return remote(
            here, here, self.y_send.at[relation, column], self.y_recv.at[relation, column], self.place.across_y
        )

    def far_quarter(self, relation, column):
        return self.piece(
            DOWN_W, self.place.source(relation, column), 2 * (1 - self.place.y) + self.place.c
        )

    def from_y(self, relation, column):
        here = self.far_quarter(relation, column)
        return remote(
            here, here, self.y_send.at[relation, column], self.y_recv.at[relation, column], self.place.across_y
        )

    def far_to_core(self, relation, column):
        here = self.far_quarter(relation, column)
        return remote(
            here, here, self.d_send.at[relation, column], self.d_recv.at[relation, column], self.place.core
        )

    def when(self, relation, action):
        if relation == OWN:
            action()
        else:
            pl.when(self.place.has(relation))(action)

    def arrive_z(self, array, relation, along=True, across=True):
        def action():
            if relation != OWN:
                self.wait_z(array, relation)
            for way, holds in self.z_ways(relation) if along else ():
                pl.when(holds)(lambda way=way: self.along_z(array, relation, way).start())
            if array != OUT_W and across:
                self.over_x(array, relation).start()
            if array != QKV_W and relation != OWN:
                self.to_core(array, relation, 0).start()
                if array == DOWN_W:
                    self.over_y(relation, 0).start()

        self.when(relation, action)

    def cross_out(self):
        self.over_x(OUT_W, OWN).start()

    def pair_out(self, own_copy):
        own_copy.wait()
        self.from_x(OUT_W, OWN).wait_recv()
        self.to_core(OUT_W, OWN, 1).start()
        for way, holds in self.z_ways(OWN):
            pl.when(holds)(lambda way=way: self.along_z(OUT_W, OWN, way).start())

    def arrive_x(self, array, relation):
        def action():
            self.from_x(array, relation).wait_recv()
            if array != QKV_W:
                self.to_core(array, relation, 1).start()
                if array == DOWN_W:
                    self.over_y(relation, 1).start()

        self.when(relation, action)

    def arrive_y(self, relation, column):
        def action():
            self.from_y(relation, column).wait_recv()
            self.far_to_core(relation, column).start()

        if (relation, column) != (OWN, 0):
            self.when(relation, action)

    def finish(self, array):
        for relation in range(RELATIONS):
            def action():
                if array != OUT_W or relation == OWN:
                    self.over_x(array, relation).wait_send()
                for way, holds in self.z_ways(relation):
                    pl.when(holds)(lambda way=way: self.along_z(array, relation, way).wait_send())
                if array == QKV_W:
                    return
                for column in range(2):
                    if (relation, column) == (OWN, 0) or (array == OUT_W and relation != OWN and column == 1):
                        continue
                    self.to_core(array, relation, column).wait()
                    if array == DOWN_W:
                        self.over_y(relation, column).wait_send()
                        self.far_to_core(relation, column).wait()

            self.when(relation, action)


def front_kernel(
    length_ref, tokens, read_rows, write_rows, qkv_in, vectors_in, up_in, down_in, out_in,
    small, up_bias, rows_out, weight_out, q_out, k_out, k_wide_out, v_wide_out, mixed_out, stats_out, up_full,
    down_full, out_full, attended,
    rows_ref, weight_ref, pieces, memory, q_x, k_t, k_wide, v_wide, v_x, mixed, mixed_low, row_stats,
    row_send, row_recv, far_send, far_recv, mix_send, mix_recv, local_sem, save_sem, head_sem, *gather_sems,
):
    place = Place()
    slot_rows, width = rows_ref.shape
    local_rows = tokens.shape[0]
    head_cols = k_t.shape[0]
    heads = head_cols // HEAD
    shard = width // 8
    length = length_ref[0]
    own_shards = {UP_W: up_in, DOWN_W: down_in, OUT_W: out_in}
    whole = {UP_W: up_full, DOWN_W: down_full, OUT_W: out_full, QKV_W: pieces}
    gather = Gather(place, own_shards, whole, gather_sems)

    memory[...] = jnp.zeros_like(memory)
    memory[:MEM, :] = read_rows[...]
    memory[16 : 16 + MEM, :] = write_rows[...]
    line = lax.broadcasted_iota(jnp.int32, (local_rows, 32), 1)
    at = place.s * local_rows + lax.broadcasted_iota(jnp.int32, (local_rows, 32), 0)
    wanted = jnp.where(line < 16, line, length - MEM + line - 16)
    used = (line < MEM) | ((line >= 16) & (line < 16 + MEM))
    pick = jnp.where(used & (wanted == at), 1.0, 0.0)
    taken = mul(pick.astype(low), memory[...]).astype(low)
    is_memory = jnp.sum(pick, axis=1, keepdims=True) > 0.5
    own_start = pl.multiple_of(place.s * local_rows, local_rows)
    rows_ref[pl.ds(own_start, local_rows), :] = jnp.where(is_memory, taken, tokens[...])
    for member in range(4):

        @pl.when(place.s == member)
        def _(member=member):
            for h in range(heads):
                for kind in range(3):
                    start = kind * width + (member * heads + h) * HEAD
                    to = (3 * h + kind) * HEAD
                    pieces[place.f, :, to : to + HEAD] = qkv_in[:, start : start + HEAD]

    columns = 3 * head_cols
    pieces[place.f, :, columns:] = jnp.zeros((shard, HEAD), low)
    for line in range(18):
        pieces[place.f, line : line + 1, columns:] = vectors_in[:, line * HEAD : (line + 1) * HEAD].astype(low)
    greet(place, False)

    halves = 2
    part = local_rows // halves

    def rows_of(member, half):
        return pl.ds(pl.multiple_of(member * local_rows + half * part, part), part)

    def send_rows(half, index):
        where = (place.core, place.across_y)[index]
        here = rows_ref.at[rows_of(place.s, half)]
        return remote(here, here, row_send.at[index, half], row_recv.at[index, half], where)

    def rows_from(half, index):
        member = (2 * place.y + 1 - place.c, 2 * (1 - place.y) + place.c)[index]
        here = rows_ref.at[rows_of(member, half)]
        where = (place.core, place.across_y)[index]
        return remote(here, here, row_send.at[index, half], row_recv.at[index, half], where)

    def pass_rows(half, arriving):
        flip = place.c if not arriving else 1 - place.c
        here = rows_ref.at[rows_of(2 * (1 - place.y) + flip, half)]
        return remote(here, here, far_send.at[half], far_recv.at[half], place.core)

    def own_copies():
        copies = []
        for index, array in enumerate((UP_W, DOWN_W, OUT_W)):
            rows = own_shards[array].shape[0]
            copies.append(pltpu.make_async_copy(
                own_shards[array], whole[array].at[pl.ds(pl.multiple_of(place.f * rows, rows), rows)],
                local_sem.at[index],
            ))
        return copies

    gather.arrive_z(QKV_W, OWN)
    for half in range(halves):
        send_rows(half, 1).start()
        send_rows(half, 0).start()
    gather.cross_out()
    for copy in own_copies():
        copy.start()
    for relation in (1, 4):
        gather.arrive_z(QKV_W, relation)
    gather.pair_out(own_copies()[2])
    for relation in (2, 5):
        gather.arrive_z(QKV_W, relation)
    gather.arrive_z(UP_W, OWN, across=False)
    rows_from(0, 1).wait_recv()
    pass_rows(0, False).start()
    for relation in (3, 6):
        gather.arrive_z(QKV_W, relation)
    gather.arrive_z(UP_W, OWN, along=False)
    gather.arrive_z(DOWN_W, OWN)
    for relation in range(RELATIONS):
        gather.arrive_x(QKV_W, relation)

    for source in range(8):
        weight_ref[source * shard : (source + 1) * shard, :] = pieces[source, :, :columns]
    tile = slice(columns - HEAD, columns + HEAD)
    bias_q = jnp.transpose(pieces[place.s, 0:16, tile].astype(full))[HEAD:]
    bias_v = jnp.transpose(pieces[4 + place.s, 0:16, tile].astype(full))[HEAD:]
    bias_q = jnp.concatenate([bias_q[:, h : h + 1] for h in range(heads)], axis=0)
    bias_v = jnp.concatenate([bias_v[:, h : h + 1] for h in range(heads)], axis=0)

    def project(member):
        start = pl.multiple_of(member * local_rows, local_rows)
        project_block(
            start, length, rows_ref, weight_ref, bias_q, bias_v, q_x, k_t, v_x, k_wide, v_wide, local_rows
        )

    project(place.s)
    for half in range(halves):
        rows_from(half, 0).wait_recv()
    project(2 * place.y + 1 - place.c)
    rows_from(1, 1).wait_recv()
    pass_rows(1, False).start()
    for relation in (1, 4):
        gather.arrive_z(UP_W, relation)
        gather.arrive_z(OUT_W, relation)
    project(2 * (1 - place.y) + place.c)
    for relation in (1, 4):
        gather.arrive_z(DOWN_W, relation)

    def scatter_vector(target, index, size, first):
        for source in range(8):
            done = 0
            while done < size:
                line, lane = divmod(first + done, HEAD)
                count = min(HEAD - lane, size - done)
                target[index : index + 1, source * size + done : source * size + done + count] = pieces[
                    source, line : line + 1, columns + lane : columns + lane + count
                ].astype(full)
                done += count

    for index, first in enumerate((2, 3, 4, 9, 10, 11)):
        scatter_vector(small, index, shard, first * shard)
    scatter_vector(up_bias, 0, 4 * shard, 5 * shard)
    for half in range(halves):
        pass_rows(half, True).wait_recv()
    project(2 * (1 - place.y) + 1 - place.c)

    def saves():
        pairs = [(rows_ref, rows_out), (weight_ref, weight_out), (k_t, k_out), (k_wide, k_wide_out), (v_wide, v_wide_out)]
        pairs += [(q_x.at[h, pl.ds(0, HEAD)], q_out.at[h]) for h in range(heads)]
        return [pltpu.make_async_copy(src, dst, save_sem.at[index]) for index, (src, dst) in enumerate(pairs)]

    for save in saves():
        save.start()

    def head_saves(h):
        own = pl.ds(h * HEAD, HEAD)
        return [
            pltpu.make_async_copy(mixed.at[own], mixed_out.at[own], head_sem.at[h, 0]),
            pltpu.make_async_copy(row_stats.at[h], stats_out.at[h], head_sem.at[h, 1]),
        ]

    def chores(step):
        if step == 1:
            gather.arrive_x(UP_W, OWN)
        elif step == 2:
            for relation in (2, 5):
                gather.arrive_z(UP_W, relation)
            gather.arrive_x(DOWN_W, OWN)
        elif step == 3:
            for relation in (1, 4):
                gather.arrive_y(relation, 0)
        elif step == 4:
            for relation in (2, 5):
                gather.arrive_z(OUT_W, relation)
            for save in head_saves(0):
                save.start()
        elif step == 5:
            for relation in (2, 5):
                gather.arrive_z(DOWN_W, relation)
            gather.arrive_y(OWN, 1)
        elif step == 6:
            for relation in (1, 4):
                gather.arrive_x(UP_W, relation)
        elif step == 8:
            for relation in (2, 5):
                gather.arrive_y(relation, 0)
            for save in head_saves(1):
                save.start()
        elif step == 9:
            for relation in (3, 6):
                gather.arrive_z(UP_W, relation)
            for relation in (2, 5):
                gather.arrive_x(UP_W, relation)
        elif step == 11:
            for relation in (3, 6):
                gather.arrive_z(OUT_W, relation)
                gather.arrive_z(DOWN_W, relation)
            for relation in (1, 4):
                gather.arrive_x(DOWN_W, relation)

    def send_mixed(h, turn, arriving=False):
        member = place.member(turn)
        own = pl.ds(pl.multiple_of(h * HEAD, HEAD), HEAD)
        lanes = pl.ds(pl.multiple_of(member * local_rows, local_rows), local_rows)
        owner = member if arriving else place.s
        there = attended.at[pl.ds(pl.multiple_of(owner * head_cols + h * HEAD, HEAD), HEAD)]
        return remote(
            mixed_low.at[own, lanes], there, mix_send.at[h, turn], mix_recv.at[h, turn], (place.f, member)
        )

    def keep_mixed(h):
        own = pl.ds(pl.multiple_of(h * HEAD, HEAD), HEAD)
        lanes = pl.ds(pl.multiple_of(place.s * local_rows, local_rows), local_rows)
        there = attended.at[pl.ds(pl.multiple_of(place.s * head_cols + h * HEAD, HEAD), HEAD)]
        return pltpu.make_async_copy(mixed_low.at[own, lanes], there, mix_send.at[h, 3])

    turns = slot_rows // local_rows

    def pass_on(index):
        h, turn = index // turns, lax.rem(index, turns)

        @pl.when(turn < turns - 1)
        def _():
            send_mixed(h, turn).start()

        @pl.when(turn == turns - 1)
        def _():
            keep_mixed(h).start()

    def step(index, carry):
        for when in range(12):
            pl.when(index == when)(lambda when=when: chores(when))
        h, turn = index // turns, lax.rem(index, turns)
        start = pl.multiple_of(place.member(turn) * local_rows, local_rows)
        attend_block(h, pl.ds(start, local_rows), q_x, k_wide, v_x, mixed, mixed_low, row_stats)

        @pl.when(index > 0)
        def _():
            pass_on(index - 1)

        return carry

    lax.fori_loop(0, heads * turns, step, 0)
    pass_on(heads * turns - 1)
    for save in head_saves(2):
        save.start()
    for relation in (3, 6):
        gather.arrive_x(UP_W, relation)
    for relation in (2, 5):
        gather.arrive_x(DOWN_W, relation)
    for relation in (1, 4):
        gather.arrive_y(relation, 1)
    for relation in (3, 6):
        gather.arrive_y(relation, 0)
        gather.arrive_x(DOWN_W, relation)
    for relation in (2, 5, 3, 6):
        gather.arrive_y(relation, 1)
    for array in (UP_W, OUT_W, DOWN_W, QKV_W):
        gather.finish(array)
    for copy in own_copies()[:2]:
        copy.wait()
    for half in range(halves):
        for index in range(2):
            send_rows(half, index).wait_send()
        pass_rows(half, False).wait_send()
    for h in range(heads):
        for turn in range(turns - 1):
            send_mixed(h, turn).wait_send()
            send_mixed(h, turn, True).wait_recv()
        keep_mixed(h).wait()
        for save in head_saves(h):
            save.wait()
    for save in saves():
        save.wait()


def front(lengths, tokens, read_rows, write_rows, qkv_shard, vectors, up_weight, down_weight, out_weight):
    local_rows, width = tokens.shape
    slot_rows = local_rows * 4
    head_cols = width // 4
    heads = head_cols // HEAD
    shard = width // 8
    vmem = pl.BlockSpec(memory_space=pltpu.VMEM)
    anywhere = pl.BlockSpec(memory_space=pl.ANY)
    dma = pltpu.SemaphoreType.DMA
    hidden = up_weight.shape[1]

    def held(*shape, kind=low):
        return pltpu.VMEM(shape, kind)

    def shaped(*shape, kind=low):
        return jax.ShapeDtypeStruct(shape, kind)

    return pl.pallas_call(
        front_kernel,
        in_specs=[pl.BlockSpec(memory_space=pltpu.SMEM)] + [vmem] * 8,
        out_specs=[vmem] * 2 + [anywhere] * 12,
        out_shape=[
            shaped(8, width, kind=full), shaped(8, hidden, kind=full),
            shaped(slot_rows, width), shaped(width, 3 * head_cols), shaped(heads, HEAD, slot_rows),
            shaped(head_cols, slot_rows), shaped(heads, slot_rows, WIDE), shaped(heads, slot_rows, WIDE),
            shaped(head_cols, slot_rows, kind=full), shaped(heads, 8, slot_rows, kind=full),
            shaped(width, hidden), shaped(hidden, width), shaped(width, width), shaped(width, local_rows),
        ],
        scratch_shapes=[
            held(slot_rows, width), held(width, 3 * head_cols), held(8, shard, 3 * head_cols + HEAD),
            held(32, width), held(heads, WIDE, slot_rows), held(head_cols, slot_rows),
            held(heads, slot_rows, WIDE), held(heads, slot_rows, WIDE), held(heads, WIDE, slot_rows),
            held(head_cols, slot_rows, kind=full), held(head_cols, slot_rows), held(heads, 8, slot_rows, kind=full),
            dma((2, 2)), dma((2, 2)), dma((2,)), dma((2,)), dma((heads, 4)), dma((heads, 4)), dma((3,)),
            dma((5 + heads,)), dma((heads, 2)),
            dma((4, 2, 3)), dma((4, 2, 3)), dma((4, 7)), dma((4, 7)), dma((3, 7, 2)), dma((3, 7, 2)),
            dma((7, 2)), dma((7, 2)), dma((7, 2)), dma((7, 2)),
        ],
        compiler_params=pltpu.CompilerParams(
            vmem_limit_bytes=VMEM_BYTES, collective_id=0, has_side_effects=True
        ),
        name="front",
    )(lengths, tokens, read_rows, write_rows, qkv_shard, vectors, up_weight, down_weight, out_weight)


DW_FIRST = 3
LINES = (3, 0, 2, 1)


def add_low(left, right):
    return (left.astype(full) + right.astype(full)).astype(low)


class Reduce:
    def __init__(self, place, given, sums, across, from_y, from_x, from_z, last, sems):
        self.across, self.last, self.far_up = across, last, last + 1
        self.place, self.given, self.sums = place, given, sums
        self.from_y, self.from_x, self.from_z = from_y, from_x, from_z
        self.y_send, self.y_recv, self.x_send, self.x_recv, self.z_send, self.z_recv = sems

    def dest(self, column, line):
        x = self.place.x
        return 2 * line + (x if column == 0 else 1 - x)

    def slot(self, array, line, column=0):
        if DW_FIRST <= array <= self.last:
            rows = 4 * HEAD if array == self.last else 3 * HEAD
            return self.sums[array].at[self.dest(column, line), pl.ds(0, rows // 4)]
        return self.sums[array].at[line]

    def cut(self, array, ref):
        if DW_FIRST <= array < self.last:
            return ref.at[pl.ds(0, 3 * HEAD // 4)]
        return ref

    def load(self, array, column, line, sem):
        if array == OUT_W:
            return pltpu.make_async_copy(self.given[array].at[line, 0], self.sums[array].at[line], sem)
        source = self.given[UP_W if array == self.far_up else array].at[column, line, 1 if array == self.far_up else 0]
        target = self.across if column == 1 else self.sums[array]
        return pltpu.make_async_copy(source, target.at[line], sem)

    def over_y(self, array, line):
        column, index = (1, 1) if array == UP_W else (0, 0)
        return remote(
            self.given[array].at[column, line, 1], self.from_y.at[index, line], self.y_send.at[index, line],
            self.y_recv.at[index, line], self.place.across_y,
        )

    def add_y(self, array, line):
        self.over_y(array, line).wait_recv()
        slot = self.across.at[line] if array == UP_W else self.slot(DOWN_W, line)
        slot[...] = add_low(slot[...], self.from_y[1 if array == UP_W else 0, line])

    def over_x(self, array, line):
        if array == OUT_W:
            start = self.given[array].at[line, 1]
        elif array == UP_W:
            start = self.across.at[line]
        elif array == DOWN_W:
            start = self.given[array].at[1, line, 0]
        else:
            start = self.slot(array, line, 1)
        return remote(
            start, self.cut(array, self.from_x[array].at[line]), self.x_send.at[array, line],
            self.x_recv.at[array, line], self.place.across_x,
        )

    def add_x(self, array, line):
        self.over_x(array, line).wait_recv()
        slot = self.slot(array, line)
        slot[...] = add_low(slot[...], self.cut(array, self.from_x[array].at[line])[...])

    def along_z(self, array, way, line):
        return remote(
            self.slot(array, line), self.cut(array, self.from_z[array].at[way, line]),
            self.z_send.at[array, way, line], self.z_recv.at[array, way, line],
            self.place.above if way == 0 else self.place.below,
        )

    def add_z(self, array, way, line):
        self.along_z(array, way, line).wait_recv()
        slot = self.slot(array, line)
        slot[...] = add_low(slot[...], self.cut(array, self.from_z[array].at[way, line])[...])

    def hop(self, array, level, lines=(0, 1, 2, 3)):
        @pl.when(self.place.z == level)
        def _():
            for line in range(3, level, -1):
                if line in lines:
                    if level > 0:
                        self.add_z(array, 0, line)
                    self.along_z(array, 0, line).start()

        @pl.when(self.place.z == 3 - level)
        def _():
            for line in range(0, 3 - level):
                if line in lines:
                    if level > 0:
                        self.add_z(array, 1, line)
                    self.along_z(array, 1, line).start()

    def direct(self, array):
        return array != self.far_up

    def to_line(self, array, line):
        where = (2 * line + self.place.x, self.place.s)
        return remote(
            self.slot(array, line), self.cut(array, self.from_z[array].at[self.place.z]),
            self.z_send.at[array, 0, line], self.z_recv.at[array, 0, self.place.z], where,
        )

    def fling(self, array, lines=LINES):
        for line in lines:
            pl.when(self.place.z != line)(lambda line=line: self.to_line(array, line).start())

    def settle(self, array):
        if self.direct(array):
            slot = self.slot(array, self.place.z)
            for line in range(4):

                @pl.when(self.place.z != line)
                def _(line=line):
                    came = self.cut(array, self.from_z[array].at[line])
                    remote(
                        came, came, self.z_send.at[array, 0, line], self.z_recv.at[array, 0, line], self.place.core
                    ).wait_recv()
                    slot[...] = add_low(slot[...], came[...])

            return
        for line in range(4):

            @pl.when(self.place.z == line)
            def _(line=line):
                if line > 0:
                    self.add_z(array, 0, line)
                if line < 3:
                    self.add_z(array, 1, line)

    def finish(self, array):
        for line in range(4):
            if array != self.far_up:
                self.over_x(array, line).wait_send()
            if self.direct(array):
                pl.when(self.place.z != line)(lambda line=line: self.to_line(array, line).wait_send())
            else:
                pl.when(self.place.z < line)(lambda line=line: self.along_z(array, 0, line).wait_send())
                pl.when(self.place.z > line)(lambda line=line: self.along_z(array, 1, line).wait_send())
            if array in (UP_W, DOWN_W):
                self.over_y(array, line).wait_send()


class Spread:
    def __init__(self, place, blocks, source, send, recv):
        self.place, self.blocks, self.source, self.send, self.recv = place, blocks, source, send, recv
        self.near = 2 * place.y + 1 - place.c
        self.far = 2 * (1 - place.y) + place.c
        self.last = 2 * (1 - place.y) + 1 - place.c

    def copy(self, kind, arriving=False):
        place = self.place
        if kind == 2:
            here = self.blocks.at[self.last if arriving else self.far]
            return remote(here, here, self.send.at[2], self.recv.at[2], place.core)
        member = (self.near, self.far)[kind] if arriving else place.s
        return remote(
            self.source, self.blocks.at[member], self.send.at[kind], self.recv.at[kind],
            (place.core, place.across_y)[kind],
        )

    def start(self):
        self.copy(1).start()
        self.copy(0).start()

    def pass_on(self):
        self.copy(1, True).wait_recv()
        self.copy(2).start()

    def finish(self):
        self.blocks[self.place.s] = self.source[...]
        self.copy(0, True).wait_recv()
        self.copy(2, True).wait_recv()
        for kind in range(3):
            self.copy(kind).wait_send()


def back_kernel(
    length_ref, grad_own, vectors_in, q_in, k_in, k_wide_in, v_wide_in, mixed_in, stats_in, rows_in, weight_in, resid_in, up_given, down_given, out_given,
    input_out, read_out, write_out, qkv_out, vector_out, up_out, down_out, out_out,
    q_x, k_t, k_wide, v_wide, mixed, row_stats, grad_t, q_here, do_x, grads, grad_k, grad_v, rows_ref, weight_ref, resid_ref,
    up_sum, out_sum, down_sum, far_sum_up, across_up, dw, both_y, up_x, out_x, down_x, dw_x, up_z, out_z, down_z, dw_z, far_z,
    up_last, out_last, up_all, out_other, down_all, dw_all,
    near_send, near_recv, far_sum, far_recv, memory_all, memory_own,
    mix_send, mix_recv, local_sem, saved_sem, mine_sem, share_send, share_recv, near_s, near_r, far_s, far_r, cross_s, cross_r,
    *sems,
):
    place = Place()
    heads, _, slot_rows = q_in.shape
    width, local_rows = grad_own.shape
    head_cols = heads * HEAD
    last = DW_FIRST + heads - 1
    far_up = last + 1
    given = {UP_W: up_given, OUT_W: out_given, DOWN_W: down_given}
    sums = {UP_W: up_sum, OUT_W: out_sum, DOWN_W: down_sum}
    from_x = {UP_W: up_x, OUT_W: out_x, DOWN_W: down_x}
    from_z = {UP_W: up_z, OUT_W: out_z, DOWN_W: down_z}
    for h in range(heads):
        sums[DW_FIRST + h], from_x[DW_FIRST + h] = dw.at[h], dw_x.at[h]
        from_z[DW_FIRST + h] = dw_z.at[h]
    sums[far_up], from_z[far_up] = far_sum_up, far_z
    reduce = Reduce(place, given, sums, across_up, both_y, from_x, from_z, last, sems)
    greet(place, True)

    peers = (place.across_y, place.diagonal, place.core)

    def member_rows(turn):
        member = place.member(turn)
        return member, pl.ds(pl.multiple_of(member * local_rows, local_rows), local_rows)

    def send_grad(turn, arriving=False):
        member, lanes = member_rows(turn)
        own_lanes = pl.ds(pl.multiple_of(place.s * local_rows, local_rows), local_rows)
        src = grad_own.at[pl.ds(pl.multiple_of(member * head_cols, head_cols), head_cols)]
        return remote(
            src, grad_t.at[:, lanes if arriving else own_lanes], mix_send.at[turn], mix_recv.at[turn], peers[turn]
        )

    def saved_loads(h):
        own = pl.ds(h * HEAD, HEAD)
        pairs = (
            (k_wide_in.at[h], k_wide.at[h]), (q_in.at[h], q_x.at[h]), (v_wide_in.at[h], v_wide.at[h]),
            (mixed_in.at[own], mixed.at[own]), (stats_in.at[h], row_stats.at[h]), (k_in.at[own], k_t.at[own]),
        )
        return [pltpu.make_async_copy(src, dst, saved_sem.at[h, i]) for i, (src, dst) in enumerate(pairs)]

    def sum_loads(array):
        index = array if array < DW_FIRST else DW_FIRST
        return [reduce.load(array, 0, line, mine_sem.at[index, line]) for line in LINES]

    def across_loads():
        return [reduce.load(UP_W, 1, line, mine_sem.at[DW_FIRST + 1, line]) for line in LINES]

    for turn in range(3):
        send_grad(turn).start()
    for load in sum_loads(far_up):
        load.start()
    for load in saved_loads(0):
        load.start()
    loads = []
    for index, (src, dst) in enumerate(((rows_in, rows_ref), (weight_in, weight_ref), (resid_in, resid_ref))):
        loads.append(pltpu.make_async_copy(src, dst, local_sem.at[index]))

    def send_x(array, lines=LINES):
        for line in lines:
            reduce.over_x(array, line).start()

    send_x(DOWN_W)
    send_x(OUT_W)
    for array in (DOWN_W, UP_W):
        for line in LINES:
            reduce.over_y(array, line).start()
    for load in across_loads() + sum_loads(UP_W) + sum_loads(OUT_W) + sum_loads(DOWN_W):
        load.start()
    for load in loads:
        load.start()

    for h in range(1, heads):
        for load in saved_loads(h):
            load.start()

    own_lanes = pl.ds(pl.multiple_of(place.s * local_rows, local_rows), local_rows)
    grad_t[:, own_lanes] = grad_own[pl.ds(pl.multiple_of(place.s * head_cols, head_cols), head_cols), :]

    def take_x(array, lines=LINES):
        for line in lines:
            reduce.add_x(array, line)

    turns = slot_rows // local_rows

    def weight_part(h):
        if h == 0:
            loads[0].wait()
        base = 3 * h * HEAD
        part = jnp.transpose(mul(grads[base : base + 3 * HEAD, :], rows_ref[...])).astype(low)
        half = width // 16
        for dest in range(8):
            start = 2 * half * dest
            dw[h, dest, :half, :] = jnp.concatenate(
                [part[start : start + half], part[start + half : start + 2 * half]], axis=1
            )
            if h == heads - 1:
                dw[h, dest, half:, :] = vectors_in[dest].astype(low)
        if h == heads - 1:
            total = jnp.sum(grads[...].astype(full), axis=1, keepdims=True)
            spread = jnp.transpose(jnp.broadcast_to(total, (total.shape[0], WIDE)))[0:1]
            for kind, first_dest in ((0, 0), (2, 4)):
                for head in range(heads):
                    start = (3 * head + kind) * HEAD
                    dw[h, first_dest + place.s, half : half + 1, head * HEAD : (head + 1) * HEAD] = spread[
                        :, start : start + HEAD
                    ].astype(low)
        send_x(DW_FIRST + h)

    share = {OUT_W: (out_last, out_other)}

    def settled(array):
        return sums[array].at[place.z]

    def sum_y(array):
        mine_now = settled(array)
        return remote(mine_now, share[array][0], share_send.at[array, 0], share_recv.at[array, 0], place.across_y)

    def half_to_core(array):
        mine_now = settled(array)
        return remote(mine_now, share[array][1], share_send.at[array, 1], share_recv.at[array, 1], place.core)

    def spread_of(array):
        if array in (UP_W, DOWN_W):
            return Spread(
                place, {UP_W: up_all, DOWN_W: down_all}[array], sums[array].at[place.z], share_send.at[array],
                share_recv.at[array],
            )
        h = array - DW_FIRST
        return Spread(
            place, dw_all.at[h, :, pl.ds(0, reduce.slot(array, 0).shape[0])], reduce.slot(array, place.z),
            share_send.at[array], share_recv.at[array],
        )

    def cross_up():
        return remote(far_sum_up.at[place.z], up_last, cross_s.at[0], cross_r.at[0], place.across_y)

    def settle_up():
        reduce.settle(UP_W)
        cross_up().wait_recv()
        slot = sums[UP_W].at[place.z]
        slot[...] = add_low(slot[...], up_last[...])
        spread_of(UP_W).start()

    def add_last(array):
        sum_y(array).wait()
        slot = settled(array)
        slot[...] = add_low(slot[...], share[array][0][...])
        half_to_core(array).start()

    first, second = DW_FIRST, DW_FIRST + 1

    def pass_up(lines):
        for line in lines:
            reduce.add_y(UP_W, line)
            reduce.over_x(UP_W, line).start()

    def chores(index):
        if index == 1:
            send_grad(2, True).wait_recv()
            for load in across_loads() + sum_loads(UP_W) + sum_loads(OUT_W) + sum_loads(DOWN_W):
                load.wait()
        elif index == 2:
            send_grad(1, True).wait_recv()
            reduce.hop(far_up, 1, (3, 0))
        elif index == 3:
            send_grad(0, True).wait_recv()
            reduce.hop(far_up, 1, (2, 1))
        elif index == 4:
            for load in saved_loads(1):
                load.wait()
            weight_part(0)
            reduce.hop(far_up, 2)
        elif index == 5:
            take_x(DOWN_W)
            for line in (3, 0):
                reduce.add_y(DOWN_W, line)
                reduce.fling(DOWN_W, (line,))
        elif index == 6:
            for line in (2, 1):
                reduce.add_y(DOWN_W, line)
                reduce.fling(DOWN_W, (line,))
            take_x(OUT_W)
            reduce.fling(OUT_W)
            reduce.settle(far_up)
            cross_up().start()
        elif index == 7:
            take_x(first)
            reduce.fling(first)
        elif index == 8:
            for load in saved_loads(2):
                load.wait()
            weight_part(1)
            pass_up((3, 0))
        elif index == 9:
            pass_up((2,))
        elif index == 10:
            pass_up((1,))
            reduce.settle(DOWN_W)
            spread_of(DOWN_W).start()
        elif index == 11:
            take_x(UP_W, (3, 0))
            reduce.fling(UP_W, (3, 0))
            take_x(second)
            reduce.fling(second)

    def step(index, carry):
        for when in range(1, 12):
            pl.when(index == when)(lambda when=when: chores(when))
        h, turn = index // turns, lax.rem(index, turns)
        _, lanes = member_rows(turns - 1 - turn)
        attend_back(
            h, lanes, q_x, q_here, do_x, grad_t, mixed, row_stats, k_t, k_wide, v_wide, grads, grad_k, grad_v, turn == 0
        )

        @pl.when(turn == turns - 1)
        def _():
            base = pl.multiple_of(3 * h * HEAD, HEAD)
            grads[pl.ds(base + HEAD, HEAD), :] = grad_k[...].astype(low)
            grads[pl.ds(base + 2 * HEAD, HEAD), :] = grad_v[...].astype(low)

        return carry

    for load in sum_loads(far_up):
        load.wait()
    reduce.hop(far_up, 0)
    for load in saved_loads(0):
        load.wait()
    lax.fori_loop(0, heads * turns, step, 0)

    loads[1].wait()
    loads[2].wait()

    halves, part = 2, local_rows // 2
    length = length_ref[0]

    def memory_pick(rows, start):
        line = lax.broadcasted_iota(jnp.int32, (32, rows), 0)
        row = start + lax.broadcasted_iota(jnp.int32, (32, rows), 1)
        wanted = jnp.where(line < 16, line, length - MEM + line - 16)
        used = (line < MEM) | ((line >= 16) & (line < 16 + MEM))
        return jnp.where(used & (wanted == row), 1.0, 0.0).astype(low)

    def part_for(turn, half):
        start = pl.multiple_of(place.member(turn) * local_rows + half * part, part)
        return mul(grads[:, pl.ds(start, part)], weight_ref[...], TT)

    def share_near(index, half):
        rows = pl.ds(half * part, part)
        return remote(
            near_send.at[index, rows], near_recv.at[index, rows], near_s.at[index, half], near_r.at[index, half],
            place.core,
        )

    def share_far(half):
        rows = pl.ds(half * part, part)
        return remote(far_sum.at[rows], far_recv.at[rows], far_s.at[half], far_r.at[half], place.across_y)

    for half in range(halves):
        near_send[0, half * part : (half + 1) * part, :] = part_for(1, half).astype(low)
        share_near(0, half).start()
    for half in range(halves):
        rows = slice(half * part, (half + 1) * part)
        far_part = part_for(0, half)
        share_near(0, half).wait_recv()
        far_sum[rows, :] = (far_part + near_recv[0, rows, :].astype(full)).astype(low)
        share_far(half).start()
    reduce.settle(OUT_W)
    sum_y(OUT_W).start()
    weight_part(heads - 1)
    take_x(UP_W, (2, 1))
    reduce.fling(UP_W, (2, 1))
    taken = mul(memory_pick(slot_rows, 0), grads[...], NT).astype(low)
    own_part = mul(memory_pick(local_rows, place.s * local_rows), resid_ref[...].astype(low))
    memory_own[...] = (mul(taken, weight_ref[...], NT) + own_part).astype(low)
    memory = Spread(place, memory_all, memory_own, share_send.at[DW_FIRST + heads], share_recv.at[DW_FIRST + heads])
    memory.start()
    for half in range(halves):
        rows = slice(half * part, (half + 1) * part)
        near_send[1, rows, :] = part_for(2, half).astype(low)
        share_near(1, half).start()
    for half in range(halves):
        resid_ref[half * part : (half + 1) * part, :] += part_for(3, half)
    take_x(last)
    reduce.fling(last)
    reduce.settle(first)
    spread_of(first).start()
    add_last(OUT_W)
    reduce.settle(second)
    spread_of(second).start()
    settle_up()
    reduce.settle(last)
    spread_of(last).start()
    memory.pass_on()
    for h in (heads - 1, 0, 1):
        spread_of(DW_FIRST + h).pass_on()
    for array in (UP_W, DOWN_W):
        spread_of(array).pass_on()
    for array, out in ((OUT_W, out_out),):
        columns = out.shape[1] // 2
        out[:, pl.ds(pl.multiple_of(place.c * columns, columns), columns)] = settled(array)[...]
        half_to_core(array).wait()
        out[:, pl.ds(pl.multiple_of((1 - place.c) * columns, columns), columns)] = share[array][1][...]
    for h in range(heads):
        spread_of(DW_FIRST + h).finish()
    spread_of(UP_W).finish()
    spread_of(DOWN_W).finish()
    quarter = down_out.shape[0] // 4
    part_columns = up_out.shape[1] // 4
    for member in range(4):
        start = (2 * (member % 2) + member // 2) * part_columns
        up_out[:, start : start + part_columns] = up_all[member]
        down_out[member * quarter : (member + 1) * quarter, :] = down_all[member]
    half = qkv_out.shape[0] // 2
    for kind in range(3):
        for member in range(4):
            for h in range(heads):
                start = kind * width + (member * heads + h) * HEAD
                for side in range(2):
                    lanes = (3 * side + kind) * HEAD
                    qkv_out[side * half : (side + 1) * half, start : start + HEAD] = dw_all[
                        h, member, :half, lanes : lanes + HEAD
                    ]
    vector_sum = dw_all[heads - 1, 0, half:, :].astype(full)
    for member in range(1, 4):
        vector_sum = vector_sum + dw_all[heads - 1, member, half:, :].astype(full)
    vector_out[...] = vector_sum
    memory.finish()
    total = memory_all[0].astype(full)
    for member in range(1, 4):
        total = total + memory_all[member].astype(full)
    read_out[...] = total[:MEM]
    write_out[...] = total[16 : 16 + MEM]
    for half in range(halves):
        rows = slice(half * part, (half + 1) * part)
        share_near(1, half).wait_recv()
        share_far(half).wait_recv()
        grad_layer = resid_ref[rows, :] + near_recv[1, rows, :].astype(full) + far_recv[rows, :].astype(full)
        rows_at = place.s * local_rows + half * part + lax.broadcasted_iota(jnp.int32, (part, 1), 0)
        in_write = (rows_at >= length - MEM) & (rows_at < length)
        input_out[rows, :] = jnp.where((rows_at < MEM) | in_write, 0.0, grad_layer)
    for array in range(DW_FIRST + heads + 1):
        reduce.finish(array)
    cross_up().wait_send()
    for turn in range(3):
        send_grad(turn).wait_send()
    for half in range(halves):
        for index in range(2):
            share_near(index, half).wait_send()
        share_far(half).wait_send()


def back(lengths, grad_own, saved, vectors, rows, weight, resid, up_given, down_given, out_given):
    q_x, k_t, k_wide, v_wide, mixed, row_stats = saved
    heads, _, slot_rows = q_x.shape
    width, local_rows = grad_own.shape
    hidden = 32 * up_given.shape[3]
    shard, head_cols = width // 8, heads * HEAD
    half, small, piece = hidden // 2, width // 2, hidden // 32
    vmem = pl.BlockSpec(memory_space=pltpu.VMEM)
    anywhere = pl.BlockSpec(memory_space=pl.ANY)
    dma = pltpu.SemaphoreType.DMA
    arrays = DW_FIRST + heads

    def held(*shape, kind=low):
        return pltpu.VMEM(shape, kind)

    tall = (shard // 2 + 16, 6 * HEAD)
    return pl.pallas_call(
        back_kernel,
        in_specs=[pl.BlockSpec(memory_space=pltpu.SMEM)] + [vmem] * 2 + [anywhere] * 12,
        out_specs=[vmem] * 8,
        out_shape=[
            jax.ShapeDtypeStruct((local_rows, width), full),
            jax.ShapeDtypeStruct((MEM, width), full),
            jax.ShapeDtypeStruct((MEM, width), full),
            jax.ShapeDtypeStruct((shard, 3 * width), low),
            jax.ShapeDtypeStruct((16, 6 * HEAD), full),
            jax.ShapeDtypeStruct((shard, hidden), low),
            jax.ShapeDtypeStruct((hidden // 8, width), low),
            jax.ShapeDtypeStruct((shard, width), low),
        ],
        scratch_shapes=[
            held(heads, HEAD, slot_rows), held(head_cols, slot_rows), held(heads, slot_rows, WIDE),
            held(heads, slot_rows, WIDE), held(head_cols, slot_rows, kind=full), held(heads, 8, slot_rows, kind=full),
            held(head_cols, slot_rows), held(WIDE, local_rows), held(WIDE, local_rows), held(3 * head_cols, slot_rows),
            held(HEAD, slot_rows, kind=full), held(HEAD, slot_rows, kind=full),
            held(slot_rows, width), held(width, 3 * head_cols), held(local_rows, width, kind=full),
            held(4, piece, width), held(4, shard, small), held(4, piece, width), held(4, piece, width),
            held(4, piece, width), held(heads, 8, *tall), held(2, 4, piece, width),
            held(4, piece, width), held(4, shard, small), held(4, piece, width), held(heads, 4, *tall),
            held(4, piece, width), held(4, shard, small), held(4, piece, width), held(heads, 4, *tall),
            held(2, 4, piece, width),
            held(piece, width), held(shard, small), held(4, piece, width), held(shard, small),
            held(4, piece, width), held(heads, 4, *tall),
            held(2, local_rows, width), held(2, local_rows, width), held(local_rows, width),
            held(local_rows, width), held(4, 32, width), held(32, width),
            dma((3,)), dma((3,)), dma((3,)), dma((heads, 6)), dma((5, 4)), dma((arrays + 1, 3)),
            dma((arrays + 1, 3)), dma((2, 2)), dma((2, 2)), dma((2,)), dma((2,)),
            dma((1,)), dma((1,)),
            dma((2, 4)), dma((2, 4)), dma((arrays, 4)), dma((arrays, 4)),
            dma((arrays + 1, 2, 4)), dma((arrays + 1, 2, 4)),
        ],
        compiler_params=pltpu.CompilerParams(
            vmem_limit_bytes=VMEM_BYTES, collective_id=1, has_side_effects=True
        ),
        name="back",
    )(
        lengths, grad_own, vectors, q_x, k_t, k_wide, v_wide, mixed, row_stats, rows, weight, resid,
        up_given, down_given, out_given,
    )


def phi_parts(value):
    normal = 0.5 * (1.0 + lax.erf(value * (0.5**0.5)))
    density = jnp.exp(-0.5 * value * value) * (0.5 * 2.0**0.5 * 3.141592653589793**-0.5)
    return normal, normal + value * density


def statistics(values):
    centre = values - jnp.mean(values, axis=1, keepdims=True)
    factor = lax.rsqrt(jnp.mean(centre * centre, axis=1, keepdims=True) + norm_epsilon)
    return centre * factor, factor


def norm_back(grad, gain, normed, factor):
    scaled = grad * gain
    first = jnp.mean(scaled, axis=1, keepdims=True)
    second = jnp.mean(scaled * normed, axis=1, keepdims=True)
    return factor * (scaled - first - normed * second)


def column_total(values):
    return jnp.sum(values, axis=0, keepdims=True)


def middle_kernel(
    length_ref, cotangent, small, up_bias, rows_in, attended_in, up_in, down_in, out_in,
    output, resid_out, grad_own, vector_out, up_out, down_out, out_out,
    layer_in, attended, up_w, down_w, out_w, hidden, slope, normed_one, middle_low, grad_down,
    grad_two, grad_mid, totals, up_total, up_grad, down_grad, out_grad, up_sum, down_sum, out_sum,
    from_y, load_sem, save_sem, c_send, c_recv, y_send, y_recv,
):
    place = Place()
    rows, width = cotangent.shape
    ff = up_w.shape[1]
    chunk = ff // 4
    shard = width // 8
    barrier = pltpu.get_barrier_semaphore()
    for where in (place.core, place.across_y):
        pl.semaphore_signal(barrier, inc=1, device_id=where, device_id_type=MESH)

    def chunk_lanes(j):
        return pl.ds(pl.multiple_of(j * chunk, chunk), chunk)

    def up_load(j):
        return pltpu.make_async_copy(up_in.at[:, chunk_lanes(j)], up_w.at[:, chunk_lanes(j)], load_sem.at[j])

    def down_load(j):
        return pltpu.make_async_copy(down_in.at[chunk_lanes(j)], down_w.at[chunk_lanes(j)], load_sem.at[4 + j])

    first_loads = [
        pltpu.make_async_copy(
            rows_in.at[pl.ds(pl.multiple_of(place.s * rows, rows), rows)], layer_in, load_sem.at[8]
        ),
        pltpu.make_async_copy(attended_in, attended, load_sem.at[9]),
        pltpu.make_async_copy(out_in, out_w, load_sem.at[10]),
    ]
    for load in first_loads:
        load.start()
    for j in range(4):
        up_load(j).start()
        down_load(j).start()
    out_bias, gain_one, shift_one = small[0:1, :], small[1:2, :], small[2:3, :]
    down_bias, gain_two, shift_two = small[3:4, :], small[4:5, :], small[5:6, :]
    for load in first_loads:
        load.wait()

    branch = mul(attended[...], out_w[...], TN)
    normed, factor_one = statistics(layer_in[...].astype(full) + branch + out_bias)
    normed_one[...] = normed
    middle_low[...] = (normed * gain_one + shift_one).astype(low)
    grad_mid[...] = jnp.zeros_like(grad_mid)

    def forward_chunk(j, carry):
        up_load(j).wait()
        lanes = chunk_lanes(j)
        value = mul(middle_low[...], up_w[:, lanes]) + up_bias[0:1, lanes]
        normal, slope_here = phi_parts(value)
        hidden[:, lanes] = (value * normal).astype(low)
        slope[:, lanes] = slope_here
        down_load(j).wait()
        grad_mid[...] += mul(hidden[:, lanes], down_w[lanes, :])
        return carry

    lax.fori_loop(0, 4, forward_chunk, 0)
    middle = normed_one[...] * gain_one + shift_one
    normed_two, factor_two = statistics(middle + grad_mid[...] + down_bias)
    places = place.s * rows + lax.broadcasted_iota(jnp.int32, (rows, 1), 0)
    in_slot = places < length_ref[0]
    output[...] = jnp.where(in_slot, normed_two * gain_two + shift_two, 0.0).astype(low)
    grad_final = jnp.where(in_slot, cotangent[...].astype(full), 0.0)
    totals[4:5, :] = column_total(grad_final * normed_two)
    totals[5:6, :] = column_total(grad_final)
    grad_resid = norm_back(grad_final, gain_two, normed_two, factor_two)
    grad_two[...] = grad_resid
    grad_down[...] = grad_resid.astype(low)
    totals[3:4, :] = column_total(grad_down[...].astype(full))
    pl.semaphore_wait(barrier, 2)

    def down_piece(ref, line, column, far, core):
        dest = 2 * line + (place.x if column == 0 else 1 - place.x)
        y = place.y if far == 0 else 1 - place.y
        return ref.at[pl.ds(pl.multiple_of(dest * 4 * shard + (2 * y + core) * shard, shard), shard)]

    def side_piece(ref, line, column, core):
        dest = 2 * line + (place.x if column == 0 else 1 - place.x)
        half = ref.shape[1] // 2
        return ref.at[
            pl.ds(pl.multiple_of(dest * shard, shard), shard), pl.ds(pl.multiple_of(core * half, half), half)
        ]

    def down_share(line, column, far):
        return remote(
            down_piece(down_grad, line, column, far, 1 - place.c), down_sum.at[column, line, far],
            c_send.at[2 + far, column, line], c_recv.at[2 + far, column, line], place.core,
        )

    def side_slot(array, line, column):
        return out_sum.at[line, column] if array == 1 else up_sum.at[column, line]

    def over_y(line):
        return remote(down_sum.at[1, line, 1], from_y.at[line], y_send.at[line], y_recv.at[line], place.across_y)

    def side_share(array, line, column):
        grad = (up_grad, out_grad)[array]
        return remote(
            side_piece(grad, line, column, 1 - place.c), side_slot(array, line, column),
            c_send.at[array, column, line], c_recv.at[array, column, line], place.core,
        )

    def down_save(column, line):
        return pltpu.make_async_copy(down_sum.at[column, line], down_out.at[column, line], save_sem.at[2, column, line])

    def side_saves(array, column, line):
        if array == 1:
            return [pltpu.make_async_copy(
                side_slot(1, line, column), out_out.at[line, column], save_sem.at[1, column, line]
            )]
        return [
            pltpu.make_async_copy(
                up_sum.at[column, line, :, chunk_lanes(place.y if far == 0 else 1 - place.y)],
                up_out.at[column, line, far], save_sem.at[3 * far, column, line],
            )
            for far in range(2)
        ]

    def add_far(column, line):
        down_share(line, column, 1).wait_recv()
        down_sum[column, line, 1] = add_low(
            down_sum[column, line, 1], down_piece(down_grad, line, column, 1, place.c)[...]
        )

    def down_chunk(line, carry):
        lanes = chunk_lanes(line)
        down_grad[lanes, :] = mul(hidden[:, lanes], grad_down[...], TN).astype(low)
        for far in (1, 0):
            for column in (1, 0):
                down_share(line, column, far).start()

        @pl.when(line > 0)
        def _():
            add_far(1, line - 1)
            over_y(line - 1).start()

        return carry

    lax.fori_loop(0, 4, down_chunk, 0)
    add_far(1, 3)
    over_y(3).start()
    grad_mid[...] = grad_two[...]

    def back_chunk(turn, carry):
        j = lax.rem(2 * (1 - place.c) + turn, 4)
        lanes = chunk_lanes(j)
        grad_up = (mul(grad_down[...], down_w[lanes, :], NT) * slope[:, lanes]).astype(low)
        up_total[0:1, lanes] = column_total(grad_up.astype(full))
        up_grad[:, lanes] = mul(middle_low[...], grad_up, TN).astype(low)
        grad_mid[...] += mul(grad_up, up_w[:, lanes], NT)

        @pl.when(turn == 1)
        def _():
            for column in (1, 0):
                for line in LINES:
                    side_share(0, line, column).start()

        return carry

    lax.fori_loop(0, 4, back_chunk, 0)
    grad_middle = grad_mid[...]
    normed = normed_one[...]
    totals[1:2, :] = column_total(grad_middle * normed)
    totals[2:3, :] = column_total(grad_middle)
    grad_one = norm_back(grad_middle, gain_one, normed, factor_one)
    resid_out[...] = grad_one
    grad_branch = grad_one.astype(low)
    totals[0:1, :] = column_total(grad_branch.astype(full))
    out_grad[...] = mul(attended[...], grad_branch).astype(low)
    for column in (1, 0):
        for line in LINES:
            side_share(1, line, column).start()
    grad_own[...] = mul(out_w[...], grad_branch, NT).astype(low)

    def add_down(column, line):
        down_share(line, column, 0).wait_recv()
        down_sum[column, line, 0] = add_low(
            down_sum[column, line, 0], down_piece(down_grad, line, column, 0, place.c)[...]
        )
        if column == 0:
            add_far(column, line)
        else:
            over_y(line).wait()
            down_sum[column, line, 0] = add_low(down_sum[column, line, 0], from_y[line])
        down_save(column, line).start()

    def add_side(array, column, line):
        slot = side_slot(array, line, column)
        side_share(array, line, column).wait_recv()
        slot[...] = add_low(slot[...], side_piece((up_grad, out_grad)[array], line, column, place.c)[...])
        for save in side_saves(array, column, line):
            save.start()

    for line in LINES:
        add_down(0, line)
    for column in (1, 0):
        for line in LINES:
            add_side(0, column, line)
    vector_out[...] = jnp.zeros_like(vector_out)
    for dest in range(8):
        for index, (line, start) in enumerate(((0, 2), (0, 3), (1, 0), (2, 1), (2, 2), (2, 3))):
            vector_out[dest, line : line + 1, start * shard : (start + 1) * shard] = totals[
                index : index + 1, dest * shard : (dest + 1) * shard
            ]
        base = dest * 4 * shard
        vector_out[dest, 1:2, shard:] = up_total[0:1, base : base + 3 * shard]
        vector_out[dest, 2:3, :shard] = up_total[0:1, base + 3 * shard : base + 4 * shard]
    for column in range(2):
        for line in range(4):
            add_side(1, column, line)
    for line in LINES:
        add_down(1, line)
    for column in range(2):
        for line in range(4):
            for array in range(2):
                side_share(array, line, column).wait_send()
                for save in side_saves(array, column, line):
                    save.wait()
            for far in range(2):
                down_share(line, column, far).wait_send()
            down_save(column, line).wait()


def middle_part(lengths, cotangent, small, up_bias, rows_full, attended, up_full, down_full, out_full):
    rows, width = cotangent.shape
    ff = up_full.shape[1]
    shard = width // 8
    vmem = pl.BlockSpec(memory_space=pltpu.VMEM)
    anywhere = pl.BlockSpec(memory_space=pl.ANY)
    dma = pltpu.SemaphoreType.DMA

    def held(*shape, kind=low):
        return pltpu.VMEM(shape, kind)

    def shaped(*shape, kind=low):
        return jax.ShapeDtypeStruct(shape, kind)

    up_parts, down_parts, out_parts = (2, 4, shard, ff // 2), (2, 4, 2, ff // 32, width), (4, 2, shard, width // 2)
    return pl.pallas_call(
        middle_kernel,
        in_specs=[pl.BlockSpec(memory_space=pltpu.SMEM)] + [vmem] * 3 + [anywhere] * 5,
        out_specs=[vmem] * 4 + [anywhere] * 3,
        out_shape=[
            shaped(rows, width), shaped(rows, width, kind=full), shaped(width, rows),
            shaped(8, 16, 4 * shard, kind=full), shaped(*down_parts), shaped(*down_parts), shaped(*out_parts),
        ],
        scratch_shapes=[
            held(rows, width), held(width, rows), held(width, ff), held(ff, width), held(width, width), held(rows, ff), held(rows, ff, kind=full),
            held(rows, width, kind=full), held(rows, width), held(rows, width), held(rows, width, kind=full),
            held(rows, width, kind=full), held(8, width, kind=full), held(8, ff, kind=full),
            held(width, ff), held(ff, width), held(width, width), held(*up_parts), held(*down_parts),
            held(*out_parts), held(4, ff // 32, width), dma((11,)), dma((4, 2, 4)), dma((4, 2, 4)),
            dma((4, 2, 4)), dma((4,)), dma((4,)),
        ],
        compiler_params=pltpu.CompilerParams(
            vmem_limit_bytes=VMEM_BYTES, collective_id=2, has_side_effects=True
        ),
        name="middle",
    )(lengths, cotangent, small, up_bias, rows_full, attended, up_full, down_full, out_full)


def finish_kernel(
    output_in, input_in, qkv_in, vector_in, up_in, down_in, out_in, read_in, write_in,
    output, input_out, read_out, write_out, qkv_out, qv_out, out_out, out_b, gain_one, shift_one, up_out, up_b,
    down_out, down_b, gain_two, shift_two,
):
    shard = out_b.shape[1]
    output[...] = output_in[...]
    input_out[...] = input_in[...]
    for given, out in ((read_in, read_out), (write_in, write_out)):
        for line in range(given.shape[0]):
            out[line] = given[line : line + 1]
    for given, out in ((qkv_in, qkv_out), (up_in, up_out), (down_in, down_out), (out_in, out_out)):
        out[...] = given[...].astype(full)
    qv_out[...] = vector_in[0:1, : 2 * shard]
    out_b[...] = vector_in[0:1, 2 * shard : 3 * shard]
    gain_one[...] = vector_in[0:1, 3 * shard :]
    shift_one[...] = vector_in[1:2, :shard]
    up_b[:, : 3 * shard] = vector_in[1:2, shard:]
    up_b[:, 3 * shard :] = vector_in[2:3, :shard]
    down_b[...] = vector_in[2:3, shard : 2 * shard]
    gain_two[...] = vector_in[2:3, 2 * shard : 3 * shard]
    shift_two[...] = vector_in[2:3, 3 * shard :]


def finish(output, input_grad, qkv_grad, vectors, up_grad, down_grad, out_grad, grad_read, grad_write):
    shard = qkv_grad.shape[0]

    def shaped(*shape, kind=full):
        return jax.ShapeDtypeStruct(shape, kind)

    line = shaped(1, shard)
    steps = 2

    def rows(array):
        return pl.BlockSpec((array.shape[0] // steps,) + array.shape[1:], lambda i: (i, 0))

    def once(*shape):
        return pl.BlockSpec(shape, lambda i: (0,) * len(shape))

    lone = once(1, shard)
    memory = (grad_read.shape[0], 1, grad_read.shape[1])
    return pl.pallas_call(
        finish_kernel,
        grid=(steps,),
        in_specs=[
            rows(output), rows(input_grad), rows(qkv_grad), once(*vectors.shape), rows(up_grad), rows(down_grad),
            rows(out_grad), once(*grad_read.shape), once(*grad_write.shape),
        ],
        out_specs=[
            rows(output), rows(input_grad), once(*memory), once(*memory), rows(qkv_grad), once(1, 2 * shard),
            rows(out_grad), lone, lone, lone, rows(up_grad), once(1, 4 * shard), rows(down_grad), lone, lone, lone,
        ],
        out_shape=[
            shaped(*output.shape, kind=low), shaped(*input_grad.shape), shaped(*memory), shaped(*memory),
            shaped(*qkv_grad.shape), shaped(1, 2 * shard), shaped(*out_grad.shape), line, line, line,
            shaped(*up_grad.shape), shaped(1, 4 * shard), shaped(*down_grad.shape), line, line, line,
        ],
        compiler_params=pltpu.CompilerParams(vmem_limit_bytes=VMEM_BYTES),
        name="finish",
    )(output, input_grad, qkv_grad, vectors, up_grad, down_grad, out_grad, grad_read, grad_write)


def normalize(values, gain_vec, shift_vec):
    centre = values - jnp.mean(values, axis=-1, keepdims=True)
    factor = lax.rsqrt(jnp.mean(centre * centre, axis=-1, keepdims=True) + norm_epsilon)
    return centre * factor * gain_vec + shift_vec


def column_sums(values):
    return jnp.sum(values, axis=0, dtype=full)


def on_block(
    tokens, read_rows, write_rows, lengths, qkv_weight, vectors, out_weight, up_weight, down_weight, cotangent
):
    total = sum(vector.shape[0] for vector in vectors)
    packed, start = jnp.zeros((1, total), full), 0
    for vector in vectors:
        size = vector.shape[0]
        packed = packed + jnp.pad(vector.astype(full).reshape(1, -1), ((0, 0), (start, total - start - size)))
        start += size
    (small, up_bias, rows, weight, q_t, k_t, k_wide, v_wide, mixed, row_stats, up_full, down_full, out_full,
     attended) = front(
        lengths, tokens, read_rows, write_rows, qkv_weight, packed, up_weight, down_weight, out_weight
    )
    output, resid, grad_own, vector_parts, up_parts, down_parts, out_parts = middle_part(
        lengths, cotangent, small, up_bias, rows, attended, up_full, down_full, out_full
    )
    saved = (q_t, k_t, k_wide, v_wide, mixed, row_stats)
    input_grad, grad_read, grad_write, qkv_grad, vector_sum, up_grad, down_grad, out_grad = back(
        lengths, grad_own, saved, vector_parts, rows, weight, resid, up_parts, down_parts, out_parts
    )
    results = finish(
        output, input_grad, qkv_grad, vector_sum, up_grad, down_grad, out_grad, grad_read, grad_write
    )
    shaped = [jnp.swapaxes(result, 0, 1) if index in (2, 3) else result for index, result in enumerate(results)]
    return tuple(result.reshape(-1) if result.shape[0] == 1 and result.ndim == 2 else result for result in shaped)


def per_device(
    tokens, read_memory, write_memory, lengths, qkv_weight, qv_bias, out_weight, out_bias, norm1_gain,
    norm1_bias, up_weight, up_bias, down_weight, down_bias, norm2_gain, norm2_bias, cotangent,
):
    seq_count = lax.axis_size("seq")
    fsdp_count = lax.axis_size("fsdp")
    seq_place = lax.axis_index("seq")
    local_rows, width = tokens.shape
    head_cols = width // seq_count
    shard = width // fsdp_count
    length = lengths[0]
    heads = head_cols // HEAD
    vectors = (qv_bias, out_bias, norm1_gain, norm1_bias, up_bias, down_bias, norm2_gain, norm2_bias)
    if (fsdp_count, seq_count) == (8, 4):
        return on_block(
            tokens, read_memory[0], write_memory[0], lengths, qkv_weight, vectors, out_weight, up_weight, down_weight,
            cotangent,
        )
    places = seq_place * local_rows + jnp.arange(local_rows, dtype=jnp.int32)
    in_slot = (places < length)[:, None]
    memory_slots = jnp.arange(MEM, dtype=jnp.int32)
    pick_read = places[:, None] == memory_slots[None, :]
    pick_write = places[:, None] == length - MEM + memory_slots[None, :]
    is_memory = jnp.any(pick_read | pick_write, axis=1)[:, None]
    picks = jnp.concatenate([pick_read, pick_write], axis=1).astype(full)
    memory = jnp.concatenate([read_memory[0], write_memory[0]], axis=0)
    layer_in = jnp.where(is_memory, mul(picks.astype(low), memory).astype(low), tokens)

    own_shard = lax.dynamic_slice_in_dim(
        qkv_weight.reshape(shard, 3, seq_count, heads, HEAD), seq_place, 1, 2
    )
    own_shard = jnp.transpose(own_shard[:, :, 0], (0, 2, 1, 3)).reshape(shard, 3 * head_cols)
    packed = jnp.concatenate(vectors)
    rows = lax.all_gather(layer_in, "seq", axis=0, tiled=True)
    weight = lax.all_gather(own_shard, "fsdp", axis=0, tiled=True)
    packed = lax.all_gather(packed.reshape(1, -1), "fsdp", axis=0, tiled=True).astype(full)
    whole, start = [], 0
    for vector in vectors:
        whole.append(packed[:, start : start + vector.shape[0]].reshape(-1))
        start += vector.shape[0]
    qv_vec, out_vec, gain_one, shift_one, up_vec, down_vec, gain_two, shift_two = whole
    own_qv = lax.dynamic_slice_in_dim(qv_vec.reshape(2, seq_count, head_cols), seq_place, 1, 1)
    bias = jnp.concatenate([own_qv[0, 0], own_qv[1, 0]])
    bias = jnp.broadcast_to(bias, (8, bias.shape[0]))
    out_full = lax.all_gather(out_weight, "fsdp", axis=0, tiled=True)
    up_full = lax.all_gather(up_weight, "fsdp", axis=0, tiled=True)
    down_full = lax.all_gather(down_weight, "fsdp", axis=0, tiled=True)
    q_x, k_t, k_wide, v_wide, mixed, mixed_low, row_stats = attention_forward(lengths, rows, weight, bias)
    attended = lax.all_to_all(mixed_low, "seq", split_axis=1, concat_axis=0, tiled=True)
    resid_one = layer_in.astype(full) + mul(attended, out_full, TN) + out_vec
    middle, norm_one_back = jax.vjp(normalize, resid_one, gain_one, shift_one)
    middle_low = middle.astype(low)
    up_pre = mul(middle_low, up_full) + up_vec
    gelu_out, gelu_back = jax.vjp(partial(jax.nn.gelu, approximate=False), up_pre)
    hidden = gelu_out.astype(low)
    down_pre = mul(hidden, down_full) + down_vec
    final, norm_two_back = jax.vjp(normalize, middle + down_pre, gain_two, shift_two)
    output = jnp.where(in_slot, final, 0.0).astype(low)
    grad_final = jnp.where(in_slot, cotangent.astype(full), 0.0)
    grad_resid_two, grad_gain_two, grad_shift_two = norm_two_back(grad_final)
    grad_down = grad_resid_two.astype(low)
    grad_down_weight = mul(hidden, grad_down, TN)
    (grad_up_pre,) = gelu_back(mul(grad_down, down_full, NT))
    grad_up = grad_up_pre.astype(low)
    grad_up_weight = mul(middle_low, grad_up, TN)
    grad_middle = grad_resid_two + mul(grad_up, up_full, NT)
    grad_resid_one, grad_gain_one, grad_shift_one = norm_one_back(grad_middle)
    grad_branch = grad_resid_one.astype(low)
    grad_out_weight = mul(attended, grad_branch)
    grad_attended = mul(out_full, grad_branch, NT).astype(low)
    vector_grads = [
        column_sums(grad_branch), grad_gain_one, grad_shift_one, column_sums(grad_up),
        column_sums(grad_down), grad_gain_two, grad_shift_two,
    ]
    packed_grad = jnp.concatenate([v.reshape(fsdp_count, -1) for v in vector_grads], axis=1)
    saved = (q_x, k_t, k_wide, v_wide, mixed, row_stats)
    grad_t = lax.all_to_all(grad_attended, "seq", split_axis=0, concat_axis=1, tiled=True)
    partial_in, weight_part, sums = attention_backward(*saved, grad_t, rows, weight)
    from_heads = lax.psum_scatter(partial_in, "seq", scatter_dimension=0, tiled=True).astype(full)
    grad_layer_in = grad_resid_one + from_heads
    input_grad = jnp.where(is_memory, 0.0, grad_layer_in)
    grad_memory = lax.dot_general(
        picks, grad_layer_in, TN, precision=lax.Precision.HIGHEST, preferred_element_type=full
    )
    grad_memory = lax.psum(grad_memory.astype(low), "seq").astype(full)
    grad_read, grad_write = grad_memory[:MEM], grad_memory[MEM:]
    sums = sums[:, 0].reshape(heads, 3, HEAD)
    own_sums = jnp.stack([sums[:, 0].reshape(-1), sums[:, 2].reshape(-1)])[:, None]
    zero_qv = jnp.zeros((2, seq_count, head_cols), full)
    qv_grad = lax.dynamic_update_slice_in_dim(zero_qv, own_sums, seq_place, 1)
    packed_grad = jnp.concatenate([qv_grad.reshape(fsdp_count, -1), packed_grad], axis=1)
    packed_sum = lax.psum(packed_grad, ("fsdp", "seq"))
    own_vectors = lax.dynamic_index_in_dim(packed_sum, lax.axis_index("fsdp"), 0, False)

    def both_axes(part):
        piece = lax.psum_scatter(part.astype(low), "fsdp", scatter_dimension=0, tiled=True)
        return lax.psum(piece, "seq").astype(full)

    qkv_piece = lax.psum_scatter(weight_part, "fsdp", scatter_dimension=0, tiled=True)
    qkv_parts = lax.all_gather(qkv_piece, "seq", axis=0).reshape(seq_count, shard, heads, 3, HEAD)
    qkv_out = jnp.transpose(qkv_parts, (1, 3, 0, 2, 4)).reshape(shard, 3 * width).astype(full)
    up_out, down_out, out_out = both_axes(grad_up_weight), both_axes(grad_down_weight), both_axes(grad_out_weight)
    vector_outs, start = [], 0
    for vector in vectors:
        vector_outs.append(own_vectors[start : start + vector.shape[0]])
        start += vector.shape[0]
    qv_out, out_b_out, gain_one_out, shift_one_out, up_b_out, down_b_out, gain_two_out, shift_two_out = vector_outs
    return (
        output, input_grad, grad_read[None], grad_write[None], qkv_out, qv_out, out_out, out_b_out, gain_one_out,
        shift_one_out, up_out, up_b_out, down_out, down_b_out, gain_two_out, shift_two_out,
    )


def solution(mesh):
    rows, piece = P(("fsdp", "seq"), None), P("fsdp")
    matrix, memory = P("fsdp", None), P("fsdp", None, None)
    in_specs = (
        rows, memory, memory, piece, matrix, piece, matrix, piece, piece, piece, matrix, piece, matrix,
        piece, piece, piece, rows,
    )
    out_specs = (
        rows, rows, memory, memory, matrix, piece, matrix, piece, piece, piece, matrix, piece, matrix,
        piece, piece, piece,
    )
    return jax.shard_map(per_device, mesh=mesh, in_specs=in_specs, out_specs=out_specs, check_vma=False)
```

```python
from functools import partial

import jax
import jax.numpy as jnp
from jax import lax
from jax.experimental import pallas as pl
from jax.experimental.pallas import tpu as pltpu
from jax.sharding import PartitionSpec as P

HEAD = 64
MEM = 10
WIDE = 128
VMEM_BYTES = 64000 * 1024

norm_epsilon = 1e-06
masked_score = -1e30
low = jnp.bfloat16
full = jnp.float32

NN = (((1,), (0,)), ((), ()))
NT = (((1,), (1,)), ((), ()))
TN = (((0,), (0,)), ((), ()))
TT = (((0,), (1,)), ((), ()))


def mul(left, right, dims=NN):
    return lax.dot_general(left, right, dims, preferred_element_type=full)


def three_parts(value):
    high = value.astype(low)
    rest = value - high.astype(full)
    middle = rest.astype(low)
    return high, middle, (rest - middle.astype(full)).astype(low)


def stack_rows(rows, columns):
    place = lax.broadcasted_iota(jnp.int32, (HEAD, columns), 0)
    block = jnp.zeros((HEAD, columns), full)
    for index, row in enumerate(rows):
        block = jnp.where(place == index, row, block)
    return block.astype(low)


def project_block(start, length, rows_ref, weight_ref, bias_q, bias_v, q_x, k_t, v_x, k_wide, v_wide, step):
    head_cols = k_t.shape[0]
    lanes = pl.ds(start, step)
    made = mul(weight_ref[...], rows_ref[lanes, :], TT)
    place = start + lax.broadcasted_iota(jnp.int32, (1, step), 1)
    key_bias = jnp.where(place < length, 0.0, masked_score)
    one = jnp.ones((1, step), full)
    query_extra = stack_rows([one], step)
    key_extra = stack_rows([key_bias, one, one, one], step)
    value_extra = stack_rows([one, one, one], step)
    for h in range(head_cols // HEAD):
        own = slice(h * HEAD, (h + 1) * HEAD)
        base = 3 * h * HEAD
        query = (made[base : base + HEAD] + bias_q[own]).astype(low)
        q_x[h, :HEAD, lanes] = query * jnp.asarray(HEAD**-0.5, low)
        q_x[h, HEAD:, lanes] = query_extra
        k_t[own, lanes] = made[base + HEAD : base + 2 * HEAD].astype(low)
        v_x[h, :HEAD, lanes] = (made[base + 2 * HEAD : base + 3 * HEAD] + bias_v[own]).astype(low)
        v_x[h, HEAD:, lanes] = value_extra
        k_wide[h, lanes, :] = jnp.transpose(jnp.concatenate([k_t[own, lanes], key_extra], axis=0))
        v_wide[h, lanes, :] = jnp.transpose(v_x[h, :, lanes])


def project_heads(length, rows_ref, weight_ref, bias_ref, q_x, k_t, v_x, k_wide, v_wide):
    head_cols = k_t.shape[0]
    bias = jnp.transpose(bias_ref[...])[:, 0:1]
    for start in range(0, rows_ref.shape[0], 512):
        project_block(
            start, length, rows_ref, weight_ref, bias[:head_cols], bias[head_cols:],
            q_x, k_t, v_x, k_wide, v_wide, 512,
        )


def attend_block(h, lanes, q_x, k_wide, v_x, mixed, mixed_low, row_stats):
    scores = mul(k_wide[h], q_x[h, :, lanes])
    row_max = jnp.max(scores, axis=0, keepdims=True)
    probs = jnp.exp(scores - row_max).astype(low)
    total = mul(v_x[h, : HEAD + 16], probs)
    row_sum = total[HEAD : HEAD + 1]
    own = pl.ds(h * HEAD, HEAD)
    result = total[:HEAD] / row_sum
    mixed[own, lanes] = result
    mixed_low[own, lanes] = result.astype(low)
    row_stats[h, :, lanes] = jnp.broadcast_to(row_max + jnp.log(row_sum), (8, result.shape[1]))


def forward_kernel(
    length_ref, rows_ref, weight_ref, bias_ref, q_x, k_t, k_wide, v_wide, mixed, mixed_low, row_stats, v_x
):
    project_heads(length_ref[0], rows_ref, weight_ref, bias_ref, q_x, k_t, v_x, k_wide, v_wide)
    heads = q_x.shape[0]
    block = 512
    blocks = q_x.shape[2] // block

    def step(index, carry):
        h = index // blocks
        start = pl.multiple_of(lax.rem(index, blocks) * block, block)
        attend_block(h, pl.ds(start, block), q_x, k_wide, v_x, mixed, mixed_low, row_stats)
        return carry

    lax.fori_loop(0, heads * blocks, step, 0)


def attention_forward(length, rows, weight, bias):
    slot_rows = rows.shape[0]
    head_cols = weight.shape[1] // 3
    heads = head_cols // HEAD
    vmem = pl.BlockSpec(memory_space=pltpu.VMEM)
    return pl.pallas_call(
        forward_kernel,
        in_specs=[pl.BlockSpec(memory_space=pltpu.SMEM), vmem, vmem, vmem],
        out_specs=[vmem] * 7,
        out_shape=[
            jax.ShapeDtypeStruct((heads, WIDE, slot_rows), low),
            jax.ShapeDtypeStruct((head_cols, slot_rows), low),
            jax.ShapeDtypeStruct((heads, slot_rows, WIDE), low),
            jax.ShapeDtypeStruct((heads, slot_rows, WIDE), low),
            jax.ShapeDtypeStruct((head_cols, slot_rows), full),
            jax.ShapeDtypeStruct((head_cols, slot_rows), low),
            jax.ShapeDtypeStruct((heads, 8, slot_rows), full),
        ],
        scratch_shapes=[pltpu.VMEM((heads, WIDE, slot_rows), low)],
        compiler_params=pltpu.CompilerParams(vmem_limit_bytes=VMEM_BYTES),
        name="attention_forward",
    )(length, rows, weight, bias)


def attend_back(h, lanes, q_x, q_here, do_x, grad_t, mixed, row_stats, k_t, k_wide, v_wide, grads, grad_k, grad_v, first):
    own = pl.ds(pl.multiple_of(h * HEAD, HEAD), HEAD)
    grad = grad_t[own, lanes]
    columns = grad.shape[1]
    delta = jnp.sum(grad.astype(full) * mixed[own, lanes], axis=0, keepdims=True)
    parts = [part.astype(full) for part in three_parts(-delta)]
    do_x[:HEAD, :] = grad
    do_x[HEAD:, :] = stack_rows(parts, columns)
    parts = [part.astype(full) for part in three_parts(-row_stats[h, 0:1, lanes])]
    q_here[:HEAD, :] = q_x[h, :HEAD, lanes]
    q_here[HEAD:, :] = stack_rows([jnp.ones((1, columns), full)] + parts, columns)
    probs = jnp.exp(mul(k_wide[h], q_here[...]))
    grad_scores = (probs * mul(v_wide[h], do_x[...])).astype(low)
    value_part = mul(grad, probs.astype(low), NT)
    key_part = mul(q_here[:HEAD, :], grad_scores, NT)

    @pl.when(first)
    def _():
        grad_v[...] = value_part
        grad_k[...] = key_part

    @pl.when(jnp.logical_not(first))
    def _():
        grad_v[...] += value_part
        grad_k[...] += key_part

    query_part = mul(k_t[own, :], grad_scores) * HEAD**-0.5
    grads[pl.ds(pl.multiple_of(3 * h * HEAD, HEAD), HEAD), lanes] = query_part.astype(low)


def backward_kernel(
    q_in, k_t, k_wide, v_wide, mixed, row_stats, grad_t, rows_ref, weight_ref,
    partial_out, weight_out, sums_out, q_here, do_x, grads, grad_k, grad_v,
):
    heads, _, slot_rows = q_in.shape
    block = 512
    blocks = slot_rows // block

    def step(index, carry):
        h = index // blocks
        turn = lax.rem(index, blocks)
        start = pl.multiple_of(turn * block, block)
        attend_back(
            h, pl.ds(start, block), q_in, q_here, do_x, grad_t, mixed, row_stats, k_t, k_wide, v_wide, grads, grad_k,
            grad_v, turn == 0,
        )

        @pl.when(turn == blocks - 1)
        def _():
            base = pl.multiple_of(3 * h * HEAD, HEAD)
            grads[pl.ds(base + HEAD, HEAD), :] = grad_k[...].astype(low)
            grads[pl.ds(base + 2 * HEAD, HEAD), :] = grad_v[...].astype(low)

        return carry

    lax.fori_loop(0, heads * blocks, step, 0)
    for start in range(0, slot_rows, block):
        partial_out[start : start + block, :] = mul(
            grads[:, start : start + block], weight_ref[...], TT
        ).astype(partial_out.dtype)
    weight_out[...] = jnp.transpose(mul(grads[...], rows_ref[...])).astype(weight_out.dtype)
    sums_out[...] = jnp.broadcast_to(
        jnp.sum(grads[...].astype(full), axis=1, keepdims=True), sums_out.shape
    )


def attention_backward(q_x, k_t, k_wide, v_wide, mixed, row_stats, grad_t, rows, weight):
    heads, _, slot_rows = q_x.shape
    width, all_cols = weight.shape
    vmem = pl.BlockSpec(memory_space=pltpu.VMEM)
    return pl.pallas_call(
        backward_kernel,
        in_specs=[vmem] * 9,
        out_specs=[vmem] * 3,
        out_shape=[
            jax.ShapeDtypeStruct((slot_rows, width), low),
            jax.ShapeDtypeStruct((width, all_cols), low),
            jax.ShapeDtypeStruct((all_cols, WIDE), full),
        ],
        scratch_shapes=[
            pltpu.VMEM((WIDE, 512), low),
            pltpu.VMEM((WIDE, 512), low),
            pltpu.VMEM((all_cols, slot_rows), low),
            pltpu.VMEM((HEAD, slot_rows), full),
            pltpu.VMEM((HEAD, slot_rows), full),
        ],
        compiler_params=pltpu.CompilerParams(vmem_limit_bytes=VMEM_BYTES),
        name="attention_backward",
    )(q_x, k_t, k_wide, v_wide, mixed, row_stats, grad_t, rows, weight)


MESH = pl.DeviceIdType.MESH
OWN, RELATIONS = 0, 7
UP_W, OUT_W, DOWN_W, QKV_W = 0, 1, 2, 3


def offset_of(relation):
    return (0, -1, -2, -3, 1, 2, 3)[relation]


class Place:
    def __init__(self):
        self.f, self.s = lax.axis_index("fsdp"), lax.axis_index("seq")
        self.z, self.x = self.f // 2, lax.rem(self.f, 2)
        self.y, self.c = self.s // 2, lax.rem(self.s, 2)
        self.core = (self.f, 2 * self.y + 1 - self.c)
        self.across_y = (self.f, 2 * (1 - self.y) + self.c)
        self.diagonal = (self.f, 2 * (1 - self.y) + 1 - self.c)
        self.across_x = (2 * self.z + 1 - self.x, self.s)
        self.above = (self.f + 2, self.s)
        self.below = (self.f - 2, self.s)

    def has(self, relation):
        offset = offset_of(relation)
        return (self.z + offset >= 0) & (self.z + offset <= 3)

    def source(self, relation, column):
        own_column = self.f + 2 * offset_of(relation)
        return own_column if column == 0 else own_column + 1 - 2 * self.x

    def member(self, turn):
        flip_y = 1 - turn // 2
        flip_c = lax.rem(turn, 2) if not isinstance(turn, int) else turn % 2
        flip_c = flip_c + (1 - 2 * flip_c) * (turn // 2)
        return 2 * lax.rem(self.y + flip_y, 2) + lax.rem(self.c + flip_c, 2)


def remote(src, dst, send, recv, where):
    return pltpu.make_async_remote_copy(
        src_ref=src, dst_ref=dst, send_sem=send, recv_sem=recv, device_id=where, device_id_type=MESH
    )


def greet(place, all_lines):
    barrier = pltpu.get_barrier_semaphore()
    near = [place.core, place.across_y, place.diagonal, place.across_x]
    for where in near:
        pl.semaphore_signal(barrier, inc=1, device_id=where, device_id_type=MESH)
    for line in range(4):
        gap = place.z - line
        meets = gap != 0 if all_lines else (gap == 1) | (gap == -1)

        @pl.when(meets)
        def _(line=line):
            pl.semaphore_signal(
                barrier, inc=1, device_id=(2 * line + place.x, place.s), device_id_type=MESH
            )

    ends = 3 if all_lines else jnp.where((place.z == 0) | (place.z == 3), 1, 2)
    pl.semaphore_wait(barrier, len(near) + ends)


class Gather:
    def __init__(self, place, own, whole, sems):
        self.place, self.own, self.whole = place, own, whole
        (self.z_send, self.z_recv, self.x_send, self.x_recv, self.c_send, self.c_recv,
         self.y_send, self.y_recv, self.d_send, self.d_recv) = sems

    def piece(self, array, source, quarter=None, pair=False):
        c = self.place.c
        ref = self.whole[array]
        if array == QKV_W:
            return ref.at[source]
        if array == DOWN_W:
            rows = ref.shape[0] // 8
            part = rows // 4
            quarter = self.place.s if quarter is None else quarter
            return ref.at[pl.ds(pl.multiple_of(source * rows + quarter * part, part), part)]
        rows, columns = ref.shape[0] // 8, ref.shape[1] // 2
        count = 2 if pair else 1
        return ref.at[
            pl.ds(pl.multiple_of(source * rows, rows), count * rows),
            pl.ds(pl.multiple_of(c * columns, columns), columns),
        ]

    def own_piece(self, array):
        if array == QKV_W:
            return self.piece(array, self.place.f)
        ref = self.own[array]
        if array == DOWN_W:
            part = ref.shape[0] // 4
            return ref.at[pl.ds(pl.multiple_of(self.place.s * part, part), part)]
        columns = ref.shape[1] // 2
        return ref.at[:, pl.ds(pl.multiple_of(self.place.c * columns, columns), columns)]

    def z_piece(self, array, relation):
        source = self.place.source(relation, 0)
        if array == OUT_W:
            return self.piece(array, source - self.place.x, pair=True)
        return self.piece(array, source)

    def along_z(self, array, relation, way):
        here = self.z_piece(array, relation)
        src = self.own_piece(array) if relation == OWN and array != OUT_W else here
        step = abs(offset_of(relation))
        where = self.place.above if way == 0 else self.place.below
        return remote(src, here, self.z_send.at[array, way, step], self.z_recv.at[array, way, step], where)

    def z_ways(self, relation):
        place = self.place
        ways = []
        if offset_of(relation) <= 0:
            ways.append((0, place.has(relation) & (place.z < 3)))
        if offset_of(relation) >= 0:
            ways.append((1, place.has(relation) & (place.z > 0)))
        return ways

    def wait_z(self, array, relation):
        way = 0 if offset_of(relation) < 0 else 1
        step = abs(offset_of(relation)) - 1
        here = self.z_piece(array, relation)
        where = self.place.below if way == 0 else self.place.above
        remote(
            here, here, self.z_send.at[array, way, step], self.z_recv.at[array, way, step], where
        ).wait_recv()

    def over_x(self, array, relation):
        here = self.piece(array, self.place.source(relation, 0))
        src = self.own_piece(array) if relation == OWN else here
        return remote(
            src, here, self.x_send.at[array, relation], self.x_recv.at[array, relation], self.place.across_x
        )

    def from_x(self, array, relation):
        here = self.piece(array, self.place.source(relation, 1))
        return remote(
            here, here, self.x_send.at[array, relation], self.x_recv.at[array, relation], self.place.across_x
        )

    def to_core(self, array, relation, column):
        if array == OUT_W and relation != OWN:
            here = self.z_piece(array, relation)
        else:
            here = self.piece(array, self.place.source(relation, column))
        return remote(
            here, here, self.c_send.at[array, relation, column], self.c_recv.at[array, relation, column],
            self.place.core,
        )

    def over_y(self, relation, column):
        here = self.piece(DOWN_W, self.place.source(relation, column))
        return remote(
            here, here, self.y_send.at[relation, column], self.y_recv.at[relation, column], self.place.across_y
        )

    def far_quarter(self, relation, column):
        return self.piece(
            DOWN_W, self.place.source(relation, column), 2 * (1 - self.place.y) + self.place.c
        )

    def from_y(self, relation, column):
        here = self.far_quarter(relation, column)
        return remote(
            here, here, self.y_send.at[relation, column], self.y_recv.at[relation, column], self.place.across_y
        )

    def far_to_core(self, relation, column):
        here = self.far_quarter(relation, column)
        return remote(
            here, here, self.d_send.at[relation, column], self.d_recv.at[relation, column], self.place.core
        )

    def when(self, relation, action):
        if relation == OWN:
            action()
        else:
            pl.when(self.place.has(relation))(action)

    def arrive_z(self, array, relation, along=True, across=True):
        def action():
            if relation != OWN:
                self.wait_z(array, relation)
            for way, holds in self.z_ways(relation) if along else ():
                pl.when(holds)(lambda way=way: self.along_z(array, relation, way).start())
            if array != OUT_W and across:
                self.over_x(array, relation).start()
            if array != QKV_W and relation != OWN:
                self.to_core(array, relation, 0).start()
                if array == DOWN_W:
                    self.over_y(relation, 0).start()

        self.when(relation, action)

    def cross_out(self):
        self.over_x(OUT_W, OWN).start()

    def pair_out(self, own_copy):
        own_copy.wait()
        self.from_x(OUT_W, OWN).wait_recv()
        self.to_core(OUT_W, OWN, 1).start()
        for way, holds in self.z_ways(OWN):
            pl.when(holds)(lambda way=way: self.along_z(OUT_W, OWN, way).start())

    def arrive_x(self, array, relation):
        def action():
            self.from_x(array, relation).wait_recv()
            if array != QKV_W:
                self.to_core(array, relation, 1).start()
                if array == DOWN_W:
                    self.over_y(relation, 1).start()

        self.when(relation, action)

    def arrive_y(self, relation, column):
        def action():
            self.from_y(relation, column).wait_recv()
            self.far_to_core(relation, column).start()

        if (relation, column) != (OWN, 0):
            self.when(relation, action)

    def finish(self, array):
        for relation in range(RELATIONS):
            def action():
                if array != OUT_W or relation == OWN:
                    self.over_x(array, relation).wait_send()
                for way, holds in self.z_ways(relation):
                    pl.when(holds)(lambda way=way: self.along_z(array, relation, way).wait_send())
                if array == QKV_W:
                    return
                for column in range(2):
                    if (relation, column) == (OWN, 0) or (array == OUT_W and relation != OWN and column == 1):
                        continue
                    self.to_core(array, relation, column).wait()
                    if array == DOWN_W:
                        self.over_y(relation, column).wait_send()
                        self.far_to_core(relation, column).wait()

            self.when(relation, action)


def front_kernel(
    length_ref, tokens, read_rows, write_rows, qkv_in, vectors_in, up_in, down_in, out_in,
    small, up_bias, rows_out, weight_out, q_out, k_out, k_wide_out, v_wide_out, mixed_out, stats_out, up_full,
    down_full, out_full, attended,
    rows_ref, weight_ref, pieces, memory, q_x, k_t, k_wide, v_wide, v_x, mixed, mixed_low, row_stats,
    row_send, row_recv, far_send, far_recv, mix_send, mix_recv, local_sem, save_sem, head_sem, *gather_sems,
):
    place = Place()
    slot_rows, width = rows_ref.shape
    local_rows = tokens.shape[0]
    head_cols = k_t.shape[0]
    heads = head_cols // HEAD
    shard = width // 8
    length = length_ref[0]
    own_shards = {UP_W: up_in, DOWN_W: down_in, OUT_W: out_in}
    whole = {UP_W: up_full, DOWN_W: down_full, OUT_W: out_full, QKV_W: pieces}
    gather = Gather(place, own_shards, whole, gather_sems)

    memory[...] = jnp.zeros_like(memory)
    memory[:MEM, :] = read_rows[...]
    memory[16 : 16 + MEM, :] = write_rows[...]
    line = lax.broadcasted_iota(jnp.int32, (local_rows, 32), 1)
    at = place.s * local_rows + lax.broadcasted_iota(jnp.int32, (local_rows, 32), 0)
    wanted = jnp.where(line < 16, line, length - MEM + line - 16)
    used = (line < MEM) | ((line >= 16) & (line < 16 + MEM))
    pick = jnp.where(used & (wanted == at), 1.0, 0.0)
    taken = mul(pick.astype(low), memory[...]).astype(low)
    is_memory = jnp.sum(pick, axis=1, keepdims=True) > 0.5
    own_start = pl.multiple_of(place.s * local_rows, local_rows)
    rows_ref[pl.ds(own_start, local_rows), :] = jnp.where(is_memory, taken, tokens[...])
    for member in range(4):

        @pl.when(place.s == member)
        def _(member=member):
            for h in range(heads):
                for kind in range(3):
                    start = kind * width + (member * heads + h) * HEAD
                    to = (3 * h + kind) * HEAD
                    pieces[place.f, :, to : to + HEAD] = qkv_in[:, start : start + HEAD]

    columns = 3 * head_cols
    pieces[place.f, :, columns:] = jnp.zeros((shard, HEAD), low)
    for line in range(18):
        pieces[place.f, line : line + 1, columns:] = vectors_in[:, line * HEAD : (line + 1) * HEAD].astype(low)
    greet(place, False)

    halves = 2
    part = local_rows // halves

    def rows_of(member, half):
        return pl.ds(pl.multiple_of(member * local_rows + half * part, part), part)

    def send_rows(half, index):
        where = (place.core, place.across_y)[index]
        here = rows_ref.at[rows_of(place.s, half)]
        return remote(here, here, row_send.at[index, half], row_recv.at[index, half], where)

    def rows_from(half, index):
        member = (2 * place.y + 1 - place.c, 2 * (1 - place.y) + place.c)[index]
        here = rows_ref.at[rows_of(member, half)]
        where = (place.core, place.across_y)[index]
        return remote(here, here, row_send.at[index, half], row_recv.at[index, half], where)

    def pass_rows(half, arriving):
        flip = place.c if not arriving else 1 - place.c
        here = rows_ref.at[rows_of(2 * (1 - place.y) + flip, half)]
        return remote(here, here, far_send.at[half], far_recv.at[half], place.core)

    def own_copies():
        copies = []
        for index, array in enumerate((UP_W, DOWN_W, OUT_W)):
            rows = own_shards[array].shape[0]
            copies.append(pltpu.make_async_copy(
                own_shards[array], whole[array].at[pl.ds(pl.multiple_of(place.f * rows, rows), rows)],
                local_sem.at[index],
            ))
        return copies

    gather.arrive_z(QKV_W, OWN)
    for half in range(halves):
        send_rows(half, 1).start()
        send_rows(half, 0).start()
    gather.cross_out()
    for copy in own_copies():
        copy.start()
    for relation in (1, 4):
        gather.arrive_z(QKV_W, relation)
    gather.arrive_z(DOWN_W, OWN, along=False)
    gather.pair_out(own_copies()[2])
    for relation in (2, 5):
        gather.arrive_z(QKV_W, relation)
    gather.arrive_z(DOWN_W, OWN, across=False)
    gather.arrive_z(UP_W, OWN)
    rows_from(0, 1).wait_recv()
    pass_rows(0, False).start()
    for relation in (3, 6):
        gather.arrive_z(QKV_W, relation)
    for relation in (1, 4):
        gather.arrive_z(DOWN_W, relation)
    for relation in range(RELATIONS):
        gather.arrive_x(QKV_W, relation)
    for relation in (1, 4):
        gather.arrive_z(OUT_W, relation)
        gather.arrive_z(UP_W, relation)

    for source in range(8):
        weight_ref[source * shard : (source + 1) * shard, :] = pieces[source, :, :columns]
    tile = slice(columns - HEAD, columns + HEAD)
    bias_q = jnp.transpose(pieces[place.s, 0:16, tile].astype(full))[HEAD:]
    bias_v = jnp.transpose(pieces[4 + place.s, 0:16, tile].astype(full))[HEAD:]
    bias_q = jnp.concatenate([bias_q[:, h : h + 1] for h in range(heads)], axis=0)
    bias_v = jnp.concatenate([bias_v[:, h : h + 1] for h in range(heads)], axis=0)

    def project(member):
        start = pl.multiple_of(member * local_rows, local_rows)
        project_block(
            start, length, rows_ref, weight_ref, bias_q, bias_v, q_x, k_t, v_x, k_wide, v_wide, local_rows
        )

    project(place.s)
    for half in range(halves):
        rows_from(half, 0).wait_recv()
    project(2 * place.y + 1 - place.c)
    rows_from(1, 1).wait_recv()
    pass_rows(1, False).start()
    project(2 * (1 - place.y) + place.c)

    def scatter_vector(target, index, size, first):
        for source in range(8):
            done = 0
            while done < size:
                line, lane = divmod(first + done, HEAD)
                count = min(HEAD - lane, size - done)
                target[index : index + 1, source * size + done : source * size + done + count] = pieces[
                    source, line : line + 1, columns + lane : columns + lane + count
                ].astype(full)
                done += count

    for index, first in enumerate((2, 3, 4, 9, 10, 11)):
        scatter_vector(small, index, shard, first * shard)
    scatter_vector(up_bias, 0, 4 * shard, 5 * shard)
    for half in range(halves):
        pass_rows(half, True).wait_recv()
    project(2 * (1 - place.y) + 1 - place.c)

    def saves():
        pairs = [(rows_ref, rows_out), (weight_ref, weight_out), (k_t, k_out), (k_wide, k_wide_out), (v_wide, v_wide_out)]
        pairs += [(q_x.at[h, pl.ds(0, HEAD)], q_out.at[h]) for h in range(heads)]
        return [pltpu.make_async_copy(src, dst, save_sem.at[index]) for index, (src, dst) in enumerate(pairs)]

    for save in saves():
        save.start()

    def head_saves(h):
        own = pl.ds(h * HEAD, HEAD)
        return [
            pltpu.make_async_copy(mixed.at[own], mixed_out.at[own], head_sem.at[h, 0]),
            pltpu.make_async_copy(row_stats.at[h], stats_out.at[h], head_sem.at[h, 1]),
        ]

    def chores(step):
        if step == 0:
            gather.arrive_x(DOWN_W, OWN)
            for relation in (2, 5):
                gather.arrive_z(DOWN_W, relation)
        elif step == 1:
            gather.arrive_x(UP_W, OWN)
            for relation in (2, 5):
                gather.arrive_z(OUT_W, relation)
        elif step == 2:
            for relation in (1, 4):
                gather.arrive_x(DOWN_W, relation)
                gather.arrive_y(relation, 0)
        elif step == 4:
            for relation in (2, 5):
                gather.arrive_z(UP_W, relation)
            gather.arrive_y(OWN, 1)
            for save in head_saves(0):
                save.start()
        elif step == 5:
            for relation in (1, 4):
                gather.arrive_x(UP_W, relation)
            for relation in (3, 6):
                gather.arrive_z(DOWN_W, relation)
        elif step == 6:
            for relation in (2, 5):
                gather.arrive_x(DOWN_W, relation)
                gather.arrive_y(relation, 0)
        elif step == 7:
            for relation in (3, 6):
                gather.arrive_z(OUT_W, relation)
        elif step == 8:
            for relation in (1, 4):
                gather.arrive_y(relation, 1)
            for save in head_saves(1):
                save.start()
        elif step == 9:
            for relation in (3, 6):
                gather.arrive_z(UP_W, relation)
            for relation in (2, 5):
                gather.arrive_x(UP_W, relation)
        elif step == 10:
            for relation in (3, 6):
                gather.arrive_x(DOWN_W, relation)
                gather.arrive_y(relation, 0)
        elif step == 11:
            for relation in (2, 5):
                gather.arrive_y(relation, 1)

    def send_mixed(h, turn, arriving=False):
        member = place.member(turn)
        own = pl.ds(pl.multiple_of(h * HEAD, HEAD), HEAD)
        lanes = pl.ds(pl.multiple_of(member * local_rows, local_rows), local_rows)
        owner = member if arriving else place.s
        there = attended.at[pl.ds(pl.multiple_of(owner * head_cols + h * HEAD, HEAD), HEAD)]
        return remote(
            mixed_low.at[own, lanes], there, mix_send.at[h, turn], mix_recv.at[h, turn], (place.f, member)
        )

    def keep_mixed(h):
        own = pl.ds(pl.multiple_of(h * HEAD, HEAD), HEAD)
        lanes = pl.ds(pl.multiple_of(place.s * local_rows, local_rows), local_rows)
        there = attended.at[pl.ds(pl.multiple_of(place.s * head_cols + h * HEAD, HEAD), HEAD)]
        return pltpu.make_async_copy(mixed_low.at[own, lanes], there, mix_send.at[h, 3])

    turns = slot_rows // local_rows

    def pass_on(index):
        h, turn = index // turns, lax.rem(index, turns)

        @pl.when(turn < turns - 1)
        def _():
            send_mixed(h, turn).start()

        @pl.when(turn == turns - 1)
        def _():
            keep_mixed(h).start()

    def step(index, carry):
        for when in range(12):
            pl.when(index == when)(lambda when=when: chores(when))
        h, turn = index // turns, lax.rem(index, turns)
        start = pl.multiple_of(place.member(turn) * local_rows, local_rows)
        attend_block(h, pl.ds(start, local_rows), q_x, k_wide, v_x, mixed, mixed_low, row_stats)

        @pl.when(index > 0)
        def _():
            pass_on(index - 1)

        return carry

    lax.fori_loop(0, heads * turns, step, 0)
    pass_on(heads * turns - 1)
    for save in head_saves(2):
        save.start()
    for relation in (3, 6):
        gather.arrive_y(relation, 1)
    for relation in (3, 6):
        gather.arrive_x(UP_W, relation)
    for array in (UP_W, OUT_W, DOWN_W, QKV_W):
        gather.finish(array)
    for copy in own_copies()[:2]:
        copy.wait()
    for half in range(halves):
        for index in range(2):
            send_rows(half, index).wait_send()
        pass_rows(half, False).wait_send()
    for h in range(heads):
        for turn in range(turns - 1):
            send_mixed(h, turn).wait_send()
            send_mixed(h, turn, True).wait_recv()
        keep_mixed(h).wait()
        for save in head_saves(h):
            save.wait()
    for save in saves():
        save.wait()


def front(lengths, tokens, read_rows, write_rows, qkv_shard, vectors, up_weight, down_weight, out_weight):
    local_rows, width = tokens.shape
    slot_rows = local_rows * 4
    head_cols = width // 4
    heads = head_cols // HEAD
    shard = width // 8
    vmem = pl.BlockSpec(memory_space=pltpu.VMEM)
    anywhere = pl.BlockSpec(memory_space=pl.ANY)
    dma = pltpu.SemaphoreType.DMA
    hidden = up_weight.shape[1]

    def held(*shape, kind=low):
        return pltpu.VMEM(shape, kind)

    def shaped(*shape, kind=low):
        return jax.ShapeDtypeStruct(shape, kind)

    return pl.pallas_call(
        front_kernel,
        in_specs=[pl.BlockSpec(memory_space=pltpu.SMEM)] + [vmem] * 8,
        out_specs=[vmem] * 2 + [anywhere] * 12,
        out_shape=[
            shaped(8, width, kind=full), shaped(8, hidden, kind=full),
            shaped(slot_rows, width), shaped(width, 3 * head_cols), shaped(heads, HEAD, slot_rows),
            shaped(head_cols, slot_rows), shaped(heads, slot_rows, WIDE), shaped(heads, slot_rows, WIDE),
            shaped(head_cols, slot_rows, kind=full), shaped(heads, 8, slot_rows, kind=full),
            shaped(width, hidden), shaped(hidden, width), shaped(width, width), shaped(width, local_rows),
        ],
        scratch_shapes=[
            held(slot_rows, width), held(width, 3 * head_cols), held(8, shard, 3 * head_cols + HEAD),
            held(32, width), held(heads, WIDE, slot_rows), held(head_cols, slot_rows),
            held(heads, slot_rows, WIDE), held(heads, slot_rows, WIDE), held(heads, WIDE, slot_rows),
            held(head_cols, slot_rows, kind=full), held(head_cols, slot_rows), held(heads, 8, slot_rows, kind=full),
            dma((2, 2)), dma((2, 2)), dma((2,)), dma((2,)), dma((heads, 4)), dma((heads, 4)), dma((3,)),
            dma((5 + heads,)), dma((heads, 2)),
            dma((4, 2, 3)), dma((4, 2, 3)), dma((4, 7)), dma((4, 7)), dma((3, 7, 2)), dma((3, 7, 2)),
            dma((7, 2)), dma((7, 2)), dma((7, 2)), dma((7, 2)),
        ],
        compiler_params=pltpu.CompilerParams(
            vmem_limit_bytes=VMEM_BYTES, collective_id=0, has_side_effects=True
        ),
        name="front",
    )(lengths, tokens, read_rows, write_rows, qkv_shard, vectors, up_weight, down_weight, out_weight)


DW_FIRST = 3
LINES = (3, 0, 2, 1)


def add_low(left, right):
    return (left.astype(full) + right.astype(full)).astype(low)


class Reduce:
    def __init__(self, place, given, sums, across, from_y, from_x, from_z, last, sems):
        self.across, self.last, self.far_up = across, last, last + 1
        self.place, self.given, self.sums = place, given, sums
        self.from_y, self.from_x, self.from_z = from_y, from_x, from_z
        self.y_send, self.y_recv, self.x_send, self.x_recv, self.z_send, self.z_recv = sems

    def dest(self, column, line):
        x = self.place.x
        return 2 * line + (x if column == 0 else 1 - x)

    def slot(self, array, line, column=0):
        if DW_FIRST <= array <= self.last:
            rows = 4 * HEAD if array == self.last else 3 * HEAD
            return self.sums[array].at[self.dest(column, line), pl.ds(0, rows // 4)]
        return self.sums[array].at[line]

    def cut(self, array, ref):
        if DW_FIRST <= array < self.last:
            return ref.at[pl.ds(0, 3 * HEAD // 4)]
        return ref

    def load(self, array, column, line, sem):
        if array == OUT_W:
            return pltpu.make_async_copy(self.given[array].at[line, 0], self.sums[array].at[line], sem)
        source = self.given[UP_W if array == self.far_up else array].at[column, line, 1 if array == self.far_up else 0]
        target = self.across if column == 1 else self.sums[array]
        return pltpu.make_async_copy(source, target.at[line], sem)

    def over_y(self, array, line):
        column, index = (1, 1) if array == UP_W else (0, 0)
        return remote(
            self.given[array].at[column, line, 1], self.from_y.at[index, line], self.y_send.at[index, line],
            self.y_recv.at[index, line], self.place.across_y,
        )

    def add_y(self, array, line):
        self.over_y(array, line).wait_recv()
        slot = self.across.at[line] if array == UP_W else self.slot(DOWN_W, line)
        slot[...] = add_low(slot[...], self.from_y[1 if array == UP_W else 0, line])

    def over_x(self, array, line):
        if array == OUT_W:
            start = self.given[array].at[line, 1]
        elif array == UP_W:
            start = self.across.at[line]
        elif array == DOWN_W:
            start = self.given[array].at[1, line, 0]
        else:
            start = self.slot(array, line, 1)
        return remote(
            start, self.cut(array, self.from_x[array].at[line]), self.x_send.at[array, line],
            self.x_recv.at[array, line], self.place.across_x,
        )

    def add_x(self, array, line):
        self.over_x(array, line).wait_recv()
        slot = self.slot(array, line)
        slot[...] = add_low(slot[...], self.cut(array, self.from_x[array].at[line])[...])

    def along_z(self, array, way, line):
        return remote(
            self.slot(array, line), self.cut(array, self.from_z[array].at[way, line]),
            self.z_send.at[array, way, line], self.z_recv.at[array, way, line],
            self.place.above if way == 0 else self.place.below,
        )

    def add_z(self, array, way, line):
        self.along_z(array, way, line).wait_recv()
        slot = self.slot(array, line)
        slot[...] = add_low(slot[...], self.cut(array, self.from_z[array].at[way, line])[...])

    def hop(self, array, level, lines=(0, 1, 2, 3)):
        @pl.when(self.place.z == level)
        def _():
            for line in range(3, level, -1):
                if line in lines:
                    if level > 0:
                        self.add_z(array, 0, line)
                    self.along_z(array, 0, line).start()

        @pl.when(self.place.z == 3 - level)
        def _():
            for line in range(0, 3 - level):
                if line in lines:
                    if level > 0:
                        self.add_z(array, 1, line)
                    self.along_z(array, 1, line).start()

    def direct(self, array):
        return array != self.far_up

    def to_line(self, array, line):
        where = (2 * line + self.place.x, self.place.s)
        return remote(
            self.slot(array, line), self.cut(array, self.from_z[array].at[self.place.z]),
            self.z_send.at[array, 0, line], self.z_recv.at[array, 0, self.place.z], where,
        )

    def fling(self, array, lines=LINES):
        for line in lines:
            pl.when(self.place.z != line)(lambda line=line: self.to_line(array, line).start())

    def settle(self, array):
        if self.direct(array):
            slot = self.slot(array, self.place.z)
            for line in range(4):

                @pl.when(self.place.z != line)
                def _(line=line):
                    came = self.cut(array, self.from_z[array].at[line])
                    remote(
                        came, came, self.z_send.at[array, 0, line], self.z_recv.at[array, 0, line], self.place.core
                    ).wait_recv()
                    slot[...] = add_low(slot[...], came[...])

            return
        for line in range(4):

            @pl.when(self.place.z == line)
            def _(line=line):
                if line > 0:
                    self.add_z(array, 0, line)
                if line < 3:
                    self.add_z(array, 1, line)

    def finish(self, array):
        for line in range(4):
            if array != self.far_up:
                self.over_x(array, line).wait_send()
            if self.direct(array):
                pl.when(self.place.z != line)(lambda line=line: self.to_line(array, line).wait_send())
            else:
                pl.when(self.place.z < line)(lambda line=line: self.along_z(array, 0, line).wait_send())
                pl.when(self.place.z > line)(lambda line=line: self.along_z(array, 1, line).wait_send())
            if array in (UP_W, DOWN_W):
                self.over_y(array, line).wait_send()


class Spread:
    def __init__(self, place, blocks, source, send, recv):
        self.place, self.blocks, self.source, self.send, self.recv = place, blocks, source, send, recv
        self.near = 2 * place.y + 1 - place.c
        self.far = 2 * (1 - place.y) + place.c
        self.last = 2 * (1 - place.y) + 1 - place.c

    def copy(self, kind, arriving=False):
        place = self.place
        if kind == 2:
            here = self.blocks.at[self.last if arriving else self.far]
            return remote(here, here, self.send.at[2], self.recv.at[2], place.core)
        member = (self.near, self.far)[kind] if arriving else place.s
        return remote(
            self.source, self.blocks.at[member], self.send.at[kind], self.recv.at[kind],
            (place.core, place.across_y)[kind],
        )

    def start(self):
        self.copy(1).start()
        self.copy(0).start()

    def pass_on(self):
        self.copy(1, True).wait_recv()
        self.copy(2).start()

    def finish(self):
        self.blocks[self.place.s] = self.source[...]
        self.copy(0, True).wait_recv()
        self.copy(2, True).wait_recv()
        for kind in range(3):
            self.copy(kind).wait_send()


def back_kernel(
    length_ref, grad_own, vectors_in, q_in, k_in, k_wide_in, v_wide_in, mixed_in, stats_in, rows_in, weight_in, resid_in, up_given, down_given, out_given,
    input_out, read_out, write_out, qkv_out, vector_out, up_out, down_out, out_out,
    q_x, k_t, k_wide, v_wide, mixed, row_stats, grad_t, q_here, do_x, grads, grad_k, grad_v, rows_ref, weight_ref, resid_ref,
    up_sum, out_sum, down_sum, far_sum_up, across_up, dw, both_y, up_x, out_x, down_x, dw_x, up_z, out_z, down_z, dw_z, far_z,
    up_last, out_last, up_all, out_other, down_all, dw_all,
    near_send, near_recv, far_sum, far_recv, memory_all, memory_own,
    mix_send, mix_recv, local_sem, saved_sem, mine_sem, share_send, share_recv, near_s, near_r, far_s, far_r, cross_s, cross_r,
    *sems,
):
    place = Place()
    heads, _, slot_rows = q_in.shape
    width, local_rows = grad_own.shape
    head_cols = heads * HEAD
    last = DW_FIRST + heads - 1
    far_up = last + 1
    given = {UP_W: up_given, OUT_W: out_given, DOWN_W: down_given}
    sums = {UP_W: up_sum, OUT_W: out_sum, DOWN_W: down_sum}
    from_x = {UP_W: up_x, OUT_W: out_x, DOWN_W: down_x}
    from_z = {UP_W: up_z, OUT_W: out_z, DOWN_W: down_z}
    for h in range(heads):
        sums[DW_FIRST + h], from_x[DW_FIRST + h] = dw.at[h], dw_x.at[h]
        from_z[DW_FIRST + h] = dw_z.at[h]
    sums[far_up], from_z[far_up] = far_sum_up, far_z
    reduce = Reduce(place, given, sums, across_up, both_y, from_x, from_z, last, sems)

    peers = (place.across_y, place.diagonal, place.core)

    def member_rows(turn):
        member = place.member(turn)
        return member, pl.ds(pl.multiple_of(member * local_rows, local_rows), local_rows)

    def send_grad(turn, arriving=False):
        member, lanes = member_rows(turn)
        own_lanes = pl.ds(pl.multiple_of(place.s * local_rows, local_rows), local_rows)
        src = grad_own.at[pl.ds(pl.multiple_of(member * head_cols, head_cols), head_cols)]
        return remote(
            src, grad_t.at[:, lanes if arriving else own_lanes], mix_send.at[turn], mix_recv.at[turn], peers[turn]
        )

    def saved_loads(h):
        own = pl.ds(h * HEAD, HEAD)
        pairs = (
            (k_wide_in.at[h], k_wide.at[h]), (q_in.at[h], q_x.at[h]), (v_wide_in.at[h], v_wide.at[h]),
            (mixed_in.at[own], mixed.at[own]), (stats_in.at[h], row_stats.at[h]), (k_in.at[own], k_t.at[own]),
        )
        return [pltpu.make_async_copy(src, dst, saved_sem.at[h, i]) for i, (src, dst) in enumerate(pairs)]

    def sum_loads(array):
        index = array if array < DW_FIRST else DW_FIRST
        return [reduce.load(array, 0, line, mine_sem.at[index, line]) for line in LINES]

    def across_loads():
        return [reduce.load(UP_W, 1, line, mine_sem.at[DW_FIRST + 1, line]) for line in LINES]

    for load in sum_loads(far_up):
        load.start()
    for load in saved_loads(0):
        load.start()
    greet(place, True)
    for turn in (1, 0, 2):
        send_grad(turn).start()
    loads = []
    for index, (src, dst) in enumerate(((rows_in, rows_ref), (weight_in, weight_ref), (resid_in, resid_ref))):
        loads.append(pltpu.make_async_copy(src, dst, local_sem.at[index]))

    def send_x(array, lines=LINES):
        for line in lines:
            reduce.over_x(array, line).start()

    send_x(DOWN_W)
    send_x(OUT_W)
    for array in (DOWN_W, UP_W):
        for line in LINES:
            reduce.over_y(array, line).start()
    for load in across_loads() + sum_loads(UP_W) + sum_loads(OUT_W) + sum_loads(DOWN_W):
        load.start()
    for load in loads:
        load.start()

    for h in range(1, heads):
        for load in saved_loads(h):
            load.start()

    own_lanes = pl.ds(pl.multiple_of(place.s * local_rows, local_rows), local_rows)
    grad_t[:, own_lanes] = grad_own[pl.ds(pl.multiple_of(place.s * head_cols, head_cols), head_cols), :]

    def take_x(array, lines=LINES):
        for line in lines:
            reduce.add_x(array, line)

    turns = slot_rows // local_rows

    def weight_part(h):
        if h == 0:
            loads[0].wait()
        base = 3 * h * HEAD
        part = jnp.transpose(mul(grads[base : base + 3 * HEAD, :], rows_ref[...])).astype(low)
        half = width // 16
        for dest in range(8):
            start = 2 * half * dest
            dw[h, dest, :half, :] = jnp.concatenate(
                [part[start : start + half], part[start + half : start + 2 * half]], axis=1
            )
            if h == heads - 1:
                dw[h, dest, half:, :] = vectors_in[dest].astype(low)
        if h == heads - 1:
            total = jnp.sum(grads[...].astype(full), axis=1, keepdims=True)
            spread = jnp.transpose(jnp.broadcast_to(total, (total.shape[0], WIDE)))[0:1]
            for kind, first_dest in ((0, 0), (2, 4)):
                for head in range(heads):
                    start = (3 * head + kind) * HEAD
                    dw[h, first_dest + place.s, half : half + 1, head * HEAD : (head + 1) * HEAD] = spread[
                        :, start : start + HEAD
                    ].astype(low)
        send_x(DW_FIRST + h)

    share = {OUT_W: (out_last, out_other)}

    def settled(array):
        return sums[array].at[place.z]

    def sum_y(array):
        mine_now = settled(array)
        return remote(mine_now, share[array][0], share_send.at[array, 0], share_recv.at[array, 0], place.across_y)

    def half_to_core(array):
        mine_now = settled(array)
        return remote(mine_now, share[array][1], share_send.at[array, 1], share_recv.at[array, 1], place.core)

    def spread_of(array):
        if array in (UP_W, DOWN_W):
            return Spread(
                place, {UP_W: up_all, DOWN_W: down_all}[array], sums[array].at[place.z], share_send.at[array],
                share_recv.at[array],
            )
        h = array - DW_FIRST
        return Spread(
            place, dw_all.at[h, :, pl.ds(0, reduce.slot(array, 0).shape[0])], reduce.slot(array, place.z),
            share_send.at[array], share_recv.at[array],
        )

    def cross_up():
        return remote(far_sum_up.at[place.z], up_last, cross_s.at[0], cross_r.at[0], place.across_y)

    def settle_up():
        reduce.settle(UP_W)
        cross_up().wait_recv()
        slot = sums[UP_W].at[place.z]
        slot[...] = add_low(slot[...], up_last[...])
        spread_of(UP_W).start()

    def add_last(array):
        sum_y(array).wait()
        slot = settled(array)
        slot[...] = add_low(slot[...], share[array][0][...])
        half_to_core(array).start()

    first, second = DW_FIRST, DW_FIRST + 1

    def pass_up(lines):
        for line in lines:
            reduce.add_y(UP_W, line)
            reduce.over_x(UP_W, line).start()

    def chores(index):
        if index == 1:
            send_grad(2, True).wait_recv()
            for load in across_loads() + sum_loads(UP_W) + sum_loads(OUT_W) + sum_loads(DOWN_W):
                load.wait()
        elif index == 2:
            send_grad(1, True).wait_recv()
            reduce.hop(far_up, 1, (3, 0))
        elif index == 3:
            send_grad(0, True).wait_recv()
            reduce.hop(far_up, 1, (2, 1))
        elif index == 4:
            for load in saved_loads(1):
                load.wait()
            weight_part(0)
            reduce.hop(far_up, 2)
        elif index == 5:
            take_x(DOWN_W)
            for line in (3, 0):
                reduce.add_y(DOWN_W, line)
                reduce.fling(DOWN_W, (line,))
        elif index == 6:
            for line in (2, 1):
                reduce.add_y(DOWN_W, line)
                reduce.fling(DOWN_W, (line,))
            take_x(OUT_W)
            reduce.fling(OUT_W)
            reduce.settle(far_up)
            cross_up().start()
        elif index == 7:
            take_x(first)
            reduce.fling(first)
        elif index == 8:
            for load in saved_loads(2):
                load.wait()
            weight_part(1)
            pass_up((3, 0))
        elif index == 9:
            pass_up((2,))
        elif index == 10:
            pass_up((1,))
            reduce.settle(DOWN_W)
            spread_of(DOWN_W).start()
        elif index == 11:
            take_x(UP_W, (3, 0))
            reduce.fling(UP_W, (3, 0))
            take_x(second)
            reduce.fling(second)

    def step(index, carry):
        for when in range(1, 12):
            pl.when(index == when)(lambda when=when: chores(when))
        h, turn = index // turns, lax.rem(index, turns)
        _, lanes = member_rows(turns - 1 - turn)
        attend_back(
            h, lanes, q_x, q_here, do_x, grad_t, mixed, row_stats, k_t, k_wide, v_wide, grads, grad_k, grad_v, turn == 0
        )

        @pl.when(turn == turns - 1)
        def _():
            base = pl.multiple_of(3 * h * HEAD, HEAD)
            grads[pl.ds(base + HEAD, HEAD), :] = grad_k[...].astype(low)
            grads[pl.ds(base + 2 * HEAD, HEAD), :] = grad_v[...].astype(low)

        return carry

    for load in sum_loads(far_up):
        load.wait()
    reduce.hop(far_up, 0)
    for load in saved_loads(0):
        load.wait()
    lax.fori_loop(0, heads * turns, step, 0)

    loads[1].wait()
    loads[2].wait()

    halves, part = 2, local_rows // 2
    length = length_ref[0]

    def memory_pick(rows, start):
        line = lax.broadcasted_iota(jnp.int32, (32, rows), 0)
        row = start + lax.broadcasted_iota(jnp.int32, (32, rows), 1)
        wanted = jnp.where(line < 16, line, length - MEM + line - 16)
        used = (line < MEM) | ((line >= 16) & (line < 16 + MEM))
        return jnp.where(used & (wanted == row), 1.0, 0.0).astype(low)

    def part_for(turn, half):
        start = pl.multiple_of(place.member(turn) * local_rows + half * part, part)
        return mul(grads[:, pl.ds(start, part)], weight_ref[...], TT)

    def share_near(index, half):
        rows = pl.ds(half * part, part)
        return remote(
            near_send.at[index, rows], near_recv.at[index, rows], near_s.at[index, half], near_r.at[index, half],
            place.core,
        )

    def share_far(quarter):
        rows = pl.ds(quarter * (part // 2), part // 2)
        return remote(far_sum.at[rows], far_recv.at[rows], far_s.at[quarter], far_r.at[quarter], place.across_y)

    for half in range(halves):
        near_send[0, half * part : (half + 1) * part, :] = part_for(1, half).astype(low)
        share_near(0, half).start()
    for half in range(halves):
        rows = slice(half * part, (half + 1) * part)
        far_part = part_for(0, half)
        share_near(0, half).wait_recv()
        far_sum[rows, :] = (far_part + near_recv[0, rows, :].astype(full)).astype(low)
        share_far(2 * half).start()
        if half == 0:
            share_far(1).start()
    weight_part(heads - 1)
    reduce.settle(OUT_W)
    sum_y(OUT_W).start()
    take_x(UP_W, (2, 1))
    reduce.fling(UP_W, (2, 1))
    taken = mul(memory_pick(slot_rows, 0), grads[...], NT).astype(low)
    own_part = mul(memory_pick(local_rows, place.s * local_rows), resid_ref[...].astype(low))
    memory_own[...] = (mul(taken, weight_ref[...], NT) + own_part).astype(low)
    memory = Spread(place, memory_all, memory_own, share_send.at[DW_FIRST + heads], share_recv.at[DW_FIRST + heads])
    memory.start()
    for half in range(halves):
        rows = slice(half * part, (half + 1) * part)
        near_send[1, rows, :] = part_for(2, half).astype(low)
        share_near(1, half).start()
    for half in range(halves):
        resid_ref[half * part : (half + 1) * part, :] += part_for(3, half)
    take_x(last)
    reduce.fling(last)
    reduce.settle(first)
    spread_of(first).start()
    add_last(OUT_W)
    reduce.settle(second)
    spread_of(second).start()
    settle_up()
    reduce.settle(last)
    spread_of(last).start()
    share_far(3).start()
    memory.pass_on()
    for h in (heads - 1, 0, 1):
        spread_of(DW_FIRST + h).pass_on()
    for array in (UP_W, DOWN_W):
        spread_of(array).pass_on()
    for array, out in ((OUT_W, out_out),):
        columns = out.shape[1] // 2
        out[:, pl.ds(pl.multiple_of(place.c * columns, columns), columns)] = settled(array)[...]
        half_to_core(array).wait()
        out[:, pl.ds(pl.multiple_of((1 - place.c) * columns, columns), columns)] = share[array][1][...]
    for h in range(heads):
        spread_of(DW_FIRST + h).finish()
    spread_of(UP_W).finish()
    spread_of(DOWN_W).finish()
    quarter = down_out.shape[0] // 4
    part_columns = up_out.shape[1] // 4
    for member in range(4):
        start = (2 * (member % 2) + member // 2) * part_columns
        up_out[:, start : start + part_columns] = up_all[member]
        down_out[member * quarter : (member + 1) * quarter, :] = down_all[member]
    half = qkv_out.shape[0] // 2
    for kind in range(3):
        for member in range(4):
            for h in range(heads):
                start = kind * width + (member * heads + h) * HEAD
                for side in range(2):
                    lanes = (3 * side + kind) * HEAD
                    qkv_out[side * half : (side + 1) * half, start : start + HEAD] = dw_all[
                        h, member, :half, lanes : lanes + HEAD
                    ]
    vector_sum = dw_all[heads - 1, 0, half:, :].astype(full)
    for member in range(1, 4):
        vector_sum = vector_sum + dw_all[heads - 1, member, half:, :].astype(full)
    vector_out[...] = vector_sum
    memory.finish()
    total = memory_all[0].astype(full)
    for member in range(1, 4):
        total = total + memory_all[member].astype(full)
    read_out[...] = total[:MEM]
    write_out[...] = total[16 : 16 + MEM]
    for half in range(halves):
        rows = slice(half * part, (half + 1) * part)
        share_near(1, half).wait_recv()
        for quarter in (2 * half, 2 * half + 1):
            share_far(quarter).wait_recv()
        grad_layer = resid_ref[rows, :] + near_recv[1, rows, :].astype(full) + far_recv[rows, :].astype(full)
        rows_at = place.s * local_rows + half * part + lax.broadcasted_iota(jnp.int32, (part, 1), 0)
        in_write = (rows_at >= length - MEM) & (rows_at < length)
        input_out[rows, :] = jnp.where((rows_at < MEM) | in_write, 0.0, grad_layer)
    for array in range(DW_FIRST + heads + 1):
        reduce.finish(array)
    cross_up().wait_send()
    for turn in range(3):
        send_grad(turn).wait_send()
    for half in range(halves):
        for index in range(2):
            share_near(index, half).wait_send()
        for quarter in (2 * half, 2 * half + 1):
            share_far(quarter).wait_send()


def back(lengths, grad_own, saved, vectors, rows, weight, resid, up_given, down_given, out_given):
    q_x, k_t, k_wide, v_wide, mixed, row_stats = saved
    heads, _, slot_rows = q_x.shape
    width, local_rows = grad_own.shape
    hidden = 32 * up_given.shape[3]
    shard, head_cols = width // 8, heads * HEAD
    half, small, piece = hidden // 2, width // 2, hidden // 32
    vmem = pl.BlockSpec(memory_space=pltpu.VMEM)
    anywhere = pl.BlockSpec(memory_space=pl.ANY)
    dma = pltpu.SemaphoreType.DMA
    arrays = DW_FIRST + heads

    def held(*shape, kind=low):
        return pltpu.VMEM(shape, kind)

    tall = (shard // 2 + 16, 6 * HEAD)
    return pl.pallas_call(
        back_kernel,
        in_specs=[pl.BlockSpec(memory_space=pltpu.SMEM)] + [vmem] * 2 + [anywhere] * 12,
        out_specs=[vmem] * 8,
        out_shape=[
            jax.ShapeDtypeStruct((local_rows, width), full),
            jax.ShapeDtypeStruct((MEM, width), full),
            jax.ShapeDtypeStruct((MEM, width), full),
            jax.ShapeDtypeStruct((shard, 3 * width), low),
            jax.ShapeDtypeStruct((16, 6 * HEAD), full),
            jax.ShapeDtypeStruct((shard, hidden), low),
            jax.ShapeDtypeStruct((hidden // 8, width), low),
            jax.ShapeDtypeStruct((shard, width), low),
        ],
        scratch_shapes=[
            held(heads, HEAD, slot_rows), held(head_cols, slot_rows), held(heads, slot_rows, WIDE),
            held(heads, slot_rows, WIDE), held(head_cols, slot_rows, kind=full), held(heads, 8, slot_rows, kind=full),
            held(head_cols, slot_rows), held(WIDE, local_rows), held(WIDE, local_rows), held(3 * head_cols, slot_rows),
            held(HEAD, slot_rows, kind=full), held(HEAD, slot_rows, kind=full),
            held(slot_rows, width), held(width, 3 * head_cols), held(local_rows, width, kind=full),
            held(4, piece, width), held(4, shard, small), held(4, piece, width), held(4, piece, width),
            held(4, piece, width), held(heads, 8, *tall), held(2, 4, piece, width),
            held(4, piece, width), held(4, shard, small), held(4, piece, width), held(heads, 4, *tall),
            held(4, piece, width), held(4, shard, small), held(4, piece, width), held(heads, 4, *tall),
            held(2, 4, piece, width),
            held(piece, width), held(shard, small), held(4, piece, width), held(shard, small),
            held(4, piece, width), held(heads, 4, *tall),
            held(2, local_rows, width), held(2, local_rows, width), held(local_rows, width),
            held(local_rows, width), held(4, 32, width), held(32, width),
            dma((3,)), dma((3,)), dma((3,)), dma((heads, 6)), dma((5, 4)), dma((arrays + 1, 3)),
            dma((arrays + 1, 3)), dma((2, 2)), dma((2, 2)), dma((4,)), dma((4,)),
            dma((1,)), dma((1,)),
            dma((2, 4)), dma((2, 4)), dma((arrays, 4)), dma((arrays, 4)),
            dma((arrays + 1, 2, 4)), dma((arrays + 1, 2, 4)),
        ],
        compiler_params=pltpu.CompilerParams(
            vmem_limit_bytes=VMEM_BYTES, collective_id=1, has_side_effects=True
        ),
        name="back",
    )(
        lengths, grad_own, vectors, q_x, k_t, k_wide, v_wide, mixed, row_stats, rows, weight, resid,
        up_given, down_given, out_given,
    )


def phi_parts(value):
    normal = 0.5 * (1.0 + lax.erf(value * (0.5**0.5)))
    density = jnp.exp(-0.5 * value * value) * (0.5 * 2.0**0.5 * 3.141592653589793**-0.5)
    return normal, normal + value * density


def statistics(values):
    centre = values - jnp.mean(values, axis=1, keepdims=True)
    factor = lax.rsqrt(jnp.mean(centre * centre, axis=1, keepdims=True) + norm_epsilon)
    return centre * factor, factor


def norm_back(grad, gain, normed, factor):
    scaled = grad * gain
    first = jnp.mean(scaled, axis=1, keepdims=True)
    second = jnp.mean(scaled * normed, axis=1, keepdims=True)
    return factor * (scaled - first - normed * second)


def column_total(values):
    return jnp.sum(values, axis=0, keepdims=True)


def middle_kernel(
    length_ref, cotangent, small, up_bias, rows_in, attended_in, up_in, down_in, out_in,
    output, resid_out, grad_own, vector_out, up_out, down_out, out_out,
    layer_in, attended, up_w, down_w, out_w, hidden, slope, normed_one, middle_low, grad_down,
    grad_two, grad_mid, totals, up_total, up_grad, down_grad, out_grad, up_sum, down_sum, out_sum,
    from_y, load_sem, save_sem, c_send, c_recv, y_send, y_recv,
):
    place = Place()
    rows, width = cotangent.shape
    ff = up_w.shape[1]
    chunk = ff // 4
    shard = width // 8
    barrier = pltpu.get_barrier_semaphore()
    for where in (place.core, place.across_y):
        pl.semaphore_signal(barrier, inc=1, device_id=where, device_id_type=MESH)

    def chunk_lanes(j):
        return pl.ds(pl.multiple_of(j * chunk, chunk), chunk)

    def up_load(j):
        return pltpu.make_async_copy(up_in.at[:, chunk_lanes(j)], up_w.at[:, chunk_lanes(j)], load_sem.at[j])

    def down_load(j):
        return pltpu.make_async_copy(down_in.at[chunk_lanes(j)], down_w.at[chunk_lanes(j)], load_sem.at[4 + j])

    first_loads = [
        pltpu.make_async_copy(
            rows_in.at[pl.ds(pl.multiple_of(place.s * rows, rows), rows)], layer_in, load_sem.at[8]
        ),
        pltpu.make_async_copy(attended_in, attended, load_sem.at[9]),
        pltpu.make_async_copy(out_in, out_w, load_sem.at[10]),
    ]
    for load in first_loads:
        load.start()
    for j in range(4):
        up_load(j).start()
        down_load(j).start()
    out_bias, gain_one, shift_one = small[0:1, :], small[1:2, :], small[2:3, :]
    down_bias, gain_two, shift_two = small[3:4, :], small[4:5, :], small[5:6, :]
    for load in first_loads:
        load.wait()

    branch = mul(attended[...], out_w[...], TN)
    normed, factor_one = statistics(layer_in[...].astype(full) + branch + out_bias)
    normed_one[...] = normed
    middle_low[...] = (normed * gain_one + shift_one).astype(low)
    grad_mid[...] = jnp.zeros_like(grad_mid)

    def forward_chunk(j, carry):
        up_load(j).wait()
        lanes = chunk_lanes(j)
        value = mul(middle_low[...], up_w[:, lanes]) + up_bias[0:1, lanes]
        normal, slope_here = phi_parts(value)
        hidden[:, lanes] = (value * normal).astype(low)
        slope[:, lanes] = slope_here
        down_load(j).wait()
        grad_mid[...] += mul(hidden[:, lanes], down_w[lanes, :])
        return carry

    lax.fori_loop(0, 4, forward_chunk, 0)
    middle = normed_one[...] * gain_one + shift_one
    normed_two, factor_two = statistics(middle + grad_mid[...] + down_bias)
    places = place.s * rows + lax.broadcasted_iota(jnp.int32, (rows, 1), 0)
    in_slot = places < length_ref[0]
    output[...] = jnp.where(in_slot, normed_two * gain_two + shift_two, 0.0).astype(low)
    grad_final = jnp.where(in_slot, cotangent[...].astype(full), 0.0)
    totals[4:5, :] = column_total(grad_final * normed_two)
    totals[5:6, :] = column_total(grad_final)
    grad_resid = norm_back(grad_final, gain_two, normed_two, factor_two)
    grad_two[...] = grad_resid
    grad_down[...] = grad_resid.astype(low)
    totals[3:4, :] = column_total(grad_down[...].astype(full))
    pl.semaphore_wait(barrier, 2)

    def down_piece(ref, line, column, far, core):
        dest = 2 * line + (place.x if column == 0 else 1 - place.x)
        y = place.y if far == 0 else 1 - place.y
        return ref.at[pl.ds(pl.multiple_of(dest * 4 * shard + (2 * y + core) * shard, shard), shard)]

    def side_piece(ref, line, column, core):
        dest = 2 * line + (place.x if column == 0 else 1 - place.x)
        half = ref.shape[1] // 2
        return ref.at[
            pl.ds(pl.multiple_of(dest * shard, shard), shard), pl.ds(pl.multiple_of(core * half, half), half)
        ]

    def down_share(line, column, far):
        return remote(
            down_piece(down_grad, line, column, far, 1 - place.c), down_sum.at[column, line, far],
            c_send.at[2 + far, column, line], c_recv.at[2 + far, column, line], place.core,
        )

    def side_slot(array, line, column):
        return out_sum.at[line, column] if array == 1 else up_sum.at[column, line]

    def over_y(line):
        return remote(down_sum.at[1, line, 1], from_y.at[line], y_send.at[line], y_recv.at[line], place.across_y)

    def side_share(array, line, column):
        grad = (up_grad, out_grad)[array]
        return remote(
            side_piece(grad, line, column, 1 - place.c), side_slot(array, line, column),
            c_send.at[array, column, line], c_recv.at[array, column, line], place.core,
        )

    def down_save(column, line):
        return pltpu.make_async_copy(down_sum.at[column, line], down_out.at[column, line], save_sem.at[2, column, line])

    def side_saves(array, column, line):
        if array == 1:
            return [pltpu.make_async_copy(
                side_slot(1, line, column), out_out.at[line, column], save_sem.at[1, column, line]
            )]
        return [
            pltpu.make_async_copy(
                up_sum.at[column, line, :, chunk_lanes(place.y if far == 0 else 1 - place.y)],
                up_out.at[column, line, far], save_sem.at[3 * far, column, line],
            )
            for far in range(2)
        ]

    def add_far(column, line):
        down_share(line, column, 1).wait_recv()
        down_sum[column, line, 1] = add_low(
            down_sum[column, line, 1], down_piece(down_grad, line, column, 1, place.c)[...]
        )

    def down_chunk(line, carry):
        lanes = chunk_lanes(line)
        down_grad[lanes, :] = mul(hidden[:, lanes], grad_down[...], TN).astype(low)
        for far in (1, 0):
            for column in (1, 0):
                down_share(line, column, far).start()

        @pl.when(line > 0)
        def _():
            add_far(1, line - 1)
            over_y(line - 1).start()

        return carry

    lax.fori_loop(0, 4, down_chunk, 0)
    add_far(1, 3)
    over_y(3).start()
    grad_mid[...] = grad_two[...]

    def back_chunk(turn, carry):
        j = lax.rem(2 * (1 - place.c) + turn, 4)
        lanes = chunk_lanes(j)
        grad_up = (mul(grad_down[...], down_w[lanes, :], NT) * slope[:, lanes]).astype(low)
        up_total[0:1, lanes] = column_total(grad_up.astype(full))
        up_grad[:, lanes] = mul(middle_low[...], grad_up, TN).astype(low)
        grad_mid[...] += mul(grad_up, up_w[:, lanes], NT)

        @pl.when(turn == 1)
        def _():
            for column in (1, 0):
                for line in LINES:
                    side_share(0, line, column).start()

        return carry

    lax.fori_loop(0, 4, back_chunk, 0)
    grad_middle = grad_mid[...]
    normed = normed_one[...]
    totals[1:2, :] = column_total(grad_middle * normed)
    totals[2:3, :] = column_total(grad_middle)
    grad_one = norm_back(grad_middle, gain_one, normed, factor_one)
    resid_out[...] = grad_one
    grad_branch = grad_one.astype(low)
    totals[0:1, :] = column_total(grad_branch.astype(full))
    out_grad[...] = mul(attended[...], grad_branch).astype(low)
    for column in (1, 0):
        for line in LINES:
            side_share(1, line, column).start()
    grad_own[...] = mul(out_w[...], grad_branch, NT).astype(low)

    def add_down(column, line):
        down_share(line, column, 0).wait_recv()
        down_sum[column, line, 0] = add_low(
            down_sum[column, line, 0], down_piece(down_grad, line, column, 0, place.c)[...]
        )
        if column == 0:
            add_far(column, line)
        else:
            over_y(line).wait()
            down_sum[column, line, 0] = add_low(down_sum[column, line, 0], from_y[line])
        down_save(column, line).start()

    def add_side(array, column, line):
        slot = side_slot(array, line, column)
        side_share(array, line, column).wait_recv()
        slot[...] = add_low(slot[...], side_piece((up_grad, out_grad)[array], line, column, place.c)[...])
        for save in side_saves(array, column, line):
            save.start()

    for line in LINES:
        add_down(0, line)
    for column in (1, 0):
        for line in LINES:
            add_side(0, column, line)
    vector_out[...] = jnp.zeros_like(vector_out)
    for dest in range(8):
        for index, (line, start) in enumerate(((0, 2), (0, 3), (1, 0), (2, 1), (2, 2), (2, 3))):
            vector_out[dest, line : line + 1, start * shard : (start + 1) * shard] = totals[
                index : index + 1, dest * shard : (dest + 1) * shard
            ]
        base = dest * 4 * shard
        vector_out[dest, 1:2, shard:] = up_total[0:1, base : base + 3 * shard]
        vector_out[dest, 2:3, :shard] = up_total[0:1, base + 3 * shard : base + 4 * shard]
    for column in range(2):
        for line in range(4):
            add_side(1, column, line)
    for line in LINES:
        add_down(1, line)
    for column in range(2):
        for line in range(4):
            for array in range(2):
                side_share(array, line, column).wait_send()
                for save in side_saves(array, column, line):
                    save.wait()
            for far in range(2):
                down_share(line, column, far).wait_send()
            down_save(column, line).wait()


def middle_part(lengths, cotangent, small, up_bias, rows_full, attended, up_full, down_full, out_full):
    rows, width = cotangent.shape
    ff = up_full.shape[1]
    shard = width // 8
    vmem = pl.BlockSpec(memory_space=pltpu.VMEM)
    anywhere = pl.BlockSpec(memory_space=pl.ANY)
    dma = pltpu.SemaphoreType.DMA

    def held(*shape, kind=low):
        return pltpu.VMEM(shape, kind)

    def shaped(*shape, kind=low):
        return jax.ShapeDtypeStruct(shape, kind)

    up_parts, down_parts, out_parts = (2, 4, shard, ff // 2), (2, 4, 2, ff // 32, width), (4, 2, shard, width // 2)
    return pl.pallas_call(
        middle_kernel,
        in_specs=[pl.BlockSpec(memory_space=pltpu.SMEM)] + [vmem] * 3 + [anywhere] * 5,
        out_specs=[vmem] * 4 + [anywhere] * 3,
        out_shape=[
            shaped(rows, width), shaped(rows, width, kind=full), shaped(width, rows),
            shaped(8, 16, 4 * shard, kind=full), shaped(*down_parts), shaped(*down_parts), shaped(*out_parts),
        ],
        scratch_shapes=[
            held(rows, width), held(width, rows), held(width, ff), held(ff, width), held(width, width), held(rows, ff), held(rows, ff, kind=full),
            held(rows, width, kind=full), held(rows, width), held(rows, width), held(rows, width, kind=full),
            held(rows, width, kind=full), held(8, width, kind=full), held(8, ff, kind=full),
            held(width, ff), held(ff, width), held(width, width), held(*up_parts), held(*down_parts),
            held(*out_parts), held(4, ff // 32, width), dma((11,)), dma((4, 2, 4)), dma((4, 2, 4)),
            dma((4, 2, 4)), dma((4,)), dma((4,)),
        ],
        compiler_params=pltpu.CompilerParams(
            vmem_limit_bytes=VMEM_BYTES, collective_id=2, has_side_effects=True
        ),
        name="middle",
    )(lengths, cotangent, small, up_bias, rows_full, attended, up_full, down_full, out_full)


def finish_kernel(
    output_in, input_in, qkv_in, vector_in, up_in, down_in, out_in, read_in, write_in,
    output, input_out, read_out, write_out, qkv_out, qv_out, out_out, out_b, gain_one, shift_one, up_out, up_b,
    down_out, down_b, gain_two, shift_two,
):
    shard = out_b.shape[1]
    output[...] = output_in[...]
    input_out[...] = input_in[...]
    for given, out in ((read_in, read_out), (write_in, write_out)):
        for line in range(given.shape[0]):
            out[line] = given[line : line + 1]
    for given, out in ((qkv_in, qkv_out), (up_in, up_out), (down_in, down_out), (out_in, out_out)):
        out[...] = given[...].astype(full)
    qv_out[...] = vector_in[0:1, : 2 * shard]
    out_b[...] = vector_in[0:1, 2 * shard : 3 * shard]
    gain_one[...] = vector_in[0:1, 3 * shard :]
    shift_one[...] = vector_in[1:2, :shard]
    up_b[:, : 3 * shard] = vector_in[1:2, shard:]
    up_b[:, 3 * shard :] = vector_in[2:3, :shard]
    down_b[...] = vector_in[2:3, shard : 2 * shard]
    gain_two[...] = vector_in[2:3, 2 * shard : 3 * shard]
    shift_two[...] = vector_in[2:3, 3 * shard :]


def finish(output, input_grad, qkv_grad, vectors, up_grad, down_grad, out_grad, grad_read, grad_write):
    shard = qkv_grad.shape[0]

    def shaped(*shape, kind=full):
        return jax.ShapeDtypeStruct(shape, kind)

    line = shaped(1, shard)
    steps = 2

    def rows(array):
        return pl.BlockSpec((array.shape[0] // steps,) + array.shape[1:], lambda i: (i, 0))

    def once(*shape):
        return pl.BlockSpec(shape, lambda i: (0,) * len(shape))

    lone = once(1, shard)
    memory = (grad_read.shape[0], 1, grad_read.shape[1])
    return pl.pallas_call(
        finish_kernel,
        grid=(steps,),
        in_specs=[
            rows(output), rows(input_grad), rows(qkv_grad), once(*vectors.shape), rows(up_grad), rows(down_grad),
            rows(out_grad), once(*grad_read.shape), once(*grad_write.shape),
        ],
        out_specs=[
            rows(output), rows(input_grad), once(*memory), once(*memory), rows(qkv_grad), once(1, 2 * shard),
            rows(out_grad), lone, lone, lone, rows(up_grad), once(1, 4 * shard), rows(down_grad), lone, lone, lone,
        ],
        out_shape=[
            shaped(*output.shape, kind=low), shaped(*input_grad.shape), shaped(*memory), shaped(*memory),
            shaped(*qkv_grad.shape), shaped(1, 2 * shard), shaped(*out_grad.shape), line, line, line,
            shaped(*up_grad.shape), shaped(1, 4 * shard), shaped(*down_grad.shape), line, line, line,
        ],
        compiler_params=pltpu.CompilerParams(vmem_limit_bytes=VMEM_BYTES),
        name="finish",
    )(output, input_grad, qkv_grad, vectors, up_grad, down_grad, out_grad, grad_read, grad_write)


def normalize(values, gain_vec, shift_vec):
    centre = values - jnp.mean(values, axis=-1, keepdims=True)
    factor = lax.rsqrt(jnp.mean(centre * centre, axis=-1, keepdims=True) + norm_epsilon)
    return centre * factor * gain_vec + shift_vec


def column_sums(values):
    return jnp.sum(values, axis=0, dtype=full)


def on_block(
    tokens, read_rows, write_rows, lengths, qkv_weight, vectors, out_weight, up_weight, down_weight, cotangent
):
    total = sum(vector.shape[0] for vector in vectors)
    packed, start = jnp.zeros((1, total), full), 0
    for vector in vectors:
        size = vector.shape[0]
        packed = packed + jnp.pad(vector.astype(full).reshape(1, -1), ((0, 0), (start, total - start - size)))
        start += size
    (small, up_bias, rows, weight, q_t, k_t, k_wide, v_wide, mixed, row_stats, up_full, down_full, out_full,
     attended) = front(
        lengths, tokens, read_rows, write_rows, qkv_weight, packed, up_weight, down_weight, out_weight
    )
    output, resid, grad_own, vector_parts, up_parts, down_parts, out_parts = middle_part(
        lengths, cotangent, small, up_bias, rows, attended, up_full, down_full, out_full
    )
    saved = (q_t, k_t, k_wide, v_wide, mixed, row_stats)
    input_grad, grad_read, grad_write, qkv_grad, vector_sum, up_grad, down_grad, out_grad = back(
        lengths, grad_own, saved, vector_parts, rows, weight, resid, up_parts, down_parts, out_parts
    )
    results = finish(
        output, input_grad, qkv_grad, vector_sum, up_grad, down_grad, out_grad, grad_read, grad_write
    )
    shaped = [jnp.swapaxes(result, 0, 1) if index in (2, 3) else result for index, result in enumerate(results)]
    return tuple(result.reshape(-1) if result.shape[0] == 1 and result.ndim == 2 else result for result in shaped)


def per_device(
    tokens, read_memory, write_memory, lengths, qkv_weight, qv_bias, out_weight, out_bias, norm1_gain,
    norm1_bias, up_weight, up_bias, down_weight, down_bias, norm2_gain, norm2_bias, cotangent,
):
    seq_count = lax.axis_size("seq")
    fsdp_count = lax.axis_size("fsdp")
    seq_place = lax.axis_index("seq")
    local_rows, width = tokens.shape
    head_cols = width // seq_count
    shard = width // fsdp_count
    length = lengths[0]
    heads = head_cols // HEAD
    vectors = (qv_bias, out_bias, norm1_gain, norm1_bias, up_bias, down_bias, norm2_gain, norm2_bias)
    if (fsdp_count, seq_count) == (8, 4):
        return on_block(
            tokens, read_memory[0], write_memory[0], lengths, qkv_weight, vectors, out_weight, up_weight, down_weight,
            cotangent,
        )
    places = seq_place * local_rows + jnp.arange(local_rows, dtype=jnp.int32)
    in_slot = (places < length)[:, None]
    memory_slots = jnp.arange(MEM, dtype=jnp.int32)
    pick_read = places[:, None] == memory_slots[None, :]
    pick_write = places[:, None] == length - MEM + memory_slots[None, :]
    is_memory = jnp.any(pick_read | pick_write, axis=1)[:, None]
    picks = jnp.concatenate([pick_read, pick_write], axis=1).astype(full)
    memory = jnp.concatenate([read_memory[0], write_memory[0]], axis=0)
    layer_in = jnp.where(is_memory, mul(picks.astype(low), memory).astype(low), tokens)

    own_shard = lax.dynamic_slice_in_dim(
        qkv_weight.reshape(shard, 3, seq_count, heads, HEAD), seq_place, 1, 2
    )
    own_shard = jnp.transpose(own_shard[:, :, 0], (0, 2, 1, 3)).reshape(shard, 3 * head_cols)
    packed = jnp.concatenate(vectors)
    rows = lax.all_gather(layer_in, "seq", axis=0, tiled=True)
    weight = lax.all_gather(own_shard, "fsdp", axis=0, tiled=True)
    packed = lax.all_gather(packed.reshape(1, -1), "fsdp", axis=0, tiled=True).astype(full)
    whole, start = [], 0
    for vector in vectors:
        whole.append(packed[:, start : start + vector.shape[0]].reshape(-1))
        start += vector.shape[0]
    qv_vec, out_vec, gain_one, shift_one, up_vec, down_vec, gain_two, shift_two = whole
    own_qv = lax.dynamic_slice_in_dim(qv_vec.reshape(2, seq_count, head_cols), seq_place, 1, 1)
    bias = jnp.concatenate([own_qv[0, 0], own_qv[1, 0]])
    bias = jnp.broadcast_to(bias, (8, bias.shape[0]))
    out_full = lax.all_gather(out_weight, "fsdp", axis=0, tiled=True)
    up_full = lax.all_gather(up_weight, "fsdp", axis=0, tiled=True)
    down_full = lax.all_gather(down_weight, "fsdp", axis=0, tiled=True)
    q_x, k_t, k_wide, v_wide, mixed, mixed_low, row_stats = attention_forward(lengths, rows, weight, bias)
    attended = lax.all_to_all(mixed_low, "seq", split_axis=1, concat_axis=0, tiled=True)
    resid_one = layer_in.astype(full) + mul(attended, out_full, TN) + out_vec
    middle, norm_one_back = jax.vjp(normalize, resid_one, gain_one, shift_one)
    middle_low = middle.astype(low)
    up_pre = mul(middle_low, up_full) + up_vec
    gelu_out, gelu_back = jax.vjp(partial(jax.nn.gelu, approximate=False), up_pre)
    hidden = gelu_out.astype(low)
    down_pre = mul(hidden, down_full) + down_vec
    final, norm_two_back = jax.vjp(normalize, middle + down_pre, gain_two, shift_two)
    output = jnp.where(in_slot, final, 0.0).astype(low)
    grad_final = jnp.where(in_slot, cotangent.astype(full), 0.0)
    grad_resid_two, grad_gain_two, grad_shift_two = norm_two_back(grad_final)
    grad_down = grad_resid_two.astype(low)
    grad_down_weight = mul(hidden, grad_down, TN)
    (grad_up_pre,) = gelu_back(mul(grad_down, down_full, NT))
    grad_up = grad_up_pre.astype(low)
    grad_up_weight = mul(middle_low, grad_up, TN)
    grad_middle = grad_resid_two + mul(grad_up, up_full, NT)
    grad_resid_one, grad_gain_one, grad_shift_one = norm_one_back(grad_middle)
    grad_branch = grad_resid_one.astype(low)
    grad_out_weight = mul(attended, grad_branch)
    grad_attended = mul(out_full, grad_branch, NT).astype(low)
    vector_grads = [
        column_sums(grad_branch), grad_gain_one, grad_shift_one, column_sums(grad_up),
        column_sums(grad_down), grad_gain_two, grad_shift_two,
    ]
    packed_grad = jnp.concatenate([v.reshape(fsdp_count, -1) for v in vector_grads], axis=1)
    saved = (q_x, k_t, k_wide, v_wide, mixed, row_stats)
    grad_t = lax.all_to_all(grad_attended, "seq", split_axis=0, concat_axis=1, tiled=True)
    partial_in, weight_part, sums = attention_backward(*saved, grad_t, rows, weight)
    from_heads = lax.psum_scatter(partial_in, "seq", scatter_dimension=0, tiled=True).astype(full)
    grad_layer_in = grad_resid_one + from_heads
    input_grad = jnp.where(is_memory, 0.0, grad_layer_in)
    grad_memory = lax.dot_general(
        picks, grad_layer_in, TN, precision=lax.Precision.HIGHEST, preferred_element_type=full
    )
    grad_memory = lax.psum(grad_memory.astype(low), "seq").astype(full)
    grad_read, grad_write = grad_memory[:MEM], grad_memory[MEM:]
    sums = sums[:, 0].reshape(heads, 3, HEAD)
    own_sums = jnp.stack([sums[:, 0].reshape(-1), sums[:, 2].reshape(-1)])[:, None]
    zero_qv = jnp.zeros((2, seq_count, head_cols), full)
    qv_grad = lax.dynamic_update_slice_in_dim(zero_qv, own_sums, seq_place, 1)
    packed_grad = jnp.concatenate([qv_grad.reshape(fsdp_count, -1), packed_grad], axis=1)
    packed_sum = lax.psum(packed_grad, ("fsdp", "seq"))
    own_vectors = lax.dynamic_index_in_dim(packed_sum, lax.axis_index("fsdp"), 0, False)

    def both_axes(part):
        piece = lax.psum_scatter(part.astype(low), "fsdp", scatter_dimension=0, tiled=True)
        return lax.psum(piece, "seq").astype(full)

    qkv_piece = lax.psum_scatter(weight_part, "fsdp", scatter_dimension=0, tiled=True)
    qkv_parts = lax.all_gather(qkv_piece, "seq", axis=0).reshape(seq_count, shard, heads, 3, HEAD)
    qkv_out = jnp.transpose(qkv_parts, (1, 3, 0, 2, 4)).reshape(shard, 3 * width).astype(full)
    up_out, down_out, out_out = both_axes(grad_up_weight), both_axes(grad_down_weight), both_axes(grad_out_weight)
    vector_outs, start = [], 0
    for vector in vectors:
        vector_outs.append(own_vectors[start : start + vector.shape[0]])
        start += vector.shape[0]
    qv_out, out_b_out, gain_one_out, shift_one_out, up_b_out, down_b_out, gain_two_out, shift_two_out = vector_outs
    return (
        output, input_grad, grad_read[None], grad_write[None], qkv_out, qv_out, out_out, out_b_out, gain_one_out,
        shift_one_out, up_out, up_b_out, down_out, down_b_out, gain_two_out, shift_two_out,
    )


def solution(mesh):
    rows, piece = P(("fsdp", "seq"), None), P("fsdp")
    matrix, memory = P("fsdp", None), P("fsdp", None, None)
    in_specs = (
        rows, memory, memory, piece, matrix, piece, matrix, piece, piece, piece, matrix, piece, matrix,
        piece, piece, piece, rows,
    )
    out_specs = (
        rows, rows, memory, memory, matrix, piece, matrix, piece, piece, piece, matrix, piece, matrix,
        piece, piece, piece,
    )
    return jax.shard_map(per_device, mesh=mesh, in_specs=in_specs, out_specs=out_specs, check_vma=False)
```

```python
from functools import partial

import jax
import jax.numpy as jnp
from jax import lax
from jax.experimental import pallas as pl
from jax.experimental.pallas import tpu as pltpu
from jax.sharding import PartitionSpec as P

HEAD = 64
MEM = 10
WIDE = 128
VMEM_BYTES = 64000 * 1024

norm_epsilon = 1e-06
masked_score = -1e30
low = jnp.bfloat16
full = jnp.float32

NN = (((1,), (0,)), ((), ()))
NT = (((1,), (1,)), ((), ()))
TN = (((0,), (0,)), ((), ()))
TT = (((0,), (1,)), ((), ()))


def mul(left, right, dims=NN):
    return lax.dot_general(left, right, dims, preferred_element_type=full)


def three_parts(value):
    high = value.astype(low)
    rest = value - high.astype(full)
    middle = rest.astype(low)
    return high, middle, (rest - middle.astype(full)).astype(low)


def stack_rows(rows, columns):
    place = lax.broadcasted_iota(jnp.int32, (HEAD, columns), 0)
    block = jnp.zeros((HEAD, columns), full)
    for index, row in enumerate(rows):
        block = jnp.where(place == index, row, block)
    return block.astype(low)


def project_block(start, length, rows_ref, weight_ref, bias_q, bias_v, q_x, k_t, v_x, k_wide, v_wide, step):
    head_cols = k_t.shape[0]
    lanes = pl.ds(start, step)
    made = mul(weight_ref[...], rows_ref[lanes, :], TT)
    place = start + lax.broadcasted_iota(jnp.int32, (1, step), 1)
    key_bias = jnp.where(place < length, 0.0, masked_score)
    one = jnp.ones((1, step), full)
    query_extra = stack_rows([one], step)
    key_extra = stack_rows([key_bias, one, one, one], step)
    value_extra = stack_rows([one, one, one], step)
    for h in range(head_cols // HEAD):
        own = slice(h * HEAD, (h + 1) * HEAD)
        base = 3 * h * HEAD
        query = (made[base : base + HEAD] + bias_q[own]).astype(low)
        q_x[h, :HEAD, lanes] = query * jnp.asarray(HEAD**-0.5, low)
        q_x[h, HEAD:, lanes] = query_extra
        k_t[own, lanes] = made[base + HEAD : base + 2 * HEAD].astype(low)
        v_x[h, :HEAD, lanes] = (made[base + 2 * HEAD : base + 3 * HEAD] + bias_v[own]).astype(low)
        v_x[h, HEAD:, lanes] = value_extra
        k_wide[h, lanes, :] = jnp.transpose(jnp.concatenate([k_t[own, lanes], key_extra], axis=0))
        v_wide[h, lanes, :] = jnp.transpose(v_x[h, :, lanes])


def project_heads(length, rows_ref, weight_ref, bias_ref, q_x, k_t, v_x, k_wide, v_wide):
    head_cols = k_t.shape[0]
    bias = jnp.transpose(bias_ref[...])[:, 0:1]
    for start in range(0, rows_ref.shape[0], 512):
        project_block(
            start, length, rows_ref, weight_ref, bias[:head_cols], bias[head_cols:],
            q_x, k_t, v_x, k_wide, v_wide, 512,
        )


def attend_block(h, lanes, q_x, k_wide, v_x, mixed, mixed_low, row_stats):
    scores = mul(k_wide[h], q_x[h, :, lanes])
    row_max = jnp.max(scores, axis=0, keepdims=True)
    probs = jnp.exp(scores - row_max).astype(low)
    total = mul(v_x[h, : HEAD + 16], probs)
    row_sum = total[HEAD : HEAD + 1]
    own = pl.ds(h * HEAD, HEAD)
    result = total[:HEAD] / row_sum
    mixed[own, lanes] = result
    mixed_low[own, lanes] = result.astype(low)
    row_stats[h, :, lanes] = jnp.broadcast_to(row_max + jnp.log(row_sum), (8, result.shape[1]))


def forward_kernel(
    length_ref, rows_ref, weight_ref, bias_ref, q_x, k_t, k_wide, v_wide, mixed, mixed_low, row_stats, v_x
):
    project_heads(length_ref[0], rows_ref, weight_ref, bias_ref, q_x, k_t, v_x, k_wide, v_wide)
    heads = q_x.shape[0]
    block = 512
    blocks = q_x.shape[2] // block

    def step(index, carry):
        h = index // blocks
        start = pl.multiple_of(lax.rem(index, blocks) * block, block)
        attend_block(h, pl.ds(start, block), q_x, k_wide, v_x, mixed, mixed_low, row_stats)
        return carry

    lax.fori_loop(0, heads * blocks, step, 0)


def attention_forward(length, rows, weight, bias):
    slot_rows = rows.shape[0]
    head_cols = weight.shape[1] // 3
    heads = head_cols // HEAD
    vmem = pl.BlockSpec(memory_space=pltpu.VMEM)
    return pl.pallas_call(
        forward_kernel,
        in_specs=[pl.BlockSpec(memory_space=pltpu.SMEM), vmem, vmem, vmem],
        out_specs=[vmem] * 7,
        out_shape=[
            jax.ShapeDtypeStruct((heads, WIDE, slot_rows), low),
            jax.ShapeDtypeStruct((head_cols, slot_rows), low),
            jax.ShapeDtypeStruct((heads, slot_rows, WIDE), low),
            jax.ShapeDtypeStruct((heads, slot_rows, WIDE), low),
            jax.ShapeDtypeStruct((head_cols, slot_rows), full),
            jax.ShapeDtypeStruct((head_cols, slot_rows), low),
            jax.ShapeDtypeStruct((heads, 8, slot_rows), full),
        ],
        scratch_shapes=[pltpu.VMEM((heads, WIDE, slot_rows), low)],
        compiler_params=pltpu.CompilerParams(vmem_limit_bytes=VMEM_BYTES),
        name="attention_forward",
    )(length, rows, weight, bias)


def attend_back(h, lanes, q_x, q_here, do_x, grad_t, mixed, row_stats, k_t, k_wide, v_wide, grads, grad_k, grad_v, first):
    own = pl.ds(pl.multiple_of(h * HEAD, HEAD), HEAD)
    grad = grad_t[own, lanes]
    columns = grad.shape[1]
    delta = jnp.sum(grad.astype(full) * mixed[own, lanes], axis=0, keepdims=True)
    parts = [part.astype(full) for part in three_parts(-delta)]
    do_x[:HEAD, :] = grad
    do_x[HEAD:, :] = stack_rows(parts, columns)
    parts = [part.astype(full) for part in three_parts(-row_stats[h, 0:1, lanes])]
    q_here[:HEAD, :] = q_x[h, :HEAD, lanes]
    q_here[HEAD:, :] = stack_rows([jnp.ones((1, columns), full)] + parts, columns)
    value_part, key_part, query_parts = None, None, []
    for start in range(0, columns, columns // 2):
        side = slice(start, start + columns // 2)
        probs = jnp.exp(mul(k_wide[h], q_here[:, side]))
        grad_scores = (probs * mul(v_wide[h], do_x[:, side])).astype(low)
        value_more = mul(do_x[:HEAD, side], probs.astype(low), NT)
        key_more = mul(q_here[:HEAD, side], grad_scores, NT)
        value_part = value_more if value_part is None else value_part + value_more
        key_part = key_more if key_part is None else key_part + key_more
        query_parts.append(mul(k_t[own, :], grad_scores) * HEAD**-0.5)

    @pl.when(first)
    def _():
        grad_v[...] = value_part
        grad_k[...] = key_part

    @pl.when(jnp.logical_not(first))
    def _():
        grad_v[...] += value_part
        grad_k[...] += key_part

    query_part = jnp.concatenate(query_parts, axis=1)
    grads[pl.ds(pl.multiple_of(3 * h * HEAD, HEAD), HEAD), lanes] = query_part.astype(low)


def backward_kernel(
    q_in, k_t, k_wide, v_wide, mixed, row_stats, grad_t, rows_ref, weight_ref,
    partial_out, weight_out, sums_out, q_here, do_x, grads, grad_k, grad_v,
):
    heads, _, slot_rows = q_in.shape
    block = 512
    blocks = slot_rows // block

    def step(index, carry):
        h = index // blocks
        turn = lax.rem(index, blocks)
        start = pl.multiple_of(turn * block, block)
        attend_back(
            h, pl.ds(start, block), q_in, q_here, do_x, grad_t, mixed, row_stats, k_t, k_wide, v_wide, grads, grad_k,
            grad_v, turn == 0,
        )

        @pl.when(turn == blocks - 1)
        def _():
            base = pl.multiple_of(3 * h * HEAD, HEAD)
            grads[pl.ds(base + HEAD, HEAD), :] = grad_k[...].astype(low)
            grads[pl.ds(base + 2 * HEAD, HEAD), :] = grad_v[...].astype(low)

        return carry

    lax.fori_loop(0, heads * blocks, step, 0)
    for start in range(0, slot_rows, block):
        partial_out[start : start + block, :] = mul(
            grads[:, start : start + block], weight_ref[...], TT
        ).astype(partial_out.dtype)
    weight_out[...] = jnp.transpose(mul(grads[...], rows_ref[...])).astype(weight_out.dtype)
    sums_out[...] = jnp.broadcast_to(
        jnp.sum(grads[...].astype(full), axis=1, keepdims=True), sums_out.shape
    )


def attention_backward(q_x, k_t, k_wide, v_wide, mixed, row_stats, grad_t, rows, weight):
    heads, _, slot_rows = q_x.shape
    width, all_cols = weight.shape
    vmem = pl.BlockSpec(memory_space=pltpu.VMEM)
    return pl.pallas_call(
        backward_kernel,
        in_specs=[vmem] * 9,
        out_specs=[vmem] * 3,
        out_shape=[
            jax.ShapeDtypeStruct((slot_rows, width), low),
            jax.ShapeDtypeStruct((width, all_cols), low),
            jax.ShapeDtypeStruct((all_cols, WIDE), full),
        ],
        scratch_shapes=[
            pltpu.VMEM((WIDE, 512), low),
            pltpu.VMEM((WIDE, 512), low),
            pltpu.VMEM((all_cols, slot_rows), low),
            pltpu.VMEM((HEAD, slot_rows), full),
            pltpu.VMEM((HEAD, slot_rows), full),
        ],
        compiler_params=pltpu.CompilerParams(vmem_limit_bytes=VMEM_BYTES),
        name="attention_backward",
    )(q_x, k_t, k_wide, v_wide, mixed, row_stats, grad_t, rows, weight)


MESH = pl.DeviceIdType.MESH
OWN, RELATIONS = 0, 7
UP_W, OUT_W, DOWN_W, QKV_W = 0, 1, 2, 3


def offset_of(relation):
    return (0, -1, -2, -3, 1, 2, 3)[relation]


class Place:
    def __init__(self):
        self.f, self.s = lax.axis_index("fsdp"), lax.axis_index("seq")
        self.z, self.x = self.f // 2, lax.rem(self.f, 2)
        self.y, self.c = self.s // 2, lax.rem(self.s, 2)
        self.core = (self.f, 2 * self.y + 1 - self.c)
        self.across_y = (self.f, 2 * (1 - self.y) + self.c)
        self.diagonal = (self.f, 2 * (1 - self.y) + 1 - self.c)
        self.across_x = (2 * self.z + 1 - self.x, self.s)
        self.above = (self.f + 2, self.s)
        self.below = (self.f - 2, self.s)

    def has(self, relation):
        offset = offset_of(relation)
        return (self.z + offset >= 0) & (self.z + offset <= 3)

    def source(self, relation, column):
        own_column = self.f + 2 * offset_of(relation)
        return own_column if column == 0 else own_column + 1 - 2 * self.x

    def member(self, turn):
        flip_y = 1 - turn // 2
        flip_c = lax.rem(turn, 2) if not isinstance(turn, int) else turn % 2
        flip_c = flip_c + (1 - 2 * flip_c) * (turn // 2)
        return 2 * lax.rem(self.y + flip_y, 2) + lax.rem(self.c + flip_c, 2)


def remote(src, dst, send, recv, where):
    return pltpu.make_async_remote_copy(
        src_ref=src, dst_ref=dst, send_sem=send, recv_sem=recv, device_id=where, device_id_type=MESH
    )


def greet(place, all_lines):
    barrier = pltpu.get_barrier_semaphore()
    near = [place.core, place.across_y, place.diagonal, place.across_x]
    for where in near:
        pl.semaphore_signal(barrier, inc=1, device_id=where, device_id_type=MESH)
    for line in range(4):
        gap = place.z - line
        meets = gap != 0 if all_lines else (gap == 1) | (gap == -1)

        @pl.when(meets)
        def _(line=line):
            pl.semaphore_signal(
                barrier, inc=1, device_id=(2 * line + place.x, place.s), device_id_type=MESH
            )

    ends = 3 if all_lines else jnp.where((place.z == 0) | (place.z == 3), 1, 2)
    pl.semaphore_wait(barrier, len(near) + ends)


class Gather:
    def __init__(self, place, own, whole, sems):
        self.place, self.own, self.whole = place, own, whole
        (self.z_send, self.z_recv, self.x_send, self.x_recv, self.c_send, self.c_recv,
         self.y_send, self.y_recv, self.d_send, self.d_recv) = sems

    def piece(self, array, source, quarter=None, pair=False):
        c = self.place.c
        ref = self.whole[array]
        if array == QKV_W:
            return ref.at[source]
        if array == DOWN_W:
            rows = ref.shape[0] // 8
            part = rows // 4
            quarter = self.place.s if quarter is None else quarter
            return ref.at[pl.ds(pl.multiple_of(source * rows + quarter * part, part), part)]
        rows, columns = ref.shape[0] // 8, ref.shape[1] // 2
        count = 2 if pair else 1
        return ref.at[
            pl.ds(pl.multiple_of(source * rows, rows), count * rows),
            pl.ds(pl.multiple_of(c * columns, columns), columns),
        ]

    def own_piece(self, array):
        if array == QKV_W:
            return self.piece(array, self.place.f)
        ref = self.own[array]
        if array == DOWN_W:
            part = ref.shape[0] // 4
            return ref.at[pl.ds(pl.multiple_of(self.place.s * part, part), part)]
        columns = ref.shape[1] // 2
        return ref.at[:, pl.ds(pl.multiple_of(self.place.c * columns, columns), columns)]

    def z_piece(self, array, relation):
        source = self.place.source(relation, 0)
        if array == OUT_W:
            return self.piece(array, source - self.place.x, pair=True)
        return self.piece(array, source)

    def along_z(self, array, relation, way):
        here = self.z_piece(array, relation)
        src = self.own_piece(array) if relation == OWN and array != OUT_W else here
        step = abs(offset_of(relation))
        where = self.place.above if way == 0 else self.place.below
        return remote(src, here, self.z_send.at[array, way, step], self.z_recv.at[array, way, step], where)

    def z_ways(self, relation):
        place = self.place
        ways = []
        if offset_of(relation) <= 0:
            ways.append((0, place.has(relation) & (place.z < 3)))
        if offset_of(relation) >= 0:
            ways.append((1, place.has(relation) & (place.z > 0)))
        return ways

    def wait_z(self, array, relation):
        way = 0 if offset_of(relation) < 0 else 1
        step = abs(offset_of(relation)) - 1
        here = self.z_piece(array, relation)
        where = self.place.below if way == 0 else self.place.above
        remote(
            here, here, self.z_send.at[array, way, step], self.z_recv.at[array, way, step], where
        ).wait_recv()

    def over_x(self, array, relation):
        here = self.piece(array, self.place.source(relation, 0))
        src = self.own_piece(array) if relation == OWN else here
        return remote(
            src, here, self.x_send.at[array, relation], self.x_recv.at[array, relation], self.place.across_x
        )

    def from_x(self, array, relation):
        here = self.piece(array, self.place.source(relation, 1))
        return remote(
            here, here, self.x_send.at[array, relation], self.x_recv.at[array, relation], self.place.across_x
        )

    def to_core(self, array, relation, column):
        if array == OUT_W and relation != OWN:
            here = self.z_piece(array, relation)
        else:
            here = self.piece(array, self.place.source(relation, column))
        return remote(
            here, here, self.c_send.at[array, relation, column], self.c_recv.at[array, relation, column],
            self.place.core,
        )

    def over_y(self, relation, column):
        here = self.piece(DOWN_W, self.place.source(relation, column))
        return remote(
            here, here, self.y_send.at[relation, column], self.y_recv.at[relation, column], self.place.across_y
        )

    def far_quarter(self, relation, column):
        return self.piece(
            DOWN_W, self.place.source(relation, column), 2 * (1 - self.place.y) + self.place.c
        )

    def from_y(self, relation, column):
        here = self.far_quarter(relation, column)
        return remote(
            here, here, self.y_send.at[relation, column], self.y_recv.at[relation, column], self.place.across_y
        )

    def far_to_core(self, relation, column):
        here = self.far_quarter(relation, column)
        return remote(
            here, here, self.d_send.at[relation, column], self.d_recv.at[relation, column], self.place.core
        )

    def when(self, relation, action):
        if relation == OWN:
            action()
        else:
            pl.when(self.place.has(relation))(action)

    def arrive_z(self, array, relation, along=True, across=True):
        def action():
            if relation != OWN:
                self.wait_z(array, relation)
            for way, holds in self.z_ways(relation) if along else ():
                pl.when(holds)(lambda way=way: self.along_z(array, relation, way).start())
            if array != OUT_W and across:
                self.over_x(array, relation).start()
            if array != QKV_W and relation != OWN:
                self.to_core(array, relation, 0).start()
                if array == DOWN_W:
                    self.over_y(relation, 0).start()

        self.when(relation, action)

    def cross_out(self):
        self.over_x(OUT_W, OWN).start()

    def pair_out(self, own_copy):
        own_copy.wait()
        self.from_x(OUT_W, OWN).wait_recv()
        self.to_core(OUT_W, OWN, 1).start()
        for way, holds in self.z_ways(OWN):
            pl.when(holds)(lambda way=way: self.along_z(OUT_W, OWN, way).start())

    def arrive_x(self, array, relation):
        def action():
            self.from_x(array, relation).wait_recv()
            if array != QKV_W:
                self.to_core(array, relation, 1).start()
                if array == DOWN_W:
                    self.over_y(relation, 1).start()

        self.when(relation, action)

    def arrive_y(self, relation, column):
        def action():
            self.from_y(relation, column).wait_recv()
            self.far_to_core(relation, column).start()

        if (relation, column) != (OWN, 0):
            self.when(relation, action)

    def finish(self, array):
        for relation in range(RELATIONS):
            def action():
                if array != OUT_W or relation == OWN:
                    self.over_x(array, relation).wait_send()
                for way, holds in self.z_ways(relation):
                    pl.when(holds)(lambda way=way: self.along_z(array, relation, way).wait_send())
                if array == QKV_W:
                    return
                for column in range(2):
                    if (relation, column) == (OWN, 0) or (array == OUT_W and relation != OWN and column == 1):
                        continue
                    self.to_core(array, relation, column).wait()
                    if array == DOWN_W:
                        self.over_y(relation, column).wait_send()
                        self.far_to_core(relation, column).wait()

            self.when(relation, action)


def front_kernel(
    length_ref, tokens, read_rows, write_rows, qkv_in, vectors_in, up_in, down_in, out_in,
    small, up_bias, rows_out, weight_out, q_out, k_out, k_wide_out, v_wide_out, mixed_out, stats_out, up_full,
    down_full, out_full, attended,
    rows_ref, weight_ref, pieces, memory, q_x, k_t, k_wide, v_wide, v_x, mixed, mixed_low, row_stats,
    row_send, row_recv, far_send, far_recv, mix_send, mix_recv, local_sem, save_sem, head_sem, *gather_sems,
):
    place = Place()
    slot_rows, width = rows_ref.shape
    local_rows = tokens.shape[0]
    head_cols = k_t.shape[0]
    heads = head_cols // HEAD
    shard = width // 8
    length = length_ref[0]
    own_shards = {UP_W: up_in, DOWN_W: down_in, OUT_W: out_in}
    whole = {UP_W: up_full, DOWN_W: down_full, OUT_W: out_full, QKV_W: pieces}
    gather = Gather(place, own_shards, whole, gather_sems)

    memory[...] = jnp.zeros_like(memory)
    memory[:MEM, :] = read_rows[...]
    memory[16 : 16 + MEM, :] = write_rows[...]
    line = lax.broadcasted_iota(jnp.int32, (local_rows, 32), 1)
    at = place.s * local_rows + lax.broadcasted_iota(jnp.int32, (local_rows, 32), 0)
    wanted = jnp.where(line < 16, line, length - MEM + line - 16)
    used = (line < MEM) | ((line >= 16) & (line < 16 + MEM))
    pick = jnp.where(used & (wanted == at), 1.0, 0.0)
    taken = mul(pick.astype(low), memory[...]).astype(low)
    is_memory = jnp.sum(pick, axis=1, keepdims=True) > 0.5
    own_start = pl.multiple_of(place.s * local_rows, local_rows)
    rows_ref[pl.ds(own_start, local_rows), :] = jnp.where(is_memory, taken, tokens[...])
    for member in range(4):

        @pl.when(place.s == member)
        def _(member=member):
            for h in range(heads):
                for kind in range(3):
                    start = kind * width + (member * heads + h) * HEAD
                    to = (3 * h + kind) * HEAD
                    pieces[place.f, :, to : to + HEAD] = qkv_in[:, start : start + HEAD]

    columns = 3 * head_cols
    pieces[place.f, :, columns:] = jnp.zeros((shard, HEAD), low)
    for line in range(18):
        pieces[place.f, line : line + 1, columns:] = vectors_in[:, line * HEAD : (line + 1) * HEAD].astype(low)
    greet(place, False)

    halves = 2
    part = local_rows // halves

    def rows_of(member, half):
        return pl.ds(pl.multiple_of(member * local_rows + half * part, part), part)

    def send_rows(half, index):
        where = (place.core, place.across_y)[index]
        here = rows_ref.at[rows_of(place.s, half)]
        return remote(here, here, row_send.at[index, half], row_recv.at[index, half], where)

    def rows_from(half, index):
        member = (2 * place.y + 1 - place.c, 2 * (1 - place.y) + place.c)[index]
        here = rows_ref.at[rows_of(member, half)]
        where = (place.core, place.across_y)[index]
        return remote(here, here, row_send.at[index, half], row_recv.at[index, half], where)

    def pass_rows(half, arriving):
        flip = place.c if not arriving else 1 - place.c
        here = rows_ref.at[rows_of(2 * (1 - place.y) + flip, half)]
        return remote(here, here, far_send.at[half], far_recv.at[half], place.core)

    def own_copies():
        copies = []
        for index, array in enumerate((UP_W, DOWN_W, OUT_W)):
            rows = own_shards[array].shape[0]
            copies.append(pltpu.make_async_copy(
                own_shards[array], whole[array].at[pl.ds(pl.multiple_of(place.f * rows, rows), rows)],
                local_sem.at[index],
            ))
        return copies

    gather.arrive_z(QKV_W, OWN)
    for half in range(halves):
        send_rows(half, 1).start()
        send_rows(half, 0).start()
    gather.cross_out()
    for copy in own_copies():
        copy.start()
    for relation in (1, 4):
        gather.arrive_z(QKV_W, relation)
    gather.arrive_z(DOWN_W, OWN, along=False)
    gather.pair_out(own_copies()[2])
    for relation in (2, 5):
        gather.arrive_z(QKV_W, relation)
    gather.arrive_z(DOWN_W, OWN, across=False)
    gather.arrive_z(UP_W, OWN)
    rows_from(0, 1).wait_recv()
    pass_rows(0, False).start()
    for relation in (3, 6):
        gather.arrive_z(QKV_W, relation)
    for relation in (1, 4):
        gather.arrive_z(DOWN_W, relation)
    for relation in range(RELATIONS):
        gather.arrive_x(QKV_W, relation)
    for relation in (1, 4):
        gather.arrive_z(OUT_W, relation)
        gather.arrive_z(UP_W, relation)

    for source in range(8):
        weight_ref[source * shard : (source + 1) * shard, :] = pieces[source, :, :columns]
    tile = slice(columns - HEAD, columns + HEAD)
    bias_q = jnp.transpose(pieces[place.s, 0:16, tile].astype(full))[HEAD:]
    bias_v = jnp.transpose(pieces[4 + place.s, 0:16, tile].astype(full))[HEAD:]
    bias_q = jnp.concatenate([bias_q[:, h : h + 1] for h in range(heads)], axis=0)
    bias_v = jnp.concatenate([bias_v[:, h : h + 1] for h in range(heads)], axis=0)

    def project(member):
        start = pl.multiple_of(member * local_rows, local_rows)
        project_block(
            start, length, rows_ref, weight_ref, bias_q, bias_v, q_x, k_t, v_x, k_wide, v_wide, local_rows
        )

    project(place.s)
    for half in range(halves):
        rows_from(half, 0).wait_recv()
    project(2 * place.y + 1 - place.c)
    rows_from(1, 1).wait_recv()
    pass_rows(1, False).start()
    project(2 * (1 - place.y) + place.c)

    def scatter_vector(target, index, size, first):
        for source in range(8):
            done = 0
            while done < size:
                line, lane = divmod(first + done, HEAD)
                count = min(HEAD - lane, size - done)
                target[index : index + 1, source * size + done : source * size + done + count] = pieces[
                    source, line : line + 1, columns + lane : columns + lane + count
                ].astype(full)
                done += count

    for index, first in enumerate((2, 3, 4, 9, 10, 11)):
        scatter_vector(small, index, shard, first * shard)
    scatter_vector(up_bias, 0, 4 * shard, 5 * shard)
    for half in range(halves):
        pass_rows(half, True).wait_recv()
    project(2 * (1 - place.y) + 1 - place.c)

    def saves():
        pairs = [(rows_ref, rows_out), (weight_ref, weight_out), (k_t, k_out), (k_wide, k_wide_out), (v_wide, v_wide_out)]
        pairs += [(q_x.at[h, pl.ds(0, HEAD)], q_out.at[h]) for h in range(heads)]
        return [pltpu.make_async_copy(src, dst, save_sem.at[index]) for index, (src, dst) in enumerate(pairs)]

    for save in saves():
        save.start()

    def head_saves(h):
        own = pl.ds(h * HEAD, HEAD)
        return [
            pltpu.make_async_copy(mixed.at[own], mixed_out.at[own], head_sem.at[h, 0]),
            pltpu.make_async_copy(row_stats.at[h], stats_out.at[h], head_sem.at[h, 1]),
        ]

    def chores(step):
        if step == 0:
            gather.arrive_x(DOWN_W, OWN)
            for relation in (2, 5):
                gather.arrive_z(DOWN_W, relation)
        elif step == 1:
            gather.arrive_x(UP_W, OWN)
            for relation in (2, 5):
                gather.arrive_z(OUT_W, relation)
        elif step == 2:
            for relation in (1, 4):
                gather.arrive_x(DOWN_W, relation)
                gather.arrive_y(relation, 0)
        elif step == 4:
            for relation in (2, 5):
                gather.arrive_z(UP_W, relation)
            gather.arrive_y(OWN, 1)
            for save in head_saves(0):
                save.start()
        elif step == 5:
            for relation in (1, 4):
                gather.arrive_x(UP_W, relation)
            for relation in (3, 6):
                gather.arrive_z(DOWN_W, relation)
        elif step == 6:
            for relation in (2, 5):
                gather.arrive_x(DOWN_W, relation)
                gather.arrive_y(relation, 0)
        elif step == 7:
            for relation in (3, 6):
                gather.arrive_z(OUT_W, relation)
        elif step == 8:
            for relation in (1, 4):
                gather.arrive_y(relation, 1)
            for save in head_saves(1):
                save.start()
        elif step == 9:
            for relation in (3, 6):
                gather.arrive_z(UP_W, relation)
            for relation in (2, 5):
                gather.arrive_x(UP_W, relation)
        elif step == 10:
            for relation in (3, 6):
                gather.arrive_x(DOWN_W, relation)
                gather.arrive_y(relation, 0)
        elif step == 11:
            for relation in (2, 5):
                gather.arrive_y(relation, 1)

    def send_mixed(h, turn, arriving=False):
        member = place.member(turn)
        own = pl.ds(pl.multiple_of(h * HEAD, HEAD), HEAD)
        lanes = pl.ds(pl.multiple_of(member * local_rows, local_rows), local_rows)
        owner = member if arriving else place.s
        there = attended.at[pl.ds(pl.multiple_of(owner * head_cols + h * HEAD, HEAD), HEAD)]
        return remote(
            mixed_low.at[own, lanes], there, mix_send.at[h, turn], mix_recv.at[h, turn], (place.f, member)
        )

    def keep_mixed(h):
        own = pl.ds(pl.multiple_of(h * HEAD, HEAD), HEAD)
        lanes = pl.ds(pl.multiple_of(place.s * local_rows, local_rows), local_rows)
        there = attended.at[pl.ds(pl.multiple_of(place.s * head_cols + h * HEAD, HEAD), HEAD)]
        return pltpu.make_async_copy(mixed_low.at[own, lanes], there, mix_send.at[h, 3])

    turns = slot_rows // local_rows

    def pass_on(index):
        h, turn = index // turns, lax.rem(index, turns)

        @pl.when(turn < turns - 1)
        def _():
            send_mixed(h, turn).start()

        @pl.when(turn == turns - 1)
        def _():
            keep_mixed(h).start()

    def step(index, carry):
        for when in range(12):
            pl.when(index == when)(lambda when=when: chores(when))
        h, turn = index // turns, lax.rem(index, turns)
        start = pl.multiple_of(place.member(turn) * local_rows, local_rows)
        attend_block(h, pl.ds(start, local_rows), q_x, k_wide, v_x, mixed, mixed_low, row_stats)

        @pl.when(index > 0)
        def _():
            pass_on(index - 1)

        return carry

    lax.fori_loop(0, heads * turns, step, 0)
    pass_on(heads * turns - 1)
    for save in head_saves(2):
        save.start()
    for relation in (3, 6):
        gather.arrive_y(relation, 1)
    for relation in (3, 6):
        gather.arrive_x(UP_W, relation)
    for array in (UP_W, OUT_W, DOWN_W, QKV_W):
        gather.finish(array)
    for copy in own_copies()[:2]:
        copy.wait()
    for half in range(halves):
        for index in range(2):
            send_rows(half, index).wait_send()
        pass_rows(half, False).wait_send()
    for h in range(heads):
        for turn in range(turns - 1):
            send_mixed(h, turn).wait_send()
            send_mixed(h, turn, True).wait_recv()
        keep_mixed(h).wait()
        for save in head_saves(h):
            save.wait()
    for save in saves():
        save.wait()


def front(lengths, tokens, read_rows, write_rows, qkv_shard, vectors, up_weight, down_weight, out_weight):
    local_rows, width = tokens.shape
    slot_rows = local_rows * 4
    head_cols = width // 4
    heads = head_cols // HEAD
    shard = width // 8
    vmem = pl.BlockSpec(memory_space=pltpu.VMEM)
    anywhere = pl.BlockSpec(memory_space=pl.ANY)
    dma = pltpu.SemaphoreType.DMA
    hidden = up_weight.shape[1]

    def held(*shape, kind=low):
        return pltpu.VMEM(shape, kind)

    def shaped(*shape, kind=low):
        return jax.ShapeDtypeStruct(shape, kind)

    return pl.pallas_call(
        front_kernel,
        in_specs=[pl.BlockSpec(memory_space=pltpu.SMEM)] + [vmem] * 8,
        out_specs=[vmem] * 2 + [anywhere] * 12,
        out_shape=[
            shaped(8, width, kind=full), shaped(8, hidden, kind=full),
            shaped(slot_rows, width), shaped(width, 3 * head_cols), shaped(heads, HEAD, slot_rows),
            shaped(head_cols, slot_rows), shaped(heads, slot_rows, WIDE), shaped(heads, slot_rows, WIDE),
            shaped(head_cols, slot_rows, kind=full), shaped(heads, 8, slot_rows, kind=full),
            shaped(width, hidden), shaped(hidden, width), shaped(width, width), shaped(width, local_rows),
        ],
        scratch_shapes=[
            held(slot_rows, width), held(width, 3 * head_cols), held(8, shard, 3 * head_cols + HEAD),
            held(32, width), held(heads, WIDE, slot_rows), held(head_cols, slot_rows),
            held(heads, slot_rows, WIDE), held(heads, slot_rows, WIDE), held(heads, WIDE, slot_rows),
            held(head_cols, slot_rows, kind=full), held(head_cols, slot_rows), held(heads, 8, slot_rows, kind=full),
            dma((2, 2)), dma((2, 2)), dma((2,)), dma((2,)), dma((heads, 4)), dma((heads, 4)), dma((3,)),
            dma((5 + heads,)), dma((heads, 2)),
            dma((4, 2, 3)), dma((4, 2, 3)), dma((4, 7)), dma((4, 7)), dma((3, 7, 2)), dma((3, 7, 2)),
            dma((7, 2)), dma((7, 2)), dma((7, 2)), dma((7, 2)),
        ],
        compiler_params=pltpu.CompilerParams(
            vmem_limit_bytes=VMEM_BYTES, collective_id=0, has_side_effects=True
        ),
        name="front",
    )(lengths, tokens, read_rows, write_rows, qkv_shard, vectors, up_weight, down_weight, out_weight)


DW_FIRST = 3
LINES = (3, 0, 2, 1)


def add_low(left, right):
    return (left.astype(full) + right.astype(full)).astype(low)


class Reduce:
    def __init__(self, place, given, sums, across, from_y, from_x, from_z, last, sems):
        self.across, self.last, self.far_up = across, last, last + 1
        self.place, self.given, self.sums = place, given, sums
        self.from_y, self.from_x, self.from_z = from_y, from_x, from_z
        self.y_send, self.y_recv, self.x_send, self.x_recv, self.z_send, self.z_recv = sems

    def dest(self, column, line):
        x = self.place.x
        return 2 * line + (x if column == 0 else 1 - x)

    def slot(self, array, line, column=0):
        if DW_FIRST <= array <= self.last:
            rows = 4 * HEAD if array == self.last else 3 * HEAD
            return self.sums[array].at[self.dest(column, line), pl.ds(0, rows // 4)]
        return self.sums[array].at[line]

    def cut(self, array, ref):
        if DW_FIRST <= array < self.last:
            return ref.at[pl.ds(0, 3 * HEAD // 4)]
        return ref

    def load(self, array, column, line, sem):
        if array == OUT_W:
            return pltpu.make_async_copy(self.given[array].at[line, 0], self.sums[array].at[line], sem)
        source = self.given[UP_W if array == self.far_up else array].at[column, line, 1 if array == self.far_up else 0]
        target = self.across if column == 1 else self.sums[array]
        return pltpu.make_async_copy(source, target.at[line], sem)

    def over_y(self, array, line):
        column, index = (1, 1) if array == UP_W else (0, 0)
        return remote(
            self.given[array].at[column, line, 1], self.from_y.at[index, line], self.y_send.at[index, line],
            self.y_recv.at[index, line], self.place.across_y,
        )

    def add_y(self, array, line):
        self.over_y(array, line).wait_recv()
        slot = self.across.at[line] if array == UP_W else self.slot(DOWN_W, line)
        slot[...] = add_low(slot[...], self.from_y[1 if array == UP_W else 0, line])

    def over_x(self, array, line):
        if array == OUT_W:
            start = self.given[array].at[line, 1]
        elif array == UP_W:
            start = self.across.at[line]
        elif array == DOWN_W:
            start = self.given[array].at[1, line, 0]
        else:
            start = self.slot(array, line, 1)
        return remote(
            start, self.cut(array, self.from_x[array].at[line]), self.x_send.at[array, line],
            self.x_recv.at[array, line], self.place.across_x,
        )

    def add_x(self, array, line):
        self.over_x(array, line).wait_recv()
        slot = self.slot(array, line)
        slot[...] = add_low(slot[...], self.cut(array, self.from_x[array].at[line])[...])

    def along_z(self, array, way, line):
        return remote(
            self.slot(array, line), self.cut(array, self.from_z[array].at[way, line]),
            self.z_send.at[array, way, line], self.z_recv.at[array, way, line],
            self.place.above if way == 0 else self.place.below,
        )

    def add_z(self, array, way, line):
        self.along_z(array, way, line).wait_recv()
        slot = self.slot(array, line)
        slot[...] = add_low(slot[...], self.cut(array, self.from_z[array].at[way, line])[...])

    def hop(self, array, level, lines=(0, 1, 2, 3)):
        @pl.when(self.place.z == level)
        def _():
            for line in range(3, level, -1):
                if line in lines:
                    if level > 0:
                        self.add_z(array, 0, line)
                    self.along_z(array, 0, line).start()

        @pl.when(self.place.z == 3 - level)
        def _():
            for line in range(0, 3 - level):
                if line in lines:
                    if level > 0:
                        self.add_z(array, 1, line)
                    self.along_z(array, 1, line).start()

    def direct(self, array):
        return array != self.far_up

    def to_line(self, array, line):
        where = (2 * line + self.place.x, self.place.s)
        return remote(
            self.slot(array, line), self.cut(array, self.from_z[array].at[self.place.z]),
            self.z_send.at[array, 0, line], self.z_recv.at[array, 0, self.place.z], where,
        )

    def fling(self, array, lines=LINES):
        for line in lines:
            pl.when(self.place.z != line)(lambda line=line: self.to_line(array, line).start())

    def settle(self, array):
        if self.direct(array):
            slot = self.slot(array, self.place.z)
            for line in range(4):

                @pl.when(self.place.z != line)
                def _(line=line):
                    came = self.cut(array, self.from_z[array].at[line])
                    remote(
                        came, came, self.z_send.at[array, 0, line], self.z_recv.at[array, 0, line], self.place.core
                    ).wait_recv()
                    slot[...] = add_low(slot[...], came[...])

            return
        for line in range(4):

            @pl.when(self.place.z == line)
            def _(line=line):
                if line > 0:
                    self.add_z(array, 0, line)
                if line < 3:
                    self.add_z(array, 1, line)

    def finish(self, array):
        for line in range(4):
            if array != self.far_up:
                self.over_x(array, line).wait_send()
            if self.direct(array):
                pl.when(self.place.z != line)(lambda line=line: self.to_line(array, line).wait_send())
            else:
                pl.when(self.place.z < line)(lambda line=line: self.along_z(array, 0, line).wait_send())
                pl.when(self.place.z > line)(lambda line=line: self.along_z(array, 1, line).wait_send())
            if array in (UP_W, DOWN_W):
                self.over_y(array, line).wait_send()


class Spread:
    def __init__(self, place, blocks, source, send, recv):
        self.place, self.blocks, self.source, self.send, self.recv = place, blocks, source, send, recv
        self.near = 2 * place.y + 1 - place.c
        self.far = 2 * (1 - place.y) + place.c
        self.last = 2 * (1 - place.y) + 1 - place.c

    def copy(self, kind, arriving=False):
        place = self.place
        if kind == 2:
            here = self.blocks.at[self.last if arriving else self.far]
            return remote(here, here, self.send.at[2], self.recv.at[2], place.core)
        member = (self.near, self.far)[kind] if arriving else place.s
        return remote(
            self.source, self.blocks.at[member], self.send.at[kind], self.recv.at[kind],
            (place.core, place.across_y)[kind],
        )

    def start(self):
        self.copy(1).start()
        self.copy(0).start()

    def pass_on(self):
        self.copy(1, True).wait_recv()
        self.copy(2).start()

    def finish(self):
        self.blocks[self.place.s] = self.source[...]
        self.copy(0, True).wait_recv()
        self.copy(2, True).wait_recv()
        for kind in range(3):
            self.copy(kind).wait_send()


def back_kernel(
    length_ref, grad_own, vectors_in, q_in, k_in, k_wide_in, v_wide_in, mixed_in, stats_in, rows_in, weight_in, resid_in, up_given, down_given, out_given,
    input_out, read_out, write_out, qkv_out, vector_out, up_out, down_out, out_out,
    q_x, k_t, k_wide, v_wide, mixed, row_stats, grad_t, q_here, do_x, grads, grad_k, grad_v, rows_ref, weight_ref, resid_ref,
    up_sum, out_sum, down_sum, far_sum_up, across_up, dw, both_y, up_x, out_x, down_x, dw_x, up_z, out_z, down_z, dw_z, far_z,
    up_last, out_last, up_all, out_other, down_all, dw_all,
    near_send, near_recv, far_sum, far_recv, memory_all, memory_own,
    mix_send, mix_recv, local_sem, saved_sem, mine_sem, share_send, share_recv, near_s, near_r, far_s, far_r, cross_s, cross_r,
    *sems,
):
    place = Place()
    heads, _, slot_rows = q_in.shape
    width, local_rows = grad_own.shape
    head_cols = heads * HEAD
    last = DW_FIRST + heads - 1
    far_up = last + 1
    given = {UP_W: up_given, OUT_W: out_given, DOWN_W: down_given}
    sums = {UP_W: up_sum, OUT_W: out_sum, DOWN_W: down_sum}
    from_x = {UP_W: up_x, OUT_W: out_x, DOWN_W: down_x}
    from_z = {UP_W: up_z, OUT_W: out_z, DOWN_W: down_z}
    for h in range(heads):
        sums[DW_FIRST + h], from_x[DW_FIRST + h] = dw.at[h], dw_x.at[h]
        from_z[DW_FIRST + h] = dw_z.at[h]
    sums[far_up], from_z[far_up] = far_sum_up, far_z
    reduce = Reduce(place, given, sums, across_up, both_y, from_x, from_z, last, sems)

    peers = (place.across_y, place.diagonal, place.core)

    def member_rows(turn):
        member = place.member(turn)
        return member, pl.ds(pl.multiple_of(member * local_rows, local_rows), local_rows)

    def send_grad(turn, arriving=False):
        member, lanes = member_rows(turn)
        own_lanes = pl.ds(pl.multiple_of(place.s * local_rows, local_rows), local_rows)
        src = grad_own.at[pl.ds(pl.multiple_of(member * head_cols, head_cols), head_cols)]
        return remote(
            src, grad_t.at[:, lanes if arriving else own_lanes], mix_send.at[turn], mix_recv.at[turn], peers[turn]
        )

    def saved_loads(h):
        own = pl.ds(h * HEAD, HEAD)
        pairs = (
            (k_wide_in.at[h], k_wide.at[h]), (q_in.at[h], q_x.at[h]), (v_wide_in.at[h], v_wide.at[h]),
            (mixed_in.at[own], mixed.at[own]), (stats_in.at[h], row_stats.at[h]), (k_in.at[own], k_t.at[own]),
        )
        return [pltpu.make_async_copy(src, dst, saved_sem.at[h, i]) for i, (src, dst) in enumerate(pairs)]

    def sum_loads(array):
        index = array if array < DW_FIRST else DW_FIRST
        return [reduce.load(array, 0, line, mine_sem.at[index, line]) for line in LINES]

    def across_loads():
        return [reduce.load(UP_W, 1, line, mine_sem.at[DW_FIRST + 1, line]) for line in LINES]

    for load in sum_loads(far_up):
        load.start()
    for load in saved_loads(0):
        load.start()
    greet(place, True)
    for turn in (1, 0, 2):
        send_grad(turn).start()
    loads = []
    for index, (src, dst) in enumerate(((rows_in, rows_ref), (weight_in, weight_ref), (resid_in, resid_ref))):
        loads.append(pltpu.make_async_copy(src, dst, local_sem.at[index]))

    def send_x(array, lines=LINES):
        for line in lines:
            reduce.over_x(array, line).start()

    send_x(DOWN_W)
    send_x(OUT_W)
    for array in (DOWN_W, UP_W):
        for line in LINES:
            reduce.over_y(array, line).start()
    for load in across_loads() + sum_loads(UP_W) + sum_loads(OUT_W) + sum_loads(DOWN_W):
        load.start()
    for load in loads:
        load.start()

    for h in range(1, heads):
        for load in saved_loads(h):
            load.start()

    own_lanes = pl.ds(pl.multiple_of(place.s * local_rows, local_rows), local_rows)
    grad_t[:, own_lanes] = grad_own[pl.ds(pl.multiple_of(place.s * head_cols, head_cols), head_cols), :]

    def take_x(array, lines=LINES):
        for line in lines:
            reduce.add_x(array, line)

    turns = slot_rows // local_rows

    def weight_part(h):
        if h == 0:
            loads[0].wait()
        base = 3 * h * HEAD
        part = jnp.transpose(mul(grads[base : base + 3 * HEAD, :], rows_ref[...])).astype(low)
        half = width // 16
        for dest in range(8):
            start = 2 * half * dest
            dw[h, dest, :half, :] = jnp.concatenate(
                [part[start : start + half], part[start + half : start + 2 * half]], axis=1
            )
            if h == heads - 1:
                dw[h, dest, half:, :] = vectors_in[dest].astype(low)
        if h == heads - 1:
            total = jnp.sum(grads[...].astype(full), axis=1, keepdims=True)
            spread = jnp.transpose(jnp.broadcast_to(total, (total.shape[0], WIDE)))[0:1]
            for kind, first_dest in ((0, 0), (2, 4)):
                for head in range(heads):
                    start = (3 * head + kind) * HEAD
                    dw[h, first_dest + place.s, half : half + 1, head * HEAD : (head + 1) * HEAD] = spread[
                        :, start : start + HEAD
                    ].astype(low)
        send_x(DW_FIRST + h)

    share = {OUT_W: (out_last, out_other)}

    def settled(array):
        return sums[array].at[place.z]

    def sum_y(array):
        mine_now = settled(array)
        return remote(mine_now, share[array][0], share_send.at[array, 0], share_recv.at[array, 0], place.across_y)

    def half_to_core(array):
        mine_now = settled(array)
        return remote(mine_now, share[array][1], share_send.at[array, 1], share_recv.at[array, 1], place.core)

    def spread_of(array):
        if array in (UP_W, DOWN_W):
            return Spread(
                place, {UP_W: up_all, DOWN_W: down_all}[array], sums[array].at[place.z], share_send.at[array],
                share_recv.at[array],
            )
        h = array - DW_FIRST
        return Spread(
            place, dw_all.at[h, :, pl.ds(0, reduce.slot(array, 0).shape[0])], reduce.slot(array, place.z),
            share_send.at[array], share_recv.at[array],
        )

    def cross_up():
        return remote(far_sum_up.at[place.z], up_last, cross_s.at[0], cross_r.at[0], place.across_y)

    def settle_up():
        reduce.settle(UP_W)
        cross_up().wait_recv()
        slot = sums[UP_W].at[place.z]
        slot[...] = add_low(slot[...], up_last[...])
        spread_of(UP_W).start()

    def add_last(array):
        sum_y(array).wait()
        slot = settled(array)
        slot[...] = add_low(slot[...], share[array][0][...])
        half_to_core(array).start()

    first, second = DW_FIRST, DW_FIRST + 1

    def pass_up(lines):
        for line in lines:
            reduce.add_y(UP_W, line)
            reduce.over_x(UP_W, line).start()

    def chores(index):
        if index == 1:
            send_grad(2, True).wait_recv()
            for load in across_loads() + sum_loads(UP_W) + sum_loads(OUT_W) + sum_loads(DOWN_W):
                load.wait()
        elif index == 2:
            send_grad(1, True).wait_recv()
            reduce.hop(far_up, 1, (3, 0))
        elif index == 3:
            send_grad(0, True).wait_recv()
            reduce.hop(far_up, 1, (2, 1))
        elif index == 4:
            for load in saved_loads(1):
                load.wait()
            weight_part(0)
            reduce.hop(far_up, 2)
        elif index == 5:
            take_x(DOWN_W)
        elif index == 6:
            for line in LINES:
                reduce.add_y(DOWN_W, line)
                reduce.fling(DOWN_W, (line,))
            take_x(OUT_W)
            reduce.fling(OUT_W)
            reduce.settle(far_up)
            cross_up().start()
        elif index == 7:
            take_x(first)
            reduce.fling(first)
        elif index == 8:
            for load in saved_loads(2):
                load.wait()
            weight_part(1)
            pass_up((3, 0))
        elif index == 9:
            pass_up((2,))
        elif index == 10:
            pass_up((1,))
        elif index == 11:
            take_x(second)
            reduce.fling(second)
            reduce.settle(DOWN_W)
            spread_of(DOWN_W).start()

    def step(index, carry):
        for when in range(1, 12):
            pl.when(index == when)(lambda when=when: chores(when))
        h, turn = index // turns, lax.rem(index, turns)
        _, lanes = member_rows(turns - 1 - turn)
        attend_back(
            h, lanes, q_x, q_here, do_x, grad_t, mixed, row_stats, k_t, k_wide, v_wide, grads, grad_k, grad_v, turn == 0
        )

        @pl.when(turn == turns - 1)
        def _():
            base = pl.multiple_of(3 * h * HEAD, HEAD)
            grads[pl.ds(base + HEAD, HEAD), :] = grad_k[...].astype(low)
            grads[pl.ds(base + 2 * HEAD, HEAD), :] = grad_v[...].astype(low)

        return carry

    for load in sum_loads(far_up):
        load.wait()
    reduce.hop(far_up, 0)
    for load in saved_loads(0):
        load.wait()
    lax.fori_loop(0, heads * turns, step, 0)

    loads[1].wait()
    loads[2].wait()

    halves, part = 2, local_rows // 2
    length = length_ref[0]

    def memory_pick(rows, start):
        line = lax.broadcasted_iota(jnp.int32, (32, rows), 0)
        row = start + lax.broadcasted_iota(jnp.int32, (32, rows), 1)
        wanted = jnp.where(line < 16, line, length - MEM + line - 16)
        used = (line < MEM) | ((line >= 16) & (line < 16 + MEM))
        return jnp.where(used & (wanted == row), 1.0, 0.0).astype(low)

    def part_for(turn, half):
        start = pl.multiple_of(place.member(turn) * local_rows + half * part, part)
        return mul(grads[:, pl.ds(start, part)], weight_ref[...], TT)

    def share_near(index, half):
        rows = pl.ds(half * part, part)
        return remote(
            near_send.at[index, rows], near_recv.at[index, rows], near_s.at[index, half], near_r.at[index, half],
            place.core,
        )

    def share_far(quarter):
        rows = pl.ds(quarter * (part // 2), part // 2)
        return remote(far_sum.at[rows], far_recv.at[rows], far_s.at[quarter], far_r.at[quarter], place.across_y)

    for half in range(halves):
        near_send[0, half * part : (half + 1) * part, :] = part_for(1, half).astype(low)
        share_near(0, half).start()
    for half in range(halves):
        rows = slice(half * part, (half + 1) * part)
        far_part = part_for(0, half)
        share_near(0, half).wait_recv()
        far_sum[rows, :] = (far_part + near_recv[0, rows, :].astype(full)).astype(low)
        share_far(2 * half).start()
        if half == 0:
            share_far(1).start()
    take_x(UP_W)
    reduce.fling(UP_W)
    weight_part(heads - 1)
    reduce.settle(OUT_W)
    sum_y(OUT_W).start()
    taken = mul(memory_pick(slot_rows, 0), grads[...], NT).astype(low)
    own_part = mul(memory_pick(local_rows, place.s * local_rows), resid_ref[...].astype(low))
    memory_own[...] = (mul(taken, weight_ref[...], NT) + own_part).astype(low)
    memory = Spread(place, memory_all, memory_own, share_send.at[DW_FIRST + heads], share_recv.at[DW_FIRST + heads])
    memory.start()
    for half in range(halves):
        rows = slice(half * part, (half + 1) * part)
        near_send[1, rows, :] = part_for(2, half).astype(low)
        share_near(1, half).start()
    for half in range(halves):
        resid_ref[half * part : (half + 1) * part, :] += part_for(3, half)
    take_x(last)
    reduce.fling(last)
    reduce.settle(first)
    spread_of(first).start()
    add_last(OUT_W)
    reduce.settle(second)
    spread_of(second).start()
    settle_up()
    reduce.settle(last)
    spread_of(last).start()
    share_far(3).start()
    memory.pass_on()
    for h in (heads - 1, 0, 1):
        spread_of(DW_FIRST + h).pass_on()
    for array in (UP_W, DOWN_W):
        spread_of(array).pass_on()
    for array, out in ((OUT_W, out_out),):
        columns = out.shape[1] // 2
        out[:, pl.ds(pl.multiple_of(place.c * columns, columns), columns)] = settled(array)[...]
        half_to_core(array).wait()
        out[:, pl.ds(pl.multiple_of((1 - place.c) * columns, columns), columns)] = share[array][1][...]
    for h in range(heads):
        spread_of(DW_FIRST + h).finish()
    spread_of(UP_W).finish()
    spread_of(DOWN_W).finish()
    quarter = down_out.shape[0] // 4
    part_columns = up_out.shape[1] // 4
    for member in range(4):
        start = (2 * (member % 2) + member // 2) * part_columns
        up_out[:, start : start + part_columns] = up_all[member]
        down_out[member * quarter : (member + 1) * quarter, :] = down_all[member]
    half = qkv_out.shape[0] // 2
    for kind in range(3):
        for member in range(4):
            for h in range(heads):
                start = kind * width + (member * heads + h) * HEAD
                for side in range(2):
                    lanes = (3 * side + kind) * HEAD
                    qkv_out[side * half : (side + 1) * half, start : start + HEAD] = dw_all[
                        h, member, :half, lanes : lanes + HEAD
                    ]
    vector_sum = dw_all[heads - 1, 0, half:, :].astype(full)
    for member in range(1, 4):
        vector_sum = vector_sum + dw_all[heads - 1, member, half:, :].astype(full)
    vector_out[...] = vector_sum
    memory.finish()
    total = memory_all[0].astype(full)
    for member in range(1, 4):
        total = total + memory_all[member].astype(full)
    read_out[...] = total[:MEM]
    write_out[...] = total[16 : 16 + MEM]
    for half in range(halves):
        rows = slice(half * part, (half + 1) * part)
        share_near(1, half).wait_recv()
        for quarter in (2 * half, 2 * half + 1):
            share_far(quarter).wait_recv()
        grad_layer = resid_ref[rows, :] + near_recv[1, rows, :].astype(full) + far_recv[rows, :].astype(full)
        rows_at = place.s * local_rows + half * part + lax.broadcasted_iota(jnp.int32, (part, 1), 0)
        in_write = (rows_at >= length - MEM) & (rows_at < length)
        input_out[rows, :] = jnp.where((rows_at < MEM) | in_write, 0.0, grad_layer)
    for array in range(DW_FIRST + heads + 1):
        reduce.finish(array)
    cross_up().wait_send()
    for turn in range(3):
        send_grad(turn).wait_send()
    for half in range(halves):
        for index in range(2):
            share_near(index, half).wait_send()
        for quarter in (2 * half, 2 * half + 1):
            share_far(quarter).wait_send()


def back(lengths, grad_own, saved, vectors, rows, weight, resid, up_given, down_given, out_given):
    q_x, k_t, k_wide, v_wide, mixed, row_stats = saved
    heads, _, slot_rows = q_x.shape
    width, local_rows = grad_own.shape
    hidden = 32 * up_given.shape[3]
    shard, head_cols = width // 8, heads * HEAD
    half, small, piece = hidden // 2, width // 2, hidden // 32
    vmem = pl.BlockSpec(memory_space=pltpu.VMEM)
    anywhere = pl.BlockSpec(memory_space=pl.ANY)
    dma = pltpu.SemaphoreType.DMA
    arrays = DW_FIRST + heads

    def held(*shape, kind=low):
        return pltpu.VMEM(shape, kind)

    tall = (shard // 2 + 16, 6 * HEAD)
    return pl.pallas_call(
        back_kernel,
        in_specs=[pl.BlockSpec(memory_space=pltpu.SMEM)] + [vmem] * 2 + [anywhere] * 12,
        out_specs=[vmem] * 8,
        out_shape=[
            jax.ShapeDtypeStruct((local_rows, width), full),
            jax.ShapeDtypeStruct((MEM, width), full),
            jax.ShapeDtypeStruct((MEM, width), full),
            jax.ShapeDtypeStruct((shard, 3 * width), low),
            jax.ShapeDtypeStruct((16, 6 * HEAD), full),
            jax.ShapeDtypeStruct((shard, hidden), low),
            jax.ShapeDtypeStruct((hidden // 8, width), low),
            jax.ShapeDtypeStruct((shard, width), low),
        ],
        scratch_shapes=[
            held(heads, HEAD, slot_rows), held(head_cols, slot_rows), held(heads, slot_rows, WIDE),
            held(heads, slot_rows, WIDE), held(head_cols, slot_rows, kind=full), held(heads, 8, slot_rows, kind=full),
            held(head_cols, slot_rows), held(WIDE, local_rows), held(WIDE, local_rows), held(3 * head_cols, slot_rows),
            held(HEAD, slot_rows, kind=full), held(HEAD, slot_rows, kind=full),
            held(slot_rows, width), held(width, 3 * head_cols), held(local_rows, width, kind=full),
            held(4, piece, width), held(4, shard, small), held(4, piece, width), held(4, piece, width),
            held(4, piece, width), held(heads, 8, *tall), held(2, 4, piece, width),
            held(4, piece, width), held(4, shard, small), held(4, piece, width), held(heads, 4, *tall),
            held(4, piece, width), held(4, shard, small), held(4, piece, width), held(heads, 4, *tall),
            held(2, 4, piece, width),
            held(piece, width), held(shard, small), held(4, piece, width), held(shard, small),
            held(4, piece, width), held(heads, 4, *tall),
            held(2, local_rows, width), held(2, local_rows, width), held(local_rows, width),
            held(local_rows, width), held(4, 32, width), held(32, width),
            dma((3,)), dma((3,)), dma((3,)), dma((heads, 6)), dma((5, 4)), dma((arrays + 1, 3)),
            dma((arrays + 1, 3)), dma((2, 2)), dma((2, 2)), dma((4,)), dma((4,)),
            dma((1,)), dma((1,)),
            dma((2, 4)), dma((2, 4)), dma((arrays, 4)), dma((arrays, 4)),
            dma((arrays + 1, 2, 4)), dma((arrays + 1, 2, 4)),
        ],
        compiler_params=pltpu.CompilerParams(
            vmem_limit_bytes=VMEM_BYTES, collective_id=1, has_side_effects=True
        ),
        name="back",
    )(
        lengths, grad_own, vectors, q_x, k_t, k_wide, v_wide, mixed, row_stats, rows, weight, resid,
        up_given, down_given, out_given,
    )


def phi_parts(value):
    normal = 0.5 * (1.0 + lax.erf(value * (0.5**0.5)))
    density = jnp.exp(-0.5 * value * value) * (0.5 * 2.0**0.5 * 3.141592653589793**-0.5)
    return normal, normal + value * density


def statistics(values):
    centre = values - jnp.mean(values, axis=1, keepdims=True)
    factor = lax.rsqrt(jnp.mean(centre * centre, axis=1, keepdims=True) + norm_epsilon)
    return centre * factor, factor


def norm_back(grad, gain, normed, factor):
    scaled = grad * gain
    first = jnp.mean(scaled, axis=1, keepdims=True)
    second = jnp.mean(scaled * normed, axis=1, keepdims=True)
    return factor * (scaled - first - normed * second)


def column_total(values):
    return jnp.sum(values, axis=0, keepdims=True)


def middle_kernel(
    length_ref, cotangent, small, up_bias, rows_in, attended_in, up_in, down_in, out_in,
    output, resid_out, grad_own, vector_out, up_out, down_out, out_out,
    layer_in, attended, up_w, down_w, out_w, hidden, slope, normed_one, middle_low, grad_down,
    grad_two, grad_mid, totals, up_total, up_grad, down_grad, out_grad, up_sum, down_sum, out_sum,
    from_y, load_sem, save_sem, c_send, c_recv, y_send, y_recv,
):
    place = Place()
    rows, width = cotangent.shape
    ff = up_w.shape[1]
    chunk = ff // 4
    shard = width // 8
    barrier = pltpu.get_barrier_semaphore()
    for where in (place.core, place.across_y):
        pl.semaphore_signal(barrier, inc=1, device_id=where, device_id_type=MESH)

    def chunk_lanes(j):
        return pl.ds(pl.multiple_of(j * chunk, chunk), chunk)

    def up_load(j):
        return pltpu.make_async_copy(up_in.at[:, chunk_lanes(j)], up_w.at[:, chunk_lanes(j)], load_sem.at[j])

    def down_load(j):
        return pltpu.make_async_copy(down_in.at[chunk_lanes(j)], down_w.at[chunk_lanes(j)], load_sem.at[4 + j])

    first_loads = [
        pltpu.make_async_copy(
            rows_in.at[pl.ds(pl.multiple_of(place.s * rows, rows), rows)], layer_in, load_sem.at[8]
        ),
        pltpu.make_async_copy(attended_in, attended, load_sem.at[9]),
        pltpu.make_async_copy(out_in, out_w, load_sem.at[10]),
    ]
    for load in first_loads:
        load.start()
    for j in range(4):
        up_load(j).start()
        down_load(j).start()
    out_bias, gain_one, shift_one = small[0:1, :], small[1:2, :], small[2:3, :]
    down_bias, gain_two, shift_two = small[3:4, :], small[4:5, :], small[5:6, :]
    for load in first_loads:
        load.wait()

    branch = mul(attended[...], out_w[...], TN)
    normed, factor_one = statistics(layer_in[...].astype(full) + branch + out_bias)
    normed_one[...] = normed
    middle_low[...] = (normed * gain_one + shift_one).astype(low)
    grad_mid[...] = jnp.zeros_like(grad_mid)

    def forward_chunk(j, carry):
        up_load(j).wait()
        lanes = chunk_lanes(j)
        value = mul(middle_low[...], up_w[:, lanes]) + up_bias[0:1, lanes]
        normal, slope_here = phi_parts(value)
        hidden[:, lanes] = (value * normal).astype(low)
        slope[:, lanes] = slope_here
        down_load(j).wait()
        grad_mid[...] += mul(hidden[:, lanes], down_w[lanes, :])
        return carry

    lax.fori_loop(0, 4, forward_chunk, 0)
    middle = normed_one[...] * gain_one + shift_one
    normed_two, factor_two = statistics(middle + grad_mid[...] + down_bias)
    places = place.s * rows + lax.broadcasted_iota(jnp.int32, (rows, 1), 0)
    in_slot = places < length_ref[0]
    output[...] = jnp.where(in_slot, normed_two * gain_two + shift_two, 0.0).astype(low)
    grad_final = jnp.where(in_slot, cotangent[...].astype(full), 0.0)
    totals[4:5, :] = column_total(grad_final * normed_two)
    totals[5:6, :] = column_total(grad_final)
    grad_resid = norm_back(grad_final, gain_two, normed_two, factor_two)
    grad_two[...] = grad_resid
    grad_down[...] = grad_resid.astype(low)
    totals[3:4, :] = column_total(grad_down[...].astype(full))
    pl.semaphore_wait(barrier, 2)

    def down_piece(ref, line, column, far, core):
        dest = 2 * line + (place.x if column == 0 else 1 - place.x)
        y = place.y if far == 0 else 1 - place.y
        return ref.at[pl.ds(pl.multiple_of(dest * 4 * shard + (2 * y + core) * shard, shard), shard)]

    def side_piece(ref, line, column, core):
        dest = 2 * line + (place.x if column == 0 else 1 - place.x)
        half = ref.shape[1] // 2
        return ref.at[
            pl.ds(pl.multiple_of(dest * shard, shard), shard), pl.ds(pl.multiple_of(core * half, half), half)
        ]

    def down_share(line, column, far):
        return remote(
            down_piece(down_grad, line, column, far, 1 - place.c), down_sum.at[column, line, far],
            c_send.at[2 + far, column, line], c_recv.at[2 + far, column, line], place.core,
        )

    def side_slot(array, line, column):
        return out_sum.at[line, column] if array == 1 else up_sum.at[column, line]

    def over_y(line):
        return remote(down_sum.at[1, line, 1], from_y.at[line], y_send.at[line], y_recv.at[line], place.across_y)

    def side_share(array, line, column):
        grad = (up_grad, out_grad)[array]
        return remote(
            side_piece(grad, line, column, 1 - place.c), side_slot(array, line, column),
            c_send.at[array, column, line], c_recv.at[array, column, line], place.core,
        )

    def down_save(column, line):
        return pltpu.make_async_copy(down_sum.at[column, line], down_out.at[column, line], save_sem.at[2, column, line])

    def side_saves(array, column, line):
        if array == 1:
            return [pltpu.make_async_copy(
                side_slot(1, line, column), out_out.at[line, column], save_sem.at[1, column, line]
            )]
        return [
            pltpu.make_async_copy(
                up_sum.at[column, line, :, chunk_lanes(place.y if far == 0 else 1 - place.y)],
                up_out.at[column, line, far], save_sem.at[3 * far, column, line],
            )
            for far in range(2)
        ]

    def add_far(column, line):
        down_share(line, column, 1).wait_recv()
        down_sum[column, line, 1] = add_low(
            down_sum[column, line, 1], down_piece(down_grad, line, column, 1, place.c)[...]
        )

    def down_chunk(line, carry):
        lanes = chunk_lanes(line)
        down_grad[lanes, :] = mul(hidden[:, lanes], grad_down[...], TN).astype(low)
        for far in (1, 0):
            for column in (1, 0):
                down_share(line, column, far).start()

        @pl.when(line > 0)
        def _():
            add_far(1, line - 1)
            over_y(line - 1).start()

        return carry

    lax.fori_loop(0, 4, down_chunk, 0)
    add_far(1, 3)
    over_y(3).start()
    grad_mid[...] = grad_two[...]

    def back_chunk(turn, carry):
        j = lax.rem(2 * (1 - place.c) + turn, 4)
        lanes = chunk_lanes(j)
        grad_up = (mul(grad_down[...], down_w[lanes, :], NT) * slope[:, lanes]).astype(low)
        up_total[0:1, lanes] = column_total(grad_up.astype(full))
        up_grad[:, lanes] = mul(middle_low[...], grad_up, TN).astype(low)
        grad_mid[...] += mul(grad_up, up_w[:, lanes], NT)

        @pl.when(turn == 1)
        def _():
            for column in (1, 0):
                for line in LINES:
                    side_share(0, line, column).start()

        return carry

    lax.fori_loop(0, 4, back_chunk, 0)
    grad_middle = grad_mid[...]
    normed = normed_one[...]
    totals[1:2, :] = column_total(grad_middle * normed)
    totals[2:3, :] = column_total(grad_middle)
    grad_one = norm_back(grad_middle, gain_one, normed, factor_one)
    resid_out[...] = grad_one
    grad_branch = grad_one.astype(low)
    totals[0:1, :] = column_total(grad_branch.astype(full))
    out_grad[...] = mul(attended[...], grad_branch).astype(low)
    for column in (1, 0):
        for line in LINES:
            side_share(1, line, column).start()
    grad_own[...] = mul(out_w[...], grad_branch, NT).astype(low)

    def add_down(column, line):
        down_share(line, column, 0).wait_recv()
        down_sum[column, line, 0] = add_low(
            down_sum[column, line, 0], down_piece(down_grad, line, column, 0, place.c)[...]
        )
        if column == 0:
            add_far(column, line)
        else:
            over_y(line).wait()
            down_sum[column, line, 0] = add_low(down_sum[column, line, 0], from_y[line])
        down_save(column, line).start()

    def add_side(array, column, line):
        slot = side_slot(array, line, column)
        side_share(array, line, column).wait_recv()
        slot[...] = add_low(slot[...], side_piece((up_grad, out_grad)[array], line, column, place.c)[...])
        for save in side_saves(array, column, line):
            save.start()

    for line in LINES:
        add_down(0, line)
    for column in (1, 0):
        for line in LINES:
            add_side(0, column, line)
    vector_out[...] = jnp.zeros_like(vector_out)
    for dest in range(8):
        for index, (line, start) in enumerate(((0, 2), (0, 3), (1, 0), (2, 1), (2, 2), (2, 3))):
            vector_out[dest, line : line + 1, start * shard : (start + 1) * shard] = totals[
                index : index + 1, dest * shard : (dest + 1) * shard
            ]
        base = dest * 4 * shard
        vector_out[dest, 1:2, shard:] = up_total[0:1, base : base + 3 * shard]
        vector_out[dest, 2:3, :shard] = up_total[0:1, base + 3 * shard : base + 4 * shard]
    for column in range(2):
        for line in range(4):
            add_side(1, column, line)
    for line in LINES:
        add_down(1, line)
    for column in range(2):
        for line in range(4):
            for array in range(2):
                side_share(array, line, column).wait_send()
                for save in side_saves(array, column, line):
                    save.wait()
            for far in range(2):
                down_share(line, column, far).wait_send()
            down_save(column, line).wait()


def middle_part(lengths, cotangent, small, up_bias, rows_full, attended, up_full, down_full, out_full):
    rows, width = cotangent.shape
    ff = up_full.shape[1]
    shard = width // 8
    vmem = pl.BlockSpec(memory_space=pltpu.VMEM)
    anywhere = pl.BlockSpec(memory_space=pl.ANY)
    dma = pltpu.SemaphoreType.DMA

    def held(*shape, kind=low):
        return pltpu.VMEM(shape, kind)

    def shaped(*shape, kind=low):
        return jax.ShapeDtypeStruct(shape, kind)

    up_parts, down_parts, out_parts = (2, 4, shard, ff // 2), (2, 4, 2, ff // 32, width), (4, 2, shard, width // 2)
    return pl.pallas_call(
        middle_kernel,
        in_specs=[pl.BlockSpec(memory_space=pltpu.SMEM)] + [vmem] * 3 + [anywhere] * 5,
        out_specs=[vmem] * 4 + [anywhere] * 3,
        out_shape=[
            shaped(rows, width), shaped(rows, width, kind=full), shaped(width, rows),
            shaped(8, 16, 4 * shard, kind=full), shaped(*down_parts), shaped(*down_parts), shaped(*out_parts),
        ],
        scratch_shapes=[
            held(rows, width), held(width, rows), held(width, ff), held(ff, width), held(width, width), held(rows, ff), held(rows, ff, kind=full),
            held(rows, width, kind=full), held(rows, width), held(rows, width), held(rows, width, kind=full),
            held(rows, width, kind=full), held(8, width, kind=full), held(8, ff, kind=full),
            held(width, ff), held(ff, width), held(width, width), held(*up_parts), held(*down_parts),
            held(*out_parts), held(4, ff // 32, width), dma((11,)), dma((4, 2, 4)), dma((4, 2, 4)),
            dma((4, 2, 4)), dma((4,)), dma((4,)),
        ],
        compiler_params=pltpu.CompilerParams(
            vmem_limit_bytes=VMEM_BYTES, collective_id=2, has_side_effects=True
        ),
        name="middle",
    )(lengths, cotangent, small, up_bias, rows_full, attended, up_full, down_full, out_full)


def finish_kernel(
    output_in, input_in, qkv_in, vector_in, up_in, down_in, out_in, read_in, write_in,
    output, input_out, read_out, write_out, qkv_out, qv_out, out_out, out_b, gain_one, shift_one, up_out, up_b,
    down_out, down_b, gain_two, shift_two,
):
    shard = out_b.shape[1]
    output[...] = output_in[...]
    input_out[...] = input_in[...]
    for given, out in ((read_in, read_out), (write_in, write_out)):
        for line in range(given.shape[0]):
            out[line] = given[line : line + 1]
    for given, out in ((qkv_in, qkv_out), (up_in, up_out), (down_in, down_out), (out_in, out_out)):
        out[...] = given[...].astype(full)
    qv_out[...] = vector_in[0:1, : 2 * shard]
    out_b[...] = vector_in[0:1, 2 * shard : 3 * shard]
    gain_one[...] = vector_in[0:1, 3 * shard :]
    shift_one[...] = vector_in[1:2, :shard]
    up_b[:, : 3 * shard] = vector_in[1:2, shard:]
    up_b[:, 3 * shard :] = vector_in[2:3, :shard]
    down_b[...] = vector_in[2:3, shard : 2 * shard]
    gain_two[...] = vector_in[2:3, 2 * shard : 3 * shard]
    shift_two[...] = vector_in[2:3, 3 * shard :]


def finish(output, input_grad, qkv_grad, vectors, up_grad, down_grad, out_grad, grad_read, grad_write):
    shard = qkv_grad.shape[0]

    def shaped(*shape, kind=full):
        return jax.ShapeDtypeStruct(shape, kind)

    line = shaped(1, shard)
    steps = 2

    def rows(array):
        return pl.BlockSpec((array.shape[0] // steps,) + array.shape[1:], lambda i: (i, 0))

    def once(*shape):
        return pl.BlockSpec(shape, lambda i: (0,) * len(shape))

    lone = once(1, shard)
    memory = (grad_read.shape[0], 1, grad_read.shape[1])
    return pl.pallas_call(
        finish_kernel,
        grid=(steps,),
        in_specs=[
            rows(output), rows(input_grad), rows(qkv_grad), once(*vectors.shape), rows(up_grad), rows(down_grad),
            rows(out_grad), once(*grad_read.shape), once(*grad_write.shape),
        ],
        out_specs=[
            rows(output), rows(input_grad), once(*memory), once(*memory), rows(qkv_grad), once(1, 2 * shard),
            rows(out_grad), lone, lone, lone, rows(up_grad), once(1, 4 * shard), rows(down_grad), lone, lone, lone,
        ],
        out_shape=[
            shaped(*output.shape, kind=low), shaped(*input_grad.shape), shaped(*memory), shaped(*memory),
            shaped(*qkv_grad.shape), shaped(1, 2 * shard), shaped(*out_grad.shape), line, line, line,
            shaped(*up_grad.shape), shaped(1, 4 * shard), shaped(*down_grad.shape), line, line, line,
        ],
        compiler_params=pltpu.CompilerParams(vmem_limit_bytes=VMEM_BYTES),
        name="finish",
    )(output, input_grad, qkv_grad, vectors, up_grad, down_grad, out_grad, grad_read, grad_write)


def normalize(values, gain_vec, shift_vec):
    centre = values - jnp.mean(values, axis=-1, keepdims=True)
    factor = lax.rsqrt(jnp.mean(centre * centre, axis=-1, keepdims=True) + norm_epsilon)
    return centre * factor * gain_vec + shift_vec


def column_sums(values):
    return jnp.sum(values, axis=0, dtype=full)


def on_block(
    tokens, read_rows, write_rows, lengths, qkv_weight, vectors, out_weight, up_weight, down_weight, cotangent
):
    total = sum(vector.shape[0] for vector in vectors)
    packed, start = jnp.zeros((1, total), full), 0
    for vector in vectors:
        size = vector.shape[0]
        packed = packed + jnp.pad(vector.astype(full).reshape(1, -1), ((0, 0), (start, total - start - size)))
        start += size
    (small, up_bias, rows, weight, q_t, k_t, k_wide, v_wide, mixed, row_stats, up_full, down_full, out_full,
     attended) = front(
        lengths, tokens, read_rows, write_rows, qkv_weight, packed, up_weight, down_weight, out_weight
    )
    output, resid, grad_own, vector_parts, up_parts, down_parts, out_parts = middle_part(
        lengths, cotangent, small, up_bias, rows, attended, up_full, down_full, out_full
    )
    saved = (q_t, k_t, k_wide, v_wide, mixed, row_stats)
    input_grad, grad_read, grad_write, qkv_grad, vector_sum, up_grad, down_grad, out_grad = back(
        lengths, grad_own, saved, vector_parts, rows, weight, resid, up_parts, down_parts, out_parts
    )
    results = finish(
        output, input_grad, qkv_grad, vector_sum, up_grad, down_grad, out_grad, grad_read, grad_write
    )
    shaped = [jnp.swapaxes(result, 0, 1) if index in (2, 3) else result for index, result in enumerate(results)]
    return tuple(result.reshape(-1) if result.shape[0] == 1 and result.ndim == 2 else result for result in shaped)


def per_device(
    tokens, read_memory, write_memory, lengths, qkv_weight, qv_bias, out_weight, out_bias, norm1_gain,
    norm1_bias, up_weight, up_bias, down_weight, down_bias, norm2_gain, norm2_bias, cotangent,
):
    seq_count = lax.axis_size("seq")
    fsdp_count = lax.axis_size("fsdp")
    seq_place = lax.axis_index("seq")
    local_rows, width = tokens.shape
    head_cols = width // seq_count
    shard = width // fsdp_count
    length = lengths[0]
    heads = head_cols // HEAD
    vectors = (qv_bias, out_bias, norm1_gain, norm1_bias, up_bias, down_bias, norm2_gain, norm2_bias)
    if (fsdp_count, seq_count) == (8, 4):
        return on_block(
            tokens, read_memory[0], write_memory[0], lengths, qkv_weight, vectors, out_weight, up_weight, down_weight,
            cotangent,
        )
    places = seq_place * local_rows + jnp.arange(local_rows, dtype=jnp.int32)
    in_slot = (places < length)[:, None]
    memory_slots = jnp.arange(MEM, dtype=jnp.int32)
    pick_read = places[:, None] == memory_slots[None, :]
    pick_write = places[:, None] == length - MEM + memory_slots[None, :]
    is_memory = jnp.any(pick_read | pick_write, axis=1)[:, None]
    picks = jnp.concatenate([pick_read, pick_write], axis=1).astype(full)
    memory = jnp.concatenate([read_memory[0], write_memory[0]], axis=0)
    layer_in = jnp.where(is_memory, mul(picks.astype(low), memory).astype(low), tokens)

    own_shard = lax.dynamic_slice_in_dim(
        qkv_weight.reshape(shard, 3, seq_count, heads, HEAD), seq_place, 1, 2
    )
    own_shard = jnp.transpose(own_shard[:, :, 0], (0, 2, 1, 3)).reshape(shard, 3 * head_cols)
    packed = jnp.concatenate(vectors)
    rows = lax.all_gather(layer_in, "seq", axis=0, tiled=True)
    weight = lax.all_gather(own_shard, "fsdp", axis=0, tiled=True)
    packed = lax.all_gather(packed.reshape(1, -1), "fsdp", axis=0, tiled=True).astype(full)
    whole, start = [], 0
    for vector in vectors:
        whole.append(packed[:, start : start + vector.shape[0]].reshape(-1))
        start += vector.shape[0]
    qv_vec, out_vec, gain_one, shift_one, up_vec, down_vec, gain_two, shift_two = whole
    own_qv = lax.dynamic_slice_in_dim(qv_vec.reshape(2, seq_count, head_cols), seq_place, 1, 1)
    bias = jnp.concatenate([own_qv[0, 0], own_qv[1, 0]])
    bias = jnp.broadcast_to(bias, (8, bias.shape[0]))
    out_full = lax.all_gather(out_weight, "fsdp", axis=0, tiled=True)
    up_full = lax.all_gather(up_weight, "fsdp", axis=0, tiled=True)
    down_full = lax.all_gather(down_weight, "fsdp", axis=0, tiled=True)
    q_x, k_t, k_wide, v_wide, mixed, mixed_low, row_stats = attention_forward(lengths, rows, weight, bias)
    attended = lax.all_to_all(mixed_low, "seq", split_axis=1, concat_axis=0, tiled=True)
    resid_one = layer_in.astype(full) + mul(attended, out_full, TN) + out_vec
    middle, norm_one_back = jax.vjp(normalize, resid_one, gain_one, shift_one)
    middle_low = middle.astype(low)
    up_pre = mul(middle_low, up_full) + up_vec
    gelu_out, gelu_back = jax.vjp(partial(jax.nn.gelu, approximate=False), up_pre)
    hidden = gelu_out.astype(low)
    down_pre = mul(hidden, down_full) + down_vec
    final, norm_two_back = jax.vjp(normalize, middle + down_pre, gain_two, shift_two)
    output = jnp.where(in_slot, final, 0.0).astype(low)
    grad_final = jnp.where(in_slot, cotangent.astype(full), 0.0)
    grad_resid_two, grad_gain_two, grad_shift_two = norm_two_back(grad_final)
    grad_down = grad_resid_two.astype(low)
    grad_down_weight = mul(hidden, grad_down, TN)
    (grad_up_pre,) = gelu_back(mul(grad_down, down_full, NT))
    grad_up = grad_up_pre.astype(low)
    grad_up_weight = mul(middle_low, grad_up, TN)
    grad_middle = grad_resid_two + mul(grad_up, up_full, NT)
    grad_resid_one, grad_gain_one, grad_shift_one = norm_one_back(grad_middle)
    grad_branch = grad_resid_one.astype(low)
    grad_out_weight = mul(attended, grad_branch)
    grad_attended = mul(out_full, grad_branch, NT).astype(low)
    vector_grads = [
        column_sums(grad_branch), grad_gain_one, grad_shift_one, column_sums(grad_up),
        column_sums(grad_down), grad_gain_two, grad_shift_two,
    ]
    packed_grad = jnp.concatenate([v.reshape(fsdp_count, -1) for v in vector_grads], axis=1)
    saved = (q_x, k_t, k_wide, v_wide, mixed, row_stats)
    grad_t = lax.all_to_all(grad_attended, "seq", split_axis=0, concat_axis=1, tiled=True)
    partial_in, weight_part, sums = attention_backward(*saved, grad_t, rows, weight)
    from_heads = lax.psum_scatter(partial_in, "seq", scatter_dimension=0, tiled=True).astype(full)
    grad_layer_in = grad_resid_one + from_heads
    input_grad = jnp.where(is_memory, 0.0, grad_layer_in)
    grad_memory = lax.dot_general(
        picks, grad_layer_in, TN, precision=lax.Precision.HIGHEST, preferred_element_type=full
    )
    grad_memory = lax.psum(grad_memory.astype(low), "seq").astype(full)
    grad_read, grad_write = grad_memory[:MEM], grad_memory[MEM:]
    sums = sums[:, 0].reshape(heads, 3, HEAD)
    own_sums = jnp.stack([sums[:, 0].reshape(-1), sums[:, 2].reshape(-1)])[:, None]
    zero_qv = jnp.zeros((2, seq_count, head_cols), full)
    qv_grad = lax.dynamic_update_slice_in_dim(zero_qv, own_sums, seq_place, 1)
    packed_grad = jnp.concatenate([qv_grad.reshape(fsdp_count, -1), packed_grad], axis=1)
    packed_sum = lax.psum(packed_grad, ("fsdp", "seq"))
    own_vectors = lax.dynamic_index_in_dim(packed_sum, lax.axis_index("fsdp"), 0, False)

    def both_axes(part):
        piece = lax.psum_scatter(part.astype(low), "fsdp", scatter_dimension=0, tiled=True)
        return lax.psum(piece, "seq").astype(full)

    qkv_piece = lax.psum_scatter(weight_part, "fsdp", scatter_dimension=0, tiled=True)
    qkv_parts = lax.all_gather(qkv_piece, "seq", axis=0).reshape(seq_count, shard, heads, 3, HEAD)
    qkv_out = jnp.transpose(qkv_parts, (1, 3, 0, 2, 4)).reshape(shard, 3 * width).astype(full)
    up_out, down_out, out_out = both_axes(grad_up_weight), both_axes(grad_down_weight), both_axes(grad_out_weight)
    vector_outs, start = [], 0
    for vector in vectors:
        vector_outs.append(own_vectors[start : start + vector.shape[0]])
        start += vector.shape[0]
    qv_out, out_b_out, gain_one_out, shift_one_out, up_b_out, down_b_out, gain_two_out, shift_two_out = vector_outs
    return (
        output, input_grad, grad_read[None], grad_write[None], qkv_out, qv_out, out_out, out_b_out, gain_one_out,
        shift_one_out, up_out, up_b_out, down_out, down_b_out, gain_two_out, shift_two_out,
    )


def solution(mesh):
    rows, piece = P(("fsdp", "seq"), None), P("fsdp")
    matrix, memory = P("fsdp", None), P("fsdp", None, None)
    in_specs = (
        rows, memory, memory, piece, matrix, piece, matrix, piece, piece, piece, matrix, piece, matrix,
        piece, piece, piece, rows,
    )
    out_specs = (
        rows, rows, memory, memory, matrix, piece, matrix, piece, piece, piece, matrix, piece, matrix,
        piece, piece, piece,
    )
    return jax.shard_map(per_device, mesh=mesh, in_specs=in_specs, out_specs=out_specs, check_vma=False)
```

```python
from functools import partial

import jax
import jax.numpy as jnp
from jax import lax
from jax.experimental import pallas as pl
from jax.experimental.pallas import tpu as pltpu
from jax.sharding import PartitionSpec as P

HEAD = 64
MEM = 10
WIDE = 128
VMEM_BYTES = 64000 * 1024

norm_epsilon = 1e-06
masked_score = -1e30
low = jnp.bfloat16
full = jnp.float32

NN = (((1,), (0,)), ((), ()))
NT = (((1,), (1,)), ((), ()))
TN = (((0,), (0,)), ((), ()))
TT = (((0,), (1,)), ((), ()))


def mul(left, right, dims=NN):
    return lax.dot_general(left, right, dims, preferred_element_type=full)


def three_parts(value):
    high = value.astype(low)
    rest = value - high.astype(full)
    middle = rest.astype(low)
    return high, middle, (rest - middle.astype(full)).astype(low)


def stack_rows(rows, columns):
    place = lax.broadcasted_iota(jnp.int32, (HEAD, columns), 0)
    block = jnp.zeros((HEAD, columns), full)
    for index, row in enumerate(rows):
        block = jnp.where(place == index, row, block)
    return block.astype(low)


def project_block(start, length, rows_ref, weight_ref, bias_q, bias_v, q_x, k_t, v_x, k_wide, v_wide, step):
    head_cols = k_t.shape[0]
    lanes = pl.ds(start, step)
    made = mul(weight_ref[...], rows_ref[lanes, :], TT)
    place = start + lax.broadcasted_iota(jnp.int32, (1, step), 1)
    key_bias = jnp.where(place < length, 0.0, masked_score)
    one = jnp.ones((1, step), full)
    query_extra = stack_rows([one], step)
    key_extra = stack_rows([key_bias, one, one, one], step)
    value_extra = stack_rows([one, one, one], step)
    for h in range(head_cols // HEAD):
        own = slice(h * HEAD, (h + 1) * HEAD)
        base = 3 * h * HEAD
        query = (made[base : base + HEAD] + bias_q[own]).astype(low)
        q_x[h, :HEAD, lanes] = query * jnp.asarray(HEAD**-0.5, low)
        q_x[h, HEAD:, lanes] = query_extra
        k_t[own, lanes] = made[base + HEAD : base + 2 * HEAD].astype(low)
        v_x[h, :HEAD, lanes] = (made[base + 2 * HEAD : base + 3 * HEAD] + bias_v[own]).astype(low)
        v_x[h, HEAD:, lanes] = value_extra
        k_wide[h, lanes, :] = jnp.transpose(jnp.concatenate([k_t[own, lanes], key_extra], axis=0))
        v_wide[h, lanes, :] = jnp.transpose(v_x[h, :, lanes])


def project_heads(length, rows_ref, weight_ref, bias_ref, q_x, k_t, v_x, k_wide, v_wide):
    head_cols = k_t.shape[0]
    bias = jnp.transpose(bias_ref[...])[:, 0:1]
    for start in range(0, rows_ref.shape[0], 512):
        project_block(
            start, length, rows_ref, weight_ref, bias[:head_cols], bias[head_cols:],
            q_x, k_t, v_x, k_wide, v_wide, 512,
        )


def attend_block(h, lanes, q_x, k_wide, v_x, mixed, mixed_low, row_stats):
    scores = mul(k_wide[h], q_x[h, :, lanes])
    row_max = jnp.max(scores, axis=0, keepdims=True)
    probs = jnp.exp(scores - row_max).astype(low)
    total = mul(v_x[h, : HEAD + 16], probs)
    row_sum = total[HEAD : HEAD + 1]
    own = pl.ds(h * HEAD, HEAD)
    result = total[:HEAD] / row_sum
    mixed[own, lanes] = result
    mixed_low[own, lanes] = result.astype(low)
    row_stats[h, :, lanes] = jnp.broadcast_to(row_max + jnp.log(row_sum), (8, result.shape[1]))


def forward_kernel(
    length_ref, rows_ref, weight_ref, bias_ref, q_x, k_t, k_wide, v_wide, mixed, mixed_low, row_stats, v_x
):
    project_heads(length_ref[0], rows_ref, weight_ref, bias_ref, q_x, k_t, v_x, k_wide, v_wide)
    heads = q_x.shape[0]
    block = 512
    blocks = q_x.shape[2] // block

    def step(index, carry):
        h = index // blocks
        start = pl.multiple_of(lax.rem(index, blocks) * block, block)
        attend_block(h, pl.ds(start, block), q_x, k_wide, v_x, mixed, mixed_low, row_stats)
        return carry

    lax.fori_loop(0, heads * blocks, step, 0)


def attention_forward(length, rows, weight, bias):
    slot_rows = rows.shape[0]
    head_cols = weight.shape[1] // 3
    heads = head_cols // HEAD
    vmem = pl.BlockSpec(memory_space=pltpu.VMEM)
    return pl.pallas_call(
        forward_kernel,
        in_specs=[pl.BlockSpec(memory_space=pltpu.SMEM), vmem, vmem, vmem],
        out_specs=[vmem] * 7,
        out_shape=[
            jax.ShapeDtypeStruct((heads, WIDE, slot_rows), low),
            jax.ShapeDtypeStruct((head_cols, slot_rows), low),
            jax.ShapeDtypeStruct((heads, slot_rows, WIDE), low),
            jax.ShapeDtypeStruct((heads, slot_rows, WIDE), low),
            jax.ShapeDtypeStruct((head_cols, slot_rows), full),
            jax.ShapeDtypeStruct((head_cols, slot_rows), low),
            jax.ShapeDtypeStruct((heads, 8, slot_rows), full),
        ],
        scratch_shapes=[pltpu.VMEM((heads, WIDE, slot_rows), low)],
        compiler_params=pltpu.CompilerParams(vmem_limit_bytes=VMEM_BYTES),
        name="attention_forward",
    )(length, rows, weight, bias)


def attend_back(h, lanes, q_x, q_here, do_x, grad_t, mixed, row_stats, k_t, k_wide, v_wide, grads, grad_k, grad_v, first):
    own = pl.ds(pl.multiple_of(h * HEAD, HEAD), HEAD)
    grad = grad_t[own, lanes]
    columns = grad.shape[1]
    delta = jnp.sum(grad.astype(full) * mixed[own, lanes], axis=0, keepdims=True)
    parts = [part.astype(full) for part in three_parts(-delta)]
    do_x[:HEAD, :] = grad
    do_x[HEAD:, :] = stack_rows(parts, columns)
    parts = [part.astype(full) for part in three_parts(-row_stats[h, 0:1, lanes])]
    q_here[:HEAD, :] = q_x[h, :HEAD, lanes]
    q_here[HEAD:, :] = stack_rows([jnp.ones((1, columns), full)] + parts, columns)
    value_part, key_part, query_parts = None, None, []
    for start in range(0, columns, columns // 2):
        side = slice(start, start + columns // 2)
        probs = jnp.exp(mul(k_wide[h], q_here[:, side]))
        grad_scores = (probs * mul(v_wide[h], do_x[:, side])).astype(low)
        value_more = mul(do_x[:HEAD, side], probs.astype(low), NT)
        key_more = mul(q_here[:HEAD, side], grad_scores, NT)
        value_part = value_more if value_part is None else value_part + value_more
        key_part = key_more if key_part is None else key_part + key_more
        query_parts.append(mul(k_t[own, :], grad_scores) * HEAD**-0.5)

    @pl.when(first)
    def _():
        grad_v[...] = value_part
        grad_k[...] = key_part

    @pl.when(jnp.logical_not(first))
    def _():
        grad_v[...] += value_part
        grad_k[...] += key_part

    query_part = jnp.concatenate(query_parts, axis=1)
    grads[pl.ds(pl.multiple_of(3 * h * HEAD, HEAD), HEAD), lanes] = query_part.astype(low)


def backward_kernel(
    q_in, k_t, k_wide, v_wide, mixed, row_stats, grad_t, rows_ref, weight_ref,
    partial_out, weight_out, sums_out, q_here, do_x, grads, grad_k, grad_v,
):
    heads, _, slot_rows = q_in.shape
    block = 512
    blocks = slot_rows // block

    def step(index, carry):
        h = index // blocks
        turn = lax.rem(index, blocks)
        start = pl.multiple_of(turn * block, block)
        attend_back(
            h, pl.ds(start, block), q_in, q_here, do_x, grad_t, mixed, row_stats, k_t, k_wide, v_wide, grads, grad_k,
            grad_v, turn == 0,
        )

        @pl.when(turn == blocks - 1)
        def _():
            base = pl.multiple_of(3 * h * HEAD, HEAD)
            grads[pl.ds(base + HEAD, HEAD), :] = grad_k[...].astype(low)
            grads[pl.ds(base + 2 * HEAD, HEAD), :] = grad_v[...].astype(low)

        return carry

    lax.fori_loop(0, heads * blocks, step, 0)
    for start in range(0, slot_rows, block):
        partial_out[start : start + block, :] = mul(
            grads[:, start : start + block], weight_ref[...], TT
        ).astype(partial_out.dtype)
    weight_out[...] = jnp.transpose(mul(grads[...], rows_ref[...])).astype(weight_out.dtype)
    sums_out[...] = jnp.broadcast_to(
        jnp.sum(grads[...].astype(full), axis=1, keepdims=True), sums_out.shape
    )


def attention_backward(q_x, k_t, k_wide, v_wide, mixed, row_stats, grad_t, rows, weight):
    heads, _, slot_rows = q_x.shape
    width, all_cols = weight.shape
    vmem = pl.BlockSpec(memory_space=pltpu.VMEM)
    return pl.pallas_call(
        backward_kernel,
        in_specs=[vmem] * 9,
        out_specs=[vmem] * 3,
        out_shape=[
            jax.ShapeDtypeStruct((slot_rows, width), low),
            jax.ShapeDtypeStruct((width, all_cols), low),
            jax.ShapeDtypeStruct((all_cols, WIDE), full),
        ],
        scratch_shapes=[
            pltpu.VMEM((WIDE, 512), low),
            pltpu.VMEM((WIDE, 512), low),
            pltpu.VMEM((all_cols, slot_rows), low),
            pltpu.VMEM((HEAD, slot_rows), full),
            pltpu.VMEM((HEAD, slot_rows), full),
        ],
        compiler_params=pltpu.CompilerParams(vmem_limit_bytes=VMEM_BYTES),
        name="attention_backward",
    )(q_x, k_t, k_wide, v_wide, mixed, row_stats, grad_t, rows, weight)


MESH = pl.DeviceIdType.MESH
OWN, RELATIONS = 0, 7
UP_W, OUT_W, DOWN_W, QKV_W = 0, 1, 2, 3


def offset_of(relation):
    return (0, -1, -2, -3, 1, 2, 3)[relation]


class Place:
    def __init__(self):
        self.f, self.s = lax.axis_index("fsdp"), lax.axis_index("seq")
        self.z, self.x = self.f // 2, lax.rem(self.f, 2)
        self.y, self.c = self.s // 2, lax.rem(self.s, 2)
        self.core = (self.f, 2 * self.y + 1 - self.c)
        self.across_y = (self.f, 2 * (1 - self.y) + self.c)
        self.diagonal = (self.f, 2 * (1 - self.y) + 1 - self.c)
        self.across_x = (2 * self.z + 1 - self.x, self.s)
        self.above = (self.f + 2, self.s)
        self.below = (self.f - 2, self.s)

    def has(self, relation):
        offset = offset_of(relation)
        return (self.z + offset >= 0) & (self.z + offset <= 3)

    def source(self, relation, column):
        own_column = self.f + 2 * offset_of(relation)
        return own_column if column == 0 else own_column + 1 - 2 * self.x

    def member(self, turn):
        flip_y = 1 - turn // 2
        flip_c = lax.rem(turn, 2) if not isinstance(turn, int) else turn % 2
        flip_c = flip_c + (1 - 2 * flip_c) * (turn // 2)
        return 2 * lax.rem(self.y + flip_y, 2) + lax.rem(self.c + flip_c, 2)


def remote(src, dst, send, recv, where):
    return pltpu.make_async_remote_copy(
        src_ref=src, dst_ref=dst, send_sem=send, recv_sem=recv, device_id=where, device_id_type=MESH
    )


def greet(place, all_lines):
    barrier = pltpu.get_barrier_semaphore()
    near = [place.core, place.across_y, place.diagonal, place.across_x]
    for where in near:
        pl.semaphore_signal(barrier, inc=1, device_id=where, device_id_type=MESH)
    for line in range(4):
        gap = place.z - line
        meets = gap != 0 if all_lines else (gap == 1) | (gap == -1)

        @pl.when(meets)
        def _(line=line):
            pl.semaphore_signal(
                barrier, inc=1, device_id=(2 * line + place.x, place.s), device_id_type=MESH
            )

    ends = 3 if all_lines else jnp.where((place.z == 0) | (place.z == 3), 1, 2)
    pl.semaphore_wait(barrier, len(near) + ends)


class Gather:
    def __init__(self, place, own, whole, sems):
        self.place, self.own, self.whole = place, own, whole
        (self.z_send, self.z_recv, self.x_send, self.x_recv, self.c_send, self.c_recv,
         self.y_send, self.y_recv, self.d_send, self.d_recv) = sems

    def piece(self, array, source, quarter=None, pair=False):
        c = self.place.c
        ref = self.whole[array]
        if array == QKV_W:
            return ref.at[source]
        if array == DOWN_W:
            rows = ref.shape[0] // 8
            part = rows // 4
            quarter = self.place.s if quarter is None else quarter
            return ref.at[pl.ds(pl.multiple_of(source * rows + quarter * part, part), part)]
        rows, columns = ref.shape[0] // 8, ref.shape[1] // 2
        count = 2 if pair else 1
        return ref.at[
            pl.ds(pl.multiple_of(source * rows, rows), count * rows),
            pl.ds(pl.multiple_of(c * columns, columns), columns),
        ]

    def own_piece(self, array):
        if array == QKV_W:
            return self.piece(array, self.place.f)
        ref = self.own[array]
        if array == DOWN_W:
            part = ref.shape[0] // 4
            return ref.at[pl.ds(pl.multiple_of(self.place.s * part, part), part)]
        columns = ref.shape[1] // 2
        return ref.at[:, pl.ds(pl.multiple_of(self.place.c * columns, columns), columns)]

    def z_piece(self, array, relation):
        source = self.place.source(relation, 0)
        if array == OUT_W:
            return self.piece(array, source - self.place.x, pair=True)
        return self.piece(array, source)

    def along_z(self, array, relation, way):
        here = self.z_piece(array, relation)
        src = self.own_piece(array) if relation == OWN and array != OUT_W else here
        step = abs(offset_of(relation))
        where = self.place.above if way == 0 else self.place.below
        return remote(src, here, self.z_send.at[array, way, step], self.z_recv.at[array, way, step], where)

    def z_ways(self, relation):
        place = self.place
        ways = []
        if offset_of(relation) <= 0:
            ways.append((0, place.has(relation) & (place.z < 3)))
        if offset_of(relation) >= 0:
            ways.append((1, place.has(relation) & (place.z > 0)))
        return ways

    def wait_z(self, array, relation):
        way = 0 if offset_of(relation) < 0 else 1
        step = abs(offset_of(relation)) - 1
        here = self.z_piece(array, relation)
        where = self.place.below if way == 0 else self.place.above
        remote(
            here, here, self.z_send.at[array, way, step], self.z_recv.at[array, way, step], where
        ).wait_recv()

    def over_x(self, array, relation):
        here = self.piece(array, self.place.source(relation, 0))
        src = self.own_piece(array) if relation == OWN else here
        return remote(
            src, here, self.x_send.at[array, relation], self.x_recv.at[array, relation], self.place.across_x
        )

    def from_x(self, array, relation):
        here = self.piece(array, self.place.source(relation, 1))
        return remote(
            here, here, self.x_send.at[array, relation], self.x_recv.at[array, relation], self.place.across_x
        )

    def to_core(self, array, relation, column):
        if array == OUT_W and relation != OWN:
            here = self.z_piece(array, relation)
        else:
            here = self.piece(array, self.place.source(relation, column))
        return remote(
            here, here, self.c_send.at[array, relation, column], self.c_recv.at[array, relation, column],
            self.place.core,
        )

    def over_y(self, relation, column):
        here = self.piece(DOWN_W, self.place.source(relation, column))
        return remote(
            here, here, self.y_send.at[relation, column], self.y_recv.at[relation, column], self.place.across_y
        )

    def far_quarter(self, relation, column):
        return self.piece(
            DOWN_W, self.place.source(relation, column), 2 * (1 - self.place.y) + self.place.c
        )

    def from_y(self, relation, column):
        here = self.far_quarter(relation, column)
        return remote(
            here, here, self.y_send.at[relation, column], self.y_recv.at[relation, column], self.place.across_y
        )

    def far_to_core(self, relation, column):
        here = self.far_quarter(relation, column)
        return remote(
            here, here, self.d_send.at[relation, column], self.d_recv.at[relation, column], self.place.core
        )

    def when(self, relation, action):
        if relation == OWN:
            action()
        else:
            pl.when(self.place.has(relation))(action)

    def arrive_z(self, array, relation, along=True, across=True):
        def action():
            if relation != OWN:
                self.wait_z(array, relation)
            for way, holds in self.z_ways(relation) if along else ():
                pl.when(holds)(lambda way=way: self.along_z(array, relation, way).start())
            if array != OUT_W and across:
                self.over_x(array, relation).start()
            if array != QKV_W and relation != OWN:
                self.to_core(array, relation, 0).start()
                if array == DOWN_W:
                    self.over_y(relation, 0).start()

        self.when(relation, action)

    def cross_out(self):
        self.over_x(OUT_W, OWN).start()

    def pair_out(self, own_copy):
        own_copy.wait()
        self.from_x(OUT_W, OWN).wait_recv()
        self.to_core(OUT_W, OWN, 1).start()
        for way, holds in self.z_ways(OWN):
            pl.when(holds)(lambda way=way: self.along_z(OUT_W, OWN, way).start())

    def arrive_x(self, array, relation):
        def action():
            self.from_x(array, relation).wait_recv()
            if array != QKV_W:
                self.to_core(array, relation, 1).start()
                if array == DOWN_W:
                    self.over_y(relation, 1).start()

        self.when(relation, action)

    def arrive_y(self, relation, column):
        def action():
            self.from_y(relation, column).wait_recv()
            self.far_to_core(relation, column).start()

        if (relation, column) != (OWN, 0):
            self.when(relation, action)

    def finish(self, array):
        for relation in range(RELATIONS):
            def action():
                if array != OUT_W or relation == OWN:
                    self.over_x(array, relation).wait_send()
                for way, holds in self.z_ways(relation):
                    pl.when(holds)(lambda way=way: self.along_z(array, relation, way).wait_send())
                if array == QKV_W:
                    return
                for column in range(2):
                    if (relation, column) == (OWN, 0) or (array == OUT_W and relation != OWN and column == 1):
                        continue
                    self.to_core(array, relation, column).wait()
                    if array == DOWN_W:
                        self.over_y(relation, column).wait_send()
                        self.far_to_core(relation, column).wait()

            self.when(relation, action)


def front_kernel(
    length_ref, tokens, read_rows, write_rows, qkv_in, vectors_in, up_in, down_in, out_in,
    small, up_bias, rows_out, weight_out, q_out, k_out, k_wide_out, v_wide_out, mixed_out, stats_out, up_full,
    down_full, out_full, attended,
    rows_ref, weight_ref, pieces, memory, q_x, k_t, k_wide, v_wide, v_x, mixed, mixed_low, row_stats,
    row_send, row_recv, far_send, far_recv, mix_send, mix_recv, local_sem, save_sem, head_sem, *gather_sems,
):
    place = Place()
    slot_rows, width = rows_ref.shape
    local_rows = tokens.shape[0]
    head_cols = k_t.shape[0]
    heads = head_cols // HEAD
    shard = width // 8
    length = length_ref[0]
    own_shards = {UP_W: up_in, DOWN_W: down_in, OUT_W: out_in}
    whole = {UP_W: up_full, DOWN_W: down_full, OUT_W: out_full, QKV_W: pieces}
    gather = Gather(place, own_shards, whole, gather_sems)

    memory[...] = jnp.zeros_like(memory)
    memory[:MEM, :] = read_rows[...]
    memory[16 : 16 + MEM, :] = write_rows[...]
    line = lax.broadcasted_iota(jnp.int32, (local_rows, 32), 1)
    at = place.s * local_rows + lax.broadcasted_iota(jnp.int32, (local_rows, 32), 0)
    wanted = jnp.where(line < 16, line, length - MEM + line - 16)
    used = (line < MEM) | ((line >= 16) & (line < 16 + MEM))
    pick = jnp.where(used & (wanted == at), 1.0, 0.0)
    taken = mul(pick.astype(low), memory[...]).astype(low)
    is_memory = jnp.sum(pick, axis=1, keepdims=True) > 0.5
    own_start = pl.multiple_of(place.s * local_rows, local_rows)
    rows_ref[pl.ds(own_start, local_rows), :] = jnp.where(is_memory, taken, tokens[...])
    for member in range(4):

        @pl.when(place.s == member)
        def _(member=member):
            for h in range(heads):
                for kind in range(3):
                    start = kind * width + (member * heads + h) * HEAD
                    to = (3 * h + kind) * HEAD
                    pieces[place.f, :, to : to + HEAD] = qkv_in[:, start : start + HEAD]

    columns = 3 * head_cols
    pieces[place.f, :, columns:] = jnp.zeros((shard, HEAD), low)
    for line in range(18):
        pieces[place.f, line : line + 1, columns:] = vectors_in[:, line * HEAD : (line + 1) * HEAD].astype(low)
    greet(place, False)

    halves = 2
    part = local_rows // halves

    def rows_of(member, half):
        return pl.ds(pl.multiple_of(member * local_rows + half * part, part), part)

    def send_rows(half, index):
        where = (place.core, place.across_y)[index]
        here = rows_ref.at[rows_of(place.s, half)]
        return remote(here, here, row_send.at[index, half], row_recv.at[index, half], where)

    def rows_from(half, index):
        member = (2 * place.y + 1 - place.c, 2 * (1 - place.y) + place.c)[index]
        here = rows_ref.at[rows_of(member, half)]
        where = (place.core, place.across_y)[index]
        return remote(here, here, row_send.at[index, half], row_recv.at[index, half], where)

    def pass_rows(half, arriving):
        flip = place.c if not arriving else 1 - place.c
        here = rows_ref.at[rows_of(2 * (1 - place.y) + flip, half)]
        return remote(here, here, far_send.at[half], far_recv.at[half], place.core)

    def own_copies():
        copies = []
        for index, array in enumerate((UP_W, DOWN_W, OUT_W)):
            rows = own_shards[array].shape[0]
            copies.append(pltpu.make_async_copy(
                own_shards[array], whole[array].at[pl.ds(pl.multiple_of(place.f * rows, rows), rows)],
                local_sem.at[index],
            ))
        return copies

    gather.arrive_z(QKV_W, OWN)
    for half in range(halves):
        send_rows(half, 1).start()
        send_rows(half, 0).start()
    gather.cross_out()
    for copy in own_copies():
        copy.start()
    for relation in (1, 4):
        gather.arrive_z(QKV_W, relation)
    gather.arrive_z(DOWN_W, OWN, along=False)
    gather.pair_out(own_copies()[2])
    for relation in (2, 5):
        gather.arrive_z(QKV_W, relation)
    gather.arrive_z(DOWN_W, OWN, across=False)
    gather.arrive_z(UP_W, OWN)
    rows_from(0, 1).wait_recv()
    pass_rows(0, False).start()
    for relation in (3, 6):
        gather.arrive_z(QKV_W, relation)
    for relation in (1, 4):
        gather.arrive_z(DOWN_W, relation)
    for relation in range(RELATIONS):
        gather.arrive_x(QKV_W, relation)
    for relation in (1, 4):
        gather.arrive_z(OUT_W, relation)
        gather.arrive_z(UP_W, relation)

    for source in range(8):
        weight_ref[source * shard : (source + 1) * shard, :] = pieces[source, :, :columns]
    tile = slice(columns - HEAD, columns + HEAD)
    bias_q = jnp.transpose(pieces[place.s, 0:16, tile].astype(full))[HEAD:]
    bias_v = jnp.transpose(pieces[4 + place.s, 0:16, tile].astype(full))[HEAD:]
    bias_q = jnp.concatenate([bias_q[:, h : h + 1] for h in range(heads)], axis=0)
    bias_v = jnp.concatenate([bias_v[:, h : h + 1] for h in range(heads)], axis=0)

    def project(member):
        start = pl.multiple_of(member * local_rows, local_rows)
        project_block(
            start, length, rows_ref, weight_ref, bias_q, bias_v, q_x, k_t, v_x, k_wide, v_wide, local_rows
        )

    project(place.s)
    for half in range(halves):
        rows_from(half, 0).wait_recv()
    project(2 * place.y + 1 - place.c)
    rows_from(1, 1).wait_recv()
    pass_rows(1, False).start()
    project(2 * (1 - place.y) + place.c)

    def scatter_vector(target, index, size, first):
        for source in range(8):
            done = 0
            while done < size:
                line, lane = divmod(first + done, HEAD)
                count = min(HEAD - lane, size - done)
                target[index : index + 1, source * size + done : source * size + done + count] = pieces[
                    source, line : line + 1, columns + lane : columns + lane + count
                ].astype(full)
                done += count

    for index, first in enumerate((2, 3, 4, 9, 10, 11)):
        scatter_vector(small, index, shard, first * shard)
    scatter_vector(up_bias, 0, 4 * shard, 5 * shard)
    for half in range(halves):
        pass_rows(half, True).wait_recv()
    project(2 * (1 - place.y) + 1 - place.c)

    def saves():
        pairs = [(rows_ref, rows_out), (weight_ref, weight_out), (k_t, k_out), (k_wide, k_wide_out), (v_wide, v_wide_out)]
        pairs += [(q_x.at[h, pl.ds(0, HEAD)], q_out.at[h]) for h in range(heads)]
        return [pltpu.make_async_copy(src, dst, save_sem.at[index]) for index, (src, dst) in enumerate(pairs)]

    for save in saves():
        save.start()

    def head_saves(h):
        own = pl.ds(h * HEAD, HEAD)
        return [
            pltpu.make_async_copy(mixed.at[own], mixed_out.at[own], head_sem.at[h, 0]),
            pltpu.make_async_copy(row_stats.at[h], stats_out.at[h], head_sem.at[h, 1]),
        ]

    def chores(step):
        if step == 0:
            gather.arrive_x(DOWN_W, OWN)
            for relation in (2, 5):
                gather.arrive_z(DOWN_W, relation)
        elif step == 1:
            gather.arrive_x(UP_W, OWN)
            for relation in (2, 5):
                gather.arrive_z(OUT_W, relation)
        elif step == 2:
            for relation in (1, 4):
                gather.arrive_x(DOWN_W, relation)
                gather.arrive_y(relation, 0)
        elif step == 4:
            for relation in (2, 5):
                gather.arrive_z(UP_W, relation)
            gather.arrive_y(OWN, 1)
            for save in head_saves(0):
                save.start()
        elif step == 5:
            for relation in (1, 4):
                gather.arrive_x(UP_W, relation)
            for relation in (3, 6):
                gather.arrive_z(DOWN_W, relation)
        elif step == 6:
            for relation in (2, 5):
                gather.arrive_x(DOWN_W, relation)
                gather.arrive_y(relation, 0)
        elif step == 7:
            for relation in (3, 6):
                gather.arrive_z(OUT_W, relation)
        elif step == 8:
            for relation in (1, 4):
                gather.arrive_y(relation, 1)
            for save in head_saves(1):
                save.start()
        elif step == 9:
            for relation in (3, 6):
                gather.arrive_z(UP_W, relation)
            for relation in (2, 5):
                gather.arrive_x(UP_W, relation)
        elif step == 10:
            for relation in (3, 6):
                gather.arrive_x(DOWN_W, relation)
                gather.arrive_y(relation, 0)
        elif step == 11:
            for relation in (2, 5):
                gather.arrive_y(relation, 1)

    def send_mixed(h, turn, arriving=False):
        member = place.member(turn)
        own = pl.ds(pl.multiple_of(h * HEAD, HEAD), HEAD)
        lanes = pl.ds(pl.multiple_of(member * local_rows, local_rows), local_rows)
        owner = member if arriving else place.s
        there = attended.at[pl.ds(pl.multiple_of(owner * head_cols + h * HEAD, HEAD), HEAD)]
        return remote(
            mixed_low.at[own, lanes], there, mix_send.at[h, turn], mix_recv.at[h, turn], (place.f, member)
        )

    def keep_mixed(h):
        own = pl.ds(pl.multiple_of(h * HEAD, HEAD), HEAD)
        lanes = pl.ds(pl.multiple_of(place.s * local_rows, local_rows), local_rows)
        there = attended.at[pl.ds(pl.multiple_of(place.s * head_cols + h * HEAD, HEAD), HEAD)]
        return pltpu.make_async_copy(mixed_low.at[own, lanes], there, mix_send.at[h, 3])

    turns = slot_rows // local_rows

    def pass_on(index):
        h, turn = index // turns, lax.rem(index, turns)

        @pl.when(turn < turns - 1)
        def _():
            send_mixed(h, turn).start()

        @pl.when(turn == turns - 1)
        def _():
            keep_mixed(h).start()

    def step(index, carry):
        for when in range(12):
            pl.when(index == when)(lambda when=when: chores(when))
        h, turn = index // turns, lax.rem(index, turns)
        start = pl.multiple_of(place.member(turn) * local_rows, local_rows)
        attend_block(h, pl.ds(start, local_rows), q_x, k_wide, v_x, mixed, mixed_low, row_stats)

        @pl.when(index > 0)
        def _():
            pass_on(index - 1)

        return carry

    lax.fori_loop(0, heads * turns, step, 0)
    pass_on(heads * turns - 1)
    for save in head_saves(2):
        save.start()
    for relation in (3, 6):
        gather.arrive_y(relation, 1)
    for relation in (3, 6):
        gather.arrive_x(UP_W, relation)
    for array in (UP_W, OUT_W, DOWN_W, QKV_W):
        gather.finish(array)
    for copy in own_copies()[:2]:
        copy.wait()
    for half in range(halves):
        for index in range(2):
            send_rows(half, index).wait_send()
        pass_rows(half, False).wait_send()
    for h in range(heads):
        for turn in range(turns - 1):
            send_mixed(h, turn).wait_send()
            send_mixed(h, turn, True).wait_recv()
        keep_mixed(h).wait()
        for save in head_saves(h):
            save.wait()
    for save in saves():
        save.wait()


def front(lengths, tokens, read_rows, write_rows, qkv_shard, vectors, up_weight, down_weight, out_weight):
    local_rows, width = tokens.shape
    slot_rows = local_rows * 4
    head_cols = width // 4
    heads = head_cols // HEAD
    shard = width // 8
    vmem = pl.BlockSpec(memory_space=pltpu.VMEM)
    anywhere = pl.BlockSpec(memory_space=pl.ANY)
    dma = pltpu.SemaphoreType.DMA
    hidden = up_weight.shape[1]

    def held(*shape, kind=low):
        return pltpu.VMEM(shape, kind)

    def shaped(*shape, kind=low):
        return jax.ShapeDtypeStruct(shape, kind)

    return pl.pallas_call(
        front_kernel,
        in_specs=[pl.BlockSpec(memory_space=pltpu.SMEM)] + [vmem] * 8,
        out_specs=[vmem] * 2 + [anywhere] * 12,
        out_shape=[
            shaped(8, width, kind=full), shaped(8, hidden, kind=full),
            shaped(slot_rows, width), shaped(width, 3 * head_cols), shaped(heads, HEAD, slot_rows),
            shaped(head_cols, slot_rows), shaped(heads, slot_rows, WIDE), shaped(heads, slot_rows, WIDE),
            shaped(head_cols, slot_rows, kind=full), shaped(heads, 8, slot_rows, kind=full),
            shaped(width, hidden), shaped(hidden, width), shaped(width, width), shaped(width, local_rows),
        ],
        scratch_shapes=[
            held(slot_rows, width), held(width, 3 * head_cols), held(8, shard, 3 * head_cols + HEAD),
            held(32, width), held(heads, WIDE, slot_rows), held(head_cols, slot_rows),
            held(heads, slot_rows, WIDE), held(heads, slot_rows, WIDE), held(heads, WIDE, slot_rows),
            held(head_cols, slot_rows, kind=full), held(head_cols, slot_rows), held(heads, 8, slot_rows, kind=full),
            dma((2, 2)), dma((2, 2)), dma((2,)), dma((2,)), dma((heads, 4)), dma((heads, 4)), dma((3,)),
            dma((5 + heads,)), dma((heads, 2)),
            dma((4, 2, 3)), dma((4, 2, 3)), dma((4, 7)), dma((4, 7)), dma((3, 7, 2)), dma((3, 7, 2)),
            dma((7, 2)), dma((7, 2)), dma((7, 2)), dma((7, 2)),
        ],
        compiler_params=pltpu.CompilerParams(
            vmem_limit_bytes=VMEM_BYTES, collective_id=0, has_side_effects=True
        ),
        name="front",
    )(lengths, tokens, read_rows, write_rows, qkv_shard, vectors, up_weight, down_weight, out_weight)


DW_FIRST = 3
LINES = (3, 0, 2, 1)


def add_low(left, right):
    return (left.astype(full) + right.astype(full)).astype(low)


class Reduce:
    def __init__(self, place, given, sums, across, from_y, from_x, from_z, last, sems):
        self.across, self.last, self.far_up = across, last, last + 1
        self.place, self.given, self.sums = place, given, sums
        self.from_y, self.from_x, self.from_z = from_y, from_x, from_z
        self.y_send, self.y_recv, self.x_send, self.x_recv, self.z_send, self.z_recv = sems

    def dest(self, column, line):
        x = self.place.x
        return 2 * line + (x if column == 0 else 1 - x)

    def slot(self, array, line, column=0):
        if DW_FIRST <= array <= self.last:
            rows = 4 * HEAD if array == self.last else 3 * HEAD
            return self.sums[array].at[self.dest(column, line), pl.ds(0, rows // 4)]
        return self.sums[array].at[line]

    def cut(self, array, ref):
        if DW_FIRST <= array < self.last:
            return ref.at[pl.ds(0, 3 * HEAD // 4)]
        return ref

    def load(self, array, column, line, sem):
        if array == OUT_W:
            return pltpu.make_async_copy(self.given[array].at[line, 0], self.sums[array].at[line], sem)
        source = self.given[UP_W if array == self.far_up else array].at[column, line, 1 if array == self.far_up else 0]
        target = self.across if column == 1 else self.sums[array]
        return pltpu.make_async_copy(source, target.at[line], sem)

    def over_y(self, array, line):
        column, index = (1, 1) if array == UP_W else (0, 0)
        return remote(
            self.given[array].at[column, line, 1], self.from_y.at[index, line], self.y_send.at[index, line],
            self.y_recv.at[index, line], self.place.across_y,
        )

    def add_y(self, array, line):
        self.over_y(array, line).wait_recv()
        slot = self.across.at[line] if array == UP_W else self.slot(DOWN_W, line)
        slot[...] = add_low(slot[...], self.from_y[1 if array == UP_W else 0, line])

    def over_x(self, array, line):
        if array == OUT_W:
            start = self.given[array].at[line, 1]
        elif array == UP_W:
            start = self.across.at[line]
        elif array == DOWN_W:
            start = self.given[array].at[1, line, 0]
        else:
            start = self.slot(array, line, 1)
        return remote(
            start, self.cut(array, self.from_x[array].at[line]), self.x_send.at[array, line],
            self.x_recv.at[array, line], self.place.across_x,
        )

    def add_x(self, array, line):
        self.over_x(array, line).wait_recv()
        slot = self.slot(array, line)
        slot[...] = add_low(slot[...], self.cut(array, self.from_x[array].at[line])[...])

    def along_z(self, array, way, line):
        return remote(
            self.slot(array, line), self.cut(array, self.from_z[array].at[way, line]),
            self.z_send.at[array, way, line], self.z_recv.at[array, way, line],
            self.place.above if way == 0 else self.place.below,
        )

    def add_z(self, array, way, line):
        self.along_z(array, way, line).wait_recv()
        slot = self.slot(array, line)
        slot[...] = add_low(slot[...], self.cut(array, self.from_z[array].at[way, line])[...])

    def hop(self, array, level, lines=(0, 1, 2, 3)):
        @pl.when(self.place.z == level)
        def _():
            for line in range(3, level, -1):
                if line in lines:
                    if level > 0:
                        self.add_z(array, 0, line)
                    self.along_z(array, 0, line).start()

        @pl.when(self.place.z == 3 - level)
        def _():
            for line in range(0, 3 - level):
                if line in lines:
                    if level > 0:
                        self.add_z(array, 1, line)
                    self.along_z(array, 1, line).start()

    def direct(self, array):
        return array != self.far_up

    def to_line(self, array, line):
        where = (2 * line + self.place.x, self.place.s)
        return remote(
            self.slot(array, line), self.cut(array, self.from_z[array].at[self.place.z]),
            self.z_send.at[array, 0, line], self.z_recv.at[array, 0, self.place.z], where,
        )

    def fling(self, array, lines=LINES):
        for line in lines:
            pl.when(self.place.z != line)(lambda line=line: self.to_line(array, line).start())

    def settle(self, array):
        if self.direct(array):
            slot = self.slot(array, self.place.z)
            for line in range(4):

                @pl.when(self.place.z != line)
                def _(line=line):
                    came = self.cut(array, self.from_z[array].at[line])
                    remote(
                        came, came, self.z_send.at[array, 0, line], self.z_recv.at[array, 0, line], self.place.core
                    ).wait_recv()
                    slot[...] = add_low(slot[...], came[...])

            return
        for line in range(4):

            @pl.when(self.place.z == line)
            def _(line=line):
                if line > 0:
                    self.add_z(array, 0, line)
                if line < 3:
                    self.add_z(array, 1, line)

    def finish(self, array):
        for line in range(4):
            if array != self.far_up:
                self.over_x(array, line).wait_send()
            if self.direct(array):
                pl.when(self.place.z != line)(lambda line=line: self.to_line(array, line).wait_send())
            else:
                pl.when(self.place.z < line)(lambda line=line: self.along_z(array, 0, line).wait_send())
                pl.when(self.place.z > line)(lambda line=line: self.along_z(array, 1, line).wait_send())
            if array in (UP_W, DOWN_W):
                self.over_y(array, line).wait_send()


class Spread:
    def __init__(self, place, blocks, source, send, recv):
        self.place, self.blocks, self.source, self.send, self.recv = place, blocks, source, send, recv
        self.near = 2 * place.y + 1 - place.c
        self.far = 2 * (1 - place.y) + place.c
        self.last = 2 * (1 - place.y) + 1 - place.c

    def copy(self, kind, arriving=False):
        place = self.place
        if kind == 2:
            here = self.blocks.at[self.last if arriving else self.far]
            return remote(here, here, self.send.at[2], self.recv.at[2], place.core)
        member = (self.near, self.far)[kind] if arriving else place.s
        return remote(
            self.source, self.blocks.at[member], self.send.at[kind], self.recv.at[kind],
            (place.core, place.across_y)[kind],
        )

    def start(self):
        self.copy(1).start()
        self.copy(0).start()

    def pass_on(self):
        self.copy(1, True).wait_recv()
        self.copy(2).start()

    def finish(self):
        self.blocks[self.place.s] = self.source[...]
        self.copy(0, True).wait_recv()
        self.copy(2, True).wait_recv()
        for kind in range(3):
            self.copy(kind).wait_send()


def back_kernel(
    length_ref, grad_own, vectors_in, q_in, k_in, k_wide_in, v_wide_in, mixed_in, stats_in, rows_in, weight_in, resid_in, up_given, down_given, out_given,
    input_out, read_out, write_out, qkv_out, vector_out, up_out, down_out, out_out,
    q_x, k_t, k_wide, v_wide, mixed, row_stats, grad_t, q_here, do_x, grads, grad_k, grad_v, rows_ref, weight_ref, resid_ref,
    up_sum, out_sum, down_sum, far_sum_up, across_up, dw, both_y, up_x, out_x, down_x, dw_x, up_z, out_z, down_z, dw_z, far_z,
    up_last, out_last, up_all, out_other, down_all, dw_all,
    near_send, near_recv, far_sum, far_recv, memory_all, memory_own,
    mix_send, mix_recv, local_sem, saved_sem, mine_sem, share_send, share_recv, near_s, near_r, far_s, far_r, cross_s, cross_r,
    *sems,
):
    place = Place()
    heads, _, slot_rows = q_in.shape
    width, local_rows = grad_own.shape
    head_cols = heads * HEAD
    last = DW_FIRST + heads - 1
    far_up = last + 1
    given = {UP_W: up_given, OUT_W: out_given, DOWN_W: down_given}
    sums = {UP_W: up_sum, OUT_W: out_sum, DOWN_W: down_sum}
    from_x = {UP_W: up_x, OUT_W: out_x, DOWN_W: down_x}
    from_z = {UP_W: up_z, OUT_W: out_z, DOWN_W: down_z}
    for h in range(heads):
        sums[DW_FIRST + h], from_x[DW_FIRST + h] = dw.at[h], dw_x.at[h]
        from_z[DW_FIRST + h] = dw_z.at[h]
    sums[far_up], from_z[far_up] = far_sum_up, far_z
    reduce = Reduce(place, given, sums, across_up, both_y, from_x, from_z, last, sems)

    peers = (place.across_y, place.diagonal, place.core)

    def member_rows(turn):
        member = place.member(turn)
        return member, pl.ds(pl.multiple_of(member * local_rows, local_rows), local_rows)

    def send_grad(turn, arriving=False):
        member, lanes = member_rows(turn)
        own_lanes = pl.ds(pl.multiple_of(place.s * local_rows, local_rows), local_rows)
        src = grad_own.at[pl.ds(pl.multiple_of(member * head_cols, head_cols), head_cols)]
        return remote(
            src, grad_t.at[:, lanes if arriving else own_lanes], mix_send.at[turn], mix_recv.at[turn], peers[turn]
        )

    def saved_loads(h):
        own = pl.ds(h * HEAD, HEAD)
        pairs = (
            (k_wide_in.at[h], k_wide.at[h]), (q_in.at[h], q_x.at[h]), (v_wide_in.at[h], v_wide.at[h]),
            (mixed_in.at[own], mixed.at[own]), (stats_in.at[h], row_stats.at[h]), (k_in.at[own], k_t.at[own]),
        )
        return [pltpu.make_async_copy(src, dst, saved_sem.at[h, i]) for i, (src, dst) in enumerate(pairs)]

    def sum_loads(array):
        index = array if array < DW_FIRST else DW_FIRST
        return [reduce.load(array, 0, line, mine_sem.at[index, line]) for line in LINES]

    def across_loads():
        return [reduce.load(UP_W, 1, line, mine_sem.at[DW_FIRST + 1, line]) for line in LINES]

    for load in sum_loads(far_up):
        load.start()
    for load in saved_loads(0):
        load.start()
    greet(place, True)
    for turn in (1, 0, 2):
        send_grad(turn).start()
    loads = []
    for index, (src, dst) in enumerate(((rows_in, rows_ref), (weight_in, weight_ref), (resid_in, resid_ref))):
        loads.append(pltpu.make_async_copy(src, dst, local_sem.at[index]))

    def send_x(array, lines=LINES):
        for line in lines:
            reduce.over_x(array, line).start()

    send_x(DOWN_W)
    send_x(OUT_W)
    for array in (DOWN_W, UP_W):
        for line in LINES:
            reduce.over_y(array, line).start()
    for load in across_loads() + sum_loads(UP_W) + sum_loads(OUT_W) + sum_loads(DOWN_W):
        load.start()
    for load in loads:
        load.start()

    for h in range(1, heads):
        for load in saved_loads(h):
            load.start()

    own_lanes = pl.ds(pl.multiple_of(place.s * local_rows, local_rows), local_rows)
    grad_t[:, own_lanes] = grad_own[pl.ds(pl.multiple_of(place.s * head_cols, head_cols), head_cols), :]

    def take_x(array, lines=LINES):
        for line in lines:
            reduce.add_x(array, line)

    turns = slot_rows // local_rows

    def weight_part(h):
        if h == 0:
            loads[0].wait()
        base = 3 * h * HEAD
        part = jnp.transpose(mul(grads[base : base + 3 * HEAD, :], rows_ref[...])).astype(low)
        half = width // 16
        for dest in range(8):
            start = 2 * half * dest
            dw[h, dest, :half, :] = jnp.concatenate(
                [part[start : start + half], part[start + half : start + 2 * half]], axis=1
            )
            if h == heads - 1:
                dw[h, dest, half:, :] = vectors_in[dest].astype(low)
        if h == heads - 1:
            total = jnp.sum(grads[...].astype(full), axis=1, keepdims=True)
            spread = jnp.transpose(jnp.broadcast_to(total, (total.shape[0], WIDE)))[0:1]
            for kind, first_dest in ((0, 0), (2, 4)):
                for head in range(heads):
                    start = (3 * head + kind) * HEAD
                    dw[h, first_dest + place.s, half : half + 1, head * HEAD : (head + 1) * HEAD] = spread[
                        :, start : start + HEAD
                    ].astype(low)
        send_x(DW_FIRST + h)

    share = {OUT_W: (out_last, out_other)}

    def settled(array):
        return sums[array].at[place.z]

    def sum_y(array):
        mine_now = settled(array)
        return remote(mine_now, share[array][0], share_send.at[array, 0], share_recv.at[array, 0], place.across_y)

    def half_to_core(array):
        mine_now = settled(array)
        return remote(mine_now, share[array][1], share_send.at[array, 1], share_recv.at[array, 1], place.core)

    def spread_of(array):
        if array in (UP_W, DOWN_W):
            return Spread(
                place, {UP_W: up_all, DOWN_W: down_all}[array], sums[array].at[place.z], share_send.at[array],
                share_recv.at[array],
            )
        h = array - DW_FIRST
        return Spread(
            place, dw_all.at[h, :, pl.ds(0, reduce.slot(array, 0).shape[0])], reduce.slot(array, place.z),
            share_send.at[array], share_recv.at[array],
        )

    def cross_up():
        return remote(far_sum_up.at[place.z], up_last, cross_s.at[0], cross_r.at[0], place.across_y)

    def settle_up():
        reduce.settle(UP_W)
        cross_up().wait_recv()
        slot = sums[UP_W].at[place.z]
        slot[...] = add_low(slot[...], up_last[...])
        spread_of(UP_W).start()

    def add_last(array):
        sum_y(array).wait()
        slot = settled(array)
        slot[...] = add_low(slot[...], share[array][0][...])
        half_to_core(array).start()

    first, second = DW_FIRST, DW_FIRST + 1

    def pass_up(lines):
        for line in lines:
            reduce.add_y(UP_W, line)
            reduce.over_x(UP_W, line).start()

    def chores(index):
        if index == 1:
            send_grad(2, True).wait_recv()
            for load in across_loads() + sum_loads(UP_W) + sum_loads(OUT_W) + sum_loads(DOWN_W):
                load.wait()
        elif index == 2:
            send_grad(1, True).wait_recv()
            reduce.hop(far_up, 1, (3, 0))
        elif index == 3:
            send_grad(0, True).wait_recv()
            reduce.hop(far_up, 1, (2, 1))
        elif index == 4:
            for load in saved_loads(1):
                load.wait()
            weight_part(0)
            reduce.hop(far_up, 2)
        elif index == 5:
            take_x(DOWN_W)
        elif index == 6:
            for line in LINES:
                reduce.add_y(DOWN_W, line)
                reduce.fling(DOWN_W, (line,))
            take_x(OUT_W)
            reduce.fling(OUT_W)
            reduce.settle(far_up)
            cross_up().start()
        elif index == 7:
            take_x(first)
            reduce.fling(first)
        elif index == 8:
            for load in saved_loads(2):
                load.wait()
            weight_part(1)
            pass_up((3, 0))
        elif index == 9:
            pass_up((2,))
        elif index == 10:
            pass_up((1,))
        elif index == 11:
            take_x(second)
            reduce.fling(second)
            reduce.settle(DOWN_W)
            spread_of(DOWN_W).start()

    def step(index, carry):
        for when in range(1, 12):
            pl.when(index == when)(lambda when=when: chores(when))
        h, turn = index // turns, lax.rem(index, turns)
        _, lanes = member_rows(turns - 1 - turn)
        attend_back(
            h, lanes, q_x, q_here, do_x, grad_t, mixed, row_stats, k_t, k_wide, v_wide, grads, grad_k, grad_v, turn == 0
        )

        @pl.when(turn == turns - 1)
        def _():
            base = pl.multiple_of(3 * h * HEAD, HEAD)
            grads[pl.ds(base + HEAD, HEAD), :] = grad_k[...].astype(low)
            grads[pl.ds(base + 2 * HEAD, HEAD), :] = grad_v[...].astype(low)

        return carry

    for load in sum_loads(far_up):
        load.wait()
    reduce.hop(far_up, 0)
    for load in saved_loads(0):
        load.wait()
    lax.fori_loop(0, heads * turns, step, 0)

    loads[1].wait()
    loads[2].wait()

    halves, part = 2, local_rows // 2
    length = length_ref[0]

    def memory_pick(rows, start):
        line = lax.broadcasted_iota(jnp.int32, (32, rows), 0)
        row = start + lax.broadcasted_iota(jnp.int32, (32, rows), 1)
        wanted = jnp.where(line < 16, line, length - MEM + line - 16)
        used = (line < MEM) | ((line >= 16) & (line < 16 + MEM))
        return jnp.where(used & (wanted == row), 1.0, 0.0).astype(low)

    def part_for(turn, half):
        start = pl.multiple_of(place.member(turn) * local_rows + half * part, part)
        return mul(grads[:, pl.ds(start, part)], weight_ref[...], TT)

    def share_near(index, half):
        rows = pl.ds(half * part, part)
        return remote(
            near_send.at[index, rows], near_recv.at[index, rows], near_s.at[index, half], near_r.at[index, half],
            place.core,
        )

    def share_far(quarter):
        rows = pl.ds(quarter * (part // 2), part // 2)
        return remote(far_sum.at[rows], far_recv.at[rows], far_s.at[quarter], far_r.at[quarter], place.across_y)

    for half in range(halves):
        near_send[0, half * part : (half + 1) * part, :] = part_for(1, half).astype(low)
        share_near(0, half).start()
    for half in range(halves):
        rows = slice(half * part, (half + 1) * part)
        far_part = part_for(0, half)
        share_near(0, half).wait_recv()
        far_sum[rows, :] = (far_part + near_recv[0, rows, :].astype(full)).astype(low)
        if half == 0:
            share_far(0).start()
            share_far(1).start()
    take_x(UP_W)
    reduce.fling(UP_W)
    weight_part(heads - 1)
    reduce.settle(OUT_W)
    sum_y(OUT_W).start()
    taken = mul(memory_pick(slot_rows, 0), grads[...], NT).astype(low)
    own_part = mul(memory_pick(local_rows, place.s * local_rows), resid_ref[...].astype(low))
    memory_own[...] = (mul(taken, weight_ref[...], NT) + own_part).astype(low)
    memory = Spread(place, memory_all, memory_own, share_send.at[DW_FIRST + heads], share_recv.at[DW_FIRST + heads])
    memory.start()
    for half in range(halves):
        rows = slice(half * part, (half + 1) * part)
        near_send[1, rows, :] = part_for(2, half).astype(low)
        share_near(1, half).start()
    for half in range(halves):
        resid_ref[half * part : (half + 1) * part, :] += part_for(3, half)
    take_x(last)
    reduce.fling(last)
    reduce.settle(first)
    spread_of(first).start()
    reduce.settle(second)
    spread_of(second).start()
    share_far(2).start()
    settle_up()
    reduce.settle(last)
    spread_of(last).start()
    share_far(3).start()
    add_last(OUT_W)
    memory.pass_on()
    for h in (heads - 1, 0, 1):
        spread_of(DW_FIRST + h).pass_on()
    for array in (UP_W, DOWN_W):
        spread_of(array).pass_on()
    for array, out in ((OUT_W, out_out),):
        columns = out.shape[1] // 2
        out[:, pl.ds(pl.multiple_of(place.c * columns, columns), columns)] = settled(array)[...]
        half_to_core(array).wait()
        out[:, pl.ds(pl.multiple_of((1 - place.c) * columns, columns), columns)] = share[array][1][...]
    for h in range(heads):
        spread_of(DW_FIRST + h).finish()
    spread_of(UP_W).finish()
    spread_of(DOWN_W).finish()
    quarter = down_out.shape[0] // 4
    part_columns = up_out.shape[1] // 4
    for member in range(4):
        start = (2 * (member % 2) + member // 2) * part_columns
        up_out[:, start : start + part_columns] = up_all[member]
        down_out[member * quarter : (member + 1) * quarter, :] = down_all[member]
    half = qkv_out.shape[0] // 2
    for kind in range(3):
        for member in range(4):
            for h in range(heads):
                start = kind * width + (member * heads + h) * HEAD
                for side in range(2):
                    lanes = (3 * side + kind) * HEAD
                    qkv_out[side * half : (side + 1) * half, start : start + HEAD] = dw_all[
                        h, member, :half, lanes : lanes + HEAD
                    ]
    vector_sum = dw_all[heads - 1, 0, half:, :].astype(full)
    for member in range(1, 4):
        vector_sum = vector_sum + dw_all[heads - 1, member, half:, :].astype(full)
    vector_out[...] = vector_sum
    memory.finish()
    total = memory_all[0].astype(full)
    for member in range(1, 4):
        total = total + memory_all[member].astype(full)
    read_out[...] = total[:MEM]
    write_out[...] = total[16 : 16 + MEM]
    for half in range(halves):
        rows = slice(half * part, (half + 1) * part)
        share_near(1, half).wait_recv()
        for quarter in (2 * half, 2 * half + 1):
            share_far(quarter).wait_recv()
        grad_layer = resid_ref[rows, :] + near_recv[1, rows, :].astype(full) + far_recv[rows, :].astype(full)
        rows_at = place.s * local_rows + half * part + lax.broadcasted_iota(jnp.int32, (part, 1), 0)
        in_write = (rows_at >= length - MEM) & (rows_at < length)
        input_out[rows, :] = jnp.where((rows_at < MEM) | in_write, 0.0, grad_layer)
    for array in range(DW_FIRST + heads + 1):
        reduce.finish(array)
    cross_up().wait_send()
    for turn in range(3):
        send_grad(turn).wait_send()
    for half in range(halves):
        for index in range(2):
            share_near(index, half).wait_send()
        for quarter in (2 * half, 2 * half + 1):
            share_far(quarter).wait_send()


def back(lengths, grad_own, saved, vectors, rows, weight, resid, up_given, down_given, out_given):
    q_x, k_t, k_wide, v_wide, mixed, row_stats = saved
    heads, _, slot_rows = q_x.shape
    width, local_rows = grad_own.shape
    hidden = 32 * up_given.shape[3]
    shard, head_cols = width // 8, heads * HEAD
    half, small, piece = hidden // 2, width // 2, hidden // 32
    vmem = pl.BlockSpec(memory_space=pltpu.VMEM)
    anywhere = pl.BlockSpec(memory_space=pl.ANY)
    dma = pltpu.SemaphoreType.DMA
    arrays = DW_FIRST + heads

    def held(*shape, kind=low):
        return pltpu.VMEM(shape, kind)

    tall = (shard // 2 + 16, 6 * HEAD)
    return pl.pallas_call(
        back_kernel,
        in_specs=[pl.BlockSpec(memory_space=pltpu.SMEM)] + [vmem] * 2 + [anywhere] * 12,
        out_specs=[vmem] * 8,
        out_shape=[
            jax.ShapeDtypeStruct((local_rows, width), full),
            jax.ShapeDtypeStruct((MEM, width), full),
            jax.ShapeDtypeStruct((MEM, width), full),
            jax.ShapeDtypeStruct((shard, 3 * width), low),
            jax.ShapeDtypeStruct((16, 6 * HEAD), full),
            jax.ShapeDtypeStruct((shard, hidden), low),
            jax.ShapeDtypeStruct((hidden // 8, width), low),
            jax.ShapeDtypeStruct((shard, width), low),
        ],
        scratch_shapes=[
            held(heads, HEAD, slot_rows), held(head_cols, slot_rows), held(heads, slot_rows, WIDE),
            held(heads, slot_rows, WIDE), held(head_cols, slot_rows, kind=full), held(heads, 8, slot_rows, kind=full),
            held(head_cols, slot_rows), held(WIDE, local_rows), held(WIDE, local_rows), held(3 * head_cols, slot_rows),
            held(HEAD, slot_rows, kind=full), held(HEAD, slot_rows, kind=full),
            held(slot_rows, width), held(width, 3 * head_cols), held(local_rows, width, kind=full),
            held(4, piece, width), held(4, shard, small), held(4, piece, width), held(4, piece, width),
            held(4, piece, width), held(heads, 8, *tall), held(2, 4, piece, width),
            held(4, piece, width), held(4, shard, small), held(4, piece, width), held(heads, 4, *tall),
            held(4, piece, width), held(4, shard, small), held(4, piece, width), held(heads, 4, *tall),
            held(2, 4, piece, width),
            held(piece, width), held(shard, small), held(4, piece, width), held(shard, small),
            held(4, piece, width), held(heads, 4, *tall),
            held(2, local_rows, width), held(2, local_rows, width), held(local_rows, width),
            held(local_rows, width), held(4, 32, width), held(32, width),
            dma((3,)), dma((3,)), dma((3,)), dma((heads, 6)), dma((5, 4)), dma((arrays + 1, 3)),
            dma((arrays + 1, 3)), dma((2, 2)), dma((2, 2)), dma((4,)), dma((4,)),
            dma((1,)), dma((1,)),
            dma((2, 4)), dma((2, 4)), dma((arrays, 4)), dma((arrays, 4)),
            dma((arrays + 1, 2, 4)), dma((arrays + 1, 2, 4)),
        ],
        compiler_params=pltpu.CompilerParams(
            vmem_limit_bytes=VMEM_BYTES, collective_id=1, has_side_effects=True
        ),
        name="back",
    )(
        lengths, grad_own, vectors, q_x, k_t, k_wide, v_wide, mixed, row_stats, rows, weight, resid,
        up_given, down_given, out_given,
    )


def phi_parts(value):
    normal = 0.5 * (1.0 + lax.erf(value * (0.5**0.5)))
    density = jnp.exp(-0.5 * value * value) * (0.5 * 2.0**0.5 * 3.141592653589793**-0.5)
    return normal, normal + value * density


def statistics(values):
    centre = values - jnp.mean(values, axis=1, keepdims=True)
    factor = lax.rsqrt(jnp.mean(centre * centre, axis=1, keepdims=True) + norm_epsilon)
    return centre * factor, factor


def norm_back(grad, gain, normed, factor):
    scaled = grad * gain
    first = jnp.mean(scaled, axis=1, keepdims=True)
    second = jnp.mean(scaled * normed, axis=1, keepdims=True)
    return factor * (scaled - first - normed * second)


def column_total(values):
    return jnp.sum(values, axis=0, keepdims=True)


def middle_kernel(
    length_ref, cotangent, small, up_bias, rows_in, attended_in, up_in, down_in, out_in,
    output, resid_out, grad_own, vector_out, up_out, down_out, out_out,
    layer_in, attended, up_w, down_w, out_w, hidden, slope, normed_one, middle_low, grad_down,
    grad_two, grad_mid, totals, up_total, up_grad, down_grad, out_grad, up_sum, down_sum, out_sum,
    from_y, load_sem, save_sem, c_send, c_recv, y_send, y_recv,
):
    place = Place()
    rows, width = cotangent.shape
    ff = up_w.shape[1]
    chunk = ff // 4
    shard = width // 8
    barrier = pltpu.get_barrier_semaphore()
    for where in (place.core, place.across_y):
        pl.semaphore_signal(barrier, inc=1, device_id=where, device_id_type=MESH)

    def chunk_lanes(j):
        return pl.ds(pl.multiple_of(j * chunk, chunk), chunk)

    def up_load(j):
        return pltpu.make_async_copy(up_in.at[:, chunk_lanes(j)], up_w.at[:, chunk_lanes(j)], load_sem.at[j])

    def down_load(j):
        return pltpu.make_async_copy(down_in.at[chunk_lanes(j)], down_w.at[chunk_lanes(j)], load_sem.at[4 + j])

    first_loads = [
        pltpu.make_async_copy(
            rows_in.at[pl.ds(pl.multiple_of(place.s * rows, rows), rows)], layer_in, load_sem.at[8]
        ),
        pltpu.make_async_copy(attended_in, attended, load_sem.at[9]),
        pltpu.make_async_copy(out_in, out_w, load_sem.at[10]),
    ]
    for load in first_loads:
        load.start()
    for j in range(4):
        up_load(j).start()
        down_load(j).start()
    out_bias, gain_one, shift_one = small[0:1, :], small[1:2, :], small[2:3, :]
    down_bias, gain_two, shift_two = small[3:4, :], small[4:5, :], small[5:6, :]
    for load in first_loads:
        load.wait()

    branch = mul(attended[...], out_w[...], TN)
    normed, factor_one = statistics(layer_in[...].astype(full) + branch + out_bias)
    normed_one[...] = normed
    middle_low[...] = (normed * gain_one + shift_one).astype(low)
    grad_mid[...] = jnp.zeros_like(grad_mid)

    def forward_chunk(j, carry):
        up_load(j).wait()
        lanes = chunk_lanes(j)
        value = mul(middle_low[...], up_w[:, lanes]) + up_bias[0:1, lanes]
        normal, slope_here = phi_parts(value)
        hidden[:, lanes] = (value * normal).astype(low)
        slope[:, lanes] = slope_here
        down_load(j).wait()
        grad_mid[...] += mul(hidden[:, lanes], down_w[lanes, :])
        return carry

    lax.fori_loop(0, 4, forward_chunk, 0)
    middle = normed_one[...] * gain_one + shift_one
    normed_two, factor_two = statistics(middle + grad_mid[...] + down_bias)
    places = place.s * rows + lax.broadcasted_iota(jnp.int32, (rows, 1), 0)
    in_slot = places < length_ref[0]
    output[...] = jnp.where(in_slot, normed_two * gain_two + shift_two, 0.0).astype(low)
    grad_final = jnp.where(in_slot, cotangent[...].astype(full), 0.0)
    totals[4:5, :] = column_total(grad_final * normed_two)
    totals[5:6, :] = column_total(grad_final)
    grad_resid = norm_back(grad_final, gain_two, normed_two, factor_two)
    grad_two[...] = grad_resid
    grad_down[...] = grad_resid.astype(low)
    totals[3:4, :] = column_total(grad_down[...].astype(full))
    pl.semaphore_wait(barrier, 2)

    def down_piece(ref, line, column, far, core):
        dest = 2 * line + (place.x if column == 0 else 1 - place.x)
        y = place.y if far == 0 else 1 - place.y
        return ref.at[pl.ds(pl.multiple_of(dest * 4 * shard + (2 * y + core) * shard, shard), shard)]

    def side_piece(ref, line, column, core):
        dest = 2 * line + (place.x if column == 0 else 1 - place.x)
        half = ref.shape[1] // 2
        return ref.at[
            pl.ds(pl.multiple_of(dest * shard, shard), shard), pl.ds(pl.multiple_of(core * half, half), half)
        ]

    def down_share(line, column, far):
        return remote(
            down_piece(down_grad, line, column, far, 1 - place.c), down_sum.at[column, line, far],
            c_send.at[2 + far, column, line], c_recv.at[2 + far, column, line], place.core,
        )

    def side_slot(array, line, column):
        return out_sum.at[line, column] if array == 1 else up_sum.at[column, line]

    def over_y(line):
        return remote(down_sum.at[1, line, 1], from_y.at[line], y_send.at[line], y_recv.at[line], place.across_y)

    def side_share(array, line, column):
        grad = (up_grad, out_grad)[array]
        return remote(
            side_piece(grad, line, column, 1 - place.c), side_slot(array, line, column),
            c_send.at[array, column, line], c_recv.at[array, column, line], place.core,
        )

    def down_save(column, line):
        return pltpu.make_async_copy(down_sum.at[column, line], down_out.at[column, line], save_sem.at[2, column, line])

    def side_saves(array, column, line):
        if array == 1:
            return [pltpu.make_async_copy(
                side_slot(1, line, column), out_out.at[line, column], save_sem.at[1, column, line]
            )]
        return [
            pltpu.make_async_copy(
                up_sum.at[column, line, :, chunk_lanes(place.y if far == 0 else 1 - place.y)],
                up_out.at[column, line, far], save_sem.at[3 * far, column, line],
            )
            for far in range(2)
        ]

    def add_far(column, line):
        down_share(line, column, 1).wait_recv()
        down_sum[column, line, 1] = add_low(
            down_sum[column, line, 1], down_piece(down_grad, line, column, 1, place.c)[...]
        )

    def down_chunk(line, carry):
        lanes = chunk_lanes(line)
        down_grad[lanes, :] = mul(hidden[:, lanes], grad_down[...], TN).astype(low)
        for far in (1, 0):
            for column in (1, 0):
                down_share(line, column, far).start()

        @pl.when(line > 0)
        def _():
            add_far(1, line - 1)
            over_y(line - 1).start()

        return carry

    lax.fori_loop(0, 4, down_chunk, 0)
    add_far(1, 3)
    over_y(3).start()
    grad_mid[...] = grad_two[...]

    def back_chunk(turn, carry):
        j = lax.rem(2 * (1 - place.c) + turn, 4)
        lanes = chunk_lanes(j)
        grad_up = (mul(grad_down[...], down_w[lanes, :], NT) * slope[:, lanes]).astype(low)
        up_total[0:1, lanes] = column_total(grad_up.astype(full))
        up_grad[:, lanes] = mul(middle_low[...], grad_up, TN).astype(low)
        grad_mid[...] += mul(grad_up, up_w[:, lanes], NT)

        @pl.when(turn == 1)
        def _():
            for column in (1, 0):
                for line in LINES:
                    side_share(0, line, column).start()

        return carry

    lax.fori_loop(0, 4, back_chunk, 0)
    grad_middle = grad_mid[...]
    normed = normed_one[...]
    totals[1:2, :] = column_total(grad_middle * normed)
    totals[2:3, :] = column_total(grad_middle)
    grad_one = norm_back(grad_middle, gain_one, normed, factor_one)
    resid_out[...] = grad_one
    grad_branch = grad_one.astype(low)
    totals[0:1, :] = column_total(grad_branch.astype(full))
    out_grad[...] = mul(attended[...], grad_branch).astype(low)
    for column in (1, 0):
        for line in LINES:
            side_share(1, line, column).start()
    grad_own[...] = mul(out_w[...], grad_branch, NT).astype(low)

    def add_down(column, line):
        down_share(line, column, 0).wait_recv()
        down_sum[column, line, 0] = add_low(
            down_sum[column, line, 0], down_piece(down_grad, line, column, 0, place.c)[...]
        )
        if column == 0:
            add_far(column, line)
        else:
            over_y(line).wait()
            down_sum[column, line, 0] = add_low(down_sum[column, line, 0], from_y[line])
        down_save(column, line).start()

    def add_side(array, column, line):
        slot = side_slot(array, line, column)
        side_share(array, line, column).wait_recv()
        slot[...] = add_low(slot[...], side_piece((up_grad, out_grad)[array], line, column, place.c)[...])
        for save in side_saves(array, column, line):
            save.start()

    for line in LINES:
        add_down(0, line)
    for column in (1, 0):
        for line in LINES:
            add_side(0, column, line)
    vector_out[...] = jnp.zeros_like(vector_out)
    for dest in range(8):
        for index, (line, start) in enumerate(((0, 2), (0, 3), (1, 0), (2, 1), (2, 2), (2, 3))):
            vector_out[dest, line : line + 1, start * shard : (start + 1) * shard] = totals[
                index : index + 1, dest * shard : (dest + 1) * shard
            ]
        base = dest * 4 * shard
        vector_out[dest, 1:2, shard:] = up_total[0:1, base : base + 3 * shard]
        vector_out[dest, 2:3, :shard] = up_total[0:1, base + 3 * shard : base + 4 * shard]
    for column in range(2):
        for line in range(4):
            add_side(1, column, line)
    for line in LINES:
        add_down(1, line)
    for column in range(2):
        for line in range(4):
            for array in range(2):
                side_share(array, line, column).wait_send()
                for save in side_saves(array, column, line):
                    save.wait()
            for far in range(2):
                down_share(line, column, far).wait_send()
            down_save(column, line).wait()


def middle_part(lengths, cotangent, small, up_bias, rows_full, attended, up_full, down_full, out_full):
    rows, width = cotangent.shape
    ff = up_full.shape[1]
    shard = width // 8
    vmem = pl.BlockSpec(memory_space=pltpu.VMEM)
    anywhere = pl.BlockSpec(memory_space=pl.ANY)
    dma = pltpu.SemaphoreType.DMA

    def held(*shape, kind=low):
        return pltpu.VMEM(shape, kind)

    def shaped(*shape, kind=low):
        return jax.ShapeDtypeStruct(shape, kind)

    up_parts, down_parts, out_parts = (2, 4, shard, ff // 2), (2, 4, 2, ff // 32, width), (4, 2, shard, width // 2)
    return pl.pallas_call(
        middle_kernel,
        in_specs=[pl.BlockSpec(memory_space=pltpu.SMEM)] + [vmem] * 3 + [anywhere] * 5,
        out_specs=[vmem] * 4 + [anywhere] * 3,
        out_shape=[
            shaped(rows, width), shaped(rows, width, kind=full), shaped(width, rows),
            shaped(8, 16, 4 * shard, kind=full), shaped(*down_parts), shaped(*down_parts), shaped(*out_parts),
        ],
        scratch_shapes=[
            held(rows, width), held(width, rows), held(width, ff), held(ff, width), held(width, width), held(rows, ff), held(rows, ff, kind=full),
            held(rows, width, kind=full), held(rows, width), held(rows, width), held(rows, width, kind=full),
            held(rows, width, kind=full), held(8, width, kind=full), held(8, ff, kind=full),
            held(width, ff), held(ff, width), held(width, width), held(*up_parts), held(*down_parts),
            held(*out_parts), held(4, ff // 32, width), dma((11,)), dma((4, 2, 4)), dma((4, 2, 4)),
            dma((4, 2, 4)), dma((4,)), dma((4,)),
        ],
        compiler_params=pltpu.CompilerParams(
            vmem_limit_bytes=VMEM_BYTES, collective_id=2, has_side_effects=True
        ),
        name="middle",
    )(lengths, cotangent, small, up_bias, rows_full, attended, up_full, down_full, out_full)


def finish_kernel(
    output_in, input_in, qkv_in, vector_in, up_in, down_in, out_in, read_in, write_in,
    output, input_out, read_out, write_out, qkv_out, qv_out, out_out, out_b, gain_one, shift_one, up_out, up_b,
    down_out, down_b, gain_two, shift_two,
):
    shard = out_b.shape[1]
    output[...] = output_in[...]
    input_out[...] = input_in[...]
    for given, out in ((read_in, read_out), (write_in, write_out)):
        for line in range(given.shape[0]):
            out[line] = given[line : line + 1]
    for given, out in ((qkv_in, qkv_out), (up_in, up_out), (down_in, down_out), (out_in, out_out)):
        out[...] = given[...].astype(full)
    qv_out[...] = vector_in[0:1, : 2 * shard]
    out_b[...] = vector_in[0:1, 2 * shard : 3 * shard]
    gain_one[...] = vector_in[0:1, 3 * shard :]
    shift_one[...] = vector_in[1:2, :shard]
    up_b[:, : 3 * shard] = vector_in[1:2, shard:]
    up_b[:, 3 * shard :] = vector_in[2:3, :shard]
    down_b[...] = vector_in[2:3, shard : 2 * shard]
    gain_two[...] = vector_in[2:3, 2 * shard : 3 * shard]
    shift_two[...] = vector_in[2:3, 3 * shard :]


def finish(output, input_grad, qkv_grad, vectors, up_grad, down_grad, out_grad, grad_read, grad_write):
    shard = qkv_grad.shape[0]

    def shaped(*shape, kind=full):
        return jax.ShapeDtypeStruct(shape, kind)

    line = shaped(1, shard)
    steps = 2

    def rows(array):
        return pl.BlockSpec((array.shape[0] // steps,) + array.shape[1:], lambda i: (i, 0))

    def once(*shape):
        return pl.BlockSpec(shape, lambda i: (0,) * len(shape))

    lone = once(1, shard)
    memory = (grad_read.shape[0], 1, grad_read.shape[1])
    return pl.pallas_call(
        finish_kernel,
        grid=(steps,),
        in_specs=[
            rows(output), rows(input_grad), rows(qkv_grad), once(*vectors.shape), rows(up_grad), rows(down_grad),
            rows(out_grad), once(*grad_read.shape), once(*grad_write.shape),
        ],
        out_specs=[
            rows(output), rows(input_grad), once(*memory), once(*memory), rows(qkv_grad), once(1, 2 * shard),
            rows(out_grad), lone, lone, lone, rows(up_grad), once(1, 4 * shard), rows(down_grad), lone, lone, lone,
        ],
        out_shape=[
            shaped(*output.shape, kind=low), shaped(*input_grad.shape), shaped(*memory), shaped(*memory),
            shaped(*qkv_grad.shape), shaped(1, 2 * shard), shaped(*out_grad.shape), line, line, line,
            shaped(*up_grad.shape), shaped(1, 4 * shard), shaped(*down_grad.shape), line, line, line,
        ],
        compiler_params=pltpu.CompilerParams(vmem_limit_bytes=VMEM_BYTES),
        name="finish",
    )(output, input_grad, qkv_grad, vectors, up_grad, down_grad, out_grad, grad_read, grad_write)


def normalize(values, gain_vec, shift_vec):
    centre = values - jnp.mean(values, axis=-1, keepdims=True)
    factor = lax.rsqrt(jnp.mean(centre * centre, axis=-1, keepdims=True) + norm_epsilon)
    return centre * factor * gain_vec + shift_vec


def column_sums(values):
    return jnp.sum(values, axis=0, dtype=full)


def on_block(
    tokens, read_rows, write_rows, lengths, qkv_weight, vectors, out_weight, up_weight, down_weight, cotangent
):
    total = sum(vector.shape[0] for vector in vectors)
    packed, start = jnp.zeros((1, total), full), 0
    for vector in vectors:
        size = vector.shape[0]
        packed = packed + jnp.pad(vector.astype(full).reshape(1, -1), ((0, 0), (start, total - start - size)))
        start += size
    (small, up_bias, rows, weight, q_t, k_t, k_wide, v_wide, mixed, row_stats, up_full, down_full, out_full,
     attended) = front(
        lengths, tokens, read_rows, write_rows, qkv_weight, packed, up_weight, down_weight, out_weight
    )
    output, resid, grad_own, vector_parts, up_parts, down_parts, out_parts = middle_part(
        lengths, cotangent, small, up_bias, rows, attended, up_full, down_full, out_full
    )
    saved = (q_t, k_t, k_wide, v_wide, mixed, row_stats)
    input_grad, grad_read, grad_write, qkv_grad, vector_sum, up_grad, down_grad, out_grad = back(
        lengths, grad_own, saved, vector_parts, rows, weight, resid, up_parts, down_parts, out_parts
    )
    results = finish(
        output, input_grad, qkv_grad, vector_sum, up_grad, down_grad, out_grad, grad_read, grad_write
    )
    shaped = [jnp.swapaxes(result, 0, 1) if index in (2, 3) else result for index, result in enumerate(results)]
    return tuple(result.reshape(-1) if result.shape[0] == 1 and result.ndim == 2 else result for result in shaped)


def per_device(
    tokens, read_memory, write_memory, lengths, qkv_weight, qv_bias, out_weight, out_bias, norm1_gain,
    norm1_bias, up_weight, up_bias, down_weight, down_bias, norm2_gain, norm2_bias, cotangent,
):
    seq_count = lax.axis_size("seq")
    fsdp_count = lax.axis_size("fsdp")
    seq_place = lax.axis_index("seq")
    local_rows, width = tokens.shape
    head_cols = width // seq_count
    shard = width // fsdp_count
    length = lengths[0]
    heads = head_cols // HEAD
    vectors = (qv_bias, out_bias, norm1_gain, norm1_bias, up_bias, down_bias, norm2_gain, norm2_bias)
    if (fsdp_count, seq_count) == (8, 4):
        return on_block(
            tokens, read_memory[0], write_memory[0], lengths, qkv_weight, vectors, out_weight, up_weight, down_weight,
            cotangent,
        )
    places = seq_place * local_rows + jnp.arange(local_rows, dtype=jnp.int32)
    in_slot = (places < length)[:, None]
    memory_slots = jnp.arange(MEM, dtype=jnp.int32)
    pick_read = places[:, None] == memory_slots[None, :]
    pick_write = places[:, None] == length - MEM + memory_slots[None, :]
    is_memory = jnp.any(pick_read | pick_write, axis=1)[:, None]
    picks = jnp.concatenate([pick_read, pick_write], axis=1).astype(full)
    memory = jnp.concatenate([read_memory[0], write_memory[0]], axis=0)
    layer_in = jnp.where(is_memory, mul(picks.astype(low), memory).astype(low), tokens)

    own_shard = lax.dynamic_slice_in_dim(
        qkv_weight.reshape(shard, 3, seq_count, heads, HEAD), seq_place, 1, 2
    )
    own_shard = jnp.transpose(own_shard[:, :, 0], (0, 2, 1, 3)).reshape(shard, 3 * head_cols)
    packed = jnp.concatenate(vectors)
    rows = lax.all_gather(layer_in, "seq", axis=0, tiled=True)
    weight = lax.all_gather(own_shard, "fsdp", axis=0, tiled=True)
    packed = lax.all_gather(packed.reshape(1, -1), "fsdp", axis=0, tiled=True).astype(full)
    whole, start = [], 0
    for vector in vectors:
        whole.append(packed[:, start : start + vector.shape[0]].reshape(-1))
        start += vector.shape[0]
    qv_vec, out_vec, gain_one, shift_one, up_vec, down_vec, gain_two, shift_two = whole
    own_qv = lax.dynamic_slice_in_dim(qv_vec.reshape(2, seq_count, head_cols), seq_place, 1, 1)
    bias = jnp.concatenate([own_qv[0, 0], own_qv[1, 0]])
    bias = jnp.broadcast_to(bias, (8, bias.shape[0]))
    out_full = lax.all_gather(out_weight, "fsdp", axis=0, tiled=True)
    up_full = lax.all_gather(up_weight, "fsdp", axis=0, tiled=True)
    down_full = lax.all_gather(down_weight, "fsdp", axis=0, tiled=True)
    q_x, k_t, k_wide, v_wide, mixed, mixed_low, row_stats = attention_forward(lengths, rows, weight, bias)
    attended = lax.all_to_all(mixed_low, "seq", split_axis=1, concat_axis=0, tiled=True)
    resid_one = layer_in.astype(full) + mul(attended, out_full, TN) + out_vec
    middle, norm_one_back = jax.vjp(normalize, resid_one, gain_one, shift_one)
    middle_low = middle.astype(low)
    up_pre = mul(middle_low, up_full) + up_vec
    gelu_out, gelu_back = jax.vjp(partial(jax.nn.gelu, approximate=False), up_pre)
    hidden = gelu_out.astype(low)
    down_pre = mul(hidden, down_full) + down_vec
    final, norm_two_back = jax.vjp(normalize, middle + down_pre, gain_two, shift_two)
    output = jnp.where(in_slot, final, 0.0).astype(low)
    grad_final = jnp.where(in_slot, cotangent.astype(full), 0.0)
    grad_resid_two, grad_gain_two, grad_shift_two = norm_two_back(grad_final)
    grad_down = grad_resid_two.astype(low)
    grad_down_weight = mul(hidden, grad_down, TN)
    (grad_up_pre,) = gelu_back(mul(grad_down, down_full, NT))
    grad_up = grad_up_pre.astype(low)
    grad_up_weight = mul(middle_low, grad_up, TN)
    grad_middle = grad_resid_two + mul(grad_up, up_full, NT)
    grad_resid_one, grad_gain_one, grad_shift_one = norm_one_back(grad_middle)
    grad_branch = grad_resid_one.astype(low)
    grad_out_weight = mul(attended, grad_branch)
    grad_attended = mul(out_full, grad_branch, NT).astype(low)
    vector_grads = [
        column_sums(grad_branch), grad_gain_one, grad_shift_one, column_sums(grad_up),
        column_sums(grad_down), grad_gain_two, grad_shift_two,
    ]
    packed_grad = jnp.concatenate([v.reshape(fsdp_count, -1) for v in vector_grads], axis=1)
    saved = (q_x, k_t, k_wide, v_wide, mixed, row_stats)
    grad_t = lax.all_to_all(grad_attended, "seq", split_axis=0, concat_axis=1, tiled=True)
    partial_in, weight_part, sums = attention_backward(*saved, grad_t, rows, weight)
    from_heads = lax.psum_scatter(partial_in, "seq", scatter_dimension=0, tiled=True).astype(full)
    grad_layer_in = grad_resid_one + from_heads
    input_grad = jnp.where(is_memory, 0.0, grad_layer_in)
    grad_memory = lax.dot_general(
        picks, grad_layer_in, TN, precision=lax.Precision.HIGHEST, preferred_element_type=full
    )
    grad_memory = lax.psum(grad_memory.astype(low), "seq").astype(full)
    grad_read, grad_write = grad_memory[:MEM], grad_memory[MEM:]
    sums = sums[:, 0].reshape(heads, 3, HEAD)
    own_sums = jnp.stack([sums[:, 0].reshape(-1), sums[:, 2].reshape(-1)])[:, None]
    zero_qv = jnp.zeros((2, seq_count, head_cols), full)
    qv_grad = lax.dynamic_update_slice_in_dim(zero_qv, own_sums, seq_place, 1)
    packed_grad = jnp.concatenate([qv_grad.reshape(fsdp_count, -1), packed_grad], axis=1)
    packed_sum = lax.psum(packed_grad, ("fsdp", "seq"))
    own_vectors = lax.dynamic_index_in_dim(packed_sum, lax.axis_index("fsdp"), 0, False)

    def both_axes(part):
        piece = lax.psum_scatter(part.astype(low), "fsdp", scatter_dimension=0, tiled=True)
        return lax.psum(piece, "seq").astype(full)

    qkv_piece = lax.psum_scatter(weight_part, "fsdp", scatter_dimension=0, tiled=True)
    qkv_parts = lax.all_gather(qkv_piece, "seq", axis=0).reshape(seq_count, shard, heads, 3, HEAD)
    qkv_out = jnp.transpose(qkv_parts, (1, 3, 0, 2, 4)).reshape(shard, 3 * width).astype(full)
    up_out, down_out, out_out = both_axes(grad_up_weight), both_axes(grad_down_weight), both_axes(grad_out_weight)
    vector_outs, start = [], 0
    for vector in vectors:
        vector_outs.append(own_vectors[start : start + vector.shape[0]])
        start += vector.shape[0]
    qv_out, out_b_out, gain_one_out, shift_one_out, up_b_out, down_b_out, gain_two_out, shift_two_out = vector_outs
    return (
        output, input_grad, grad_read[None], grad_write[None], qkv_out, qv_out, out_out, out_b_out, gain_one_out,
        shift_one_out, up_out, up_b_out, down_out, down_b_out, gain_two_out, shift_two_out,
    )


def solution(mesh):
    rows, piece = P(("fsdp", "seq"), None), P("fsdp")
    matrix, memory = P("fsdp", None), P("fsdp", None, None)
    in_specs = (
        rows, memory, memory, piece, matrix, piece, matrix, piece, piece, piece, matrix, piece, matrix,
        piece, piece, piece, rows,
    )
    out_specs = (
        rows, rows, memory, memory, matrix, piece, matrix, piece, piece, piece, matrix, piece, matrix,
        piece, piece, piece,
    )
    return jax.shard_map(per_device, mesh=mesh, in_specs=in_specs, out_specs=out_specs, check_vma=False)
```
